32 devices in a mesh: group: 8 (over y, x, core), expert: 4 (over z).
Axes of the slice: x: 2, y: 2, z: 4, core: 2. Of those that a mesh axis runs over, the one named last changes fastest.
Arguments:
- tokens: bfloat16 [8192, 1024], P(('group', 'expert')), may hold values from -6 to 6
- lengths: int32 [8], P('group'), may hold values from 256 to 1024, as said below
- routes: int32 [8192, 8], P(('group', 'expert')), may hold values from 0 to 31, all different within a row; in each aligned block of 256 rows (0 to 255, 256 to 511, ...) at most 96 rows name the same one
- norm_gain1: bfloat16 [1024], P('expert'), may hold values from 0.5 to 1.5
- w_query: bfloat16 [1024, 1024], P('expert'), may hold values from -0.375 to 0.375
- key_projection: bfloat16 [1024, 512], P('expert'), may hold values from -0.1875 to 0.1875
- value_projection: bfloat16 [1024, 512], P('expert'), may hold values from -0.1875 to 0.1875
- w_out: bfloat16 [1024, 1024], P('expert'), may hold values from -1.5 to 1.5
- norm_gain2: bfloat16 [1024], P('expert'), may hold values from 0.5 to 1.5
- w_router: bfloat16 [1024, 32], P('expert'), may hold values from -0.09375 to 0.09375
- w_gate: bfloat16 [32, 1024, 512], P('expert'), may hold values from -0.1875 to 0.1875
- w_up: bfloat16 [32, 1024, 512], P('expert'), may hold values from -0.1875 to 0.1875
- w_down: bfloat16 [32, 512, 1024], P('expert'), may hold values from -1 to 1
- cotangent: bfloat16 [8192, 1024], P(('group', 'expert')), may hold values from -6 to 6
Outputs:
- mixed: bfloat16 [8192, 1024], P(('group', 'expert'))
- grad_tokens: float32 [8192, 1024], P(('group', 'expert'))
- grad_gain1: float32 [1024], P('expert')
- grad_query: float32 [1024, 1024], P('expert')
- grad_key: float32 [1024, 512], P('expert')
- grad_value: float32 [1024, 512], P('expert')
- grad_out: float32 [1024, 1024], P('expert')
- grad_gain2: float32 [1024], P('expert')
- grad_router: float32 [1024, 32], P('expert')
- grad_gate: float32 [32, 1024, 512], P('expert')
- grad_up: float32 [32, 1024, 512], P('expert')
- grad_down: float32 [32, 512, 1024], P('expert')
The draws below stay inside these ranges and needn't reach their ends.
Inputs may be any that keep to these rules, and one draw needn't show every extreme that they name: The first lengths[s] slots of sequence s are valid; one sequence fills all 1024 slots and one holds 256. `routes`: a slot's 8 experts differ; among the rows of one device at most 96 name one expert, and in every draw some expert is named by exactly 96 of them.
All inputs are finite; a program needn't handle non-finite values.
Results may differ from the reference program's by a relative error of at most 0.028.
Values may be sent and summed in bfloat16 or wider, within the bound.
A program may use at most 256 MiB of HBM per device.

```python
import math
import jax
import jax.numpy as jnp
import numpy as np
from jax import lax

D = 1024
QUERY_HEADS = 16
KEY_VALUE_HEADS = 8
HEAD_DIMENSION = 64
FF = 512
EXPERTS = 32
TOP = 8
SEQUENCE_SLOTS = 1024
ROWS = 256
SEQS = 8
TOKENS = 8192
CAP = 96
QW = 1024
KW = 512
N_EXPERT = 4


def draw_lengths(key, part):
    ranking = jax.random.permutation(jax.random.fold_in(key, 1), SEQS)
    spread = jax.random.randint(jax.random.fold_in(key, 2), (SEQS,), SEQUENCE_SLOTS // 4, SEQUENCE_SLOTS + 1)
    spread = jnp.where(ranking == 0, SEQUENCE_SLOTS, spread)
    return jnp.where(ranking == 1, SEQUENCE_SLOTS // 4, spread).astype(jnp.int32)


def shard_levels(rng, dims, split, smallest, largest):
    gain, own = 1.0, jax.random.fold_in(rng, 6)
    for dim, parts in split:
        steps = jnp.exp(jax.random.uniform(jax.random.fold_in(own, dim), (parts,), jnp.float32, smallest / len(split), largest / len(split)))
        gain = gain * jnp.repeat(steps, dims[dim] // parts).reshape([-1 if axis == dim else 1 for axis in range(len(dims))])
    return gain


def deal_out(stream_key, own, number, rows, amount, top, limit, slope):
    sequence = jax.random.permutation(stream_key, amount)
    packed, usual = load_shares(amount, rows * top, limit, slope, True), load_shares(amount, rows * top, limit, slope, False)
    places = jnp.arange(amount)

    def named(sizes, rotation):
        used = int((sizes > 0).sum())
        fixed = max(1, used // 4)
        shifted = fixed + (places - fixed + rotation * (used - fixed)) % max(1, amount - fixed)
        return jnp.zeros((amount,), jnp.int32).at[sequence[jnp.where(places < fixed, places, shifted)]].set(jnp.asarray(sizes, jnp.int32))

    sizes = jnp.where(number % 4 == 0, named(packed, number // 4), named(usual, number - number // 4 - 1))
    mixed = jax.random.permutation(jax.random.fold_in(own, 3), amount)
    source_of, taker = mixed[0:amount // 2 * 2:2], mixed[1:amount // 2 * 2:2]
    room = jnp.minimum(sizes[source_of] - 1, limit - sizes[taker]) // 2
    room = jnp.where((source_of == sequence[0]) | (taker == sequence[0]) | (sizes[taker] == 0), 0, jnp.maximum(room, 0))
    shifted = jax.random.randint(jax.random.fold_in(own, 4), (amount // 2,), 0, 1 << 20) % (room + 1)
    sizes = sizes.at[source_of].add(-shifted).at[taker].add(shifted)
    items = jnp.searchsorted(jnp.cumsum(sizes), jnp.arange(rows * top), side="right").astype(jnp.int32)
    table = items.reshape(top, rows).T
    table = table[jax.random.permutation(jax.random.fold_in(own, 1), rows)]
    rotation = jax.random.randint(jax.random.fold_in(own, 2), (rows, 1), 0, top)
    return jnp.take_along_axis(table, (jnp.arange(top)[None, :] + rotation) % top, axis=1)


def load_shares(number_of, total, bound, slope, full):
    weights = [(1 << 20) // math.isqrt(grade ** slope) + 1 for grade in range(1, number_of + 1)]
    largest = bound if full else min(bound, max(-(-total // number_of), total * weights[0] // sum(weights)))
    least = 1 if total - largest >= number_of - 1 else 0
    given, rest = [largest] + [least] * (number_of - 1), total - largest - least * (number_of - 1)
    while rest > 0:
        candidates = [i for i in range(1, number_of) if given[i] < largest] or [i for i in range(1, number_of) if given[i] < bound]
        pool, left = sum([weights[i] for i in candidates]), rest
        for i in candidates:
            more = min(bound - given[i], max(1, left * weights[i] // pool), rest)
            given[i] = given[i] + more
            rest = rest - more
    return np.array(given)


def noise(key, extent, width, bound, pieces=(), held_as=jnp.bfloat16):
    level = shard_levels(key, extent, pieces, -0.22, 0.18) if pieces else 1.0
    result = jax.random.normal(key, extent, jnp.float32) * width * level
    return jnp.minimum(jnp.maximum(result, -bound), bound).astype(held_as)


def setup_inputs(seed: int = 0) -> dict:
    seeds = jax.random.split(jax.random.key(seed), 15)
    tokens = noise(seeds[0], (TOKENS, D), 1.0, 6.0, ((0, 32),))
    lengths = draw_lengths(jax.random.fold_in(seeds[14], 71), 0)
    routes_keys = jax.random.split(jax.random.fold_in(seeds[2], 1), TOKENS // ROWS)
    routes_turns = jax.random.permutation(jax.random.fold_in(seeds[2], 3), TOKENS // ROWS)
    routes = jax.vmap(lambda own, number: deal_out(jax.random.fold_in(seeds[2], 2), own, number, ROWS, EXPERTS, TOP, CAP, 1))(routes_keys, routes_turns).reshape((TOKENS, TOP))
    norm_gain1 = jnp.clip(1.0 + 0.1 * jax.random.normal(seeds[3], (D,), jnp.float32), 0.5, 1.5).astype(jnp.bfloat16)
    w_query = noise(seeds[4], (D, QW), (D // 4) ** -0.5, 0.375, ((0, 4),))
    key_projection = noise(seeds[5], (D, KW), D ** -0.5, 0.1875, ((0, 4),))
    value_projection = noise(seeds[6], (D, KW), D ** -0.5, 0.1875, ((0, 4),))
    w_out = noise(seeds[7], (QW, D), (QW // 64) ** -0.5, 1.5, ((0, 4),))
    norm_gain2 = jnp.clip(1.0 + 0.1 * jax.random.normal(seeds[8], (D,), jnp.float32), 0.5, 1.5).astype(jnp.bfloat16)
    w_router = noise(seeds[9], (D, EXPERTS), (4 * D) ** -0.5, 0.09375, ((0, 4),))
    w_gate = noise(seeds[10], (EXPERTS, D, FF), D ** -0.5, 0.1875, ((0, 4),))
    w_up = noise(seeds[11], (EXPERTS, D, FF), D ** -0.5, 0.1875, ((0, 4),))
    w_down = noise(seeds[12], (EXPERTS, FF, D), (FF // 16) ** -0.5, 1.0, ((0, 4),))
    cotangent = noise(seeds[13], (TOKENS, D), 1.0, 6.0, ((0, 32),))
    return {"tokens": tokens, "lengths": lengths, "routes": routes, "norm_gain1": norm_gain1, "w_query": w_query, "key_projection": key_projection, "value_projection": value_projection, "w_out": w_out, "norm_gain2": norm_gain2, "w_router": w_router, "w_gate": w_gate, "w_up": w_up, "w_down": w_down, "cotangent": cotangent}


EPSILON = 1e-05
NEGATIVE_LARGE = -1e+30
EXACT_MATMUL = lax.Precision.HIGHEST

@jax.custom_vjp
def reduced_precision(v):
    return lax.optimization_barrier(v.astype(jnp.bfloat16)).astype(jnp.float32)

@jax.custom_vjp
def reduced_backward(v):
    return v

def low_keep(v):
    return (reduced_precision(v), None)

def low_pass(kept, grad):
    return (grad,)

def back_keep(v):
    return (v, None)

def back_low(kept, grad):
    return (reduced_precision(grad),)
reduced_precision.defvjp(low_keep, low_pass)
reduced_backward.defvjp(back_keep, back_low)

def rms_norm(tensor_in, gain_vector):
    inverse_rms = lax.rsqrt(lax.optimization_barrier(jnp.mean(tensor_in * tensor_in, axis=-1, keepdims=True)) + EPSILON)
    return tensor_in * inverse_rms * gain_vector

def rotary(tensor_in, positions):
    half_width = tensor_in.shape[-1] // 2
    frequency = 10000.0 ** (-2.0 * jnp.arange(half_width).astype(jnp.float32) / tensor_in.shape[-1])
    angles = positions.astype(jnp.float32)[:, None] * frequency[None, :]
    cosine_lookup = jnp.cos(angles)[:, None, :]
    sine_lookup = jnp.sin(angles)[:, None, :]
    first_half = tensor_in[..., :half_width]
    second_half = tensor_in[..., half_width:]
    return jnp.concatenate([first_half * cosine_lookup - second_half * sine_lookup, second_half * cosine_lookup + first_half * sine_lookup], axis=-1)

def slot_tables(route_seq):
    flat_routes = route_seq.reshape(N_EXPERT, ROWS * TOP)
    one_hot = (flat_routes[:, :, None] == jnp.arange(EXPERTS, dtype=jnp.int32)[None, None, :]).astype(jnp.int32)
    slot_rank = lax.optimization_barrier(jnp.sum((jnp.cumsum(one_hot, axis=1) - one_hot) * one_hot, axis=-1))
    source = jnp.arange(N_EXPERT, dtype=jnp.int32)[:, None]
    slot_index = (flat_routes * (N_EXPERT * CAP) + source * CAP + slot_rank).reshape(-1).astype(jnp.int32)
    slot_table = jnp.full((EXPERTS * N_EXPERT * CAP,), SEQUENCE_SLOTS * TOP, jnp.int32)
    slot_table = slot_table.at[slot_index].set(jnp.arange(SEQUENCE_SLOTS * TOP, dtype=jnp.int32))
    return (slot_index, slot_table)

def attention(query_rows, key_heads, value_rows, length):
    rows_per_block = min(512, SEQUENCE_SLOTS)
    queries_per_group = QUERY_HEADS // KEY_VALUE_HEADS
    block_list = query_rows.reshape(SEQUENCE_SLOTS // rows_per_block, rows_per_block, KEY_VALUE_HEADS, queries_per_group, HEAD_DIMENSION)
    starts = jnp.arange(SEQUENCE_SLOTS // rows_per_block, dtype=jnp.int32) * rows_per_block
    columns = jnp.arange(SEQUENCE_SLOTS, dtype=jnp.int32)

    def one_block(block_pair):
        query_part, first_row = block_pair
        scores = jnp.einsum('qhgd,khd->hgqk', query_part, key_heads, precision=EXACT_MATMUL) * HEAD_DIMENSION ** (-0.5)
        scores = reduced_backward(scores)
        row_index = first_row + jnp.arange(rows_per_block, dtype=jnp.int32)
        allowed = (columns[None, :] <= row_index[:, None]) & (columns[None, :] < length)
        scores = jnp.where(allowed, scores, NEGATIVE_LARGE)
        probability = reduced_precision(jax.nn.softmax(scores, axis=-1))
        return jnp.einsum('hgqk,khd->qhgd', probability, value_rows, precision=EXACT_MATMUL)
    mixed = lax.map(jax.checkpoint(one_block), (block_list, starts))
    return mixed.reshape(SEQUENCE_SLOTS, QUERY_HEADS * HEAD_DIMENSION)

def block_layer(token_seq, gain_one, w_query, key_projection, value_projection, w_out, gain_two, w_router, w_gate, w_up, w_down, length, route_seq, slot_index, slot_table):
    positions = jnp.arange(SEQUENCE_SLOTS, dtype=jnp.int32)
    pre_attention_norm = reduced_precision(rms_norm(token_seq, gain_one))
    query_pre = reduced_backward(jnp.dot(pre_attention_norm, w_query, precision=EXACT_MATMUL)).reshape(SEQUENCE_SLOTS, QUERY_HEADS, HEAD_DIMENSION)
    unrotated_key = reduced_backward(jnp.dot(pre_attention_norm, key_projection, precision=EXACT_MATMUL)).reshape(SEQUENCE_SLOTS, KEY_VALUE_HEADS, HEAD_DIMENSION)
    value_rows = reduced_backward(reduced_precision(jnp.dot(pre_attention_norm, value_projection, precision=EXACT_MATMUL))).reshape(SEQUENCE_SLOTS, KEY_VALUE_HEADS, HEAD_DIMENSION)
    query_rows = reduced_precision(rotary(query_pre, positions))
    key_heads = reduced_precision(rotary(unrotated_key, positions))
    mixed = reduced_backward(reduced_precision(attention(query_rows, key_heads, value_rows, length)))
    residual = token_seq + reduced_backward(jnp.dot(mixed, w_out, precision=EXACT_MATMUL))
    second_norm = reduced_precision(rms_norm(residual, gain_two))
    logits = reduced_backward(jnp.dot(second_norm, w_router, precision=EXACT_MATMUL))
    chosen = jnp.take_along_axis(logits, route_seq, axis=1)
    gate_weights = jax.nn.softmax(chosen, axis=-1)
    copies = reduced_backward(jnp.broadcast_to(second_norm[:, None, :], (SEQUENCE_SLOTS, TOP, D))).reshape(SEQUENCE_SLOTS * TOP, D)
    padded = jnp.concatenate([copies, jnp.zeros((1, D), copies.dtype)], axis=0)
    inputs = padded[slot_table].reshape(EXPERTS, N_EXPERT * CAP, D)
    gate_pre = reduced_backward(jnp.einsum('erd,edf->erf', inputs, w_gate, precision=EXACT_MATMUL))
    up_pre = reduced_backward(jnp.einsum('erd,edf->erf', inputs, w_up, precision=EXACT_MATMUL))
    activation = reduced_precision(jax.nn.silu(gate_pre) * up_pre)
    expert_out = reduced_backward(reduced_precision(jnp.einsum('erf,efd->erd', activation, w_down, precision=EXACT_MATMUL)))
    picked = expert_out.reshape(EXPERTS * N_EXPERT * CAP, D)[slot_index].reshape(SEQUENCE_SLOTS, TOP, D)
    expert_sum = lax.optimization_barrier(jnp.sum(gate_weights[:, :, None] * picked, axis=1))
    return residual + expert_sum

def reference(tokens, lengths, routes, norm_gain1, w_query, key_projection, value_projection, w_out, norm_gain2, w_router, w_gate, w_up, w_down, cotangent):
    weights = tuple((weight.astype(jnp.float32) for weight in (norm_gain1, w_query, key_projection, value_projection, w_out, norm_gain2, w_router, w_gate, w_up, w_down)))
    token_all = tokens.astype(jnp.float32).reshape(SEQS, SEQUENCE_SLOTS, D)
    cotangent_all = cotangent.astype(jnp.float32).reshape(SEQS, SEQUENCE_SLOTS, D)
    route_all = routes.reshape(SEQS, SEQUENCE_SLOTS, TOP)

    def one_sequence(totals, sequence_item):
        token_seq, cotangent_seq, length, route_seq = sequence_item
        slot_index, slot_table = slot_tables(route_seq)
        valid_rows = (jnp.arange(SEQUENCE_SLOTS, dtype=jnp.int32) < length).astype(jnp.float32)

        def forward(token_in, *params):
            return block_layer(token_in, *params, length, route_seq, slot_index, slot_table)
        output_seq, pullback = jax.vjp(forward, token_seq, *weights)
        gradients = pullback(cotangent_seq * valid_rows[:, None])
        totals = tuple((total + grad for total, grad in zip(totals, gradients[1:])))
        return (totals, (output_seq.astype(jnp.bfloat16), gradients[0]))
    zero_filled = tuple((jnp.zeros_like(weight) for weight in weights))
    totals, (mixed, grad_tokens) = lax.scan(one_sequence, zero_filled, (token_all, cotangent_all, lengths, route_all))
    return (mixed.reshape(TOKENS, D), grad_tokens.reshape(TOKENS, D), totals[0], totals[1], totals[2], totals[3], totals[4], totals[5], totals[6], totals[7], totals[8], totals[9])
```

```python
import functools

import jax
import jax.numpy as jnp
from jax import lax
from jax.experimental import pallas as pl
from jax.experimental.pallas import tpu as pltpu
from jax.sharding import PartitionSpec as P

D = 1024
QUERY_HEADS = 16
KEY_VALUE_HEADS = 8
HEAD_DIMENSION = 64
EXPERTS = 32
TOP = 8
FF = 512
LANES = 128

EPSILON = 1e-05
NEGATIVE_LARGE = -1e30
BF = jnp.bfloat16
F32 = jnp.float32


def rotary_tables(positions, head_size):
    half_width = head_size // 2
    frequency = 10000.0 ** (-2.0 * jnp.arange(half_width).astype(F32) / head_size)
    angles = positions.astype(F32)[:, None] * frequency[None, :]
    return (jnp.cos(angles)[:, None, :], jnp.sin(angles)[:, None, :])


def apply_rotation(tensor_in, cosine_lookup, sine_lookup):
    half_width = tensor_in.shape[-1] // 2
    first_half = tensor_in[..., :half_width]
    second_half = tensor_in[..., half_width:]
    return jnp.concatenate(
        [
            first_half * cosine_lookup - second_half * sine_lookup,
            second_half * cosine_lookup + first_half * sine_lookup,
        ],
        axis=-1,
    )


def dot(a, b):
    return jnp.dot(a, b, preferred_element_type=F32)


def dot_nt(a, b):
    return lax.dot_general(a, b, (((1,), (1,)), ((), ())), preferred_element_type=F32)


def dot_tn(a, b):
    return lax.dot_general(a, b, (((0,), (0,)), ((), ())), preferred_element_type=F32)


def expert_kernel(
    sizes,
    x_ref,
    ct_ref,
    router_t_ref,
    rank_row_ref,
    rank_col_ref,
    w_gate_ref,
    w_up_ref,
    w_down_ref,
    y_ref,
    gs_ref,
    grad_gate_ref,
    grad_up_ref,
    grad_down_ref,
    xs_ref,
    g_ref,
    gate_slot_ref,
    dots_ref,
):
    blocks, rows, local, capacity = sizes
    slots = local * capacity
    step = pl.program_id(0)
    base = lax.axis_index("expert") * local

    @pl.when(step == 0)
    def _():
        logits = dot_nt(router_t_ref[...], x_ref[...])
        hot = rank_row_ref[...] < 200.0
        top = jnp.max(jnp.where(hot, logits, NEGATIVE_LARGE), axis=0, keepdims=True)
        weight = jnp.where(hot, jnp.exp(jnp.minimum(logits - top, 0.0)), 0.0)
        gates = weight / jnp.sum(weight, axis=0, keepdims=True)
        expert_id = lax.broadcasted_iota(jnp.int32, gates.shape, 0)
        slot_id = lax.broadcasted_iota(jnp.int32, (capacity, rows), 0).astype(F32)
        rank_rows, gate_rows = [], []
        for e in range(local):
            mine = expert_id == base + e
            rank_rows.append(jnp.sum(jnp.where(mine, rank_row_ref[...], 0.0), 0, keepdims=True))
            gate_rows.append(jnp.sum(jnp.where(mine, gates, 0.0), 0, keepdims=True))
        for b in range(blocks):
            here = slice(b * rows, (b + 1) * rows)
            pieces = []
            for e in range(local):
                taken = jnp.broadcast_to(rank_rows[e][:, here], (capacity, rows)) == slot_id
                gate = jnp.sum(jnp.where(taken, gate_rows[e][:, here], 0.0), 1, keepdims=True)
                gate_slot_ref[b, e * capacity : (e + 1) * capacity, :] = gate
                pieces.append(jnp.where(taken, 1.0, 0.0).astype(BF))
            pick = jnp.concatenate(pieces, axis=0)
            xs_ref[b] = dot(pick, x_ref[here, :]).astype(BF)
            g_ref[b] = dot(pick, ct_ref[here, :]).astype(BF)

    here = pl.ds(pl.multiple_of(step * capacity, capacity), capacity)
    xs = jnp.concatenate([xs_ref[b, here, :] for b in range(blocks)], axis=0)
    g = jnp.concatenate([g_ref[b, here, :] for b in range(blocks)], axis=0).astype(F32)
    gate_slot = jnp.concatenate([gate_slot_ref[b, here, :] for b in range(blocks)], axis=0)
    w_gate, w_up, w_down = w_gate_ref[0], w_up_ref[0], w_down_ref[0]
    gate_pre = dot(xs, w_gate)
    up_pre = dot(xs, w_up)
    sigmoid = jax.nn.sigmoid(gate_pre)
    silu = gate_pre * sigmoid
    activation = (silu * up_pre).astype(BF)
    expert_out = dot(activation, w_down).astype(BF).astype(F32)
    slot_dot = jnp.sum(g * expert_out, axis=1, keepdims=True)
    grad_out = (gate_slot * g).astype(BF)
    scaled_out = (gate_slot * expert_out).astype(BF)
    grad_down_ref[0] = dot_tn(activation, grad_out).astype(BF)
    grad_activation = dot_nt(grad_out, w_down)
    grad_gate_pre = (
        grad_activation * up_pre * sigmoid * (1.0 + gate_pre * (1.0 - sigmoid))
    ).astype(BF)
    grad_up_pre = (grad_activation * silu).astype(BF)
    grad_gate_ref[0] = dot_tn(xs, grad_gate_pre).astype(BF)
    grad_up_ref[0] = dot_tn(xs, grad_up_pre).astype(BF)
    grad_in = (dot_nt(grad_gate_pre, w_gate) + dot_nt(grad_up_pre, w_up)).astype(BF)
    lane = lax.broadcasted_iota(jnp.int32, (blocks * capacity, LANES), 1)
    high = slot_dot.astype(BF).astype(F32)
    middle = (slot_dot - high).astype(BF).astype(F32)
    low = slot_dot - high - middle
    mine = base + step
    dots = jnp.where(lane == mine, high, 0.0)
    dots = jnp.where(lane == mine + EXPERTS, middle, dots)
    dots = jnp.where(lane == mine + 2 * EXPERTS, low, dots).astype(BF)
    for b in range(blocks):
        part = slice(b * capacity, (b + 1) * capacity)
        xs_ref[b, here, :] = grad_in[part]
        g_ref[b, here, :] = scaled_out[part]
        dots_ref[b, here, :] = dots[part]

    @pl.when(step == local - 1)
    def _():
        slot_expert = lax.broadcasted_iota(jnp.int32, (EXPERTS, slots), 1) // capacity
        spread_row = lax.broadcasted_iota(jnp.int32, (EXPERTS, slots), 0)
        spread = jnp.where(spread_row == slot_expert + base, 1.0, 0.0).astype(BF)
        slot_rank = (lax.broadcasted_iota(jnp.int32, (rows, slots), 1) % capacity).astype(F32)
        for b in range(blocks):
            there = slice(b * rows, (b + 1) * rows)
            ranks = dot(rank_col_ref[there, :], spread)
            put = jnp.where(ranks == slot_rank, 1.0, 0.0).astype(BF)
            y_ref[there, :] = dot(put, g_ref[b]).astype(BF)
            gs_ref[there, :D] = dot(put, xs_ref[b]).astype(BF)
            gs_ref[there, D:] = dot(put, dots_ref[b]).astype(BF)


def run_experts(x_all, ct_all, router_t, rank_row, rank_col, w_gate, w_up, w_down, rows, capacity):
    total = x_all.shape[0]
    blocks, local = total // rows, w_gate.shape[0]
    slots = local * capacity
    sizes = (blocks, rows, local, capacity)
    whole = lambda shape: pl.BlockSpec(
        shape, lambda e: (0,) * len(shape), pipeline_mode=pl.Buffered(1)
    )
    per = lambda shape: pl.BlockSpec((1,) + shape, lambda e: (e, 0, 0))
    flops = 2 * total * D * slots * 4 // blocks + 18 * blocks * slots * D * FF
    return pl.pallas_call(
        functools.partial(expert_kernel, sizes),
        grid=(local,),
        out_shape=(
            jax.ShapeDtypeStruct((total, D), BF),
            jax.ShapeDtypeStruct((total, D + LANES), BF),
            jax.ShapeDtypeStruct((local, D, FF), BF),
            jax.ShapeDtypeStruct((local, D, FF), BF),
            jax.ShapeDtypeStruct((local, FF, D), BF),
        ),
        in_specs=[
            whole((total, D)),
            whole((total, D)),
            whole((EXPERTS, D)),
            whole((EXPERTS, total)),
            whole((total, EXPERTS)),
            per((D, FF)),
            per((D, FF)),
            per((FF, D)),
        ],
        out_specs=(
            whole((total, D)),
            whole((total, D + LANES)),
            per((D, FF)),
            per((D, FF)),
            per((FF, D)),
        ),
        scratch_shapes=[
            pltpu.VMEM((blocks, slots, D), BF),
            pltpu.VMEM((blocks, slots, D), BF),
            pltpu.VMEM((blocks, slots, 1), F32),
            pltpu.VMEM((blocks, slots, LANES), BF),
        ],
        compiler_params=pltpu.CompilerParams(
            dimension_semantics=("arbitrary",), vmem_limit_bytes=62 * 1024 * 1024
        ),
        cost_estimate=pl.CostEstimate(
            flops=flops, bytes_accessed=2 * (6 * local * D * FF + 4 * total * D), transcendentals=0
        ),
        name="experts",
    )(x_all, ct_all, router_t, rank_row, rank_col, w_gate, w_up, w_down)


def gather_rows(value):
    return lax.all_gather(value, "expert", axis=0, tiled=True)


def scatter_rows(value):
    return lax.psum_scatter(value, "expert", scatter_dimension=0, tiled=True)


def per_device(
    tokens,
    lengths,
    routes,
    norm_gain1,
    w_query,
    key_projection,
    value_projection,
    w_out,
    norm_gain2,
    w_router,
    w_gate,
    w_up,
    w_down,
    cotangent,
):
    rows = tokens.shape[0]
    my_index = lax.axis_index("expert")
    capacity = 3 * rows * TOP // (2 * EXPERTS)
    group_of_heads = QUERY_HEADS // KEY_VALUE_HEADS
    score_scale = HEAD_DIMENSION ** (-0.5)
    query_width, key_width = w_query.shape[1], key_projection.shape[1]
    length = lengths[0]
    positions = my_index * rows + jnp.arange(rows, dtype=jnp.int32)
    valid_rows = (positions < length)[:, None]
    grad_output = jnp.where(valid_rows, cotangent, jnp.zeros_like(cotangent))

    qkv_weight = gather_rows(jnp.concatenate([w_query, key_projection, value_projection], axis=1))
    small = jnp.concatenate([norm_gain1[:, None], norm_gain2[:, None], w_router], axis=1)
    small = gather_rows(small)
    gain_one = small[:, 0].astype(F32)
    gain_two = small[:, 1].astype(F32)
    router_weight = small[:, 2:]
    out_weight = gather_rows(w_out)

    expert_ids = jnp.arange(EXPERTS, dtype=jnp.int32)
    hot = jnp.any(routes[:, :, None] == expert_ids, axis=1)
    row_id = jnp.arange(rows, dtype=jnp.int32)
    earlier = (row_id[None, :] < row_id[:, None]).astype(BF)
    rank = jnp.where(hot, dot(earlier, hot.astype(BF)), 255.0).astype(BF)
    rank_all = gather_rows(rank)
    rank_row = rank_all.T.astype(F32)
    ct_all = gather_rows(grad_output)

    cosine_lookup, sine_lookup = rotary_tables(positions, HEAD_DIMENSION)
    token_f32 = tokens.astype(F32)
    inverse_one = lax.rsqrt(jnp.mean(token_f32 * token_f32, axis=-1, keepdims=True) + EPSILON)
    unit_one = token_f32 * inverse_one
    first_norm = (unit_one * gain_one).astype(BF)
    qkv = dot(first_norm, qkv_weight)
    query_pre = qkv[:, :query_width]
    unrotated_key = qkv[:, query_width : query_width + key_width]
    value_pre = qkv[:, query_width + key_width :]
    query_rows = apply_rotation(
        query_pre.reshape(rows, QUERY_HEADS, HEAD_DIMENSION), cosine_lookup, sine_lookup
    ).astype(BF)
    query_rows = query_rows.reshape(rows, KEY_VALUE_HEADS, group_of_heads, HEAD_DIMENSION)
    local_keys = apply_rotation(
        unrotated_key.reshape(rows, KEY_VALUE_HEADS, HEAD_DIMENSION), cosine_lookup, sine_lookup
    ).astype(BF)
    local_keys = local_keys.reshape(rows, key_width)
    kv_all = gather_rows(jnp.concatenate([local_keys, value_pre.astype(BF)], axis=1))
    key_portion = kv_all[:, :key_width].reshape(-1, KEY_VALUE_HEADS, HEAD_DIMENSION)
    value_portion = kv_all[:, key_width:].reshape(-1, KEY_VALUE_HEADS, HEAD_DIMENSION)
    key_count = kv_all.shape[0]
    scores = (
        jnp.einsum("qhgd,khd->hgqk", query_rows, key_portion, preferred_element_type=F32)
        * score_scale
    )
    columns = jnp.arange(key_count, dtype=jnp.int32)
    allowed = (columns[None, :] <= positions[:, None]) & (columns[None, :] < length)
    masked = jnp.where(allowed, scores, NEGATIVE_LARGE)
    maximum = jnp.max(masked, axis=-1)
    weights = jnp.where(allowed, jnp.exp(masked - maximum[..., None]), 0.0)
    total = jnp.sum(weights, axis=-1)
    mixed_f32 = (
        jnp.einsum(
            "hgqk,khd->hgqd", weights.astype(BF), value_portion, preferred_element_type=F32
        )
        / total[..., None]
    )
    log_total = maximum + jnp.log(total)
    mixed_low = jnp.transpose(mixed_f32, (2, 0, 1, 3)).reshape(rows, query_width).astype(BF)
    residual = token_f32 + dot(mixed_low, out_weight)
    inverse_two = lax.rsqrt(jnp.mean(residual * residual, axis=-1, keepdims=True) + EPSILON)
    unit_two = residual * inverse_two
    second_norm = (unit_two * gain_two).astype(BF)
    x_all = gather_rows(second_norm)

    y_part, gs_part, grad_gate, grad_up, grad_down = run_experts(
        x_all, ct_all, router_weight.T, rank_row, rank_all, w_gate, w_up, w_down, rows, capacity
    )
    gs = scatter_rows(gs_part).astype(F32)
    expert_sum = scatter_rows(y_part).astype(F32)
    mixed = (residual + expert_sum).astype(BF)

    logits = dot(second_norm, router_weight)
    chosen = jnp.where(hot, logits, NEGATIVE_LARGE)
    gate_weights = jnp.where(hot, jnp.exp(chosen - jnp.max(chosen, axis=-1, keepdims=True)), 0.0)
    gate_weights = gate_weights / jnp.sum(gate_weights, axis=-1, keepdims=True)
    grad_gates = gs[:, D : D + EXPERTS] + gs[:, D + EXPERTS : D + 2 * EXPERTS]
    grad_gates = grad_gates + gs[:, D + 2 * EXPERTS : D + 3 * EXPERTS]
    grad_logits = (
        gate_weights * (grad_gates - jnp.sum(gate_weights * grad_gates, axis=-1, keepdims=True))
    ).astype(BF)
    grad_second = gs[:, :D] + dot_nt(grad_logits, router_weight)
    grad_router = dot_tn(second_norm, grad_logits)
    scaled_two = grad_second * gain_two
    grad_gain2 = jnp.sum(grad_second * unit_two, axis=0)
    grad_residual = grad_output.astype(F32) + inverse_two * (
        scaled_two - unit_two * jnp.mean(scaled_two * unit_two, axis=-1, keepdims=True)
    )
    grad_attn = grad_residual.astype(BF)
    grad_out = dot_tn(mixed_low, grad_attn)
    mixed_gradient = dot_nt(grad_attn, out_weight).astype(BF)
    head_gradient = mixed_gradient.reshape(rows, KEY_VALUE_HEADS, group_of_heads, HEAD_DIMENSION)
    delta = jnp.einsum("qhgd,hgqd->hgq", head_gradient, mixed_f32, preferred_element_type=F32)
    probability = jnp.where(allowed, jnp.exp(masked - log_total[..., None]), 0.0)
    grad_prob = jnp.einsum(
        "qhgd,khd->hgqk", head_gradient, value_portion, preferred_element_type=F32
    )
    grad_scores = (probability * (grad_prob - delta[..., None])).astype(BF)
    grad_query_acc = jnp.einsum(
        "hgqk,khd->qhgd", grad_scores, key_portion, preferred_element_type=F32
    )
    key_gradient = jnp.einsum(
        "hgqk,qhgd->khd", grad_scores, query_rows, preferred_element_type=F32
    ).reshape(key_count, key_width)
    value_gradient = jnp.einsum(
        "hgqk,qhgd->khd", probability.astype(BF), head_gradient, preferred_element_type=F32
    ).reshape(key_count, key_width)
    kv_gradient = scatter_rows(
        jnp.concatenate([key_gradient.astype(BF), value_gradient.astype(BF)], axis=1)
    )
    own_key_gradient = kv_gradient[:, :key_width].astype(F32)
    grad_query_rows = grad_query_acc.reshape(rows, QUERY_HEADS, HEAD_DIMENSION) * score_scale
    grad_query_pre = (
        apply_rotation(grad_query_rows, cosine_lookup, -sine_lookup)
        .reshape(rows, query_width)
        .astype(BF)
    )
    grad_key_pre = apply_rotation(
        own_key_gradient.reshape(rows, KEY_VALUE_HEADS, HEAD_DIMENSION) * score_scale,
        cosine_lookup,
        -sine_lookup,
    )
    grad_key_pre = grad_key_pre.reshape(rows, key_width).astype(BF)
    grad_qkv_pre = jnp.concatenate(
        [grad_query_pre, grad_key_pre, kv_gradient[:, key_width:]], axis=1
    )
    grad_qkv = dot_tn(first_norm, grad_qkv_pre)
    grad_first = dot_nt(grad_qkv_pre, qkv_weight)
    scaled_one = grad_first * gain_one
    grad_gain1 = jnp.sum(grad_first * unit_one, axis=0)
    grad_tokens = grad_residual + inverse_one * (
        scaled_one - unit_one * jnp.mean(scaled_one * unit_one, axis=-1, keepdims=True)
    )
    grad_small = jnp.concatenate([grad_gain1[:, None], grad_gain2[:, None], grad_router], axis=1)

    share_qkv = lax.psum(scatter_rows(grad_qkv.astype(BF)), "group").astype(F32)
    share_out = lax.psum(scatter_rows(grad_out.astype(BF)), "group").astype(F32)
    share_small = lax.psum(scatter_rows(grad_small.astype(BF)), "group").astype(F32)

    def sum_over_groups(value, axis):
        part = lax.psum_scatter(value, "group", scatter_dimension=axis, tiled=True)
        return lax.all_gather(part, "group", axis=axis, tiled=True).astype(F32)

    return (
        mixed,
        grad_tokens,
        share_small[:, 0],
        share_qkv[:, :query_width],
        share_qkv[:, query_width : query_width + key_width],
        share_qkv[:, query_width + key_width :],
        share_out,
        share_small[:, 1],
        share_small[:, 2:],
        sum_over_groups(grad_gate, 1),
        sum_over_groups(grad_up, 1),
        sum_over_groups(grad_down, 1),
    )


def solution(mesh):
    rows = P(("group", "expert"), None)
    vector, matrix, stack = P("expert"), P("expert", None), P("expert", None, None)
    return jax.shard_map(
        per_device,
        mesh=mesh,
        in_specs=(
            rows,
            P("group"),
            rows,
            vector,
            matrix,
            matrix,
            matrix,
            matrix,
            vector,
            matrix,
            stack,
            stack,
            stack,
            rows,
        ),
        out_specs=(
            rows,
            rows,
            vector,
            matrix,
            matrix,
            matrix,
            matrix,
            vector,
            matrix,
            stack,
            stack,
            stack,
        ),
        check_vma=False,
    )
```

```python
import functools

import jax
import jax.numpy as jnp
from jax import lax
from jax.experimental import pallas as pl
from jax.experimental.pallas import tpu as pltpu
from jax.sharding import PartitionSpec as P

D = 1024
QUERY_HEADS = 16
KEY_VALUE_HEADS = 8
HEAD_DIMENSION = 64
EXPERTS = 32
TOP = 8
FF = 512
LANES = 128

EPSILON = 1e-05
NEGATIVE_LARGE = -1e30
BF = jnp.bfloat16
F32 = jnp.float32


def rotary_tables(positions, head_size):
    half_width = head_size // 2
    frequency = 10000.0 ** (-2.0 * jnp.arange(half_width).astype(F32) / head_size)
    angles = positions.astype(F32)[:, None] * frequency[None, :]
    return (jnp.cos(angles)[:, None, :], jnp.sin(angles)[:, None, :])


def apply_rotation(tensor_in, cosine_lookup, sine_lookup):
    half_width = tensor_in.shape[-1] // 2
    first_half = tensor_in[..., :half_width]
    second_half = tensor_in[..., half_width:]
    return jnp.concatenate(
        [
            first_half * cosine_lookup - second_half * sine_lookup,
            second_half * cosine_lookup + first_half * sine_lookup,
        ],
        axis=-1,
    )


def dot(a, b):
    return jnp.dot(a, b, preferred_element_type=F32)


def dot_nt(a, b):
    return lax.dot_general(a, b, (((1,), (1,)), ((), ())), preferred_element_type=F32)


def dot_tn(a, b):
    return lax.dot_general(a, b, (((0,), (0,)), ((), ())), preferred_element_type=F32)


def expert_kernel(
    sizes,
    x_ref,
    ct_ref,
    router_t_ref,
    rank_row_ref,
    rank_col_ref,
    w_gate_ref,
    w_up_ref,
    w_down_ref,
    y_ref,
    gs_ref,
    grad_gate_ref,
    grad_up_ref,
    grad_down_ref,
    xs_ref,
    g_ref,
    gate_slot_ref,
    dots_ref,
):
    blocks, rows, local, capacity = sizes
    slots = local * capacity
    step = pl.program_id(0)
    base = lax.axis_index("expert") * local

    @pl.when(step == 0)
    def _():
        logits = dot_nt(router_t_ref[...], x_ref[...])
        hot = rank_row_ref[...] < 200.0
        top = jnp.max(jnp.where(hot, logits, NEGATIVE_LARGE), axis=0, keepdims=True)
        weight = jnp.where(hot, jnp.exp(jnp.minimum(logits - top, 0.0)), 0.0)
        gates = weight / jnp.sum(weight, axis=0, keepdims=True)
        expert_id = lax.broadcasted_iota(jnp.int32, gates.shape, 0)
        slot_id = lax.broadcasted_iota(jnp.int32, (capacity, rows), 0).astype(F32)
        rank_rows, gate_rows = [], []
        for e in range(local):
            mine = expert_id == base + e
            rank_rows.append(jnp.sum(jnp.where(mine, rank_row_ref[...], 0.0), 0, keepdims=True))
            gate_rows.append(jnp.sum(jnp.where(mine, gates, 0.0), 0, keepdims=True))
        for b in range(blocks):
            here = slice(b * rows, (b + 1) * rows)
            pieces = []
            for e in range(local):
                taken = jnp.broadcast_to(rank_rows[e][:, here], (capacity, rows)) == slot_id
                gate = jnp.sum(jnp.where(taken, gate_rows[e][:, here], 0.0), 1, keepdims=True)
                gate_slot_ref[b, e * capacity : (e + 1) * capacity, :] = gate
                pieces.append(jnp.where(taken, 1.0, 0.0).astype(BF))
            pick = jnp.concatenate(pieces, axis=0)
            xs_ref[b] = dot(pick, x_ref[here, :]).astype(BF)
            g_ref[b] = dot(pick, ct_ref[here, :]).astype(BF)

    here = pl.ds(pl.multiple_of(step * capacity, capacity), capacity)
    xs = jnp.concatenate([xs_ref[b, here, :] for b in range(blocks)], axis=0)
    g = jnp.concatenate([g_ref[b, here, :] for b in range(blocks)], axis=0).astype(F32)
    gate_slot = jnp.concatenate([gate_slot_ref[b, here, :] for b in range(blocks)], axis=0)
    w_gate, w_up, w_down = w_gate_ref[0], w_up_ref[0], w_down_ref[0]
    gate_pre = dot(xs, w_gate)
    up_pre = dot(xs, w_up)
    sigmoid = jax.nn.sigmoid(gate_pre)
    silu = gate_pre * sigmoid
    activation = (silu * up_pre).astype(BF)
    expert_out = dot(activation, w_down).astype(BF).astype(F32)
    slot_dot = jnp.sum(g * expert_out, axis=1, keepdims=True)
    grad_out = (gate_slot * g).astype(BF)
    scaled_out = (gate_slot * expert_out).astype(BF)
    grad_down_ref[0] = dot_tn(activation, grad_out).astype(BF)
    grad_activation = dot_nt(grad_out, w_down)
    grad_gate_pre = (
        grad_activation * up_pre * sigmoid * (1.0 + gate_pre * (1.0 - sigmoid))
    ).astype(BF)
    grad_up_pre = (grad_activation * silu).astype(BF)
    grad_gate_ref[0] = dot_tn(xs, grad_gate_pre).astype(BF)
    grad_up_ref[0] = dot_tn(xs, grad_up_pre).astype(BF)
    grad_in = (dot_nt(grad_gate_pre, w_gate) + dot_nt(grad_up_pre, w_up)).astype(BF)
    lane = lax.broadcasted_iota(jnp.int32, (blocks * capacity, LANES), 1)
    high = slot_dot.astype(BF).astype(F32)
    middle = (slot_dot - high).astype(BF).astype(F32)
    low = slot_dot - high - middle
    mine = base + step
    dots = jnp.where(lane == mine, high, 0.0)
    dots = jnp.where(lane == mine + EXPERTS, middle, dots)
    dots = jnp.where(lane == mine + 2 * EXPERTS, low, dots).astype(BF)
    for b in range(blocks):
        part = slice(b * capacity, (b + 1) * capacity)
        xs_ref[b, here, :] = grad_in[part]
        g_ref[b, here, :] = scaled_out[part]
        dots_ref[b, here, :] = dots[part]

    @pl.when(step == local - 1)
    def _():
        slot_expert = lax.broadcasted_iota(jnp.int32, (EXPERTS, slots), 1) // capacity
        spread_row = lax.broadcasted_iota(jnp.int32, (EXPERTS, slots), 0)
        spread = jnp.where(spread_row == slot_expert + base, 1.0, 0.0).astype(BF)
        slot_rank = (lax.broadcasted_iota(jnp.int32, (rows, slots), 1) % capacity).astype(F32)
        for b in range(blocks):
            there = slice(b * rows, (b + 1) * rows)
            ranks = dot(rank_col_ref[there, :], spread)
            put = jnp.where(ranks == slot_rank, 1.0, 0.0).astype(BF)
            y_ref[there, :] = dot(put, g_ref[b]).astype(BF)
            gs_ref[there, :D] = dot(put, xs_ref[b]).astype(BF)
            gs_ref[there, D:] = dot(put, dots_ref[b]).astype(BF)


def run_experts(x_all, ct_all, router_t, rank_row, rank_col, w_gate, w_up, w_down, rows, capacity):
    total = x_all.shape[0]
    blocks, local = total // rows, w_gate.shape[0]
    slots = local * capacity
    sizes = (blocks, rows, local, capacity)
    whole = lambda shape: pl.BlockSpec(
        shape, lambda e: (0,) * len(shape), pipeline_mode=pl.Buffered(1)
    )
    per = lambda shape: pl.BlockSpec((1,) + shape, lambda e: (e, 0, 0))
    flops = 2 * total * D * slots * 4 // blocks + 18 * blocks * slots * D * FF
    return pl.pallas_call(
        functools.partial(expert_kernel, sizes),
        grid=(local,),
        out_shape=(
            jax.ShapeDtypeStruct((total, D), BF),
            jax.ShapeDtypeStruct((total, D + LANES), BF),
            jax.ShapeDtypeStruct((local, D, FF), BF),
            jax.ShapeDtypeStruct((local, D, FF), BF),
            jax.ShapeDtypeStruct((local, FF, D), BF),
        ),
        in_specs=[
            whole((total, D)),
            whole((total, D)),
            whole((EXPERTS, D)),
            whole((EXPERTS, total)),
            whole((total, EXPERTS)),
            per((D, FF)),
            per((D, FF)),
            per((FF, D)),
        ],
        out_specs=(
            whole((total, D)),
            whole((total, D + LANES)),
            per((D, FF)),
            per((D, FF)),
            per((FF, D)),
        ),
        scratch_shapes=[
            pltpu.VMEM((blocks, slots, D), BF),
            pltpu.VMEM((blocks, slots, D), BF),
            pltpu.VMEM((blocks, slots, 1), F32),
            pltpu.VMEM((blocks, slots, LANES), BF),
        ],
        compiler_params=pltpu.CompilerParams(
            dimension_semantics=("arbitrary",), vmem_limit_bytes=62 * 1024 * 1024
        ),
        cost_estimate=pl.CostEstimate(
            flops=flops, bytes_accessed=2 * (6 * local * D * FF + 4 * total * D), transcendentals=0
        ),
        name="experts",
    )(x_all, ct_all, router_t, rank_row, rank_col, w_gate, w_up, w_down)


MESH = pl.DeviceIdType.MESH
ANY = pl.BlockSpec(memory_space=pl.ANY)
IN_VMEM = pl.BlockSpec(memory_space=pltpu.VMEM)


def remote(source, target, send, receive, device):
    return pltpu.make_async_remote_copy(
        src_ref=source,
        dst_ref=target,
        send_sem=send,
        recv_sem=receive,
        device_id=device,
        device_id_type=MESH,
    )


def greet(devices):
    barrier = pltpu.get_barrier_semaphore()
    count = 0
    for condition, device in devices:
        if condition is None:
            pl.semaphore_signal(barrier, inc=1, device_id=device, device_id_type=MESH)
            count = count + 1
        else:

            @pl.when(condition)
            def _():
                pl.semaphore_signal(barrier, inc=1, device_id=device, device_id_type=MESH)

            count = count + jnp.where(condition, 1, 0)
    pl.semaphore_wait(barrier, count)


def line_gather_kernel(n, count, *refs):
    ins, outs = refs[:count], refs[count : 2 * count]
    local, send, receive = refs[2 * count :]
    group, me = lax.axis_index("group"), lax.axis_index("expert")
    left, right = (group, me - 1), (group, me + 1)
    own = [
        pltpu.make_async_copy(ins[i], outs[i].at[me], local.at[i]) for i in range(count)
    ]
    for copy in own:
        copy.start()
    greet([(me > 0, left), (me < n - 1, right)])

    def hop(i, step, side):
        block = me - step if side == 0 else me + step
        source = ins[i] if step == 0 else outs[i].at[block]
        index = (side, step, i)
        return remote(
            source, outs[i].at[block], send.at[index], receive.at[index], right if side == 0 else left
        )

    def arrival(i, step, side):
        block = me - 1 - step if side == 0 else me + 1 + step
        index = (side, step, i)
        return remote(
            outs[i].at[block], outs[i].at[block], send.at[index], receive.at[index], left if side == 0 else right
        )

    def sends(step, side):
        return (me - step >= 0) & (me < n - 1) if side == 0 else (me + step < n) & (me > 0)

    def arrives(step, side):
        return me - 1 - step >= 0 if side == 0 else me + 1 + step < n

    for step in range(n - 1):
        for side in (0, 1):

            @pl.when(sends(step, side))
            def _():
                for i in range(count):
                    hop(i, step, side).start()

        for side in (0, 1):

            @pl.when(arrives(step, side))
            def _():
                for i in range(count):
                    arrival(i, step, side).wait_recv()

    for step in range(n - 1):
        for side in (0, 1):

            @pl.when(sends(step, side))
            def _():
                for i in range(count):
                    hop(i, step, side).wait_send()

    for copy in own:
        copy.wait()


def line_gather(values, n, collective_id, name):
    count = len(values)
    outs = pl.pallas_call(
        functools.partial(line_gather_kernel, n, count),
        out_shape=[jax.ShapeDtypeStruct((n,) + v.shape, v.dtype) for v in values],
        in_specs=[IN_VMEM] * count,
        out_specs=[ANY] * count,
        scratch_shapes=[
            pltpu.SemaphoreType.DMA((count,)),
            pltpu.SemaphoreType.DMA((2, n - 1, count)),
            pltpu.SemaphoreType.DMA((2, n - 1, count)),
        ],
        compiler_params=pltpu.CompilerParams(collective_id=collective_id, has_side_effects=True),
        cost_estimate=pl.CostEstimate(flops=0, bytes_accessed=100000000, transcendentals=0),
        name=name,
    )(*values)
    return [o.reshape((n * v.shape[0],) + v.shape[1:]) for o, v in zip(outs, values)]


def line_scatter_kernel(n, part_ref, out_ref, landing, staging, send, receive):
    group, me = lax.axis_index("group"), lax.axis_index("expert")
    left, right = (group, me - 1), (group, me + 1)
    rows = part_ref.shape[1]
    tile = 32
    greet([(me > 0, left), (me < n - 1, right)])

    def add(target, first, second):
        def body(t, carry):
            span = pl.ds(pl.multiple_of(t * tile, tile), tile)
            target[span, :] = (first[span, :].astype(F32) + second[span, :].astype(F32)).astype(
                target.dtype
            )
            return carry

        lax.fori_loop(0, rows // tile, body, 0)

    def copy(source, step, side):
        return remote(
            source,
            landing.at[side, step],
            send.at[side, step],
            receive.at[side, step],
            right if side == 0 else left,
        )

    for step in range(n - 1):
        for side in (0, 1):
            owner = n - 1 - step if side == 0 else step
            beyond = me < owner if side == 0 else me > owner
            edge = me == 0 if side == 0 else me == n - 1

            @pl.when(beyond & edge)
            def _():
                copy(part_ref.at[owner], step, side).start()

            @pl.when(beyond & jnp.logical_not(edge))
            def _():
                copy(part_ref.at[owner], step, side).wait_recv()
                add(staging.at[side, step], part_ref.at[owner], landing.at[side, step])
                copy(staging.at[side, step], step, side).start()

    @pl.when(me > 0)
    def _():
        step = n - 1 - me
        copy(part_ref.at[me], step, 0).wait_recv()

    @pl.when(me < n - 1)
    def _():
        copy(part_ref.at[me], me, 1).wait_recv()

    def finish(t, carry):
        span = pl.ds(pl.multiple_of(t * tile, tile), tile)
        total = part_ref[me, span, :].astype(F32)
        from_left = landing[0, jnp.minimum(n - 1 - me, n - 2), span, :].astype(F32)
        from_right = landing[1, jnp.minimum(me, n - 2), span, :].astype(F32)
        total = total + jnp.where(me > 0, from_left, 0.0)
        total = total + jnp.where(me < n - 1, from_right, 0.0)
        out_ref[span, :] = total.astype(out_ref.dtype)
        return carry

    lax.fori_loop(0, rows // tile, finish, 0)
    for step in range(n - 1):
        for side in (0, 1):
            owner = n - 1 - step if side == 0 else step
            beyond = me < owner if side == 0 else me > owner

            @pl.when(beyond)
            def _():
                copy(part_ref.at[owner], step, side).wait_send()


def line_scatter(value, n, dtype, collective_id, name):
    total, width = value.shape
    rows = total // n
    return pl.pallas_call(
        functools.partial(line_scatter_kernel, n),
        out_shape=jax.ShapeDtypeStruct((rows, width), dtype),
        in_specs=[IN_VMEM],
        out_specs=IN_VMEM,
        scratch_shapes=[
            pltpu.VMEM((2, n - 1, rows, width), BF),
            pltpu.VMEM((2, n - 1, rows, width), BF),
            pltpu.SemaphoreType.DMA((2, n - 1)),
            pltpu.SemaphoreType.DMA((2, n - 1)),
        ],
        compiler_params=pltpu.CompilerParams(collective_id=collective_id, has_side_effects=True),
        cost_estimate=pl.CostEstimate(flops=0, bytes_accessed=100000000, transcendentals=0),
        name=name,
    )(value.reshape(n, rows, width))


def plane_position():
    group, me = lax.axis_index("group"), lax.axis_index("expert")
    c, x, y = group % 2, (group // 2) % 2, (group // 4) % 2
    by_c, by_x, by_y = (group + 1 - 2 * c, me), (group + 2 - 4 * x, me), (group + 4 - 8 * y, me)
    return group, me, (y, x, c), (by_y, by_x, by_c)


def weights_kernel(n, pieces, widths, *refs):
    wq, wk, wv, wo, small = refs[:5]
    outs, owns = refs[5:8], refs[8:11]
    load, store, zsend, zrecv, psend, precv, csend, crecv = refs[11:]
    group, me, (y, x, c), (by_y, by_x, by_c) = plane_position()
    left, right = (group, me - 1), (group, me + 1)
    eighth = owns[0].shape[0]
    span = pl.ds(pl.multiple_of((y * 4 + x * 2 + c) * eighth, eighth), eighth)
    query_width, key_width = wq.shape[1], wk.shape[1]
    targets = (
        owns[0].at[:, :query_width],
        owns[0].at[:, query_width : query_width + key_width],
        owns[0].at[:, query_width + key_width :],
        owns[1],
        owns[2],
    )
    loads = [
        pltpu.make_async_copy(source.at[span, :], target, load.at[i])
        for i, (source, target) in enumerate(zip((wq, wk, wv, wo, small), targets))
    ]
    for copy in loads:
        copy.start()
    for copy in loads:
        copy.wait()
    stores = [
        pltpu.make_async_copy(owns[i], outs[i].at[me, y, x, c], store.at[i]) for i in range(3)
    ]
    for copy in stores:
        copy.start()
    greet(
        [(me > 0, left), (me < n - 1, right), (None, by_c), (None, by_x), (None, by_y)]
    )

    def hop(i, step, side):
        block = me - step if side == 0 else me + step
        source = owns[i] if step == 0 else outs[i].at[block, y, x, c]
        index = (side, step, i)
        return remote(
            source,
            outs[i].at[block, y, x, c],
            zsend.at[index],
            zrecv.at[index],
            right if side == 0 else left,
        )

    def sends(step, side):
        return (me - step >= 0) & (me < n - 1) if side == 0 else (me + step < n) & (me > 0)

    def first(slot, block, p):
        i, start, width, along_x = pieces[p]
        spot = outs[i].at[block, y, x, c, :, start : start + width]
        source = owns[i].at[:, start : start + width] if slot == 0 else spot
        index = (0, slot, p)
        return remote(source, spot, psend.at[index], precv.at[index], by_x if along_x else by_y)

    def second(slot, block, p):
        i, start, width, along_x = pieces[p]
        columns = slice(start, start + width)
        if along_x:
            spot = outs[i].at[block, y, :, c, :, columns]
        else:
            spot = outs[i].at[block, :, x, c, :, columns]
        index = (1, slot, p)
        return remote(spot, spot, psend.at[index], precv.at[index], by_y if along_x else by_x)

    def third(slot, block, i):
        spot = outs[i].at[block, :, :, c]
        index = (slot, i)
        return remote(spot, spot, csend.at[index], crecv.at[index], by_c)

    def held(step):
        if step == 0:
            return [(0, me, me >= 0)]
        return [(step, me - step, me - step >= 0), (n - 1 + step, me + step, me + step < n)]

    count = len(pieces)
    for step in range(n + 2):
        if step < n:
            for slot, block, there in held(step):

                @pl.when(there)
                def _():
                    if step > 0:
                        side = 0 if slot < n else 1
                        for i in range(3):
                            hop(i, step - 1, side).wait_recv()
                    for p in range(count):
                        first(slot, block, p).start()

            if step < n - 1:
                for side in (0, 1):

                    @pl.when(sends(step, side))
                    def _():
                        for i in range(3):
                            hop(i, step, side).start()

        if 1 <= step < n + 1:
            if step == 1:
                for copy in stores:
                    copy.wait()
            for slot, block, there in held(step - 1):

                @pl.when(there)
                def _():
                    for p in range(count):
                        first(slot, block, p).wait_recv()
                    for p in range(count):
                        second(slot, block, p).start()

        if step >= 2:
            for slot, block, there in held(step - 2):

                @pl.when(there)
                def _():
                    for p in range(count):
                        second(slot, block, p).wait_recv()
                    for i in range(3):
                        third(slot, block, i).start()

    for step in range(n):
        for slot, block, there in held(step):

            @pl.when(there)
            def _():
                for p in range(count):
                    first(slot, block, p).wait_send()
                    second(slot, block, p).wait_send()
                for i in range(3):
                    third(slot, block, i).wait()

        if step < n - 1:
            for side in (0, 1):

                @pl.when(sends(step, side))
                def _():
                    for i in range(3):
                        hop(i, step, side).wait_send()


def path_pieces(query_width, key_width, out_width, small_width):
    half = (query_width + 2 * key_width + out_width) // 2
    return (
        (0, 0, half, True),
        (0, half, query_width + 2 * key_width - half, False),
        (1, 0, out_width, False),
        (2, 0, small_width, True),
    )


def gather_weights(wq, wk, wv, wo, small, n, collective_id):
    rows = wq.shape[0]
    eighth = rows // 8
    widths = (wq.shape[1] + wk.shape[1] + wv.shape[1], wo.shape[1], small.shape[1])
    pieces = path_pieces(wq.shape[1], wk.shape[1], wo.shape[1], small.shape[1])
    outs = pl.pallas_call(
        functools.partial(weights_kernel, n, pieces, widths),
        out_shape=[jax.ShapeDtypeStruct((n, 2, 2, 2, eighth, w), BF) for w in widths],
        in_specs=[ANY] * 5,
        out_specs=[ANY] * 3,
        scratch_shapes=[pltpu.VMEM((eighth, w), BF) for w in widths]
        + [
            pltpu.SemaphoreType.DMA((5,)),
            pltpu.SemaphoreType.DMA((3,)),
            pltpu.SemaphoreType.DMA((2, n - 1, 3)),
            pltpu.SemaphoreType.DMA((2, n - 1, 3)),
            pltpu.SemaphoreType.DMA((2, 2 * n - 1, 4)),
            pltpu.SemaphoreType.DMA((2, 2 * n - 1, 4)),
            pltpu.SemaphoreType.DMA((2 * n - 1, 3)),
            pltpu.SemaphoreType.DMA((2 * n - 1, 3)),
        ],
        compiler_params=pltpu.CompilerParams(collective_id=collective_id, has_side_effects=True),
        cost_estimate=pl.CostEstimate(flops=0, bytes_accessed=100000000, transcendentals=0),
        name="gather_weights",
    )(wq, wk, wv, wo, small)
    return [o.reshape(n * rows, w) for o, w in zip(outs, widths)]


def reduce_kernel(n, pieces, *refs):
    ins, outs = refs[:3], refs[3:5]
    pair, one, two, landing, staging = refs[5:7], refs[7:9], refs[9:11], refs[11:13], refs[13:15]
    csend, crecv, psend, precv, zsend, zrecv, gsend, grecv = refs[15:]
    group, me, (y, x, c), (by_y, by_x, by_c) = plane_position()
    left, right = (group, me - 1), (group, me + 1)
    eighth = pair[0].shape[3]
    greet(
        [(me > 0, left), (me < n - 1, right), (None, by_c), (None, by_x), (None, by_y)]
    )

    places, ends = [], [0, 0]
    for array, start, width, along_x in pieces:
        path = 0 if along_x else 1
        places.append((array, start, width, path, ends[path]))
        ends[path] += width

    def swap(p):
        array, start, width, path, at = places[p]
        return remote(
            ins[array].at[:, :, :, 1 - c, :, start : start + width],
            pair[path].at[:, :, :, :, at : at + width],
            csend.at[p],
            crecv.at[p],
            by_c,
        )

    for p in range(len(places)):
        swap(p).start()
    for p in range(len(places)):
        swap(p).wait_recv()
        array, start, width, path, at = places[p]

        def pair_sum(t, carry):
            z, a, b = t // 4, (t // 2) % 2, t % 2
            mine = ins[array][z, a, b, c, :, start : start + width].astype(F32)
            theirs = pair[path][z, a, b, :, at : at + width].astype(F32)
            pair[path][z, a, b, :, at : at + width] = (mine + theirs).astype(BF)
            return carry

        lax.fori_loop(0, 4 * n, pair_sum, 0)

    def first(path):
        source = pair[0].at[:, :, 1 - x] if path == 0 else pair[1].at[:, 1 - y]
        return remote(
            source, one[path], psend.at[0, path], precv.at[0, path], by_x if path == 0 else by_y
        )

    def second(path):
        source = one[path].at[:, 1 - y] if path == 0 else one[path].at[:, 1 - x]
        return remote(
            source, two[path], psend.at[1, path], precv.at[1, path], by_y if path == 0 else by_x
        )

    for path in (0, 1):
        first(path).start()
    for path in (0, 1):
        first(path).wait_recv()

        def first_sum(t, carry):
            z, a = t // 2, t % 2
            mine = pair[0][z, a, x] if path == 0 else pair[1][z, y, a]
            one[path][z, a] = (mine.astype(F32) + one[path][z, a].astype(F32)).astype(BF)
            return carry

        lax.fori_loop(0, 2 * n, first_sum, 0)
        second(path).start()
    for path in (0, 1):
        second(path).wait_recv()

        def second_sum(z, carry):
            mine = one[0][z, y] if path == 0 else one[1][z, x]
            two[path][z] = (mine.astype(F32) + two[path][z].astype(F32)).astype(BF)
            return carry

        lax.fori_loop(0, n, second_sum, 0)

    def hop(source, path, step, side):
        index = (path, side, step)
        return remote(
            source,
            landing[path].at[side, step],
            zsend.at[index],
            zrecv.at[index],
            right if side == 0 else left,
        )

    for step in range(n - 1):
        for side in (0, 1):
            owner = n - 1 - step if side == 0 else step
            beyond = me < owner if side == 0 else me > owner
            edge = me == 0 if side == 0 else me == n - 1

            @pl.when(beyond & edge)
            def _():
                for path in (0, 1):
                    hop(two[path].at[owner], path, step, side).start()

            @pl.when(beyond & jnp.logical_not(edge))
            def _():
                for path in (0, 1):
                    hop(two[path].at[owner], path, step, side).wait_recv()
                    staging[path][side, step] = (
                        two[path][owner].astype(F32) + landing[path][side, step].astype(F32)
                    ).astype(BF)
                    hop(staging[path].at[side, step], path, step, side).start()

    @pl.when(me > 0)
    def _():
        for path in (0, 1):
            hop(two[path].at[me], path, n - 1 - me, 0).wait_recv()

    @pl.when(me < n - 1)
    def _():
        for path in (0, 1):
            hop(two[path].at[me], path, me, 1).wait_recv()

    for path in (0, 1):
        total = two[path][me].astype(F32)
        from_left = landing[path][0, jnp.minimum(n - 1 - me, n - 2)].astype(F32)
        from_right = landing[path][1, jnp.minimum(me, n - 2)].astype(F32)
        total = total + jnp.where(me > 0, from_left, 0.0)
        total = total + jnp.where(me < n - 1, from_right, 0.0)
        outs[path][y, x, c] = total.astype(BF)

    def spread(path, stage):
        out = outs[path]
        if stage == 2:
            spot, device = out.at[:, :, c], by_c
        elif stage == 0:
            spot, device = out.at[y, x, c], by_x if path == 0 else by_y
        elif path == 0:
            spot, device = out.at[y, :, c], by_y
        else:
            spot, device = out.at[:, x, c], by_x
        return remote(spot, spot, gsend.at[path, stage], grecv.at[path, stage], device)

    for stage in range(3):
        for path in (0, 1):
            spread(path, stage).start()
        for path in (0, 1):
            spread(path, stage).wait_recv()

    for path in (0, 1):
        for stage in range(3):
            spread(path, stage).wait_send()
        first(path).wait_send()
        second(path).wait_send()
    for p in range(len(places)):
        swap(p).wait_send()
    for step in range(n - 1):
        for side in (0, 1):
            owner = n - 1 - step if side == 0 else step
            beyond = me < owner if side == 0 else me > owner

            @pl.when(beyond)
            def _():
                for path in (0, 1):
                    hop(two[path].at[owner], path, step, side).wait_send()


def reduce_weights(grad_qkv, grad_out, grad_small, query_width, n, collective_id):
    values = (grad_qkv, grad_out, grad_small)
    rows = grad_qkv.shape[0] // n
    eighth = rows // 8
    key_width = (grad_qkv.shape[1] - query_width) // 2
    pieces = path_pieces(query_width, key_width, grad_out.shape[1], grad_small.shape[1])
    widths = [sum(p[2] for p in pieces if p[3]), sum(p[2] for p in pieces if not p[3])]
    scratch = [pltpu.VMEM((n, 2, 2, eighth, w), BF) for w in widths]
    scratch += [pltpu.VMEM((n, 2, eighth, w), BF) for w in widths]
    scratch += [pltpu.VMEM((n, eighth, w), BF) for w in widths]
    scratch += [pltpu.VMEM((2, n - 1, eighth, w), BF) for w in widths] * 2
    sems = [(4,), (4,), (2, 2), (2, 2), (2, 2, n - 1), (2, 2, n - 1), (2, 3), (2, 3)]
    outs = pl.pallas_call(
        functools.partial(reduce_kernel, n, pieces),
        out_shape=[jax.ShapeDtypeStruct((2, 2, 2, eighth, w), BF) for w in widths],
        in_specs=[IN_VMEM] * 3,
        out_specs=[IN_VMEM] * 2,
        scratch_shapes=scratch + [pltpu.SemaphoreType.DMA(s) for s in sems],
        compiler_params=pltpu.CompilerParams(
            collective_id=collective_id, has_side_effects=True, vmem_limit_bytes=48 * 1024 * 1024
        ),
        cost_estimate=pl.CostEstimate(flops=0, bytes_accessed=100000000, transcendentals=0),
        name="reduce_weights",
    )(*[v.reshape(n, 2, 2, 2, eighth, v.shape[1]) for v in values])
    first, second = [o.reshape(rows, w) for o, w in zip(outs, widths)]
    cut = pieces[0][2]
    rest = pieces[1][2]
    qkv = jnp.concatenate([first[:, :cut], second[:, :rest]], axis=1)
    return qkv, second[:, rest:], first[:, cut:]


def gather_rows(value):
    return lax.all_gather(value, "expert", axis=0, tiled=True)


def scatter_rows(value):
    return lax.psum_scatter(value, "expert", scatter_dimension=0, tiled=True)


def per_device(
    tokens,
    lengths,
    routes,
    norm_gain1,
    w_query,
    key_projection,
    value_projection,
    w_out,
    norm_gain2,
    w_router,
    w_gate,
    w_up,
    w_down,
    cotangent,
):
    rows = tokens.shape[0]
    n, groups = lax.axis_size("expert"), lax.axis_size("group")
    my_index = lax.axis_index("expert")
    capacity = 3 * rows * TOP // (2 * EXPERTS)
    group_of_heads = QUERY_HEADS // KEY_VALUE_HEADS
    score_scale = HEAD_DIMENSION ** (-0.5)
    query_width, key_width = w_query.shape[1], key_projection.shape[1]
    length = lengths[0]
    positions = my_index * rows + jnp.arange(rows, dtype=jnp.int32)
    valid_rows = (positions < length)[:, None]
    grad_output = jnp.where(valid_rows, cotangent, jnp.zeros_like(cotangent))

    small = jnp.concatenate(
        [w_router, norm_gain1[:, None], norm_gain2[:, None]]
        + [jnp.zeros((w_router.shape[0], LANES - EXPERTS - 2), BF)],
        axis=1,
    )
    qkv_weight, out_weight, small = gather_weights(
        w_query, key_projection, value_projection, w_out, small, n, 1
    )
    router_weight = small[:, :EXPERTS]
    gain_one = small[:, EXPERTS].astype(F32)
    gain_two = small[:, EXPERTS + 1].astype(F32)

    expert_ids = jnp.arange(EXPERTS, dtype=jnp.int32)
    hot = jnp.any(routes[:, :, None] == expert_ids, axis=1)
    row_id = jnp.arange(rows, dtype=jnp.int32)
    earlier = (row_id[:, None] < row_id[None, :]).astype(BF)
    rank = jnp.where(hot.T, dot(hot.T.astype(BF), earlier), 255.0).astype(BF)
    ct_all = gather_rows(grad_output)

    cosine_lookup, sine_lookup = rotary_tables(positions, HEAD_DIMENSION)
    token_f32 = tokens.astype(F32)
    inverse_one = lax.rsqrt(jnp.mean(token_f32 * token_f32, axis=-1, keepdims=True) + EPSILON)
    unit_one = token_f32 * inverse_one
    first_norm = (unit_one * gain_one).astype(BF)
    qkv = dot(first_norm, qkv_weight)
    query_pre = qkv[:, :query_width]
    unrotated_key = qkv[:, query_width : query_width + key_width]
    value_pre = qkv[:, query_width + key_width :]
    query_rows = apply_rotation(
        query_pre.reshape(rows, QUERY_HEADS, HEAD_DIMENSION), cosine_lookup, sine_lookup
    ).astype(BF)
    query_rows = query_rows.reshape(rows, KEY_VALUE_HEADS, group_of_heads, HEAD_DIMENSION)
    local_keys = apply_rotation(
        unrotated_key.reshape(rows, KEY_VALUE_HEADS, HEAD_DIMENSION), cosine_lookup, sine_lookup
    ).astype(BF)
    local_keys = local_keys.reshape(rows, key_width)
    kv_all, rank_all = line_gather(
        [jnp.concatenate([local_keys, value_pre.astype(BF)], axis=1), rank], n, 2, "gather_kv"
    )
    rank_all = rank_all.reshape(n, EXPERTS, rows)
    rank_row = jnp.transpose(rank_all, (1, 0, 2)).reshape(EXPERTS, n * rows).astype(F32)
    rank_col = jnp.transpose(rank_all, (0, 2, 1)).reshape(n * rows, EXPERTS)
    key_portion = kv_all[:, :key_width].reshape(-1, KEY_VALUE_HEADS, HEAD_DIMENSION)
    value_portion = kv_all[:, key_width:].reshape(-1, KEY_VALUE_HEADS, HEAD_DIMENSION)
    key_count = kv_all.shape[0]
    scores = (
        jnp.einsum("qhgd,khd->hgqk", query_rows, key_portion, preferred_element_type=F32)
        * score_scale
    )
    columns = jnp.arange(key_count, dtype=jnp.int32)
    allowed = (columns[None, :] <= positions[:, None]) & (columns[None, :] < length)
    masked = jnp.where(allowed, scores, NEGATIVE_LARGE)
    maximum = jnp.max(masked, axis=-1)
    weights = jnp.where(allowed, jnp.exp(masked - maximum[..., None]), 0.0)
    total = jnp.sum(weights, axis=-1)
    mixed_f32 = (
        jnp.einsum(
            "hgqk,khd->hgqd", weights.astype(BF), value_portion, preferred_element_type=F32
        )
        / total[..., None]
    )
    log_total = maximum + jnp.log(total)
    mixed_low = jnp.transpose(mixed_f32, (2, 0, 1, 3)).reshape(rows, query_width).astype(BF)
    residual = token_f32 + dot(mixed_low, out_weight)
    inverse_two = lax.rsqrt(jnp.mean(residual * residual, axis=-1, keepdims=True) + EPSILON)
    unit_two = residual * inverse_two
    second_norm = (unit_two * gain_two).astype(BF)
    (x_all,) = line_gather([second_norm], n, 3, "gather_rows")

    y_part, gs_part, grad_gate, grad_up, grad_down = run_experts(
        x_all, ct_all, router_weight.T, rank_row, rank_col, w_gate, w_up, w_down, rows, capacity
    )
    gs = line_scatter(gs_part, n, F32, 4, "scatter_grads")
    expert_sum = scatter_rows(y_part).astype(F32)
    mixed = (residual + expert_sum).astype(BF)

    logits = dot(second_norm, router_weight)
    chosen = jnp.where(hot, logits, NEGATIVE_LARGE)
    gate_weights = jnp.where(hot, jnp.exp(chosen - jnp.max(chosen, axis=-1, keepdims=True)), 0.0)
    gate_weights = gate_weights / jnp.sum(gate_weights, axis=-1, keepdims=True)
    grad_gates = gs[:, D : D + EXPERTS] + gs[:, D + EXPERTS : D + 2 * EXPERTS]
    grad_gates = grad_gates + gs[:, D + 2 * EXPERTS : D + 3 * EXPERTS]
    grad_logits = (
        gate_weights * (grad_gates - jnp.sum(gate_weights * grad_gates, axis=-1, keepdims=True))
    ).astype(BF)
    grad_second = gs[:, :D] + dot_nt(grad_logits, router_weight)
    grad_router = dot_tn(second_norm, grad_logits)
    scaled_two = grad_second * gain_two
    grad_gain2 = jnp.sum(grad_second * unit_two, axis=0)
    grad_residual = grad_output.astype(F32) + inverse_two * (
        scaled_two - unit_two * jnp.mean(scaled_two * unit_two, axis=-1, keepdims=True)
    )
    grad_attn = grad_residual.astype(BF)
    grad_out = dot_tn(mixed_low, grad_attn)
    mixed_gradient = dot_nt(grad_attn, out_weight).astype(BF)
    head_gradient = mixed_gradient.reshape(rows, KEY_VALUE_HEADS, group_of_heads, HEAD_DIMENSION)
    delta = jnp.einsum("qhgd,hgqd->hgq", head_gradient, mixed_f32, preferred_element_type=F32)
    probability = jnp.where(allowed, jnp.exp(masked - log_total[..., None]), 0.0)
    grad_prob = jnp.einsum(
        "qhgd,khd->hgqk", head_gradient, value_portion, preferred_element_type=F32
    )
    grad_scores = (probability * (grad_prob - delta[..., None])).astype(BF)
    grad_query_acc = jnp.einsum(
        "hgqk,khd->qhgd", grad_scores, key_portion, preferred_element_type=F32
    )
    key_gradient = jnp.einsum(
        "hgqk,qhgd->khd", grad_scores, query_rows, preferred_element_type=F32
    ).reshape(key_count, key_width)
    value_gradient = jnp.einsum(
        "hgqk,qhgd->khd", probability.astype(BF), head_gradient, preferred_element_type=F32
    ).reshape(key_count, key_width)
    kv_gradient = line_scatter(
        jnp.concatenate([key_gradient.astype(BF), value_gradient.astype(BF)], axis=1),
        n,
        BF,
        5,
        "scatter_kv",
    )
    own_key_gradient = kv_gradient[:, :key_width].astype(F32)
    grad_query_rows = grad_query_acc.reshape(rows, QUERY_HEADS, HEAD_DIMENSION) * score_scale
    grad_query_pre = (
        apply_rotation(grad_query_rows, cosine_lookup, -sine_lookup)
        .reshape(rows, query_width)
        .astype(BF)
    )
    grad_key_pre = apply_rotation(
        own_key_gradient.reshape(rows, KEY_VALUE_HEADS, HEAD_DIMENSION) * score_scale,
        cosine_lookup,
        -sine_lookup,
    )
    grad_key_pre = grad_key_pre.reshape(rows, key_width).astype(BF)
    grad_qkv_pre = jnp.concatenate(
        [grad_query_pre, grad_key_pre, kv_gradient[:, key_width:]], axis=1
    )
    grad_qkv = dot_tn(first_norm, grad_qkv_pre)
    grad_first = dot_nt(grad_qkv_pre, qkv_weight)
    scaled_one = grad_first * gain_one
    grad_gain1 = jnp.sum(grad_first * unit_one, axis=0)
    grad_tokens = grad_residual + inverse_one * (
        scaled_one - unit_one * jnp.mean(scaled_one * unit_one, axis=-1, keepdims=True)
    )
    grad_small = jnp.concatenate(
        [grad_router, grad_gain1[:, None], grad_gain2[:, None]]
        + [jnp.zeros((D, LANES - EXPERTS - 2), F32)],
        axis=1,
    )
    shares = (grad_qkv.astype(BF), grad_out.astype(BF), grad_small.astype(BF))
    if groups == 8:
        shares = reduce_weights(*shares, query_width, n, 6)
    else:
        shares = [lax.psum(scatter_rows(share), "group") for share in shares]
    share_qkv, share_out, share_small = [share.astype(F32) for share in shares]

    def sum_over_groups(value, axis):
        part = lax.psum_scatter(value, "group", scatter_dimension=axis, tiled=True)
        return lax.all_gather(part, "group", axis=axis, tiled=True).astype(F32)

    return (
        mixed,
        grad_tokens,
        share_small[:, EXPERTS],
        share_qkv[:, :query_width],
        share_qkv[:, query_width : query_width + key_width],
        share_qkv[:, query_width + key_width :],
        share_out,
        share_small[:, EXPERTS + 1],
        share_small[:, :EXPERTS],
        sum_over_groups(grad_gate, 1),
        sum_over_groups(grad_up, 1),
        sum_over_groups(grad_down, 1),
    )


def solution(mesh):
    rows = P(("group", "expert"), None)
    vector, matrix, stack = P("expert"), P("expert", None), P("expert", None, None)
    return jax.shard_map(
        per_device,
        mesh=mesh,
        in_specs=(
            rows,
            P("group"),
            rows,
            vector,
            matrix,
            matrix,
            matrix,
            matrix,
            vector,
            matrix,
            stack,
            stack,
            stack,
            rows,
        ),
        out_specs=(
            rows,
            rows,
            vector,
            matrix,
            matrix,
            matrix,
            matrix,
            vector,
            matrix,
            stack,
            stack,
            stack,
        ),
        check_vma=False,
    )
```

```python
import functools

import jax
import jax.numpy as jnp
from jax import lax
from jax.experimental import pallas as pl
from jax.experimental.pallas import tpu as pltpu
from jax.sharding import PartitionSpec as P

D = 1024
QUERY_HEADS = 16
KEY_VALUE_HEADS = 8
HEAD_DIMENSION = 64
EXPERTS = 32
TOP = 8
FF = 512
LANES = 128

EPSILON = 1e-05
NEGATIVE_LARGE = -1e30
BF = jnp.bfloat16
F32 = jnp.float32


def rotary_tables(positions, head_size):
    half_width = head_size // 2
    frequency = 10000.0 ** (-2.0 * jnp.arange(half_width).astype(F32) / head_size)
    angles = positions.astype(F32)[:, None] * frequency[None, :]
    return (jnp.cos(angles)[:, None, :], jnp.sin(angles)[:, None, :])


def apply_rotation(tensor_in, cosine_lookup, sine_lookup):
    half_width = tensor_in.shape[-1] // 2
    first_half = tensor_in[..., :half_width]
    second_half = tensor_in[..., half_width:]
    return jnp.concatenate(
        [
            first_half * cosine_lookup - second_half * sine_lookup,
            second_half * cosine_lookup + first_half * sine_lookup,
        ],
        axis=-1,
    )


def dot(a, b):
    return jnp.dot(a, b, preferred_element_type=F32)


def dot_nt(a, b):
    return lax.dot_general(a, b, (((1,), (1,)), ((), ())), preferred_element_type=F32)


def dot_tn(a, b):
    return lax.dot_general(a, b, (((0,), (0,)), ((), ())), preferred_element_type=F32)


MESH = pl.DeviceIdType.MESH
ANY = pl.BlockSpec(memory_space=pl.ANY)
IN_VMEM = pl.BlockSpec(memory_space=pltpu.VMEM)


def remote(source, target, send, receive, device):
    return pltpu.make_async_remote_copy(
        src_ref=source,
        dst_ref=target,
        send_sem=send,
        recv_sem=receive,
        device_id=device,
        device_id_type=MESH,
    )


def greet(devices):
    barrier = pltpu.get_barrier_semaphore()
    count = 0
    for condition, device in devices:
        if condition is None:
            pl.semaphore_signal(barrier, inc=1, device_id=device, device_id_type=MESH)
            count = count + 1
        else:

            @pl.when(condition)
            def _():
                pl.semaphore_signal(barrier, inc=1, device_id=device, device_id_type=MESH)

            count = count + jnp.where(condition, 1, 0)
    pl.semaphore_wait(barrier, count)


def line_gather_kernel(n, count, *refs):
    ins, outs = refs[:count], refs[count : 2 * count]
    local, send, receive = refs[2 * count :]
    group, me = lax.axis_index("group"), lax.axis_index("expert")
    left, right = (group, me - 1), (group, me + 1)
    own = [
        pltpu.make_async_copy(ins[i], outs[i].at[me], local.at[i]) for i in range(count)
    ]
    for copy in own:
        copy.start()
    greet([(me > 0, left), (me < n - 1, right)])

    def hop(i, step, side):
        block = me - step if side == 0 else me + step
        source = ins[i] if step == 0 else outs[i].at[block]
        index = (side, step, i)
        return remote(
            source, outs[i].at[block], send.at[index], receive.at[index], right if side == 0 else left
        )

    def arrival(i, step, side):
        block = me - 1 - step if side == 0 else me + 1 + step
        index = (side, step, i)
        return remote(
            outs[i].at[block], outs[i].at[block], send.at[index], receive.at[index], left if side == 0 else right
        )

    def sends(step, side):
        return (me - step >= 0) & (me < n - 1) if side == 0 else (me + step < n) & (me > 0)

    def arrives(step, side):
        return me - 1 - step >= 0 if side == 0 else me + 1 + step < n

    for step in range(n - 1):
        for side in (0, 1):

            @pl.when(sends(step, side))
            def _():
                for i in range(count):
                    hop(i, step, side).start()

        for side in (0, 1):

            @pl.when(arrives(step, side))
            def _():
                for i in range(count):
                    arrival(i, step, side).wait_recv()

    for step in range(n - 1):
        for side in (0, 1):

            @pl.when(sends(step, side))
            def _():
                for i in range(count):
                    hop(i, step, side).wait_send()

    for copy in own:
        copy.wait()


def line_gather(values, n, collective_id, name):
    count = len(values)
    outs = pl.pallas_call(
        functools.partial(line_gather_kernel, n, count),
        out_shape=[jax.ShapeDtypeStruct((n,) + v.shape, v.dtype) for v in values],
        in_specs=[IN_VMEM] * count,
        out_specs=[ANY] * count,
        scratch_shapes=[
            pltpu.SemaphoreType.DMA((count,)),
            pltpu.SemaphoreType.DMA((2, n - 1, count)),
            pltpu.SemaphoreType.DMA((2, n - 1, count)),
        ],
        compiler_params=pltpu.CompilerParams(collective_id=collective_id, has_side_effects=True),
        cost_estimate=pl.CostEstimate(flops=0, bytes_accessed=100000000, transcendentals=0),
        name=name,
    )(*values)
    return [o.reshape((n * v.shape[0],) + v.shape[1:]) for o, v in zip(outs, values)]


def line_scatter_kernel(n, part_ref, out_ref, landing, staging, send, receive):
    group, me = lax.axis_index("group"), lax.axis_index("expert")
    left, right = (group, me - 1), (group, me + 1)
    rows = part_ref.shape[1]
    tile = 32
    greet([(me > 0, left), (me < n - 1, right)])

    def add(target, first, second):
        def body(t, carry):
            span = pl.ds(pl.multiple_of(t * tile, tile), tile)
            target[span, :] = (first[span, :].astype(F32) + second[span, :].astype(F32)).astype(
                target.dtype
            )
            return carry

        lax.fori_loop(0, rows // tile, body, 0)

    def copy(source, step, side):
        return remote(
            source,
            landing.at[side, step],
            send.at[side, step],
            receive.at[side, step],
            right if side == 0 else left,
        )

    for step in range(n - 1):
        for side in (0, 1):
            owner = n - 1 - step if side == 0 else step
            beyond = me < owner if side == 0 else me > owner
            edge = me == 0 if side == 0 else me == n - 1

            @pl.when(beyond & edge)
            def _():
                copy(part_ref.at[owner], step, side).start()

            @pl.when(beyond & jnp.logical_not(edge))
            def _():
                copy(part_ref.at[owner], step, side).wait_recv()
                add(staging.at[side, step], part_ref.at[owner], landing.at[side, step])
                copy(staging.at[side, step], step, side).start()

    @pl.when(me > 0)
    def _():
        step = n - 1 - me
        copy(part_ref.at[me], step, 0).wait_recv()

    @pl.when(me < n - 1)
    def _():
        copy(part_ref.at[me], me, 1).wait_recv()

    def finish(t, carry):
        span = pl.ds(pl.multiple_of(t * tile, tile), tile)
        total = part_ref[me, span, :].astype(F32)
        from_left = landing[0, jnp.minimum(n - 1 - me, n - 2), span, :].astype(F32)
        from_right = landing[1, jnp.minimum(me, n - 2), span, :].astype(F32)
        total = total + jnp.where(me > 0, from_left, 0.0)
        total = total + jnp.where(me < n - 1, from_right, 0.0)
        out_ref[span, :] = total.astype(out_ref.dtype)
        return carry

    lax.fori_loop(0, rows // tile, finish, 0)
    for step in range(n - 1):
        for side in (0, 1):
            owner = n - 1 - step if side == 0 else step
            beyond = me < owner if side == 0 else me > owner

            @pl.when(beyond)
            def _():
                copy(part_ref.at[owner], step, side).wait_send()


def line_scatter(value, n, dtype, collective_id, name):
    total, width = value.shape
    rows = total // n
    return pl.pallas_call(
        functools.partial(line_scatter_kernel, n),
        out_shape=jax.ShapeDtypeStruct((rows, width), dtype),
        in_specs=[IN_VMEM],
        out_specs=IN_VMEM,
        scratch_shapes=[
            pltpu.VMEM((2, n - 1, rows, width), BF),
            pltpu.VMEM((2, n - 1, rows, width), BF),
            pltpu.SemaphoreType.DMA((2, n - 1)),
            pltpu.SemaphoreType.DMA((2, n - 1)),
        ],
        compiler_params=pltpu.CompilerParams(collective_id=collective_id, has_side_effects=True),
        cost_estimate=pl.CostEstimate(flops=0, bytes_accessed=100000000, transcendentals=0),
        name=name,
    )(value.reshape(n, rows, width))


def plane_position():
    group, me = lax.axis_index("group"), lax.axis_index("expert")
    c, x, y = group % 2, (group // 2) % 2, (group // 4) % 2
    by_c, by_x, by_y = (group + 1 - 2 * c, me), (group + 2 - 4 * x, me), (group + 4 - 8 * y, me)
    return group, me, (y, x, c), (by_y, by_x, by_c)


def weights_kernel(n, pieces, widths, *refs):
    wq, wk, wv, wo, small = refs[:5]
    outs, owns = refs[5:8], refs[8:11]
    load, store, zsend, zrecv, psend, precv, csend, crecv = refs[11:]
    group, me, (y, x, c), (by_y, by_x, by_c) = plane_position()
    left, right = (group, me - 1), (group, me + 1)
    eighth = owns[0].shape[0]
    span = pl.ds(pl.multiple_of((y * 4 + x * 2 + c) * eighth, eighth), eighth)
    query_width, key_width = wq.shape[1], wk.shape[1]
    targets = (
        owns[0].at[:, :query_width],
        owns[0].at[:, query_width : query_width + key_width],
        owns[0].at[:, query_width + key_width :],
        owns[1],
        owns[2],
    )
    loads = [
        pltpu.make_async_copy(source.at[span, :], target, load.at[i])
        for i, (source, target) in enumerate(zip((wq, wk, wv, wo, small), targets))
    ]
    for copy in loads:
        copy.start()
    for copy in loads:
        copy.wait()
    stores = [
        pltpu.make_async_copy(owns[i], outs[i].at[me, y, x, c], store.at[i]) for i in range(3)
    ]
    for copy in stores:
        copy.start()
    greet(
        [(me > 0, left), (me < n - 1, right), (None, by_c), (None, by_x), (None, by_y)]
    )

    def hop(i, step, side):
        block = me - step if side == 0 else me + step
        source = owns[i] if step == 0 else outs[i].at[block, y, x, c]
        index = (side, step, i)
        return remote(
            source,
            outs[i].at[block, y, x, c],
            zsend.at[index],
            zrecv.at[index],
            right if side == 0 else left,
        )

    def sends(step, side):
        return (me - step >= 0) & (me < n - 1) if side == 0 else (me + step < n) & (me > 0)

    def first(slot, block, p):
        i, start, width, along_x = pieces[p]
        spot = outs[i].at[block, y, x, c, :, start : start + width]
        source = owns[i].at[:, start : start + width] if slot == 0 else spot
        index = (0, slot, p)
        return remote(source, spot, psend.at[index], precv.at[index], by_x if along_x else by_y)

    def second(slot, block, p):
        i, start, width, along_x = pieces[p]
        columns = slice(start, start + width)
        if along_x:
            spot = outs[i].at[block, y, :, c, :, columns]
        else:
            spot = outs[i].at[block, :, x, c, :, columns]
        index = (1, slot, p)
        return remote(spot, spot, psend.at[index], precv.at[index], by_y if along_x else by_x)

    def third(slot, block, i):
        spot = outs[i].at[block, :, :, c]
        index = (slot, i)
        return remote(spot, spot, csend.at[index], crecv.at[index], by_c)

    def held(step):
        if step == 0:
            return [(0, me, me >= 0)]
        return [(step, me - step, me - step >= 0), (n - 1 + step, me + step, me + step < n)]

    count = len(pieces)
    for step in range(n + 2):
        if step < n:
            for slot, block, there in held(step):

                @pl.when(there)
                def _():
                    if step > 0:
                        side = 0 if slot < n else 1
                        for i in range(3):
                            hop(i, step - 1, side).wait_recv()
                    for p in range(count):
                        first(slot, block, p).start()

            if step < n - 1:
                for side in (0, 1):

                    @pl.when(sends(step, side))
                    def _():
                        for i in range(3):
                            hop(i, step, side).start()

        if 1 <= step < n + 1:
            if step == 1:
                for copy in stores:
                    copy.wait()
            for slot, block, there in held(step - 1):

                @pl.when(there)
                def _():
                    for p in range(count):
                        first(slot, block, p).wait_recv()
                    for p in range(count):
                        second(slot, block, p).start()

        if step >= 2:
            for slot, block, there in held(step - 2):

                @pl.when(there)
                def _():
                    for p in range(count):
                        second(slot, block, p).wait_recv()
                    for i in range(3):
                        third(slot, block, i).start()

    for step in range(n):
        for slot, block, there in held(step):

            @pl.when(there)
            def _():
                for p in range(count):
                    first(slot, block, p).wait_send()
                    second(slot, block, p).wait_send()
                for i in range(3):
                    third(slot, block, i).wait()

        if step < n - 1:
            for side in (0, 1):

                @pl.when(sends(step, side))
                def _():
                    for i in range(3):
                        hop(i, step, side).wait_send()


def path_pieces(query_width, key_width, out_width, small_width):
    half = (query_width + 2 * key_width + out_width) // 2
    return (
        (0, 0, half, True),
        (0, half, query_width + 2 * key_width - half, False),
        (1, 0, out_width, False),
        (2, 0, small_width, True),
    )


def gather_weights(wq, wk, wv, wo, small, n, collective_id):
    rows = wq.shape[0]
    eighth = rows // 8
    widths = (wq.shape[1] + wk.shape[1] + wv.shape[1], wo.shape[1], small.shape[1])
    pieces = path_pieces(wq.shape[1], wk.shape[1], wo.shape[1], small.shape[1])
    outs = pl.pallas_call(
        functools.partial(weights_kernel, n, pieces, widths),
        out_shape=[jax.ShapeDtypeStruct((n, 2, 2, 2, eighth, w), BF) for w in widths],
        in_specs=[ANY] * 5,
        out_specs=[ANY] * 3,
        scratch_shapes=[pltpu.VMEM((eighth, w), BF) for w in widths]
        + [
            pltpu.SemaphoreType.DMA((5,)),
            pltpu.SemaphoreType.DMA((3,)),
            pltpu.SemaphoreType.DMA((2, n - 1, 3)),
            pltpu.SemaphoreType.DMA((2, n - 1, 3)),
            pltpu.SemaphoreType.DMA((2, 2 * n - 1, 4)),
            pltpu.SemaphoreType.DMA((2, 2 * n - 1, 4)),
            pltpu.SemaphoreType.DMA((2 * n - 1, 3)),
            pltpu.SemaphoreType.DMA((2 * n - 1, 3)),
        ],
        compiler_params=pltpu.CompilerParams(collective_id=collective_id, has_side_effects=True),
        cost_estimate=pl.CostEstimate(flops=0, bytes_accessed=100000000, transcendentals=0),
        name="gather_weights",
    )(wq, wk, wv, wo, small)
    return [o.reshape(n * rows, w) for o, w in zip(outs, widths)]


def reduce_kernel(n, pieces, *refs):
    ins, outs = refs[:3], refs[3:5]
    pair, one, two, landing, staging = refs[5:7], refs[7:9], refs[9:11], refs[11:13], refs[13:15]
    csend, crecv, psend, precv, zsend, zrecv, gsend, grecv = refs[15:]
    group, me, (y, x, c), (by_y, by_x, by_c) = plane_position()
    left, right = (group, me - 1), (group, me + 1)
    eighth = pair[0].shape[3]
    greet(
        [(me > 0, left), (me < n - 1, right), (None, by_c), (None, by_x), (None, by_y)]
    )

    places, ends = [], [0, 0]
    for array, start, width, along_x in pieces:
        path = 0 if along_x else 1
        places.append((array, start, width, path, ends[path]))
        ends[path] += width

    def swap(p):
        array, start, width, path, at = places[p]
        return remote(
            ins[array].at[:, :, :, 1 - c, :, start : start + width],
            pair[path].at[:, :, :, :, at : at + width],
            csend.at[p],
            crecv.at[p],
            by_c,
        )

    for p in range(len(places)):
        swap(p).start()
    for p in range(len(places)):
        swap(p).wait_recv()
        array, start, width, path, at = places[p]

        def pair_sum(t, carry):
            z, a, b = t // 4, (t // 2) % 2, t % 2
            mine = ins[array][z, a, b, c, :, start : start + width].astype(F32)
            theirs = pair[path][z, a, b, :, at : at + width].astype(F32)
            pair[path][z, a, b, :, at : at + width] = (mine + theirs).astype(BF)
            return carry

        lax.fori_loop(0, 4 * n, pair_sum, 0)

    def first(path):
        source = pair[0].at[:, :, 1 - x] if path == 0 else pair[1].at[:, 1 - y]
        return remote(
            source, one[path], psend.at[0, path], precv.at[0, path], by_x if path == 0 else by_y
        )

    def second(path):
        source = one[path].at[:, 1 - y] if path == 0 else one[path].at[:, 1 - x]
        return remote(
            source, two[path], psend.at[1, path], precv.at[1, path], by_y if path == 0 else by_x
        )

    for path in (0, 1):
        first(path).start()
    for path in (0, 1):
        first(path).wait_recv()

        def first_sum(t, carry):
            z, a = t // 2, t % 2
            mine = pair[0][z, a, x] if path == 0 else pair[1][z, y, a]
            one[path][z, a] = (mine.astype(F32) + one[path][z, a].astype(F32)).astype(BF)
            return carry

        lax.fori_loop(0, 2 * n, first_sum, 0)
        second(path).start()
    for path in (0, 1):
        second(path).wait_recv()

        def second_sum(z, carry):
            mine = one[0][z, y] if path == 0 else one[1][z, x]
            two[path][z] = (mine.astype(F32) + two[path][z].astype(F32)).astype(BF)
            return carry

        lax.fori_loop(0, n, second_sum, 0)

    def hop(source, path, step, side):
        index = (path, side, step)
        return remote(
            source,
            landing[path].at[side, step],
            zsend.at[index],
            zrecv.at[index],
            right if side == 0 else left,
        )

    for step in range(n - 1):
        for side in (0, 1):
            owner = n - 1 - step if side == 0 else step
            beyond = me < owner if side == 0 else me > owner
            edge = me == 0 if side == 0 else me == n - 1

            @pl.when(beyond & edge)
            def _():
                for path in (0, 1):
                    hop(two[path].at[owner], path, step, side).start()

            @pl.when(beyond & jnp.logical_not(edge))
            def _():
                for path in (0, 1):
                    hop(two[path].at[owner], path, step, side).wait_recv()
                    staging[path][side, step] = (
                        two[path][owner].astype(F32) + landing[path][side, step].astype(F32)
                    ).astype(BF)
                    hop(staging[path].at[side, step], path, step, side).start()

    @pl.when(me > 0)
    def _():
        for path in (0, 1):
            hop(two[path].at[me], path, n - 1 - me, 0).wait_recv()

    @pl.when(me < n - 1)
    def _():
        for path in (0, 1):
            hop(two[path].at[me], path, me, 1).wait_recv()

    for path in (0, 1):
        total = two[path][me].astype(F32)
        from_left = landing[path][0, jnp.minimum(n - 1 - me, n - 2)].astype(F32)
        from_right = landing[path][1, jnp.minimum(me, n - 2)].astype(F32)
        total = total + jnp.where(me > 0, from_left, 0.0)
        total = total + jnp.where(me < n - 1, from_right, 0.0)
        outs[path][y, x, c] = total.astype(BF)

    def spread(path, stage):
        out = outs[path]
        if stage == 2:
            spot, device = out.at[:, :, c], by_c
        elif stage == 0:
            spot, device = out.at[y, x, c], by_x if path == 0 else by_y
        elif path == 0:
            spot, device = out.at[y, :, c], by_y
        else:
            spot, device = out.at[:, x, c], by_x
        return remote(spot, spot, gsend.at[path, stage], grecv.at[path, stage], device)

    for stage in range(3):
        for path in (0, 1):
            spread(path, stage).start()
        for path in (0, 1):
            spread(path, stage).wait_recv()

    for path in (0, 1):
        for stage in range(3):
            spread(path, stage).wait_send()
        first(path).wait_send()
        second(path).wait_send()
    for p in range(len(places)):
        swap(p).wait_send()
    for step in range(n - 1):
        for side in (0, 1):
            owner = n - 1 - step if side == 0 else step
            beyond = me < owner if side == 0 else me > owner

            @pl.when(beyond)
            def _():
                for path in (0, 1):
                    hop(two[path].at[owner], path, step, side).wait_send()


def reduce_weights(grad_qkv, grad_out, grad_small, query_width, n, collective_id):
    values = (grad_qkv, grad_out, grad_small)
    rows = grad_qkv.shape[0] // n
    eighth = rows // 8
    key_width = (grad_qkv.shape[1] - query_width) // 2
    pieces = path_pieces(query_width, key_width, grad_out.shape[1], grad_small.shape[1])
    widths = [sum(p[2] for p in pieces if p[3]), sum(p[2] for p in pieces if not p[3])]
    scratch = [pltpu.VMEM((n, 2, 2, eighth, w), BF) for w in widths]
    scratch += [pltpu.VMEM((n, 2, eighth, w), BF) for w in widths]
    scratch += [pltpu.VMEM((n, eighth, w), BF) for w in widths]
    scratch += [pltpu.VMEM((2, n - 1, eighth, w), BF) for w in widths] * 2
    sems = [(4,), (4,), (2, 2), (2, 2), (2, 2, n - 1), (2, 2, n - 1), (2, 3), (2, 3)]
    outs = pl.pallas_call(
        functools.partial(reduce_kernel, n, pieces),
        out_shape=[jax.ShapeDtypeStruct((2, 2, 2, eighth, w), BF) for w in widths],
        in_specs=[IN_VMEM] * 3,
        out_specs=[IN_VMEM] * 2,
        scratch_shapes=scratch + [pltpu.SemaphoreType.DMA(s) for s in sems],
        compiler_params=pltpu.CompilerParams(
            collective_id=collective_id, has_side_effects=True, vmem_limit_bytes=48 * 1024 * 1024
        ),
        cost_estimate=pl.CostEstimate(flops=0, bytes_accessed=100000000, transcendentals=0),
        name="reduce_weights",
    )(*[v.reshape(n, 2, 2, 2, eighth, v.shape[1]) for v in values])
    first, second = [o.reshape(rows, w) for o, w in zip(outs, widths)]
    cut = pieces[0][2]
    rest = pieces[1][2]
    qkv = jnp.concatenate([first[:, :cut], second[:, :rest]], axis=1)
    return qkv, second[:, rest:], first[:, cut:]


def expert_kernel(sizes, plane, *refs):
    blocks, rows, local, capacity = sizes
    x_ref, ct_ref, router_t_ref, rank_row_ref, rank_col_ref = refs[:5]
    w_gate_ref, w_up_ref, w_down_ref = refs[5:8]
    y_ref, gs_ref, out_gate_ref, out_up_ref, out_down_ref = refs[8:13]
    xs_ref, g_ref, gate_slot_ref, dots_ref = refs[13:17]
    slots = local * capacity
    step = pl.program_id(0)
    base = lax.axis_index("expert") * local
    if plane:
        stage_refs, pair_refs, one_refs, two_refs = refs[17:20], refs[20:23], refs[23:27], refs[27:31]
        csend, crecv, psend, precv, qsend, qrecv = refs[31:]
        _, _, (y, x, c), (by_y, by_x, by_c) = plane_position()
        half = stage_refs[2].shape[4] // 2

        @pl.when(step == 0)
        def _():
            greet([(None, by_c), (None, by_x), (None, by_y)])

    @pl.when(step == 0)
    def _():
        logits = dot_nt(router_t_ref[...], x_ref[...])
        hot = rank_row_ref[...] < 200.0
        top = jnp.max(jnp.where(hot, logits, NEGATIVE_LARGE), axis=0, keepdims=True)
        weight = jnp.where(hot, jnp.exp(jnp.minimum(logits - top, 0.0)), 0.0)
        gates = weight / jnp.sum(weight, axis=0, keepdims=True)
        expert_id = lax.broadcasted_iota(jnp.int32, gates.shape, 0)
        slot_id = lax.broadcasted_iota(jnp.int32, (capacity, rows), 0).astype(F32)
        rank_rows, gate_rows = [], []
        for e in range(local):
            mine = expert_id == base + e
            rank_rows.append(jnp.sum(jnp.where(mine, rank_row_ref[...], 0.0), 0, keepdims=True))
            gate_rows.append(jnp.sum(jnp.where(mine, gates, 0.0), 0, keepdims=True))
        for b in range(blocks):
            here = slice(b * rows, (b + 1) * rows)
            pieces = []
            for e in range(local):
                taken = jnp.broadcast_to(rank_rows[e][:, here], (capacity, rows)) == slot_id
                gate = jnp.sum(jnp.where(taken, gate_rows[e][:, here], 0.0), 1, keepdims=True)
                gate_slot_ref[b, e * capacity : (e + 1) * capacity, :] = gate
                pieces.append(jnp.where(taken, 1.0, 0.0).astype(BF))
            pick = jnp.concatenate(pieces, axis=0)
            xs_ref[b] = dot(pick, x_ref[here, :]).astype(BF)
            g_ref[b] = dot(pick, ct_ref[here, :]).astype(BF)

    @pl.when(step < local)
    def _():
        here = pl.ds(pl.multiple_of(step * capacity, capacity), capacity)
        xs = jnp.concatenate([xs_ref[b, here, :] for b in range(blocks)], axis=0)
        g = jnp.concatenate([g_ref[b, here, :] for b in range(blocks)], axis=0).astype(F32)
        gate_slot = jnp.concatenate([gate_slot_ref[b, here, :] for b in range(blocks)], axis=0)
        w_gate, w_up, w_down = w_gate_ref[0], w_up_ref[0], w_down_ref[0]
        gate_pre = dot(xs, w_gate)
        up_pre = dot(xs, w_up)
        sigmoid = jax.nn.sigmoid(gate_pre)
        silu = gate_pre * sigmoid
        activation = (silu * up_pre).astype(BF)
        expert_out = dot(activation, w_down).astype(BF).astype(F32)
        slot_dot = jnp.sum(g * expert_out, axis=1, keepdims=True)
        grad_out = (gate_slot * g).astype(BF)
        scaled_out = (gate_slot * expert_out).astype(BF)
        grad_down = dot_tn(activation, grad_out).astype(BF)
        grad_activation = dot_nt(grad_out, w_down)
        grad_gate_pre = (
            grad_activation * up_pre * sigmoid * (1.0 + gate_pre * (1.0 - sigmoid))
        ).astype(BF)
        grad_up_pre = (grad_activation * silu).astype(BF)
        grad_gate = dot_tn(xs, grad_gate_pre).astype(BF)
        grad_up = dot_tn(xs, grad_up_pre).astype(BF)
        if plane:
            for ref, value in zip(stage_refs, (grad_gate, grad_up, grad_down)):
                ref[step % 2] = value.reshape(ref.shape[1:])
        else:
            out_gate_ref[0], out_up_ref[0], out_down_ref[0] = grad_gate, grad_up, grad_down
        grad_in = (dot_nt(grad_gate_pre, w_gate) + dot_nt(grad_up_pre, w_up)).astype(BF)
        lane = lax.broadcasted_iota(jnp.int32, (blocks * capacity, LANES), 1)
        high = slot_dot.astype(BF).astype(F32)
        middle = (slot_dot - high).astype(BF).astype(F32)
        low = slot_dot - high - middle
        mine = base + step
        dots = jnp.where(lane == mine, high, 0.0)
        dots = jnp.where(lane == mine + EXPERTS, middle, dots)
        dots = jnp.where(lane == mine + 2 * EXPERTS, low, dots).astype(BF)
        for b in range(blocks):
            part = slice(b * capacity, (b + 1) * capacity)
            xs_ref[b, here, :] = grad_in[part]
            g_ref[b, here, :] = scaled_out[part]
            dots_ref[b, here, :] = dots[part]

    @pl.when(step == (local if plane else local - 1))
    def _():
        slot_expert = lax.broadcasted_iota(jnp.int32, (EXPERTS, slots), 1) // capacity
        spread_row = lax.broadcasted_iota(jnp.int32, (EXPERTS, slots), 0)
        spread = jnp.where(spread_row == slot_expert + base, 1.0, 0.0).astype(BF)
        slot_rank = (lax.broadcasted_iota(jnp.int32, (rows, slots), 1) % capacity).astype(F32)
        for b in range(blocks):
            there = slice(b * rows, (b + 1) * rows)
            ranks = dot(rank_col_ref[there, :], spread)
            put = jnp.where(ranks == slot_rank, 1.0, 0.0).astype(BF)
            y_ref[there, :] = dot(put, g_ref[b]).astype(BF)
            gs_ref[there, :D] = dot(put, xs_ref[b]).astype(BF)
            gs_ref[there, D:] = dot(put, dots_ref[b]).astype(BF)

    if not plane:
        return

    gate, up, low_down, high_down = range(4)
    low_rows, high_rows = slice(0, half), slice(half, 2 * half)

    def swap(e, i):
        slot = e % 2
        return remote(
            stage_refs[i].at[slot, :, :, 1 - c],
            pair_refs[i].at[e % 3],
            csend.at[slot, i],
            crecv.at[e % 3, i],
            by_c,
        )

    def first(e, k):
        slot = e % 3
        source = {
            gate: lambda: pair_refs[0].at[slot, :, 1 - x],
            up: lambda: pair_refs[1].at[slot, 1 - y],
            low_down: lambda: pair_refs[2].at[slot, :, 1 - x, low_rows],
            high_down: lambda: pair_refs[2].at[slot, 1 - y, :, high_rows],
        }[k]()
        device = by_x if k in (gate, low_down) else by_y
        return remote(source, one_refs[k].at[slot], psend.at[slot, k], precv.at[slot, k], device)

    def second(e, k):
        along_x = k in (gate, low_down)
        source = one_refs[k].at[e % 3, 1 - y] if along_x else one_refs[k].at[e % 3, 1 - x]
        slot = e % 2
        return remote(
            source,
            two_refs[k].at[slot],
            qsend.at[slot, k],
            qrecv.at[slot, k],
            by_y if along_x else by_x,
        )

    def add(first_value, second_value):
        return (first_value.astype(F32) + second_value.astype(F32)).astype(BF)

    @pl.when(step >= 3)
    def _():
        e = step - 3
        for k in range(4):
            second(e, k).wait()
        own = [one_refs[k][e % 3, y if k in (gate, low_down) else x] for k in range(4)]
        out_gate_ref[0] = add(own[gate], two_refs[gate][e % 2])
        out_up_ref[0] = add(own[up], two_refs[up][e % 2])
        out_down_ref[0, low_rows] = add(own[low_down], two_refs[low_down][e % 2])
        out_down_ref[0, high_rows] = add(own[high_down], two_refs[high_down][e % 2])

    @pl.when((step >= 2) & (step < local + 2))
    def _():
        e = step - 2
        slot = e % 3
        for k in range(4):
            first(e, k).wait()
            for t in (0, 1):
                mine = {
                    gate: lambda: pair_refs[0][slot, t, x],
                    up: lambda: pair_refs[1][slot, y, t],
                    low_down: lambda: pair_refs[2][slot, t, x, low_rows],
                    high_down: lambda: pair_refs[2][slot, y, t, high_rows],
                }[k]()
                one_refs[k][slot, t] = add(mine, one_refs[k][slot, t])
            second(e, k).start()

    @pl.when((step >= 1) & (step < local + 1))
    def _():
        e = step - 1
        slot = e % 3
        for i in range(3):
            swap(e, i).wait()

            def pair_sum(t, carry):
                a, b = t // 2, t % 2
                pair_refs[i][slot, a, b] = add(
                    stage_refs[i][e % 2, a, b, c], pair_refs[i][slot, a, b]
                )
                return carry

            lax.fori_loop(0, 4, pair_sum, 0)
        for k in range(4):
            first(e, k).start()

    @pl.when(step < local)
    def _():
        for i in range(3):
            swap(step, i).start()


def run_experts(
    x_all, ct_all, router_t, rank_row, rank_col, w_gate, w_up, w_down, rows, capacity, plane, collective_id
):
    total = x_all.shape[0]
    blocks, local = total // rows, w_gate.shape[0]
    slots = local * capacity
    sizes = (blocks, rows, local, capacity)
    whole = lambda shape: pl.BlockSpec(
        shape, lambda e: (0,) * len(shape), pipeline_mode=pl.Buffered(1)
    )
    per = lambda shape: pl.BlockSpec((1,) + shape, lambda e: (jnp.minimum(e, local - 1), 0, 0))
    shapes = ((D, FF), (D, FF), (FF, D))
    scratch = [
        pltpu.VMEM((blocks, slots, D), BF),
        pltpu.VMEM((blocks, slots, D), BF),
        pltpu.VMEM((blocks, slots, 1), F32),
        pltpu.VMEM((blocks, slots, LANES), BF),
    ]
    params = dict(dimension_semantics=("arbitrary",), vmem_limit_bytes=62 * 1024 * 1024)
    if plane:
        eighths = [(a // 8, b) for a, b in shapes]
        out = lambda shape: pl.BlockSpec((1,) + shape, lambda e: (jnp.maximum(e - 3, 0), 0, 0))
        grad_shapes, grad_specs = eighths, [out(shape) for shape in eighths]
        low = (eighths[2][0] // 2, eighths[2][1])
        passed = (eighths[0], eighths[1], low, low)
        scratch += [pltpu.VMEM((2, 2, 2, 2) + shape, BF) for shape in eighths]
        scratch += [pltpu.VMEM((3, 2, 2) + shape, BF) for shape in eighths]
        scratch += [pltpu.VMEM((3, 2) + shape, BF) for shape in passed]
        scratch += [pltpu.VMEM((2,) + shape, BF) for shape in passed]
        sems = [(2, 3), (3, 3), (3, 4), (3, 4), (2, 4), (2, 4)]
        scratch += [pltpu.SemaphoreType.DMA(shape) for shape in sems]
        params |= dict(collective_id=collective_id, has_side_effects=True)
    else:
        grad_shapes, grad_specs = shapes, [per(shape) for shape in shapes]
    flops = 2 * total * D * slots * 4 // blocks + 18 * blocks * slots * D * FF
    return pl.pallas_call(
        functools.partial(expert_kernel, sizes, plane),
        grid=(local + 3 if plane else local,),
        out_shape=[
            jax.ShapeDtypeStruct((total, D), BF),
            jax.ShapeDtypeStruct((total, D + LANES), BF),
        ]
        + [jax.ShapeDtypeStruct((local,) + shape, BF) for shape in grad_shapes],
        in_specs=[
            whole((total, D)),
            whole((total, D)),
            whole((EXPERTS, D)),
            whole((EXPERTS, total)),
            whole((total, EXPERTS)),
        ]
        + [per(shape) for shape in shapes],
        out_specs=[whole((total, D)), whole((total, D + LANES))] + grad_specs,
        scratch_shapes=scratch,
        compiler_params=pltpu.CompilerParams(**params),
        cost_estimate=pl.CostEstimate(
            flops=flops, bytes_accessed=2 * (6 * local * D * FF + 4 * total * D), transcendentals=0
        ),
        name="experts",
    )(x_all, ct_all, router_t, rank_row, rank_col, w_gate, w_up, w_down)


def gather_rows(value):
    return lax.all_gather(value, "expert", axis=0, tiled=True)


def scatter_rows(value):
    return lax.psum_scatter(value, "expert", scatter_dimension=0, tiled=True)


def per_device(
    tokens,
    lengths,
    routes,
    norm_gain1,
    w_query,
    key_projection,
    value_projection,
    w_out,
    norm_gain2,
    w_router,
    w_gate,
    w_up,
    w_down,
    cotangent,
):
    rows = tokens.shape[0]
    n, groups = lax.axis_size("expert"), lax.axis_size("group")
    my_index = lax.axis_index("expert")
    capacity = 3 * rows * TOP // (2 * EXPERTS)
    group_of_heads = QUERY_HEADS // KEY_VALUE_HEADS
    score_scale = HEAD_DIMENSION ** (-0.5)
    query_width, key_width = w_query.shape[1], key_projection.shape[1]
    length = lengths[0]
    positions = my_index * rows + jnp.arange(rows, dtype=jnp.int32)
    valid_rows = (positions < length)[:, None]
    grad_output = jnp.where(valid_rows, cotangent, jnp.zeros_like(cotangent))

    small = jnp.concatenate(
        [w_router, norm_gain1[:, None], norm_gain2[:, None]]
        + [jnp.zeros((w_router.shape[0], LANES - EXPERTS - 2), BF)],
        axis=1,
    )
    qkv_weight, out_weight, small = gather_weights(
        w_query, key_projection, value_projection, w_out, small, n, 1
    )
    router_weight = small[:, :EXPERTS]
    gain_one = small[:, EXPERTS].astype(F32)
    gain_two = small[:, EXPERTS + 1].astype(F32)

    expert_ids = jnp.arange(EXPERTS, dtype=jnp.int32)
    hot = jnp.any(routes[:, :, None] == expert_ids, axis=1)
    row_id = jnp.arange(rows, dtype=jnp.int32)
    earlier = (row_id[:, None] < row_id[None, :]).astype(BF)
    rank = jnp.where(hot.T, dot(hot.T.astype(BF), earlier), 255.0).astype(BF)
    ct_all = gather_rows(grad_output)

    cosine_lookup, sine_lookup = rotary_tables(positions, HEAD_DIMENSION)
    token_f32 = tokens.astype(F32)
    inverse_one = lax.rsqrt(jnp.mean(token_f32 * token_f32, axis=-1, keepdims=True) + EPSILON)
    unit_one = token_f32 * inverse_one
    first_norm = (unit_one * gain_one).astype(BF)
    qkv = dot(first_norm, qkv_weight)
    query_pre = qkv[:, :query_width]
    unrotated_key = qkv[:, query_width : query_width + key_width]
    value_pre = qkv[:, query_width + key_width :]
    query_rows = apply_rotation(
        query_pre.reshape(rows, QUERY_HEADS, HEAD_DIMENSION), cosine_lookup, sine_lookup
    ).astype(BF)
    query_rows = query_rows.reshape(rows, KEY_VALUE_HEADS, group_of_heads, HEAD_DIMENSION)
    local_keys = apply_rotation(
        unrotated_key.reshape(rows, KEY_VALUE_HEADS, HEAD_DIMENSION), cosine_lookup, sine_lookup
    ).astype(BF)
    local_keys = local_keys.reshape(rows, key_width)
    kv_all, rank_all = line_gather(
        [jnp.concatenate([local_keys, value_pre.astype(BF)], axis=1), rank], n, 2, "gather_kv"
    )
    rank_all = rank_all.reshape(n, EXPERTS, rows)
    rank_row = jnp.transpose(rank_all, (1, 0, 2)).reshape(EXPERTS, n * rows).astype(F32)
    rank_col = jnp.transpose(rank_all, (0, 2, 1)).reshape(n * rows, EXPERTS)
    key_portion = kv_all[:, :key_width].reshape(-1, KEY_VALUE_HEADS, HEAD_DIMENSION)
    value_portion = kv_all[:, key_width:].reshape(-1, KEY_VALUE_HEADS, HEAD_DIMENSION)
    key_count = kv_all.shape[0]
    scores = (
        jnp.einsum("qhgd,khd->hgqk", query_rows, key_portion, preferred_element_type=F32)
        * score_scale
    )
    columns = jnp.arange(key_count, dtype=jnp.int32)
    allowed = (columns[None, :] <= positions[:, None]) & (columns[None, :] < length)
    masked = jnp.where(allowed, scores, NEGATIVE_LARGE)
    maximum = jnp.max(masked, axis=-1)
    weights = jnp.where(allowed, jnp.exp(masked - maximum[..., None]), 0.0)
    total = jnp.sum(weights, axis=-1)
    mixed_f32 = (
        jnp.einsum(
            "hgqk,khd->hgqd", weights.astype(BF), value_portion, preferred_element_type=F32
        )
        / total[..., None]
    )
    log_total = maximum + jnp.log(total)
    mixed_low = jnp.transpose(mixed_f32, (2, 0, 1, 3)).reshape(rows, query_width).astype(BF)
    residual = token_f32 + dot(mixed_low, out_weight)
    inverse_two = lax.rsqrt(jnp.mean(residual * residual, axis=-1, keepdims=True) + EPSILON)
    unit_two = residual * inverse_two
    second_norm = (unit_two * gain_two).astype(BF)
    (x_all,) = line_gather([second_norm], n, 3, "gather_rows")

    y_part, gs_part, grad_gate, grad_up, grad_down = run_experts(
        x_all, ct_all, router_weight.T, rank_row, rank_col, w_gate, w_up, w_down, rows, capacity, groups == 8, 7
    )
    gs = line_scatter(gs_part, n, F32, 4, "scatter_grads")
    expert_sum = scatter_rows(y_part).astype(F32)
    mixed = (residual + expert_sum).astype(BF)

    logits = dot(second_norm, router_weight)
    chosen = jnp.where(hot, logits, NEGATIVE_LARGE)
    gate_weights = jnp.where(hot, jnp.exp(chosen - jnp.max(chosen, axis=-1, keepdims=True)), 0.0)
    gate_weights = gate_weights / jnp.sum(gate_weights, axis=-1, keepdims=True)
    grad_gates = gs[:, D : D + EXPERTS] + gs[:, D + EXPERTS : D + 2 * EXPERTS]
    grad_gates = grad_gates + gs[:, D + 2 * EXPERTS : D + 3 * EXPERTS]
    grad_logits = (
        gate_weights * (grad_gates - jnp.sum(gate_weights * grad_gates, axis=-1, keepdims=True))
    ).astype(BF)
    grad_second = gs[:, :D] + dot_nt(grad_logits, router_weight)
    grad_router = dot_tn(second_norm, grad_logits)
    scaled_two = grad_second * gain_two
    grad_gain2 = jnp.sum(grad_second * unit_two, axis=0)
    grad_residual = grad_output.astype(F32) + inverse_two * (
        scaled_two - unit_two * jnp.mean(scaled_two * unit_two, axis=-1, keepdims=True)
    )
    grad_attn = grad_residual.astype(BF)
    grad_out = dot_tn(mixed_low, grad_attn)
    mixed_gradient = dot_nt(grad_attn, out_weight).astype(BF)
    head_gradient = mixed_gradient.reshape(rows, KEY_VALUE_HEADS, group_of_heads, HEAD_DIMENSION)
    delta = jnp.einsum("qhgd,hgqd->hgq", head_gradient, mixed_f32, preferred_element_type=F32)
    probability = jnp.where(allowed, jnp.exp(masked - log_total[..., None]), 0.0)
    grad_prob = jnp.einsum(
        "qhgd,khd->hgqk", head_gradient, value_portion, preferred_element_type=F32
    )
    grad_scores = (probability * (grad_prob - delta[..., None])).astype(BF)
    grad_query_acc = jnp.einsum(
        "hgqk,khd->qhgd", grad_scores, key_portion, preferred_element_type=F32
    )
    key_gradient = jnp.einsum(
        "hgqk,qhgd->khd", grad_scores, query_rows, preferred_element_type=F32
    ).reshape(key_count, key_width)
    value_gradient = jnp.einsum(
        "hgqk,qhgd->khd", probability.astype(BF), head_gradient, preferred_element_type=F32
    ).reshape(key_count, key_width)
    kv_gradient = line_scatter(
        jnp.concatenate([key_gradient.astype(BF), value_gradient.astype(BF)], axis=1),
        n,
        BF,
        5,
        "scatter_kv",
    )
    own_key_gradient = kv_gradient[:, :key_width].astype(F32)
    grad_query_rows = grad_query_acc.reshape(rows, QUERY_HEADS, HEAD_DIMENSION) * score_scale
    grad_query_pre = (
        apply_rotation(grad_query_rows, cosine_lookup, -sine_lookup)
        .reshape(rows, query_width)
        .astype(BF)
    )
    grad_key_pre = apply_rotation(
        own_key_gradient.reshape(rows, KEY_VALUE_HEADS, HEAD_DIMENSION) * score_scale,
        cosine_lookup,
        -sine_lookup,
    )
    grad_key_pre = grad_key_pre.reshape(rows, key_width).astype(BF)
    grad_qkv_pre = jnp.concatenate(
        [grad_query_pre, grad_key_pre, kv_gradient[:, key_width:]], axis=1
    )
    grad_qkv = dot_tn(first_norm, grad_qkv_pre)
    grad_first = dot_nt(grad_qkv_pre, qkv_weight)
    scaled_one = grad_first * gain_one
    grad_gain1 = jnp.sum(grad_first * unit_one, axis=0)
    grad_tokens = grad_residual + inverse_one * (
        scaled_one - unit_one * jnp.mean(scaled_one * unit_one, axis=-1, keepdims=True)
    )
    grad_small = jnp.concatenate(
        [grad_router, grad_gain1[:, None], grad_gain2[:, None]]
        + [jnp.zeros((D, LANES - EXPERTS - 2), F32)],
        axis=1,
    )
    shares = (grad_qkv.astype(BF), grad_out.astype(BF), grad_small.astype(BF))
    if groups == 8:
        shares = reduce_weights(*shares, query_width, n, 6)
    else:
        shares = [lax.psum(scatter_rows(share), "group") for share in shares]
    share_qkv, share_out, share_small = [share.astype(F32) for share in shares]

    def sum_over_groups(value):
        if groups != 8:
            value = lax.psum_scatter(value, "group", scatter_dimension=1, tiled=True)
        return lax.all_gather(value, "group", axis=1, tiled=True).astype(F32)

    return (
        mixed,
        grad_tokens,
        share_small[:, EXPERTS],
        share_qkv[:, :query_width],
        share_qkv[:, query_width : query_width + key_width],
        share_qkv[:, query_width + key_width :],
        share_out,
        share_small[:, EXPERTS + 1],
        share_small[:, :EXPERTS],
        sum_over_groups(grad_gate),
        sum_over_groups(grad_up),
        sum_over_groups(grad_down),
    )


def solution(mesh):
    rows = P(("group", "expert"), None)
    vector, matrix, stack = P("expert"), P("expert", None), P("expert", None, None)
    return jax.shard_map(
        per_device,
        mesh=mesh,
        in_specs=(
            rows,
            P("group"),
            rows,
            vector,
            matrix,
            matrix,
            matrix,
            matrix,
            vector,
            matrix,
            stack,
            stack,
            stack,
            rows,
        ),
        out_specs=(
            rows,
            rows,
            vector,
            matrix,
            matrix,
            matrix,
            matrix,
            vector,
            matrix,
            stack,
            stack,
            stack,
        ),
        check_vma=False,
    )
```

```python
import functools

import jax
import jax.numpy as jnp
from jax import lax
from jax.experimental import pallas as pl
from jax.experimental.pallas import tpu as pltpu
from jax.sharding import PartitionSpec as P

D = 1024
QUERY_HEADS = 16
KEY_VALUE_HEADS = 8
HEAD_DIMENSION = 64
EXPERTS = 32
TOP = 8
FF = 512
LANES = 128

EPSILON = 1e-05
NEGATIVE_LARGE = -1e30
BF = jnp.bfloat16
F32 = jnp.float32


def rotary_tables(positions, head_size):
    half_width = head_size // 2
    frequency = 10000.0 ** (-2.0 * jnp.arange(half_width).astype(F32) / head_size)
    angles = positions.astype(F32)[:, None] * frequency[None, :]
    return (jnp.cos(angles)[:, None, :], jnp.sin(angles)[:, None, :])


def apply_rotation(tensor_in, cosine_lookup, sine_lookup):
    half_width = tensor_in.shape[-1] // 2
    first_half = tensor_in[..., :half_width]
    second_half = tensor_in[..., half_width:]
    return jnp.concatenate(
        [
            first_half * cosine_lookup - second_half * sine_lookup,
            second_half * cosine_lookup + first_half * sine_lookup,
        ],
        axis=-1,
    )


def dot(a, b):
    return jnp.dot(a, b, preferred_element_type=F32)


def dot_nt(a, b):
    return lax.dot_general(a, b, (((1,), (1,)), ((), ())), preferred_element_type=F32)


def dot_tn(a, b):
    return lax.dot_general(a, b, (((0,), (0,)), ((), ())), preferred_element_type=F32)


MESH = pl.DeviceIdType.MESH
ANY = pl.BlockSpec(memory_space=pl.ANY)
IN_VMEM = pl.BlockSpec(memory_space=pltpu.VMEM)


def remote(source, target, send, receive, device):
    return pltpu.make_async_remote_copy(
        src_ref=source,
        dst_ref=target,
        send_sem=send,
        recv_sem=receive,
        device_id=device,
        device_id_type=MESH,
    )


def greet(devices):
    barrier = pltpu.get_barrier_semaphore()
    count = 0
    for condition, device in devices:
        if condition is None:
            pl.semaphore_signal(barrier, inc=1, device_id=device, device_id_type=MESH)
            count = count + 1
        else:

            @pl.when(condition)
            def _():
                pl.semaphore_signal(barrier, inc=1, device_id=device, device_id_type=MESH)

            count = count + jnp.where(condition, 1, 0)
    pl.semaphore_wait(barrier, count)


def line_gather_kernel(n, count, *refs):
    ins, outs = refs[:count], refs[count : 2 * count]
    local, send, receive = refs[2 * count :]
    group, me = lax.axis_index("group"), lax.axis_index("expert")
    left, right = (group, me - 1), (group, me + 1)
    own = [
        pltpu.make_async_copy(ins[i], outs[i].at[me], local.at[i]) for i in range(count)
    ]
    for copy in own:
        copy.start()
    greet([(me > 0, left), (me < n - 1, right)])

    def hop(i, step, side):
        block = me - step if side == 0 else me + step
        source = ins[i] if step == 0 else outs[i].at[block]
        index = (side, step, i)
        return remote(
            source, outs[i].at[block], send.at[index], receive.at[index], right if side == 0 else left
        )

    def arrival(i, step, side):
        block = me - 1 - step if side == 0 else me + 1 + step
        index = (side, step, i)
        return remote(
            outs[i].at[block], outs[i].at[block], send.at[index], receive.at[index], left if side == 0 else right
        )

    def sends(step, side):
        return (me - step >= 0) & (me < n - 1) if side == 0 else (me + step < n) & (me > 0)

    def arrives(step, side):
        return me - 1 - step >= 0 if side == 0 else me + 1 + step < n

    for step in range(n - 1):
        for side in (0, 1):

            @pl.when(sends(step, side))
            def _():
                for i in range(count):
                    hop(i, step, side).start()

        for side in (0, 1):

            @pl.when(arrives(step, side))
            def _():
                for i in range(count):
                    arrival(i, step, side).wait_recv()

    for step in range(n - 1):
        for side in (0, 1):

            @pl.when(sends(step, side))
            def _():
                for i in range(count):
                    hop(i, step, side).wait_send()

    for copy in own:
        copy.wait()


def line_gather(values, n, collective_id, name):
    count = len(values)
    outs = pl.pallas_call(
        functools.partial(line_gather_kernel, n, count),
        out_shape=[jax.ShapeDtypeStruct((n,) + v.shape, v.dtype) for v in values],
        in_specs=[IN_VMEM] * count,
        out_specs=[ANY] * count,
        scratch_shapes=[
            pltpu.SemaphoreType.DMA((count,)),
            pltpu.SemaphoreType.DMA((2, n - 1, count)),
            pltpu.SemaphoreType.DMA((2, n - 1, count)),
        ],
        compiler_params=pltpu.CompilerParams(collective_id=collective_id, has_side_effects=True),
        cost_estimate=pl.CostEstimate(flops=0, bytes_accessed=100000000, transcendentals=0),
        name=name,
    )(*values)
    return [o.reshape((n * v.shape[0],) + v.shape[1:]) for o, v in zip(outs, values)]


def line_scatter_kernel(n, part_ref, out_ref, landing, staging, send, receive):
    group, me = lax.axis_index("group"), lax.axis_index("expert")
    left, right = (group, me - 1), (group, me + 1)
    rows = part_ref.shape[1]
    tile = 32
    greet([(me > 0, left), (me < n - 1, right)])

    def add(target, first, second):
        def body(t, carry):
            span = pl.ds(pl.multiple_of(t * tile, tile), tile)
            target[span, :] = (first[span, :].astype(F32) + second[span, :].astype(F32)).astype(
                target.dtype
            )
            return carry

        lax.fori_loop(0, rows // tile, body, 0)

    def copy(source, step, side):
        return remote(
            source,
            landing.at[side, step],
            send.at[side, step],
            receive.at[side, step],
            right if side == 0 else left,
        )

    for step in range(n - 1):
        for side in (0, 1):
            owner = n - 1 - step if side == 0 else step
            beyond = me < owner if side == 0 else me > owner
            edge = me == 0 if side == 0 else me == n - 1

            @pl.when(beyond & edge)
            def _():
                copy(part_ref.at[owner], step, side).start()

            @pl.when(beyond & jnp.logical_not(edge))
            def _():
                copy(part_ref.at[owner], step, side).wait_recv()
                add(staging.at[side, step], part_ref.at[owner], landing.at[side, step])
                copy(staging.at[side, step], step, side).start()

    @pl.when(me > 0)
    def _():
        step = n - 1 - me
        copy(part_ref.at[me], step, 0).wait_recv()

    @pl.when(me < n - 1)
    def _():
        copy(part_ref.at[me], me, 1).wait_recv()

    def finish(t, carry):
        span = pl.ds(pl.multiple_of(t * tile, tile), tile)
        total = part_ref[me, span, :].astype(F32)
        from_left = landing[0, jnp.minimum(n - 1 - me, n - 2), span, :].astype(F32)
        from_right = landing[1, jnp.minimum(me, n - 2), span, :].astype(F32)
        total = total + jnp.where(me > 0, from_left, 0.0)
        total = total + jnp.where(me < n - 1, from_right, 0.0)
        out_ref[span, :] = total.astype(out_ref.dtype)
        return carry

    lax.fori_loop(0, rows // tile, finish, 0)
    for step in range(n - 1):
        for side in (0, 1):
            owner = n - 1 - step if side == 0 else step
            beyond = me < owner if side == 0 else me > owner

            @pl.when(beyond)
            def _():
                copy(part_ref.at[owner], step, side).wait_send()


def line_scatter(value, n, dtype, collective_id, name):
    total, width = value.shape
    rows = total // n
    return pl.pallas_call(
        functools.partial(line_scatter_kernel, n),
        out_shape=jax.ShapeDtypeStruct((rows, width), dtype),
        in_specs=[IN_VMEM],
        out_specs=IN_VMEM,
        scratch_shapes=[
            pltpu.VMEM((2, n - 1, rows, width), BF),
            pltpu.VMEM((2, n - 1, rows, width), BF),
            pltpu.SemaphoreType.DMA((2, n - 1)),
            pltpu.SemaphoreType.DMA((2, n - 1)),
        ],
        compiler_params=pltpu.CompilerParams(collective_id=collective_id, has_side_effects=True),
        cost_estimate=pl.CostEstimate(flops=0, bytes_accessed=100000000, transcendentals=0),
        name=name,
    )(value.reshape(n, rows, width))


def plane_position():
    group, me = lax.axis_index("group"), lax.axis_index("expert")
    c, x, y = group % 2, (group // 2) % 2, (group // 4) % 2
    by_c, by_x, by_y = (group + 1 - 2 * c, me), (group + 2 - 4 * x, me), (group + 4 - 8 * y, me)
    return group, me, (y, x, c), (by_y, by_x, by_c)


def weights_kernel(n, pieces, widths, *refs):
    wq, wk, wv, wo, small = refs[:5]
    outs, owns = refs[5:8], refs[8:11]
    load, store, zsend, zrecv, psend, precv, csend, crecv = refs[11:]
    group, me, (y, x, c), (by_y, by_x, by_c) = plane_position()
    left, right = (group, me - 1), (group, me + 1)
    eighth = owns[0].shape[0]
    span = pl.ds(pl.multiple_of((y * 4 + x * 2 + c) * eighth, eighth), eighth)
    query_width, key_width = wq.shape[1], wk.shape[1]
    targets = (
        owns[0].at[:, :query_width],
        owns[0].at[:, query_width : query_width + key_width],
        owns[0].at[:, query_width + key_width :],
        owns[1],
        owns[2],
    )
    loads = [
        pltpu.make_async_copy(source.at[span, :], target, load.at[i])
        for i, (source, target) in enumerate(zip((wq, wk, wv, wo, small), targets))
    ]
    for copy in loads:
        copy.start()
    for copy in loads:
        copy.wait()
    stores = [
        pltpu.make_async_copy(owns[i], outs[i].at[me, y, x, c], store.at[i]) for i in range(3)
    ]
    for copy in stores:
        copy.start()
    greet(
        [(me > 0, left), (me < n - 1, right), (None, by_c), (None, by_x), (None, by_y)]
    )

    def hop(i, step, side):
        block = me - step if side == 0 else me + step
        source = owns[i] if step == 0 else outs[i].at[block, y, x, c]
        index = (side, step, i)
        return remote(
            source,
            outs[i].at[block, y, x, c],
            zsend.at[index],
            zrecv.at[index],
            right if side == 0 else left,
        )

    def sends(step, side):
        return (me - step >= 0) & (me < n - 1) if side == 0 else (me + step < n) & (me > 0)

    def first(slot, block, p):
        i, start, width, along_x = pieces[p]
        spot = outs[i].at[block, y, x, c, :, start : start + width]
        source = owns[i].at[:, start : start + width] if slot == 0 else spot
        index = (0, slot, p)
        return remote(source, spot, psend.at[index], precv.at[index], by_x if along_x else by_y)

    def second(slot, block, p):
        i, start, width, along_x = pieces[p]
        columns = slice(start, start + width)
        if along_x:
            spot = outs[i].at[block, y, :, c, :, columns]
        else:
            spot = outs[i].at[block, :, x, c, :, columns]
        index = (1, slot, p)
        return remote(spot, spot, psend.at[index], precv.at[index], by_y if along_x else by_x)

    def third(slot, block, i):
        spot = outs[i].at[block, :, :, c]
        index = (slot, i)
        return remote(spot, spot, csend.at[index], crecv.at[index], by_c)

    def held(step):
        if step == 0:
            return [(0, me, me >= 0)]
        return [(step, me - step, me - step >= 0), (n - 1 + step, me + step, me + step < n)]

    count = len(pieces)
    for step in range(n + 2):
        if step < n:
            for slot, block, there in held(step):

                @pl.when(there)
                def _():
                    if step > 0:
                        side = 0 if slot < n else 1
                        for i in range(3):
                            hop(i, step - 1, side).wait_recv()
                    for p in range(count):
                        first(slot, block, p).start()

            if step < n - 1:
                for side in (0, 1):

                    @pl.when(sends(step, side))
                    def _():
                        for i in range(3):
                            hop(i, step, side).start()

        if 1 <= step < n + 1:
            if step == 1:
                for copy in stores:
                    copy.wait()
            for slot, block, there in held(step - 1):

                @pl.when(there)
                def _():
                    for p in range(count):
                        first(slot, block, p).wait_recv()
                    for p in range(count):
                        second(slot, block, p).start()

        if step >= 2:
            for slot, block, there in held(step - 2):

                @pl.when(there)
                def _():
                    for p in range(count):
                        second(slot, block, p).wait_recv()
                    for i in range(3):
                        third(slot, block, i).start()

    for step in range(n):
        for slot, block, there in held(step):

            @pl.when(there)
            def _():
                for p in range(count):
                    first(slot, block, p).wait_send()
                    second(slot, block, p).wait_send()
                for i in range(3):
                    third(slot, block, i).wait()

        if step < n - 1:
            for side in (0, 1):

                @pl.when(sends(step, side))
                def _():
                    for i in range(3):
                        hop(i, step, side).wait_send()


def path_pieces(query_width, key_width, out_width, small_width):
    half = (query_width + 2 * key_width + out_width) // 2
    return (
        (0, 0, half, True),
        (0, half, query_width + 2 * key_width - half, False),
        (1, 0, out_width, False),
        (2, 0, small_width, True),
    )


def gather_weights(wq, wk, wv, wo, small, n, collective_id):
    rows = wq.shape[0]
    eighth = rows // 8
    widths = (wq.shape[1] + wk.shape[1] + wv.shape[1], wo.shape[1], small.shape[1])
    pieces = path_pieces(wq.shape[1], wk.shape[1], wo.shape[1], small.shape[1])
    outs = pl.pallas_call(
        functools.partial(weights_kernel, n, pieces, widths),
        out_shape=[jax.ShapeDtypeStruct((n, 2, 2, 2, eighth, w), BF) for w in widths],
        in_specs=[ANY] * 5,
        out_specs=[ANY] * 3,
        scratch_shapes=[pltpu.VMEM((eighth, w), BF) for w in widths]
        + [
            pltpu.SemaphoreType.DMA((5,)),
            pltpu.SemaphoreType.DMA((3,)),
            pltpu.SemaphoreType.DMA((2, n - 1, 3)),
            pltpu.SemaphoreType.DMA((2, n - 1, 3)),
            pltpu.SemaphoreType.DMA((2, 2 * n - 1, 4)),
            pltpu.SemaphoreType.DMA((2, 2 * n - 1, 4)),
            pltpu.SemaphoreType.DMA((2 * n - 1, 3)),
            pltpu.SemaphoreType.DMA((2 * n - 1, 3)),
        ],
        compiler_params=pltpu.CompilerParams(collective_id=collective_id, has_side_effects=True),
        cost_estimate=pl.CostEstimate(flops=0, bytes_accessed=100000000, transcendentals=0),
        name="gather_weights",
    )(wq, wk, wv, wo, small)
    return [o.reshape(n * rows, w) for o, w in zip(outs, widths)]


def reduce_kernel(n, pieces, *refs):
    ins, outs = refs[:3], refs[3:5]
    pair, one, two, landing, staging = refs[5:7], refs[7:9], refs[9:11], refs[11:13], refs[13:15]
    csend, crecv, psend, precv, zsend, zrecv, gsend, grecv = refs[15:]
    group, me, (y, x, c), (by_y, by_x, by_c) = plane_position()
    left, right = (group, me - 1), (group, me + 1)
    eighth = pair[0].shape[3]
    greet(
        [(me > 0, left), (me < n - 1, right), (None, by_c), (None, by_x), (None, by_y)]
    )

    places, ends = [], [0, 0]
    for array, start, width, along_x in pieces:
        path = 0 if along_x else 1
        places.append((array, start, width, path, ends[path]))
        ends[path] += width

    def swap(p):
        array, start, width, path, at = places[p]
        return remote(
            ins[array].at[:, :, :, 1 - c, :, start : start + width],
            pair[path].at[:, :, :, :, at : at + width],
            csend.at[p],
            crecv.at[p],
            by_c,
        )

    for p in range(len(places)):
        swap(p).start()
    for p in range(len(places)):
        swap(p).wait_recv()
        array, start, width, path, at = places[p]

        def pair_sum(t, carry):
            z, a, b = t // 4, (t // 2) % 2, t % 2
            mine = ins[array][z, a, b, c, :, start : start + width].astype(F32)
            theirs = pair[path][z, a, b, :, at : at + width].astype(F32)
            pair[path][z, a, b, :, at : at + width] = (mine + theirs).astype(BF)
            return carry

        lax.fori_loop(0, 4 * n, pair_sum, 0)

    def first(path):
        source = pair[0].at[:, :, 1 - x] if path == 0 else pair[1].at[:, 1 - y]
        return remote(
            source, one[path], psend.at[0, path], precv.at[0, path], by_x if path == 0 else by_y
        )

    def second(path):
        source = one[path].at[:, 1 - y] if path == 0 else one[path].at[:, 1 - x]
        return remote(
            source, two[path], psend.at[1, path], precv.at[1, path], by_y if path == 0 else by_x
        )

    for path in (0, 1):
        first(path).start()
    for path in (0, 1):
        first(path).wait_recv()

        def first_sum(t, carry):
            z, a = t // 2, t % 2
            mine = pair[0][z, a, x] if path == 0 else pair[1][z, y, a]
            one[path][z, a] = (mine.astype(F32) + one[path][z, a].astype(F32)).astype(BF)
            return carry

        lax.fori_loop(0, 2 * n, first_sum, 0)
        second(path).start()
    for path in (0, 1):
        second(path).wait_recv()

        def second_sum(z, carry):
            mine = one[0][z, y] if path == 0 else one[1][z, x]
            two[path][z] = (mine.astype(F32) + two[path][z].astype(F32)).astype(BF)
            return carry

        lax.fori_loop(0, n, second_sum, 0)

    def hop(source, path, step, side):
        index = (path, side, step)
        return remote(
            source,
            landing[path].at[side, step],
            zsend.at[index],
            zrecv.at[index],
            right if side == 0 else left,
        )

    for step in range(n - 1):
        for side in (0, 1):
            owner = n - 1 - step if side == 0 else step
            beyond = me < owner if side == 0 else me > owner
            edge = me == 0 if side == 0 else me == n - 1

            @pl.when(beyond & edge)
            def _():
                for path in (0, 1):
                    hop(two[path].at[owner], path, step, side).start()

            @pl.when(beyond & jnp.logical_not(edge))
            def _():
                for path in (0, 1):
                    hop(two[path].at[owner], path, step, side).wait_recv()
                    staging[path][side, step] = (
                        two[path][owner].astype(F32) + landing[path][side, step].astype(F32)
                    ).astype(BF)
                    hop(staging[path].at[side, step], path, step, side).start()

    @pl.when(me > 0)
    def _():
        for path in (0, 1):
            hop(two[path].at[me], path, n - 1 - me, 0).wait_recv()

    @pl.when(me < n - 1)
    def _():
        for path in (0, 1):
            hop(two[path].at[me], path, me, 1).wait_recv()

    for path in (0, 1):
        total = two[path][me].astype(F32)
        from_left = landing[path][0, jnp.minimum(n - 1 - me, n - 2)].astype(F32)
        from_right = landing[path][1, jnp.minimum(me, n - 2)].astype(F32)
        total = total + jnp.where(me > 0, from_left, 0.0)
        total = total + jnp.where(me < n - 1, from_right, 0.0)
        outs[path][y, x, c] = total.astype(BF)

    def spread(path, stage):
        out = outs[path]
        if stage == 2:
            spot, device = out.at[:, :, c], by_c
        elif stage == 0:
            spot, device = out.at[y, x, c], by_x if path == 0 else by_y
        elif path == 0:
            spot, device = out.at[y, :, c], by_y
        else:
            spot, device = out.at[:, x, c], by_x
        return remote(spot, spot, gsend.at[path, stage], grecv.at[path, stage], device)

    for stage in range(3):
        for path in (0, 1):
            spread(path, stage).start()
        for path in (0, 1):
            spread(path, stage).wait_recv()

    for path in (0, 1):
        for stage in range(3):
            spread(path, stage).wait_send()
        first(path).wait_send()
        second(path).wait_send()
    for p in range(len(places)):
        swap(p).wait_send()
    for step in range(n - 1):
        for side in (0, 1):
            owner = n - 1 - step if side == 0 else step
            beyond = me < owner if side == 0 else me > owner

            @pl.when(beyond)
            def _():
                for path in (0, 1):
                    hop(two[path].at[owner], path, step, side).wait_send()


def reduce_weights(grad_qkv, grad_out, grad_small, query_width, n, collective_id):
    values = (grad_qkv, grad_out, grad_small)
    rows = grad_qkv.shape[0] // n
    eighth = rows // 8
    key_width = (grad_qkv.shape[1] - query_width) // 2
    pieces = path_pieces(query_width, key_width, grad_out.shape[1], grad_small.shape[1])
    widths = [sum(p[2] for p in pieces if p[3]), sum(p[2] for p in pieces if not p[3])]
    scratch = [pltpu.VMEM((n, 2, 2, eighth, w), BF) for w in widths]
    scratch += [pltpu.VMEM((n, 2, eighth, w), BF) for w in widths]
    scratch += [pltpu.VMEM((n, eighth, w), BF) for w in widths]
    scratch += [pltpu.VMEM((2, n - 1, eighth, w), BF) for w in widths] * 2
    sems = [(4,), (4,), (2, 2), (2, 2), (2, 2, n - 1), (2, 2, n - 1), (2, 3), (2, 3)]
    outs = pl.pallas_call(
        functools.partial(reduce_kernel, n, pieces),
        out_shape=[jax.ShapeDtypeStruct((2, 2, 2, eighth, w), BF) for w in widths],
        in_specs=[IN_VMEM] * 3,
        out_specs=[IN_VMEM] * 2,
        scratch_shapes=scratch + [pltpu.SemaphoreType.DMA(s) for s in sems],
        compiler_params=pltpu.CompilerParams(
            collective_id=collective_id, has_side_effects=True, vmem_limit_bytes=48 * 1024 * 1024
        ),
        cost_estimate=pl.CostEstimate(flops=0, bytes_accessed=100000000, transcendentals=0),
        name="reduce_weights",
    )(*[v.reshape(n, 2, 2, 2, eighth, v.shape[1]) for v in values])
    first, second = [o.reshape(rows, w) for o, w in zip(outs, widths)]
    cut = pieces[0][2]
    rest = pieces[1][2]
    qkv = jnp.concatenate([first[:, :cut], second[:, :rest]], axis=1)
    return qkv, second[:, rest:], first[:, cut:]


def expert_kernel(sizes, plane, *refs):
    blocks, rows, local, capacity = sizes
    x_ref, ct_ref, router_t_ref, rank_row_ref, rank_col_ref = refs[:5]
    w_gate_ref, w_up_ref, w_down_ref = refs[5:8]
    y_ref, gs_ref, out_gate_ref, out_up_ref, out_down_ref = refs[8:13]
    xs_ref, g_ref, gate_slot_ref, dots_ref = refs[13:17]
    slots = local * capacity
    step = pl.program_id(0)
    base = lax.axis_index("expert") * local
    if plane:
        stage_refs, pair_refs, one_refs, two_refs = refs[17:20], refs[20:23], refs[23:27], refs[27:31]
        csend, crecv, psend, precv, qsend, qrecv = refs[31:]
        _, _, (y, x, c), (by_y, by_x, by_c) = plane_position()
        half = stage_refs[2].shape[4] // 2

        @pl.when(step == 0)
        def _():
            greet([(None, by_c), (None, by_x), (None, by_y)])

    @pl.when(step == 0)
    def _():
        logits = dot_nt(router_t_ref[...], x_ref[...])
        hot = rank_row_ref[...] < 200.0
        top = jnp.max(jnp.where(hot, logits, NEGATIVE_LARGE), axis=0, keepdims=True)
        weight = jnp.where(hot, jnp.exp(jnp.minimum(logits - top, 0.0)), 0.0)
        gates = weight / jnp.sum(weight, axis=0, keepdims=True)
        expert_id = lax.broadcasted_iota(jnp.int32, gates.shape, 0)
        slot_id = lax.broadcasted_iota(jnp.int32, (capacity, rows), 0).astype(F32)
        rank_rows, gate_rows = [], []
        for e in range(local):
            mine = expert_id == base + e
            rank_rows.append(jnp.sum(jnp.where(mine, rank_row_ref[...], 0.0), 0, keepdims=True))
            gate_rows.append(jnp.sum(jnp.where(mine, gates, 0.0), 0, keepdims=True))
        for b in range(blocks):
            here = slice(b * rows, (b + 1) * rows)
            pieces = []
            for e in range(local):
                taken = jnp.broadcast_to(rank_rows[e][:, here], (capacity, rows)) == slot_id
                gate = jnp.sum(jnp.where(taken, gate_rows[e][:, here], 0.0), 1, keepdims=True)
                gate_slot_ref[b, e * capacity : (e + 1) * capacity, :] = gate
                pieces.append(jnp.where(taken, 1.0, 0.0).astype(BF))
            pick = jnp.concatenate(pieces, axis=0)
            xs_ref[b] = dot(pick, x_ref[here, :]).astype(BF)
            g_ref[b] = dot(pick, ct_ref[here, :]).astype(BF)

    @pl.when(step < local)
    def _():
        here = pl.ds(pl.multiple_of(step * capacity, capacity), capacity)
        xs = jnp.concatenate([xs_ref[b, here, :] for b in range(blocks)], axis=0)
        g = jnp.concatenate([g_ref[b, here, :] for b in range(blocks)], axis=0).astype(F32)
        gate_slot = jnp.concatenate([gate_slot_ref[b, here, :] for b in range(blocks)], axis=0)
        w_gate, w_up, w_down = w_gate_ref[0], w_up_ref[0], w_down_ref[0]
        gate_pre = dot(xs, w_gate)
        up_pre = dot(xs, w_up)
        sigmoid = jax.nn.sigmoid(gate_pre)
        silu = gate_pre * sigmoid
        activation = (silu * up_pre).astype(BF)
        expert_out = dot(activation, w_down).astype(BF).astype(F32)
        slot_dot = jnp.sum(g * expert_out, axis=1, keepdims=True)
        grad_out = (gate_slot * g).astype(BF)
        scaled_out = (gate_slot * expert_out).astype(BF)
        grad_down = dot_tn(activation, grad_out).astype(BF)
        grad_activation = dot_nt(grad_out, w_down)
        grad_gate_pre = (
            grad_activation * up_pre * sigmoid * (1.0 + gate_pre * (1.0 - sigmoid))
        ).astype(BF)
        grad_up_pre = (grad_activation * silu).astype(BF)
        grad_gate = dot_tn(xs, grad_gate_pre).astype(BF)
        grad_up = dot_tn(xs, grad_up_pre).astype(BF)
        if plane:
            for ref, value in zip(stage_refs, (grad_gate, grad_up, grad_down)):
                ref[step % 2] = value.reshape(ref.shape[1:])
        else:
            out_gate_ref[0], out_up_ref[0], out_down_ref[0] = grad_gate, grad_up, grad_down
        grad_in = (dot_nt(grad_gate_pre, w_gate) + dot_nt(grad_up_pre, w_up)).astype(BF)
        lane = lax.broadcasted_iota(jnp.int32, (blocks * capacity, LANES), 1)
        high = slot_dot.astype(BF).astype(F32)
        middle = (slot_dot - high).astype(BF).astype(F32)
        low = slot_dot - high - middle
        mine = base + step
        dots = jnp.where(lane == mine, high, 0.0)
        dots = jnp.where(lane == mine + EXPERTS, middle, dots)
        dots = jnp.where(lane == mine + 2 * EXPERTS, low, dots).astype(BF)
        for b in range(blocks):
            part = slice(b * capacity, (b + 1) * capacity)
            xs_ref[b, here, :] = grad_in[part]
            g_ref[b, here, :] = scaled_out[part]
            dots_ref[b, here, :] = dots[part]

    @pl.when(step == (local if plane else local - 1))
    def _():
        slot_expert = lax.broadcasted_iota(jnp.int32, (EXPERTS, slots), 1) // capacity
        spread_row = lax.broadcasted_iota(jnp.int32, (EXPERTS, slots), 0)
        spread = jnp.where(spread_row == slot_expert + base, 1.0, 0.0).astype(BF)
        slot_rank = (lax.broadcasted_iota(jnp.int32, (rows, slots), 1) % capacity).astype(F32)
        for b in range(blocks):
            there = slice(b * rows, (b + 1) * rows)
            ranks = dot(rank_col_ref[there, :], spread)
            put = jnp.where(ranks == slot_rank, 1.0, 0.0).astype(BF)
            y_ref[there, :] = dot(put, g_ref[b]).astype(BF)
            gs_ref[there, :D] = dot(put, xs_ref[b]).astype(BF)
            gs_ref[there, D:] = dot(put, dots_ref[b]).astype(BF)

    if not plane:
        return

    gate, up, low_down, high_down = range(4)
    low_rows, high_rows = slice(0, half), slice(half, 2 * half)

    def swap(e, i):
        slot = e % 2
        return remote(
            stage_refs[i].at[slot, :, :, 1 - c],
            pair_refs[i].at[e % 3],
            csend.at[slot, i],
            crecv.at[e % 3, i],
            by_c,
        )

    def first(e, k):
        slot = e % 3
        source = {
            gate: lambda: pair_refs[0].at[slot, :, 1 - x],
            up: lambda: pair_refs[1].at[slot, 1 - y],
            low_down: lambda: pair_refs[2].at[slot, :, 1 - x, low_rows],
            high_down: lambda: pair_refs[2].at[slot, 1 - y, :, high_rows],
        }[k]()
        device = by_x if k in (gate, low_down) else by_y
        return remote(source, one_refs[k].at[slot], psend.at[slot, k], precv.at[slot, k], device)

    def second(e, k):
        along_x = k in (gate, low_down)
        source = one_refs[k].at[e % 3, 1 - y] if along_x else one_refs[k].at[e % 3, 1 - x]
        slot = e % 2
        return remote(
            source,
            two_refs[k].at[slot],
            qsend.at[slot, k],
            qrecv.at[slot, k],
            by_y if along_x else by_x,
        )

    def add(first_value, second_value):
        return (first_value.astype(F32) + second_value.astype(F32)).astype(BF)

    @pl.when(step >= 3)
    def _():
        e = step - 3
        for k in range(4):
            second(e, k).wait()
        own = [one_refs[k][e % 3, y if k in (gate, low_down) else x] for k in range(4)]
        out_gate_ref[0] = add(own[gate], two_refs[gate][e % 2])
        out_up_ref[0] = add(own[up], two_refs[up][e % 2])
        out_down_ref[0, low_rows] = add(own[low_down], two_refs[low_down][e % 2])
        out_down_ref[0, high_rows] = add(own[high_down], two_refs[high_down][e % 2])

    @pl.when((step >= 2) & (step < local + 2))
    def _():
        e = step - 2
        slot = e % 3
        for k in range(4):
            first(e, k).wait()
            for t in (0, 1):
                mine = {
                    gate: lambda: pair_refs[0][slot, t, x],
                    up: lambda: pair_refs[1][slot, y, t],
                    low_down: lambda: pair_refs[2][slot, t, x, low_rows],
                    high_down: lambda: pair_refs[2][slot, y, t, high_rows],
                }[k]()
                one_refs[k][slot, t] = add(mine, one_refs[k][slot, t])
            second(e, k).start()

    @pl.when((step >= 1) & (step < local + 1))
    def _():
        e = step - 1
        slot = e % 3
        for i in range(3):
            swap(e, i).wait()

            def pair_sum(t, carry):
                a, b = t // 2, t % 2
                pair_refs[i][slot, a, b] = add(
                    stage_refs[i][e % 2, a, b, c], pair_refs[i][slot, a, b]
                )
                return carry

            lax.fori_loop(0, 4, pair_sum, 0)
        for k in range(4):
            first(e, k).start()

    @pl.when(step < local)
    def _():
        for i in range(3):
            swap(step, i).start()


def run_experts(
    x_all, ct_all, router_t, rank_row, rank_col, w_gate, w_up, w_down, rows, capacity, plane, collective_id
):
    total = x_all.shape[0]
    blocks, local = total // rows, w_gate.shape[0]
    slots = local * capacity
    sizes = (blocks, rows, local, capacity)
    whole = lambda shape: pl.BlockSpec(
        shape, lambda e: (0,) * len(shape), pipeline_mode=pl.Buffered(1)
    )
    per = lambda shape: pl.BlockSpec((1,) + shape, lambda e: (jnp.minimum(e, local - 1), 0, 0))
    shapes = ((D, FF), (D, FF), (FF, D))
    scratch = [
        pltpu.VMEM((blocks, slots, D), BF),
        pltpu.VMEM((blocks, slots, D), BF),
        pltpu.VMEM((blocks, slots, 1), F32),
        pltpu.VMEM((blocks, slots, LANES), BF),
    ]
    params = dict(dimension_semantics=("arbitrary",), vmem_limit_bytes=62 * 1024 * 1024)
    if plane:
        eighths = [(a // 8, b) for a, b in shapes]
        out = lambda shape: pl.BlockSpec((1,) + shape, lambda e: (jnp.maximum(e - 3, 0), 0, 0))
        grad_shapes, grad_specs = eighths, [out(shape) for shape in eighths]
        low = (eighths[2][0] // 2, eighths[2][1])
        passed = (eighths[0], eighths[1], low, low)
        scratch += [pltpu.VMEM((2, 2, 2, 2) + shape, BF) for shape in eighths]
        scratch += [pltpu.VMEM((3, 2, 2) + shape, BF) for shape in eighths]
        scratch += [pltpu.VMEM((3, 2) + shape, BF) for shape in passed]
        scratch += [pltpu.VMEM((2,) + shape, BF) for shape in passed]
        sems = [(2, 3), (3, 3), (3, 4), (3, 4), (2, 4), (2, 4)]
        scratch += [pltpu.SemaphoreType.DMA(shape) for shape in sems]
        params |= dict(collective_id=collective_id, has_side_effects=True)
    else:
        grad_shapes, grad_specs = shapes, [per(shape) for shape in shapes]
    flops = 2 * total * D * slots * 4 // blocks + 18 * blocks * slots * D * FF
    return pl.pallas_call(
        functools.partial(expert_kernel, sizes, plane),
        grid=(local + 3 if plane else local,),
        out_shape=[
            jax.ShapeDtypeStruct((total, D), BF),
            jax.ShapeDtypeStruct((total, D + LANES), BF),
        ]
        + [jax.ShapeDtypeStruct((local,) + shape, BF) for shape in grad_shapes],
        in_specs=[
            whole((total, D)),
            whole((total, D)),
            whole((EXPERTS, D)),
            whole((EXPERTS, total)),
            whole((total, EXPERTS)),
        ]
        + [per(shape) for shape in shapes],
        out_specs=[whole((total, D)), whole((total, D + LANES))] + grad_specs,
        scratch_shapes=scratch,
        compiler_params=pltpu.CompilerParams(**params),
        cost_estimate=pl.CostEstimate(
            flops=flops, bytes_accessed=2 * (6 * local * D * FF + 4 * total * D), transcendentals=0
        ),
        name="experts",
    )(x_all, ct_all, router_t, rank_row, rank_col, w_gate, w_up, w_down)


def mask_bias(bias_ref, length_ref, rows):
    base = lax.axis_index("expert") * rows
    key = lax.broadcasted_iota(jnp.int32, bias_ref.shape, 0)
    query = lax.broadcasted_iota(jnp.int32, bias_ref.shape, 1) + base
    allowed = (key <= query) & (key < length_ref[0])
    bias_ref[...] = jnp.where(allowed, 0.0, NEGATIVE_LARGE)


def head_columns(ref, head):
    start = 2 * HEAD_DIMENSION * head
    middle = start + HEAD_DIMENSION
    return jnp.concatenate([ref[:, start:middle], ref[:, middle : middle + HEAD_DIMENSION]], 0)


def put_heads(ref, head, transposed):
    rows = ref.shape[0]
    value = transposed.T
    start = 2 * HEAD_DIMENSION * head
    middle = start + HEAD_DIMENSION
    ref[:, start:middle] = value[:rows].astype(ref.dtype)
    ref[:, middle : middle + HEAD_DIMENSION] = value[rows:].astype(ref.dtype)


def attention_kernel(length_ref, q_ref, kv_ref, mixed_ref, log_total_ref, bias_ref):
    @pl.when(pl.program_id(0) == 0)
    def _():
        mask_bias(bias_ref, length_ref, q_ref.shape[0])

    bias = jnp.concatenate([bias_ref[...]] * 2, axis=1)
    for head in (0, 1):
        columns = slice(head * HEAD_DIMENSION, (head + 1) * HEAD_DIMENSION)
        key, value = kv_ref[:, :LANES][:, columns], kv_ref[:, LANES:][:, columns]
        query = head_columns(q_ref, head) * jnp.asarray(HEAD_DIMENSION**-0.5, BF)
        scores = dot_nt(key, query) + bias
        top = jnp.max(scores, axis=0, keepdims=True)
        weights = jnp.exp(scores - top)
        total = jnp.sum(weights, axis=0, keepdims=True)
        put_heads(mixed_ref, head, dot_tn(value, weights.astype(BF)) / total)
        log_total_ref[0, head : head + 1, :] = top + jnp.log(total)


def attention(length, query, kv_all):
    rows, keys = query.shape[0], kv_all.shape[0]
    pairs = KEY_VALUE_HEADS // 2
    return pl.pallas_call(
        attention_kernel,
        grid=(pairs,),
        out_shape=(
            jax.ShapeDtypeStruct(query.shape, BF),
            jax.ShapeDtypeStruct((pairs, 2, 2 * rows), F32),
        ),
        in_specs=[
            pl.BlockSpec(memory_space=pltpu.SMEM),
            pl.BlockSpec((rows, 2 * LANES), lambda j: (0, j)),
            pl.BlockSpec((keys, 2 * LANES), lambda j: (0, j)),
        ],
        out_specs=(
            pl.BlockSpec((rows, 2 * LANES), lambda j: (0, j)),
            pl.BlockSpec((1, 2, 2 * rows), lambda j: (j, 0, 0)),
        ),
        scratch_shapes=[pltpu.VMEM((keys, rows), F32)],
        compiler_params=pltpu.CompilerParams(
            dimension_semantics=("arbitrary",), vmem_limit_bytes=48 * 1024 * 1024
        ),
        cost_estimate=pl.CostEstimate(
            flops=16 * rows * keys * D, bytes_accessed=4 * keys * D, transcendentals=0
        ),
        name="attention",
    )(length, query, kv_all)


def attention_back_kernel(
    length_ref, q_ref, kv_ref, grad_ref, log_total_ref, grad_q_ref, grad_kv_ref, bias_ref
):
    @pl.when(pl.program_id(0) == 0)
    def _():
        mask_bias(bias_ref, length_ref, q_ref.shape[0])

    scale = HEAD_DIMENSION**-0.5
    bias = jnp.concatenate([bias_ref[...]] * 2, axis=1)
    for head in (0, 1):
        columns = slice(head * HEAD_DIMENSION, (head + 1) * HEAD_DIMENSION)
        key, value = kv_ref[:, :LANES][:, columns], kv_ref[:, LANES:][:, columns]
        query = head_columns(q_ref, head) * jnp.asarray(scale, BF)
        grad = head_columns(grad_ref, head)
        scores = dot_nt(key, query) + bias
        probs = jnp.exp(scores - log_total_ref[0, head : head + 1, :])
        grad_probs = dot_nt(value, grad)
        delta = jnp.sum(probs * grad_probs, axis=0, keepdims=True)
        grad_scores = (probs * (grad_probs - delta)).astype(BF)
        grad_kv_ref[:, head * HEAD_DIMENSION : (head + 1) * HEAD_DIMENSION] = dot(
            grad_scores, query
        ).astype(BF)
        start = LANES + head * HEAD_DIMENSION
        grad_kv_ref[:, start : start + HEAD_DIMENSION] = dot(probs.astype(BF), grad).astype(BF)
        put_heads(grad_q_ref, head, dot_tn(key, grad_scores) * scale)


def attention_back(length, query, kv_all, grad_mixed, log_total):
    rows, keys = query.shape[0], kv_all.shape[0]
    pairs = KEY_VALUE_HEADS // 2
    row_spec = pl.BlockSpec((rows, 2 * LANES), lambda j: (0, j))
    key_spec = pl.BlockSpec((keys, 2 * LANES), lambda j: (0, j))
    return pl.pallas_call(
        attention_back_kernel,
        grid=(pairs,),
        out_shape=(
            jax.ShapeDtypeStruct(query.shape, F32),
            jax.ShapeDtypeStruct(kv_all.shape, BF),
        ),
        in_specs=[
            pl.BlockSpec(memory_space=pltpu.SMEM),
            row_spec,
            key_spec,
            row_spec,
            pl.BlockSpec((1, 2, 2 * rows), lambda j: (j, 0, 0)),
        ],
        out_specs=(row_spec, key_spec),
        scratch_shapes=[pltpu.VMEM((keys, rows), F32)],
        compiler_params=pltpu.CompilerParams(
            dimension_semantics=("arbitrary",), vmem_limit_bytes=48 * 1024 * 1024
        ),
        cost_estimate=pl.CostEstimate(
            flops=40 * rows * keys * D, bytes_accessed=6 * keys * D, transcendentals=0
        ),
        name="attention_back",
    )(length, query, kv_all, grad_mixed, log_total)


def pair_columns(first, second):
    rows = first.shape[0]
    both = [value.reshape(rows, -1, 1, LANES) for value in (first, second)]
    return jnp.concatenate(both, axis=2).reshape(rows, -1)


def unpair_columns(value):
    rows = value.shape[0]
    value = value.reshape(rows, -1, 2, LANES)
    return value[:, :, 0].reshape(rows, -1), value[:, :, 1].reshape(rows, -1)


def gather_rows(value):
    return lax.all_gather(value, "expert", axis=0, tiled=True)


def scatter_rows(value):
    return lax.psum_scatter(value, "expert", scatter_dimension=0, tiled=True)


def per_device(
    tokens,
    lengths,
    routes,
    norm_gain1,
    w_query,
    key_projection,
    value_projection,
    w_out,
    norm_gain2,
    w_router,
    w_gate,
    w_up,
    w_down,
    cotangent,
):
    rows = tokens.shape[0]
    n, groups = lax.axis_size("expert"), lax.axis_size("group")
    my_index = lax.axis_index("expert")
    capacity = 3 * rows * TOP // (2 * EXPERTS)
    query_width, key_width = w_query.shape[1], key_projection.shape[1]
    length = lengths[0]
    positions = my_index * rows + jnp.arange(rows, dtype=jnp.int32)
    valid_rows = (positions < length)[:, None]
    grad_output = jnp.where(valid_rows, cotangent, jnp.zeros_like(cotangent))

    small = jnp.concatenate(
        [w_router, norm_gain1[:, None], norm_gain2[:, None]]
        + [jnp.zeros((w_router.shape[0], LANES - EXPERTS - 2), BF)],
        axis=1,
    )
    qkv_weight, out_weight, small = gather_weights(
        w_query, key_projection, value_projection, w_out, small, n, 1
    )
    router_weight = small[:, :EXPERTS]
    gain_one = small[:, EXPERTS].astype(F32)
    gain_two = small[:, EXPERTS + 1].astype(F32)

    expert_ids = jnp.arange(EXPERTS, dtype=jnp.int32)
    hot = jnp.any(routes[:, :, None] == expert_ids, axis=1)
    row_id = jnp.arange(rows, dtype=jnp.int32)
    earlier = (row_id[:, None] < row_id[None, :]).astype(BF)
    rank = jnp.where(hot.T, dot(hot.T.astype(BF), earlier), 255.0).astype(BF)

    cosine_lookup, sine_lookup = rotary_tables(positions, HEAD_DIMENSION)
    token_f32 = tokens.astype(F32)
    inverse_one = lax.rsqrt(jnp.mean(token_f32 * token_f32, axis=-1, keepdims=True) + EPSILON)
    unit_one = token_f32 * inverse_one
    first_norm = (unit_one * gain_one).astype(BF)
    qkv = dot(first_norm, qkv_weight)
    query_pre = qkv[:, :query_width]
    unrotated_key = qkv[:, query_width : query_width + key_width]
    value_pre = qkv[:, query_width + key_width :]
    query_rows = apply_rotation(
        query_pre.reshape(rows, QUERY_HEADS, HEAD_DIMENSION), cosine_lookup, sine_lookup
    ).astype(BF)
    query_rows = query_rows.reshape(rows, query_width)
    local_keys = apply_rotation(
        unrotated_key.reshape(rows, KEY_VALUE_HEADS, HEAD_DIMENSION), cosine_lookup, sine_lookup
    ).astype(BF)
    local_keys = local_keys.reshape(rows, key_width)
    kv_all, rank_all = line_gather(
        [pair_columns(local_keys, value_pre.astype(BF)), rank], n, 2, "gather_kv"
    )
    rank_all = rank_all.reshape(n, EXPERTS, rows)
    rank_row = jnp.transpose(rank_all, (1, 0, 2)).reshape(EXPERTS, n * rows).astype(F32)
    rank_col = jnp.transpose(rank_all, (0, 2, 1)).reshape(n * rows, EXPERTS)
    grad_output_late, kv_all = lax.optimization_barrier((grad_output, kv_all))
    ct_all = gather_rows(grad_output_late)
    mixed_low, log_total = attention(lengths, query_rows, kv_all)
    residual = token_f32 + dot(mixed_low, out_weight)
    inverse_two = lax.rsqrt(jnp.mean(residual * residual, axis=-1, keepdims=True) + EPSILON)
    unit_two = residual * inverse_two
    second_norm = (unit_two * gain_two).astype(BF)
    (x_all,) = line_gather([second_norm], n, 3, "gather_rows")

    y_part, gs_part, grad_gate, grad_up, grad_down = run_experts(
        x_all, ct_all, router_weight.T, rank_row, rank_col, w_gate, w_up, w_down, rows, capacity, groups == 8, 7
    )
    gs = line_scatter(gs_part, n, F32, 4, "scatter_grads")

    logits = dot(second_norm, router_weight)
    chosen = jnp.where(hot, logits, NEGATIVE_LARGE)
    gate_weights = jnp.where(hot, jnp.exp(chosen - jnp.max(chosen, axis=-1, keepdims=True)), 0.0)
    gate_weights = gate_weights / jnp.sum(gate_weights, axis=-1, keepdims=True)
    grad_gates = gs[:, D : D + EXPERTS] + gs[:, D + EXPERTS : D + 2 * EXPERTS]
    grad_gates = grad_gates + gs[:, D + 2 * EXPERTS : D + 3 * EXPERTS]
    grad_logits = (
        gate_weights * (grad_gates - jnp.sum(gate_weights * grad_gates, axis=-1, keepdims=True))
    ).astype(BF)
    grad_second = gs[:, :D] + dot_nt(grad_logits, router_weight)
    grad_router = dot_tn(second_norm, grad_logits)
    scaled_two = grad_second * gain_two
    grad_gain2 = jnp.sum(grad_second * unit_two, axis=0)
    grad_residual = grad_output.astype(F32) + inverse_two * (
        scaled_two - unit_two * jnp.mean(scaled_two * unit_two, axis=-1, keepdims=True)
    )
    grad_attn = grad_residual.astype(BF)
    grad_out = dot_tn(mixed_low, grad_attn)
    mixed_gradient = dot_nt(grad_attn, out_weight).astype(BF)
    grad_query_acc, kv_terms = attention_back(
        lengths, query_rows, kv_all, mixed_gradient, log_total
    )
    kv_gradient = line_scatter(kv_terms, n, BF, 5, "scatter_kv")
    kv_gradient, y_part = lax.optimization_barrier((kv_gradient, y_part))
    expert_sum = scatter_rows(y_part).astype(F32)
    mixed = (residual + expert_sum).astype(BF)
    own_key_gradient, own_value_gradient = unpair_columns(kv_gradient)
    grad_query_pre = (
        apply_rotation(
            grad_query_acc.reshape(rows, QUERY_HEADS, HEAD_DIMENSION), cosine_lookup, -sine_lookup
        )
        .reshape(rows, query_width)
        .astype(BF)
    )
    grad_key_pre = apply_rotation(
        own_key_gradient.astype(F32).reshape(rows, KEY_VALUE_HEADS, HEAD_DIMENSION),
        cosine_lookup,
        -sine_lookup,
    )
    grad_key_pre = grad_key_pre.reshape(rows, key_width).astype(BF)
    grad_qkv_pre = jnp.concatenate(
        [grad_query_pre, grad_key_pre, own_value_gradient], axis=1
    )
    grad_qkv = dot_tn(first_norm, grad_qkv_pre)
    grad_first = dot_nt(grad_qkv_pre, qkv_weight)
    scaled_one = grad_first * gain_one
    grad_gain1 = jnp.sum(grad_first * unit_one, axis=0)
    grad_tokens = grad_residual + inverse_one * (
        scaled_one - unit_one * jnp.mean(scaled_one * unit_one, axis=-1, keepdims=True)
    )
    grad_small = jnp.concatenate(
        [grad_router, grad_gain1[:, None], grad_gain2[:, None]]
        + [jnp.zeros((D, LANES - EXPERTS - 2), F32)],
        axis=1,
    )
    shares = (grad_qkv.astype(BF), grad_out.astype(BF), grad_small.astype(BF))
    if groups == 8:
        shares = reduce_weights(*shares, query_width, n, 6)
    else:
        shares = [lax.psum(scatter_rows(share), "group") for share in shares]
    share_qkv, share_out, share_small = [share.astype(F32) for share in shares]

    def sum_over_groups(value):
        if groups != 8:
            value = lax.psum_scatter(value, "group", scatter_dimension=1, tiled=True)
        return lax.all_gather(value, "group", axis=1, tiled=True).astype(F32)

    return (
        mixed,
        grad_tokens,
        share_small[:, EXPERTS],
        share_qkv[:, :query_width],
        share_qkv[:, query_width : query_width + key_width],
        share_qkv[:, query_width + key_width :],
        share_out,
        share_small[:, EXPERTS + 1],
        share_small[:, :EXPERTS],
        sum_over_groups(grad_gate),
        sum_over_groups(grad_up),
        sum_over_groups(grad_down),
    )


def solution(mesh):
    rows = P(("group", "expert"), None)
    vector, matrix, stack = P("expert"), P("expert", None), P("expert", None, None)
    return jax.shard_map(
        per_device,
        mesh=mesh,
        in_specs=(
            rows,
            P("group"),
            rows,
            vector,
            matrix,
            matrix,
            matrix,
            matrix,
            vector,
            matrix,
            stack,
            stack,
            stack,
            rows,
        ),
        out_specs=(
            rows,
            rows,
            vector,
            matrix,
            matrix,
            matrix,
            matrix,
            vector,
            matrix,
            stack,
            stack,
            stack,
        ),
        check_vma=False,
    )
```

```python
import functools

import jax
import jax.numpy as jnp
from jax import lax
from jax.experimental import pallas as pl
from jax.experimental.pallas import tpu as pltpu
from jax.sharding import PartitionSpec as P

D = 1024
QUERY_HEADS = 16
KEY_VALUE_HEADS = 8
HEAD_DIMENSION = 64
EXPERTS = 32
TOP = 8
FF = 512
LANES = 128

EPSILON = 1e-05
NEGATIVE_LARGE = -1e30
BF = jnp.bfloat16
F32 = jnp.float32


def rotary_tables(positions, head_size):
    half_width = head_size // 2
    frequency = 10000.0 ** (-2.0 * jnp.arange(half_width).astype(F32) / head_size)
    angles = positions.astype(F32)[:, None] * frequency[None, :]
    return (jnp.cos(angles)[:, None, :], jnp.sin(angles)[:, None, :])


def apply_rotation(tensor_in, cosine_lookup, sine_lookup):
    half_width = tensor_in.shape[-1] // 2
    first_half = tensor_in[..., :half_width]
    second_half = tensor_in[..., half_width:]
    return jnp.concatenate(
        [
            first_half * cosine_lookup - second_half * sine_lookup,
            second_half * cosine_lookup + first_half * sine_lookup,
        ],
        axis=-1,
    )


def dot(a, b):
    return jnp.dot(a, b, preferred_element_type=F32)


def dot_nt(a, b):
    return lax.dot_general(a, b, (((1,), (1,)), ((), ())), preferred_element_type=F32)


def dot_tn(a, b):
    return lax.dot_general(a, b, (((0,), (0,)), ((), ())), preferred_element_type=F32)


MESH = pl.DeviceIdType.MESH
ANY = pl.BlockSpec(memory_space=pl.ANY)
IN_VMEM = pl.BlockSpec(memory_space=pltpu.VMEM)


def remote(source, target, send, receive, device):
    return pltpu.make_async_remote_copy(
        src_ref=source,
        dst_ref=target,
        send_sem=send,
        recv_sem=receive,
        device_id=device,
        device_id_type=MESH,
    )


def greet(devices):
    barrier = pltpu.get_barrier_semaphore()
    count = 0
    for condition, device in devices:
        if condition is None:
            pl.semaphore_signal(barrier, inc=1, device_id=device, device_id_type=MESH)
            count = count + 1
        else:

            @pl.when(condition)
            def _():
                pl.semaphore_signal(barrier, inc=1, device_id=device, device_id_type=MESH)

            count = count + jnp.where(condition, 1, 0)
    pl.semaphore_wait(barrier, count)


def line_gather_kernel(n, count, *refs):
    ins, outs = refs[:count], refs[count : 2 * count]
    local, send, receive = refs[2 * count :]
    group, me = lax.axis_index("group"), lax.axis_index("expert")
    left, right = (group, me - 1), (group, me + 1)
    own = [
        pltpu.make_async_copy(ins[i], outs[i].at[me], local.at[i]) for i in range(count)
    ]
    for copy in own:
        copy.start()
    greet([(me > 0, left), (me < n - 1, right)])

    def hop(i, step, side):
        block = me - step if side == 0 else me + step
        source = ins[i] if step == 0 else outs[i].at[block]
        index = (side, step, i)
        return remote(
            source, outs[i].at[block], send.at[index], receive.at[index], right if side == 0 else left
        )

    def arrival(i, step, side):
        block = me - 1 - step if side == 0 else me + 1 + step
        index = (side, step, i)
        return remote(
            outs[i].at[block], outs[i].at[block], send.at[index], receive.at[index], left if side == 0 else right
        )

    def sends(step, side):
        return (me - step >= 0) & (me < n - 1) if side == 0 else (me + step < n) & (me > 0)

    def arrives(step, side):
        return me - 1 - step >= 0 if side == 0 else me + 1 + step < n

    for step in range(n - 1):
        for side in (0, 1):

            @pl.when(sends(step, side))
            def _():
                for i in range(count):
                    hop(i, step, side).start()

        for side in (0, 1):

            @pl.when(arrives(step, side))
            def _():
                for i in range(count):
                    arrival(i, step, side).wait_recv()

    for step in range(n - 1):
        for side in (0, 1):

            @pl.when(sends(step, side))
            def _():
                for i in range(count):
                    hop(i, step, side).wait_send()

    for copy in own:
        copy.wait()


def line_gather(values, n, collective_id, name):
    count = len(values)
    outs = pl.pallas_call(
        functools.partial(line_gather_kernel, n, count),
        out_shape=[jax.ShapeDtypeStruct((n,) + v.shape, v.dtype) for v in values],
        in_specs=[IN_VMEM] * count,
        out_specs=[ANY] * count,
        scratch_shapes=[
            pltpu.SemaphoreType.DMA((count,)),
            pltpu.SemaphoreType.DMA((2, n - 1, count)),
            pltpu.SemaphoreType.DMA((2, n - 1, count)),
        ],
        compiler_params=pltpu.CompilerParams(collective_id=collective_id, has_side_effects=True),
        cost_estimate=pl.CostEstimate(flops=0, bytes_accessed=100000000, transcendentals=0),
        name=name,
    )(*values)
    return [o.reshape((n * v.shape[0],) + v.shape[1:]) for o, v in zip(outs, values)]


class LineSum:
    def __init__(self, n, part, landing, staging, send, receive):
        self.n, self.part, self.landing, self.staging = n, part, landing, staging
        self.send, self.receive = send, receive
        self.group, self.me = lax.axis_index("group"), lax.axis_index("expert")
        self.rows = part.shape[1]
        self.tile = min(32, self.rows)

    def neighbours(self):
        left, right = (self.group, self.me - 1), (self.group, self.me + 1)
        return [(self.me > 0, left), (self.me < self.n - 1, right)]

    def copy(self, source, step, side):
        index = (side, step)
        device = (self.group, self.me + 1 if side == 0 else self.me - 1)
        return remote(
            source, self.landing.at[index], self.send.at[index], self.receive.at[index], device
        )

    def places(self):
        me, n = self.me, self.n
        for step in range(n - 1):
            for side in (0, 1):
                owner = n - 1 - step if side == 0 else step
                beyond = me < owner if side == 0 else me > owner
                edge = me == 0 if side == 0 else me == n - 1
                yield step, side, owner, beyond, edge

    def start(self):
        for step, side, owner, beyond, edge in self.places():

            @pl.when(beyond & edge)
            def _():
                self.copy(self.part.at[owner], step, side).start()

    def spans(self, body):
        def tile_body(t, carry):
            body(pl.ds(pl.multiple_of(t * self.tile, self.tile), self.tile))
            return carry

        lax.fori_loop(0, self.rows // self.tile, tile_body, 0)

    def forward(self, only):
        for step, side, owner, beyond, edge in self.places():
            if step != only:
                continue

            @pl.when(beyond & jnp.logical_not(edge))
            def _():
                self.copy(self.part.at[owner], step, side).wait_recv()

                def add(span):
                    total = self.part[owner, span, :].astype(F32)
                    total = total + self.landing[side, step, span, :].astype(F32)
                    self.staging[side, step, span, :] = total.astype(BF)

                self.spans(add)
                self.copy(self.staging.at[side, step], step, side).start()

    def finish(self, out_ref):
        me, n = self.me, self.n

        @pl.when(me > 0)
        def _():
            self.copy(self.part.at[me], n - 1 - me, 0).wait_recv()

        @pl.when(me < n - 1)
        def _():
            self.copy(self.part.at[me], me, 1).wait_recv()

        def total(span):
            value = self.part[me, span, :].astype(F32)
            from_left = self.landing[0, jnp.minimum(n - 1 - me, n - 2), span, :].astype(F32)
            from_right = self.landing[1, jnp.minimum(me, n - 2), span, :].astype(F32)
            value = value + jnp.where(me > 0, from_left, 0.0)
            value = value + jnp.where(me < n - 1, from_right, 0.0)
            out_ref[span, :] = value.astype(out_ref.dtype)

        self.spans(total)
        for step, side, owner, beyond, edge in self.places():

            @pl.when(beyond)
            def _():
                self.copy(self.part.at[owner], step, side).wait_send()


def line_sum_scratch(n, rows, width):
    return [
        pltpu.VMEM((2, n - 1, rows, width), BF),
        pltpu.VMEM((2, n - 1, rows, width), BF),
        pltpu.SemaphoreType.DMA((2, n - 1)),
        pltpu.SemaphoreType.DMA((2, n - 1)),
    ]


def line_scatter_kernel(n, part_ref, out_ref, *scratch):
    line = LineSum(n, part_ref, *scratch)
    greet(line.neighbours())
    line.start()
    for step in range(n - 1):
        line.forward(step)
    line.finish(out_ref)


def line_scatter(value, n, dtype, collective_id, name):
    total, width = value.shape
    rows = total // n
    return pl.pallas_call(
        functools.partial(line_scatter_kernel, n),
        out_shape=jax.ShapeDtypeStruct((rows, width), dtype),
        in_specs=[IN_VMEM],
        out_specs=IN_VMEM,
        scratch_shapes=line_sum_scratch(n, rows, width),
        compiler_params=pltpu.CompilerParams(collective_id=collective_id, has_side_effects=True),
        cost_estimate=pl.CostEstimate(flops=0, bytes_accessed=100000000, transcendentals=0),
        name=name,
    )(value.reshape(n, rows, width))


def plane_position():
    group, me = lax.axis_index("group"), lax.axis_index("expert")
    c, x, y = group % 2, (group // 2) % 2, (group // 4) % 2
    by_c, by_x, by_y = (group + 1 - 2 * c, me), (group + 2 - 4 * x, me), (group + 4 - 8 * y, me)
    return group, me, (y, x, c), (by_y, by_x, by_c)


def weights_kernel(n, pieces, widths, *refs):
    wq, wk, wv, wo, small, extra = refs[:6]
    outs, extra_out, owns = refs[6:9], refs[9], refs[10:13]
    load, store, zsend, zrecv, psend, precv, csend, crecv, xsend, xrecv = refs[13:]
    group, me, (y, x, c), (by_y, by_x, by_c) = plane_position()
    left, right = (group, me - 1), (group, me + 1)
    eighth = owns[0].shape[0]
    span = pl.ds(pl.multiple_of((y * 4 + x * 2 + c) * eighth, eighth), eighth)
    query_width, key_width = wq.shape[1], wk.shape[1]
    targets = (
        owns[0].at[:, :query_width],
        owns[0].at[:, query_width : query_width + key_width],
        owns[0].at[:, query_width + key_width :],
        owns[1],
        owns[2],
    )
    loads = [
        pltpu.make_async_copy(source.at[span, :], target, load.at[i])
        for i, (source, target) in enumerate(zip((wq, wk, wv, wo, small), targets))
    ]
    for copy in loads:
        copy.start()
    for copy in loads:
        copy.wait()
    stores = [
        pltpu.make_async_copy(owns[i], outs[i].at[me, y, x, c], store.at[i]) for i in range(3)
    ]
    stores.append(pltpu.make_async_copy(extra, extra_out.at[me], store.at[3]))
    for copy in stores:
        copy.start()
    greet(
        [(me > 0, left), (me < n - 1, right), (None, by_c), (None, by_x), (None, by_y)]
    )

    def hop(i, step, side):
        block = me - step if side == 0 else me + step
        source = owns[i] if step == 0 else outs[i].at[block, y, x, c]
        index = (side, step, i)
        return remote(
            source,
            outs[i].at[block, y, x, c],
            zsend.at[index],
            zrecv.at[index],
            right if side == 0 else left,
        )

    def sends(step, side):
        return (me - step >= 0) & (me < n - 1) if side == 0 else (me + step < n) & (me > 0)

    def extra_hop(step, side):
        block = me - step if side == 0 else me + step
        source = extra if step == 0 else extra_out.at[block]
        return remote(
            source,
            extra_out.at[block],
            xsend.at[side, step],
            xrecv.at[side, step],
            right if side == 0 else left,
        )

    def first(slot, block, p):
        i, start, width, along_x = pieces[p]
        spot = outs[i].at[block, y, x, c, :, start : start + width]
        source = owns[i].at[:, start : start + width] if slot == 0 else spot
        index = (0, slot, p)
        return remote(source, spot, psend.at[index], precv.at[index], by_x if along_x else by_y)

    def second(slot, block, p):
        i, start, width, along_x = pieces[p]
        columns = slice(start, start + width)
        if along_x:
            spot = outs[i].at[block, y, :, c, :, columns]
        else:
            spot = outs[i].at[block, :, x, c, :, columns]
        index = (1, slot, p)
        return remote(spot, spot, psend.at[index], precv.at[index], by_y if along_x else by_x)

    def third(slot, block, i):
        spot = outs[i].at[block, :, :, c]
        index = (slot, i)
        return remote(spot, spot, csend.at[index], crecv.at[index], by_c)

    def held(step):
        if step == 0:
            return [(0, me, me >= 0)]
        return [(step, me - step, me - step >= 0), (n - 1 + step, me + step, me + step < n)]

    count = len(pieces)
    for step in range(n + 2):
        if step < n:
            for slot, block, there in held(step):

                @pl.when(there)
                def _():
                    if step > 0:
                        side = 0 if slot < n else 1
                        for i in range(3):
                            hop(i, step - 1, side).wait_recv()
                    for p in range(count):
                        first(slot, block, p).start()

            if step < n - 1:
                for side in (0, 1):

                    @pl.when(sends(step, side))
                    def _():
                        for i in range(3):
                            hop(i, step, side).start()

        if 1 <= step < n + 1:
            if step == 1:
                for copy in stores:
                    copy.wait()
            for slot, block, there in held(step - 1):

                @pl.when(there)
                def _():
                    for p in range(count):
                        first(slot, block, p).wait_recv()
                    for p in range(count):
                        second(slot, block, p).start()

        if step >= 2:
            for slot, block, there in held(step - 2):

                @pl.when(there)
                def _():
                    for p in range(count):
                        second(slot, block, p).wait_recv()
                    for i in range(3):
                        third(slot, block, i).start()

            for side in (0, 1):
                if step > 2:

                    @pl.when(me - step + 2 >= 0 if side == 0 else me + step - 2 < n)
                    def _():
                        extra_hop(step - 3, side).wait_recv()

                if step < n + 1:

                    @pl.when(sends(step - 2, side))
                    def _():
                        extra_hop(step - 2, side).start()

    for step in range(n):
        for slot, block, there in held(step):

            @pl.when(there)
            def _():
                for p in range(count):
                    first(slot, block, p).wait_send()
                    second(slot, block, p).wait_send()
                for i in range(3):
                    third(slot, block, i).wait()

        if step < n - 1:
            for side in (0, 1):

                @pl.when(sends(step, side))
                def _():
                    for i in range(3):
                        hop(i, step, side).wait_send()
                    extra_hop(step, side).wait_send()


def path_pieces(query_width, key_width, out_width, small_width):
    half = (query_width + 2 * key_width + out_width) // 2
    return (
        (0, 0, half, True),
        (0, half, query_width + 2 * key_width - half, False),
        (1, 0, out_width, False),
        (2, 0, small_width, True),
    )


def gather_weights(wq, wk, wv, wo, small, extra, n, collective_id):
    rows = wq.shape[0]
    eighth = rows // 8
    widths = (wq.shape[1] + wk.shape[1] + wv.shape[1], wo.shape[1], small.shape[1])
    pieces = path_pieces(wq.shape[1], wk.shape[1], wo.shape[1], small.shape[1])
    outs = pl.pallas_call(
        functools.partial(weights_kernel, n, pieces, widths),
        out_shape=[jax.ShapeDtypeStruct((n, 2, 2, 2, eighth, w), BF) for w in widths]
        + [jax.ShapeDtypeStruct((n,) + extra.shape, BF)],
        in_specs=[ANY] * 5 + [IN_VMEM],
        out_specs=[ANY] * 4,
        scratch_shapes=[pltpu.VMEM((eighth, w), BF) for w in widths]
        + [
            pltpu.SemaphoreType.DMA((5,)),
            pltpu.SemaphoreType.DMA((4,)),
            pltpu.SemaphoreType.DMA((2, n - 1, 3)),
            pltpu.SemaphoreType.DMA((2, n - 1, 3)),
            pltpu.SemaphoreType.DMA((2, 2 * n - 1, 4)),
            pltpu.SemaphoreType.DMA((2, 2 * n - 1, 4)),
            pltpu.SemaphoreType.DMA((2 * n - 1, 3)),
            pltpu.SemaphoreType.DMA((2 * n - 1, 3)),
            pltpu.SemaphoreType.DMA((2, n - 1)),
            pltpu.SemaphoreType.DMA((2, n - 1)),
        ],
        compiler_params=pltpu.CompilerParams(collective_id=collective_id, has_side_effects=True),
        cost_estimate=pl.CostEstimate(flops=0, bytes_accessed=100000000, transcendentals=0),
        name="gather_weights",
    )(wq, wk, wv, wo, small, extra)
    weights = [o.reshape(n * rows, w) for o, w in zip(outs, widths)]
    return weights + [outs[3].reshape(-1, extra.shape[1])]


def reduce_kernel(n, pieces, *refs):
    ins, y_part, outs, y_out = refs[:3], refs[3], refs[4:6], refs[6]
    refs = refs[7:]
    pair, one, two, landing, staging = refs[:2], refs[2:4], refs[4:6], refs[6:8], refs[8:10]
    csend, crecv, psend, precv, zsend, zrecv, gsend, grecv = refs[10:18]
    line = LineSum(n, y_part, *refs[18:])
    group, me, (y, x, c), (by_y, by_x, by_c) = plane_position()
    left, right = (group, me - 1), (group, me + 1)
    eighth = pair[0].shape[3]
    greet(
        [(me > 0, left), (me < n - 1, right), (None, by_c), (None, by_x), (None, by_y)]
    )

    places, ends = [], [0, 0]
    for array, start, width, along_x in pieces:
        path = 0 if along_x else 1
        places.append((array, start, width, path, ends[path]))
        ends[path] += width

    def swap(p):
        array, start, width, path, at = places[p]
        return remote(
            ins[array].at[:, :, :, 1 - c, :, start : start + width],
            pair[path].at[:, :, :, :, at : at + width],
            csend.at[p],
            crecv.at[p],
            by_c,
        )

    for p in range(len(places)):
        swap(p).start()
    line.start()
    for p in range(len(places)):
        swap(p).wait_recv()
        array, start, width, path, at = places[p]

        def pair_sum(t, carry):
            z, a, b = t // 4, (t // 2) % 2, t % 2
            mine = ins[array][z, a, b, c, :, start : start + width].astype(F32)
            theirs = pair[path][z, a, b, :, at : at + width].astype(F32)
            pair[path][z, a, b, :, at : at + width] = (mine + theirs).astype(BF)
            return carry

        lax.fori_loop(0, 4 * n, pair_sum, 0)

    def first(path):
        source = pair[0].at[:, :, 1 - x] if path == 0 else pair[1].at[:, 1 - y]
        return remote(
            source, one[path], psend.at[0, path], precv.at[0, path], by_x if path == 0 else by_y
        )

    def second(path):
        source = one[path].at[:, 1 - y] if path == 0 else one[path].at[:, 1 - x]
        return remote(
            source, two[path], psend.at[1, path], precv.at[1, path], by_y if path == 0 else by_x
        )

    for path in (0, 1):
        first(path).start()
    line.forward(0)
    for path in (0, 1):
        first(path).wait_recv()

        def first_sum(t, carry):
            z, a = t // 2, t % 2
            mine = pair[0][z, a, x] if path == 0 else pair[1][z, y, a]
            one[path][z, a] = (mine.astype(F32) + one[path][z, a].astype(F32)).astype(BF)
            return carry

        lax.fori_loop(0, 2 * n, first_sum, 0)
        second(path).start()
    for step in range(1, n - 1):
        line.forward(step)
    for path in (0, 1):
        second(path).wait_recv()

        def second_sum(z, carry):
            mine = one[0][z, y] if path == 0 else one[1][z, x]
            two[path][z] = (mine.astype(F32) + two[path][z].astype(F32)).astype(BF)
            return carry

        lax.fori_loop(0, n, second_sum, 0)

    def hop(source, path, step, side):
        index = (path, side, step)
        return remote(
            source,
            landing[path].at[side, step],
            zsend.at[index],
            zrecv.at[index],
            right if side == 0 else left,
        )

    for step in range(n - 1):
        for side in (0, 1):
            owner = n - 1 - step if side == 0 else step
            beyond = me < owner if side == 0 else me > owner
            edge = me == 0 if side == 0 else me == n - 1

            @pl.when(beyond & edge)
            def _():
                for path in (0, 1):
                    hop(two[path].at[owner], path, step, side).start()

            @pl.when(beyond & jnp.logical_not(edge))
            def _():
                for path in (0, 1):
                    hop(two[path].at[owner], path, step, side).wait_recv()
                    staging[path][side, step] = (
                        two[path][owner].astype(F32) + landing[path][side, step].astype(F32)
                    ).astype(BF)
                    hop(staging[path].at[side, step], path, step, side).start()

    @pl.when(me > 0)
    def _():
        for path in (0, 1):
            hop(two[path].at[me], path, n - 1 - me, 0).wait_recv()

    @pl.when(me < n - 1)
    def _():
        for path in (0, 1):
            hop(two[path].at[me], path, me, 1).wait_recv()

    for path in (0, 1):
        total = two[path][me].astype(F32)
        from_left = landing[path][0, jnp.minimum(n - 1 - me, n - 2)].astype(F32)
        from_right = landing[path][1, jnp.minimum(me, n - 2)].astype(F32)
        total = total + jnp.where(me > 0, from_left, 0.0)
        total = total + jnp.where(me < n - 1, from_right, 0.0)
        outs[path][y, x, c] = total.astype(BF)

    def spread(path, stage):
        out = outs[path]
        if stage == 2:
            spot, device = out.at[:, :, c], by_c
        elif stage == 0:
            spot, device = out.at[y, x, c], by_x if path == 0 else by_y
        elif path == 0:
            spot, device = out.at[y, :, c], by_y
        else:
            spot, device = out.at[:, x, c], by_x
        return remote(spot, spot, gsend.at[path, stage], grecv.at[path, stage], device)

    for stage in range(3):
        for path in (0, 1):
            spread(path, stage).start()
        if stage == 0:
            line.finish(y_out)
        for path in (0, 1):
            spread(path, stage).wait_recv()

    for path in (0, 1):
        for stage in range(3):
            spread(path, stage).wait_send()
        first(path).wait_send()
        second(path).wait_send()
    for p in range(len(places)):
        swap(p).wait_send()
    for step in range(n - 1):
        for side in (0, 1):
            owner = n - 1 - step if side == 0 else step
            beyond = me < owner if side == 0 else me > owner

            @pl.when(beyond)
            def _():
                for path in (0, 1):
                    hop(two[path].at[owner], path, step, side).wait_send()


def reduce_weights(grad_qkv, grad_out, grad_small, y_part, query_width, n, collective_id):
    values = (grad_qkv, grad_out, grad_small)
    rows = grad_qkv.shape[0] // n
    eighth = rows // 8
    key_width = (grad_qkv.shape[1] - query_width) // 2
    pieces = path_pieces(query_width, key_width, grad_out.shape[1], grad_small.shape[1])
    widths = [sum(p[2] for p in pieces if p[3]), sum(p[2] for p in pieces if not p[3])]
    scratch = [pltpu.VMEM((n, 2, 2, eighth, w), BF) for w in widths]
    scratch += [pltpu.VMEM((n, 2, eighth, w), BF) for w in widths]
    scratch += [pltpu.VMEM((n, eighth, w), BF) for w in widths]
    scratch += [pltpu.VMEM((2, n - 1, eighth, w), BF) for w in widths] * 2
    sems = [(4,), (4,), (2, 2), (2, 2), (2, 2, n - 1), (2, 2, n - 1), (2, 3), (2, 3)]
    y_rows = y_part.shape[0] // n
    outs = pl.pallas_call(
        functools.partial(reduce_kernel, n, pieces),
        out_shape=[jax.ShapeDtypeStruct((2, 2, 2, eighth, w), BF) for w in widths]
        + [jax.ShapeDtypeStruct((y_rows, y_part.shape[1]), F32)],
        in_specs=[IN_VMEM] * 4,
        out_specs=[IN_VMEM] * 3,
        scratch_shapes=scratch
        + [pltpu.SemaphoreType.DMA(s) for s in sems]
        + line_sum_scratch(n, y_rows, y_part.shape[1]),
        compiler_params=pltpu.CompilerParams(
            collective_id=collective_id, has_side_effects=True, vmem_limit_bytes=48 * 1024 * 1024
        ),
        cost_estimate=pl.CostEstimate(flops=0, bytes_accessed=100000000, transcendentals=0),
        name="reduce_weights",
    )(
        *[v.reshape(n, 2, 2, 2, eighth, v.shape[1]) for v in values],
        y_part.reshape(n, y_rows, y_part.shape[1]),
    )
    first, second = [o.reshape(rows, w) for o, w in zip(outs, widths)]
    cut = pieces[0][2]
    rest = pieces[1][2]
    qkv = jnp.concatenate([first[:, :cut], second[:, :rest]], axis=1)
    return qkv, second[:, rest:], first[:, cut:], outs[2]


def expert_kernel(sizes, plane, *refs):
    blocks, rows, local, capacity = sizes
    x_ref, ct_low_ref, ct_high_ref, router_t_ref, rank_row_ref, rank_col_ref = refs[:6]
    w_gate_ref, w_up_ref, w_down_ref = refs[6:9]
    y_ref, gs_ref, out_gate_ref, out_up_ref, out_down_ref = refs[9:14]
    xs_ref, g_ref, gate_slot_ref, dots_ref = refs[14:18]
    refs = refs[18:]
    slots = local * capacity
    step = pl.program_id(0)
    base = lax.axis_index("expert") * local
    if plane:
        stage_refs, pair_refs, one_refs, two_refs = refs[:3], refs[3:6], refs[6:10], refs[10:14]
        csend, crecv, psend, precv, qsend, qrecv = refs[14:20]
        gs_part = refs[20]
        line = LineSum(blocks, gs_part, *refs[21:])
        _, _, (y, x, c), (by_y, by_x, by_c) = plane_position()
        half = stage_refs[2].shape[4] // 2

        @pl.when(step == 0)
        def _():
            greet([(None, by_c), (None, by_x), (None, by_y)] + line.neighbours())

    @pl.when(step == 0)
    def _():
        logits = dot_nt(router_t_ref[...], x_ref[...])
        hot = rank_row_ref[...] < 200.0
        top = jnp.max(jnp.where(hot, logits, NEGATIVE_LARGE), axis=0, keepdims=True)
        weight = jnp.where(hot, jnp.exp(jnp.minimum(logits - top, 0.0)), 0.0)
        gates = weight / jnp.sum(weight, axis=0, keepdims=True)
        expert_id = lax.broadcasted_iota(jnp.int32, gates.shape, 0)
        slot_id = lax.broadcasted_iota(jnp.int32, (capacity, rows), 0).astype(F32)
        rank_rows, gate_rows = [], []
        for e in range(local):
            mine = expert_id == base + e
            rank_rows.append(jnp.sum(jnp.where(mine, rank_row_ref[...], 0.0), 0, keepdims=True))
            gate_rows.append(jnp.sum(jnp.where(mine, gates, 0.0), 0, keepdims=True))
        for b in range(blocks):
            here = slice(b * rows, (b + 1) * rows)
            pieces = []
            for e in range(local):
                taken = jnp.broadcast_to(rank_rows[e][:, here], (capacity, rows)) == slot_id
                gate = jnp.sum(jnp.where(taken, gate_rows[e][:, here], 0.0), 1, keepdims=True)
                gate_slot_ref[b, e * capacity : (e + 1) * capacity, :] = gate
                pieces.append(jnp.where(taken, 1.0, 0.0).astype(BF))
            pick = jnp.concatenate(pieces, axis=0)
            xs_ref[b] = dot(pick, x_ref[here, :]).astype(BF)
            middle = ct_low_ref.shape[1]
            g_ref[b, :, :middle] = dot(pick, ct_low_ref[here, :]).astype(BF)
            g_ref[b, :, middle:] = dot(pick, ct_high_ref[here, :]).astype(BF)

    @pl.when(step < local)
    def _():
        here = pl.ds(pl.multiple_of(step * capacity, capacity), capacity)
        xs = jnp.concatenate([xs_ref[b, here, :] for b in range(blocks)], axis=0)
        g = jnp.concatenate([g_ref[b, here, :] for b in range(blocks)], axis=0).astype(F32)
        gate_slot = jnp.concatenate([gate_slot_ref[b, here, :] for b in range(blocks)], axis=0)
        w_gate, w_up, w_down = w_gate_ref[0], w_up_ref[0], w_down_ref[0]
        gate_pre = dot(xs, w_gate)
        up_pre = dot(xs, w_up)
        sigmoid = jax.nn.sigmoid(gate_pre)
        silu = gate_pre * sigmoid
        activation = (silu * up_pre).astype(BF)
        expert_out = dot(activation, w_down).astype(BF).astype(F32)
        slot_dot = jnp.sum(g * expert_out, axis=1, keepdims=True)
        grad_out = (gate_slot * g).astype(BF)
        scaled_out = (gate_slot * expert_out).astype(BF)
        grad_down = dot_tn(activation, grad_out).astype(BF)
        grad_activation = dot_nt(grad_out, w_down)
        grad_gate_pre = (
            grad_activation * up_pre * sigmoid * (1.0 + gate_pre * (1.0 - sigmoid))
        ).astype(BF)
        grad_up_pre = (grad_activation * silu).astype(BF)
        grad_gate = dot_tn(xs, grad_gate_pre).astype(BF)
        grad_up = dot_tn(xs, grad_up_pre).astype(BF)
        if plane:
            for ref, value in zip(stage_refs, (grad_gate, grad_up, grad_down)):
                ref[step % 2] = value.reshape(ref.shape[1:])
        else:
            out_gate_ref[0], out_up_ref[0], out_down_ref[0] = grad_gate, grad_up, grad_down
        grad_in = (dot_nt(grad_gate_pre, w_gate) + dot_nt(grad_up_pre, w_up)).astype(BF)
        lane = lax.broadcasted_iota(jnp.int32, (blocks * capacity, LANES), 1)
        high = slot_dot.astype(BF).astype(F32)
        middle = (slot_dot - high).astype(BF).astype(F32)
        low = slot_dot - high - middle
        mine = base + step
        dots = jnp.where(lane == mine, high, 0.0)
        dots = jnp.where(lane == mine + EXPERTS, middle, dots)
        dots = jnp.where(lane == mine + 2 * EXPERTS, low, dots).astype(BF)
        for b in range(blocks):
            part = slice(b * capacity, (b + 1) * capacity)
            xs_ref[b, here, :] = grad_in[part]
            g_ref[b, here, :] = scaled_out[part]
            dots_ref[b, here, :] = dots[part]

    @pl.when(step == (local if plane else local - 1))
    def _():
        slot_expert = lax.broadcasted_iota(jnp.int32, (EXPERTS, slots), 1) // capacity
        spread_row = lax.broadcasted_iota(jnp.int32, (EXPERTS, slots), 0)
        spread = jnp.where(spread_row == slot_expert + base, 1.0, 0.0).astype(BF)
        slot_rank = (lax.broadcasted_iota(jnp.int32, (rows, slots), 1) % capacity).astype(F32)
        for b in range(blocks):
            there = slice(b * rows, (b + 1) * rows)
            ranks = dot(rank_col_ref[there, :], spread)
            put = jnp.where(ranks == slot_rank, 1.0, 0.0).astype(BF)
            y_ref[there, :] = dot(put, g_ref[b]).astype(BF)
            back = dot(put, xs_ref[b]).astype(BF), dot(put, dots_ref[b]).astype(BF)
            if plane:
                gs_part[b, :, :D], gs_part[b, :, D:] = back
            else:
                gs_ref[there, :D], gs_ref[there, D:] = back
        if plane:
            line.start()

    if not plane:
        return

    gate, up, low_down, high_down = range(4)
    low_rows, high_rows = slice(0, half), slice(half, 2 * half)

    def swap(e, i):
        slot = e % 2
        return remote(
            stage_refs[i].at[slot, :, :, 1 - c],
            pair_refs[i].at[e % 3],
            csend.at[slot, i],
            crecv.at[e % 3, i],
            by_c,
        )

    def first(e, k):
        slot = e % 3
        source = {
            gate: lambda: pair_refs[0].at[slot, :, 1 - x],
            up: lambda: pair_refs[1].at[slot, 1 - y],
            low_down: lambda: pair_refs[2].at[slot, :, 1 - x, low_rows],
            high_down: lambda: pair_refs[2].at[slot, 1 - y, :, high_rows],
        }[k]()
        device = by_x if k in (gate, low_down) else by_y
        return remote(source, one_refs[k].at[slot], psend.at[slot, k], precv.at[slot, k], device)

    def second(e, k):
        along_x = k in (gate, low_down)
        source = one_refs[k].at[e % 3, 1 - y] if along_x else one_refs[k].at[e % 3, 1 - x]
        slot = e % 2
        return remote(
            source,
            two_refs[k].at[slot],
            qsend.at[slot, k],
            qrecv.at[slot, k],
            by_y if along_x else by_x,
        )

    def add(first_value, second_value):
        return (first_value.astype(F32) + second_value.astype(F32)).astype(BF)

    @pl.when(step >= 3)
    def _():
        e = step - 3
        for k in range(4):
            second(e, k).wait()
        own = [one_refs[k][e % 3, y if k in (gate, low_down) else x] for k in range(4)]
        out_gate_ref[0] = add(own[gate], two_refs[gate][e % 2])
        out_up_ref[0] = add(own[up], two_refs[up][e % 2])
        out_down_ref[0, low_rows] = add(own[low_down], two_refs[low_down][e % 2])
        out_down_ref[0, high_rows] = add(own[high_down], two_refs[high_down][e % 2])

    @pl.when((step >= 2) & (step < local + 2))
    def _():
        e = step - 2
        slot = e % 3
        for k in range(4):
            first(e, k).wait()
            for t in (0, 1):
                mine = {
                    gate: lambda: pair_refs[0][slot, t, x],
                    up: lambda: pair_refs[1][slot, y, t],
                    low_down: lambda: pair_refs[2][slot, t, x, low_rows],
                    high_down: lambda: pair_refs[2][slot, y, t, high_rows],
                }[k]()
                one_refs[k][slot, t] = add(mine, one_refs[k][slot, t])
            second(e, k).start()

    @pl.when((step >= 1) & (step < local + 1))
    def _():
        e = step - 1
        slot = e % 3
        for i in range(3):
            swap(e, i).wait()

            def pair_sum(t, carry):
                a, b = t // 2, t % 2
                pair_refs[i][slot, a, b] = add(
                    stage_refs[i][e % 2, a, b, c], pair_refs[i][slot, a, b]
                )
                return carry

            lax.fori_loop(0, 4, pair_sum, 0)
        for k in range(4):
            first(e, k).start()

    @pl.when(step < local)
    def _():
        for i in range(3):
            swap(step, i).start()

    @pl.when(step == local + 1)
    def _():
        line.forward(0)

    @pl.when(step == local + 2)
    def _():
        for k in range(1, blocks - 1):
            line.forward(k)
        line.finish(gs_ref)


def run_experts(
    x_all,
    ct_low,
    ct_high,
    router_t,
    rank_row,
    rank_col,
    w_gate,
    w_up,
    w_down,
    rows,
    capacity,
    plane,
    collective_id,
):
    total = x_all.shape[0]
    blocks, local = total // rows, w_gate.shape[0]
    slots = local * capacity
    sizes = (blocks, rows, local, capacity)
    whole = lambda shape: pl.BlockSpec(
        shape, lambda e: (0,) * len(shape), pipeline_mode=pl.Buffered(1)
    )
    per = lambda shape: pl.BlockSpec((1,) + shape, lambda e: (jnp.minimum(e, local - 1), 0, 0))
    shapes = ((D, FF), (D, FF), (FF, D))
    scratch = [
        pltpu.VMEM((blocks, slots, D), BF),
        pltpu.VMEM((blocks, slots, D), BF),
        pltpu.VMEM((blocks, slots, 1), F32),
        pltpu.VMEM((blocks, slots, LANES), BF),
    ]
    params = dict(dimension_semantics=("arbitrary",), vmem_limit_bytes=62 * 1024 * 1024)
    if plane:
        eighths = [(a // 8, b) for a, b in shapes]
        out = lambda shape: pl.BlockSpec((1,) + shape, lambda e: (jnp.maximum(e - 3, 0), 0, 0))
        grad_shapes, grad_specs = eighths, [out(shape) for shape in eighths]
        low = (eighths[2][0] // 2, eighths[2][1])
        passed = (eighths[0], eighths[1], low, low)
        scratch += [pltpu.VMEM((2, 2, 2, 2) + shape, BF) for shape in eighths]
        scratch += [pltpu.VMEM((3, 2, 2) + shape, BF) for shape in eighths]
        scratch += [pltpu.VMEM((3, 2) + shape, BF) for shape in passed]
        scratch += [pltpu.VMEM((2,) + shape, BF) for shape in passed]
        sems = [(2, 3), (3, 3), (3, 4), (3, 4), (2, 4), (2, 4)]
        scratch += [pltpu.SemaphoreType.DMA(shape) for shape in sems]
        scratch += [pltpu.VMEM((blocks, rows, D + LANES), BF)]
        scratch += line_sum_scratch(blocks, rows, D + LANES)
        gs_shape, gs_type = (rows, D + LANES), F32
        params |= dict(collective_id=collective_id, has_side_effects=True)
    else:
        grad_shapes, grad_specs = shapes, [per(shape) for shape in shapes]
        gs_shape, gs_type = (total, D + LANES), BF
    flops = 2 * total * D * slots * 4 // blocks + 18 * blocks * slots * D * FF
    return pl.pallas_call(
        functools.partial(expert_kernel, sizes, plane),
        grid=(local + 3 if plane else local,),
        out_shape=[
            jax.ShapeDtypeStruct((total, D), BF),
            jax.ShapeDtypeStruct(gs_shape, gs_type),
        ]
        + [jax.ShapeDtypeStruct((local,) + shape, BF) for shape in grad_shapes],
        in_specs=[
            whole((total, D)),
            whole(ct_low.shape),
            whole(ct_high.shape),
            whole((EXPERTS, D)),
            whole((EXPERTS, total)),
            whole((total, EXPERTS)),
        ]
        + [per(shape) for shape in shapes],
        out_specs=[whole((total, D)), whole(gs_shape)] + grad_specs,
        scratch_shapes=scratch,
        compiler_params=pltpu.CompilerParams(**params),
        cost_estimate=pl.CostEstimate(
            flops=flops, bytes_accessed=2 * (6 * local * D * FF + 4 * total * D), transcendentals=0
        ),
        name="experts",
    )(x_all, ct_low, ct_high, router_t, rank_row, rank_col, w_gate, w_up, w_down)


def mask_bias(bias_ref, length_ref, rows):
    base = lax.axis_index("expert") * rows
    key = lax.broadcasted_iota(jnp.int32, bias_ref.shape, 0)
    query = lax.broadcasted_iota(jnp.int32, bias_ref.shape, 1) + base
    allowed = (key <= query) & (key < length_ref[0])
    bias_ref[...] = jnp.where(allowed, 0.0, NEGATIVE_LARGE)


def head_columns(ref, head):
    start = 2 * HEAD_DIMENSION * head
    middle = start + HEAD_DIMENSION
    return jnp.concatenate([ref[:, start:middle], ref[:, middle : middle + HEAD_DIMENSION]], 0)


def put_heads(ref, head, transposed):
    rows = ref.shape[0]
    value = transposed.T
    start = 2 * HEAD_DIMENSION * head
    middle = start + HEAD_DIMENSION
    ref[:, start:middle] = value[:rows].astype(ref.dtype)
    ref[:, middle : middle + HEAD_DIMENSION] = value[rows:].astype(ref.dtype)


def attention_kernel(
    n, length_ref, q_ref, kv_ref, rank_ref, mixed_ref, log_total_ref, kv_all_ref, rank_all_ref, *scratch
):
    bias_ref, chunk_ref, rank_buffer, send, recv, rank_send, rank_recv = scratch
    pair, pairs = pl.program_id(0), pl.num_programs(0)
    group, me = lax.axis_index("group"), lax.axis_index("expert")
    left, right = (group, me - 1), (group, me + 1)
    rows, width = kv_ref.shape[1:]

    def hop(j, step, side):
        block = me - step if side == 0 else me + step
        source = kv_ref.at[j] if step == 0 else chunk_ref.at[j, block]
        index = (j, side, step)
        return remote(
            source,
            chunk_ref.at[j, block],
            send.at[index],
            recv.at[index],
            right if side == 0 else left,
        )

    def rank_hop(step, side):
        block = me - step if side == 0 else me + step
        source = rank_ref if step == 0 else rank_buffer.at[block]
        index = (side, step)
        return remote(
            source,
            rank_buffer.at[block],
            rank_send.at[index],
            rank_recv.at[index],
            right if side == 0 else left,
        )

    def sends(step, side):
        return (me - step >= 0) & (me < n - 1) if side == 0 else (me + step < n) & (me > 0)

    def arrives(step, side):
        return me - 1 - step >= 0 if side == 0 else me + 1 + step < n

    def launch(make, step):
        for side in (0, 1):

            @pl.when(sends(step, side))
            def _():
                make(step, side).start()

    def await_hop(make, step):
        for side in (0, 1):

            @pl.when(arrives(step, side))
            def _():
                make(step, side).wait_recv()

    def drain(make):
        for step in range(n - 1):
            for side in (0, 1):

                @pl.when(sends(step, side))
                def _():
                    make(step, side).wait_send()

    def chunk(j):
        return lambda step, side: hop(j, step, side)

    @pl.when(pair == 0)
    def _():
        greet([(me > 0, left), (me < n - 1, right)])
        launch(chunk(0), 0)
        rank_buffer[me] = rank_ref[...]
        launch(chunk(1), 0)
        mask_bias(bias_ref, length_ref, rows)
        await_hop(chunk(0), 0)
        launch(chunk(0), 1)

    for step in range(1, n - 1):
        await_hop(chunk(pair), step)
        if step < n - 2:
            launch(chunk(pair), step + 1)

    @pl.when(pair + 1 < pairs)
    def _():
        await_hop(chunk(pair + 1), 0)
        launch(chunk(pair + 1), 1)

    @pl.when(pair + 2 < pairs)
    def _():
        launch(chunk(pair + 2), 0)

    @pl.when(pair == 1)
    def _():
        launch(rank_hop, 0)

    for step in range(n - 1):

        @pl.when(pair == jnp.minimum(2 + step, pairs - 1))
        def _():
            await_hop(rank_hop, step)
            if step < n - 2:
                launch(rank_hop, step + 1)

    chunk_ref[pair, me] = kv_ref[pair]
    kv = chunk_ref[pair].reshape(n * rows, width)
    kv_all_ref[...] = kv
    bias = jnp.concatenate([bias_ref[...]] * 2, axis=1)
    for head in (0, 1):
        start = head * HEAD_DIMENSION
        key = kv[:, start : start + HEAD_DIMENSION]
        value = kv[:, LANES + start : LANES + start + HEAD_DIMENSION]
        query = head_columns(q_ref, head) * jnp.asarray(HEAD_DIMENSION**-0.5, BF)
        scores = dot_nt(key, query) + bias
        top = jnp.max(scores, axis=0, keepdims=True)
        weights = jnp.exp(scores - top)
        total = jnp.sum(weights, axis=0, keepdims=True)
        put_heads(mixed_ref, head, dot_tn(value, weights.astype(BF)) / total)
        log_total_ref[0, head : head + 1, :] = top + jnp.log(total)

    @pl.when(pair == pairs - 1)
    def _():
        drain(rank_hop)
        rank_all_ref[...] = rank_buffer[...]
        for j in range(KEY_VALUE_HEADS // 2):
            drain(chunk(j))


def attention(length, query, kv, rank, n, collective_id):
    rows = query.shape[0]
    keys, width = n * rows, 2 * LANES
    pairs = KEY_VALUE_HEADS // 2
    return pl.pallas_call(
        functools.partial(attention_kernel, n),
        grid=(pairs,),
        out_shape=(
            jax.ShapeDtypeStruct(query.shape, BF),
            jax.ShapeDtypeStruct((pairs, 2, 2 * rows), F32),
            jax.ShapeDtypeStruct((keys, pairs * width), BF),
            jax.ShapeDtypeStruct((n,) + rank.shape, rank.dtype),
        ),
        in_specs=[
            pl.BlockSpec(memory_space=pltpu.SMEM),
            pl.BlockSpec((rows, width), lambda j: (0, j)),
            IN_VMEM,
            IN_VMEM,
        ],
        out_specs=(
            pl.BlockSpec((rows, width), lambda j: (0, j)),
            pl.BlockSpec((1, 2, 2 * rows), lambda j: (j, 0, 0)),
            pl.BlockSpec((keys, width), lambda j: (0, j)),
            IN_VMEM,
        ),
        scratch_shapes=[
            pltpu.VMEM((keys, rows), F32),
            pltpu.VMEM((pairs, n, rows, width), BF),
            pltpu.VMEM((n,) + rank.shape, rank.dtype),
            pltpu.SemaphoreType.DMA((pairs, 2, n - 1)),
            pltpu.SemaphoreType.DMA((pairs, 2, n - 1)),
            pltpu.SemaphoreType.DMA((2, n - 1)),
            pltpu.SemaphoreType.DMA((2, n - 1)),
        ],
        compiler_params=pltpu.CompilerParams(
            dimension_semantics=("arbitrary",),
            vmem_limit_bytes=56 * 1024 * 1024,
            collective_id=collective_id,
            has_side_effects=True,
        ),
        cost_estimate=pl.CostEstimate(
            flops=16 * rows * keys * D, bytes_accessed=100000000, transcendentals=0
        ),
        name="attention",
    )(length, query, kv, rank)


def attention_back_kernel(
    n,
    length_ref,
    q_ref,
    kv_ref,
    grad_ref,
    log_total_ref,
    grad_q_ref,
    grad_kv_ref,
    bias_ref,
    terms_ref,
    landing,
    staging,
    send,
    recv,
):
    step, pairs = pl.program_id(0), pl.num_programs(0) - 1

    def line(j):
        return LineSum(
            n, terms_ref.at[j], landing.at[j], staging.at[j], send.at[j], recv.at[j]
        )

    @pl.when(step == 0)
    def _():
        greet(line(0).neighbours())
        mask_bias(bias_ref, length_ref, q_ref.shape[0])

    @pl.when(step < pairs)
    def _():
        attention_back_pair(
            q_ref, kv_ref, grad_ref, log_total_ref, grad_q_ref, terms_ref.at[step], bias_ref
        )
        line(step).start()

    @pl.when(step > 0)
    def _():
        for k in range(n - 1):
            line(step - 1).forward(k)
        line(step - 1).finish(grad_kv_ref)


def attention_back_pair(q_ref, kv_ref, grad_ref, log_total_ref, grad_q_ref, grad_kv_ref, bias_ref):
    scale = HEAD_DIMENSION**-0.5
    blocks, rows, _ = grad_kv_ref.shape
    bias = jnp.concatenate([bias_ref[...]] * 2, axis=1)
    for head in (0, 1):
        columns = slice(head * HEAD_DIMENSION, (head + 1) * HEAD_DIMENSION)
        key, value = kv_ref[:, :LANES][:, columns], kv_ref[:, LANES:][:, columns]
        query = head_columns(q_ref, head) * jnp.asarray(scale, BF)
        grad = head_columns(grad_ref, head)
        scores = dot_nt(key, query) + bias
        probs = jnp.exp(scores - log_total_ref[0, head : head + 1, :])
        grad_probs = dot_nt(value, grad)
        delta = jnp.sum(probs * grad_probs, axis=0, keepdims=True)
        grad_scores = (probs * (grad_probs - delta)).astype(BF)
        grad_key = dot(grad_scores, query).astype(BF).reshape(blocks, rows, HEAD_DIMENSION)
        grad_kv_ref[:, :, columns] = grad_key
        grad_value = dot(probs.astype(BF), grad).astype(BF).reshape(blocks, rows, HEAD_DIMENSION)
        start = LANES + head * HEAD_DIMENSION
        grad_kv_ref[:, :, start : start + HEAD_DIMENSION] = grad_value
        put_heads(grad_q_ref, head, dot_tn(key, grad_scores) * scale)


def attention_back(length, query, kv_all, grad_mixed, log_total, n, collective_id):
    rows, keys = query.shape[0], kv_all.shape[0]
    pairs, width = KEY_VALUE_HEADS // 2, 2 * LANES
    now = lambda j: jnp.minimum(j, pairs - 1)
    row_spec = pl.BlockSpec((rows, width), lambda j: (0, now(j)))
    return pl.pallas_call(
        functools.partial(attention_back_kernel, n),
        grid=(pairs + 1,),
        out_shape=(
            jax.ShapeDtypeStruct(query.shape, F32),
            jax.ShapeDtypeStruct((rows, pairs * width), BF),
        ),
        in_specs=[
            pl.BlockSpec(memory_space=pltpu.SMEM),
            row_spec,
            pl.BlockSpec((keys, width), lambda j: (0, now(j))),
            row_spec,
            pl.BlockSpec((1, 2, 2 * rows), lambda j: (now(j), 0, 0)),
        ],
        out_specs=(
            row_spec,
            pl.BlockSpec((rows, width), lambda j: (0, jnp.maximum(j - 1, 0))),
        ),
        scratch_shapes=[
            pltpu.VMEM((keys, rows), F32),
            pltpu.VMEM((pairs, n, rows, width), BF),
            pltpu.VMEM((pairs, 2, n - 1, rows, width), BF),
            pltpu.VMEM((pairs, 2, n - 1, rows, width), BF),
            pltpu.SemaphoreType.DMA((pairs, 2, n - 1)),
            pltpu.SemaphoreType.DMA((pairs, 2, n - 1)),
        ],
        compiler_params=pltpu.CompilerParams(
            dimension_semantics=("arbitrary",),
            vmem_limit_bytes=60 * 1024 * 1024,
            collective_id=collective_id,
            has_side_effects=True,
        ),
        cost_estimate=pl.CostEstimate(
            flops=40 * rows * keys * D, bytes_accessed=100000000, transcendentals=0
        ),
        name="attention_back",
    )(length, query, kv_all, grad_mixed, log_total)


def widen_kernel(value_ref, out_ref):
    out_ref[...] = value_ref[...].astype(F32)


def widen(value):
    block = (1,) + value.shape[1:]
    spec = pl.BlockSpec(block, lambda e: (e, 0, 0))
    return pl.pallas_call(
        widen_kernel,
        grid=(value.shape[0],),
        out_shape=jax.ShapeDtypeStruct(value.shape, F32),
        in_specs=[spec],
        out_specs=spec,
        compiler_params=pltpu.CompilerParams(dimension_semantics=("arbitrary",)),
        cost_estimate=pl.CostEstimate(flops=0, bytes_accessed=6 * value.size, transcendentals=0),
        name="widen",
    )(value)


def unpair_columns(value):
    rows = value.shape[0]
    value = value.reshape(rows, -1, 2, LANES)
    return value[:, :, 0].reshape(rows, -1), value[:, :, 1].reshape(rows, -1)


def gather_rows(value):
    return lax.all_gather(value, "expert", axis=0, tiled=True)


def scatter_rows(value):
    return lax.psum_scatter(value, "expert", scatter_dimension=0, tiled=True)


def per_device(
    tokens,
    lengths,
    routes,
    norm_gain1,
    w_query,
    key_projection,
    value_projection,
    w_out,
    norm_gain2,
    w_router,
    w_gate,
    w_up,
    w_down,
    cotangent,
):
    rows = tokens.shape[0]
    n, groups = lax.axis_size("expert"), lax.axis_size("group")
    my_index = lax.axis_index("expert")
    capacity = 3 * rows * TOP // (2 * EXPERTS)
    query_width, key_width = w_query.shape[1], key_projection.shape[1]
    length = lengths[0]
    positions = my_index * rows + jnp.arange(rows, dtype=jnp.int32)
    valid_rows = (positions < length)[:, None]
    grad_output = jnp.where(valid_rows, cotangent, jnp.zeros_like(cotangent))

    small = jnp.concatenate(
        [w_router, norm_gain1[:, None], norm_gain2[:, None]]
        + [jnp.zeros((w_router.shape[0], LANES - EXPERTS - 2), BF)],
        axis=1,
    )
    middle = D // 2
    qkv_weight, out_weight, small, ct_low = gather_weights(
        w_query, key_projection, value_projection, w_out, small, grad_output[:, :middle], n, 1
    )
    qkv_weight, ct_high = lax.optimization_barrier((qkv_weight, grad_output[:, middle:]))
    ct_high = gather_rows(ct_high)
    router_weight = small[:, :EXPERTS]
    gain_one = small[:, EXPERTS].astype(F32)
    gain_two = small[:, EXPERTS + 1].astype(F32)

    expert_ids = jnp.arange(EXPERTS, dtype=jnp.int32)
    hot = jnp.any(routes[:, :, None] == expert_ids, axis=1)
    row_id = jnp.arange(rows, dtype=jnp.int32)
    earlier = (row_id[:, None] < row_id[None, :]).astype(BF)
    rank = jnp.where(hot.T, dot(hot.T.astype(BF), earlier), 255.0).astype(BF)

    cosine_lookup, sine_lookup = rotary_tables(positions, HEAD_DIMENSION)
    token_f32 = tokens.astype(F32)
    inverse_one = lax.rsqrt(jnp.mean(token_f32 * token_f32, axis=-1, keepdims=True) + EPSILON)
    unit_one = token_f32 * inverse_one
    first_norm = (unit_one * gain_one).astype(BF)
    qkv = dot(first_norm, qkv_weight)
    query_pre = qkv[:, :query_width]
    unrotated_key = qkv[:, query_width : query_width + key_width]
    value_pre = qkv[:, query_width + key_width :]
    query_rows = apply_rotation(
        query_pre.reshape(rows, QUERY_HEADS, HEAD_DIMENSION), cosine_lookup, sine_lookup
    ).astype(BF)
    query_rows = query_rows.reshape(rows, query_width)
    local_keys = apply_rotation(
        unrotated_key.reshape(rows, KEY_VALUE_HEADS, HEAD_DIMENSION), cosine_lookup, sine_lookup
    ).astype(BF)
    local_keys = local_keys.reshape(rows, key_width)
    own_kv = jnp.stack(
        [
            jnp.concatenate([local_keys[:, cut], value_pre[:, cut].astype(BF)], axis=1)
            for cut in [slice(i, i + LANES) for i in range(0, key_width, LANES)]
        ]
    )
    mixed_low, log_total, kv_all, rank_all = attention(lengths, query_rows, own_kv, rank, n, 2)
    rank_row = jnp.transpose(rank_all, (1, 0, 2)).reshape(EXPERTS, n * rows).astype(F32)
    rank_col = jnp.transpose(rank_all, (0, 2, 1)).reshape(n * rows, EXPERTS)
    residual = token_f32 + dot(mixed_low, out_weight)
    inverse_two = lax.rsqrt(jnp.mean(residual * residual, axis=-1, keepdims=True) + EPSILON)
    unit_two = residual * inverse_two
    second_norm = (unit_two * gain_two).astype(BF)
    (x_all,) = line_gather([second_norm], n, 3, "gather_rows")

    y_part, gs, grad_gate, grad_up, grad_down = run_experts(
        x_all,
        ct_low,
        ct_high,
        router_weight.T,
        rank_row,
        rank_col,
        w_gate,
        w_up,
        w_down,
        rows,
        capacity,
        groups == 8,
        7,
    )
    if groups != 8:
        gs = line_scatter(gs, n, F32, 4, "scatter_grads")

    logits = dot(second_norm, router_weight)
    chosen = jnp.where(hot, logits, NEGATIVE_LARGE)
    gate_weights = jnp.where(hot, jnp.exp(chosen - jnp.max(chosen, axis=-1, keepdims=True)), 0.0)
    gate_weights = gate_weights / jnp.sum(gate_weights, axis=-1, keepdims=True)
    grad_gates = gs[:, D : D + EXPERTS] + gs[:, D + EXPERTS : D + 2 * EXPERTS]
    grad_gates = grad_gates + gs[:, D + 2 * EXPERTS : D + 3 * EXPERTS]
    grad_logits = (
        gate_weights * (grad_gates - jnp.sum(gate_weights * grad_gates, axis=-1, keepdims=True))
    ).astype(BF)
    grad_second = gs[:, :D] + dot_nt(grad_logits, router_weight)
    grad_router = dot_tn(second_norm, grad_logits)
    scaled_two = grad_second * gain_two
    grad_gain2 = jnp.sum(grad_second * unit_two, axis=0)
    grad_residual = grad_output.astype(F32) + inverse_two * (
        scaled_two - unit_two * jnp.mean(scaled_two * unit_two, axis=-1, keepdims=True)
    )
    grad_attn = grad_residual.astype(BF)
    grad_out = dot_tn(mixed_low, grad_attn)
    mixed_gradient = dot_nt(grad_attn, out_weight).astype(BF)
    grad_query_acc, kv_gradient = attention_back(
        lengths, query_rows, kv_all, mixed_gradient, log_total, n, 5
    )
    own_key_gradient, own_value_gradient = unpair_columns(kv_gradient)
    grad_query_pre = (
        apply_rotation(
            grad_query_acc.reshape(rows, QUERY_HEADS, HEAD_DIMENSION), cosine_lookup, -sine_lookup
        )
        .reshape(rows, query_width)
        .astype(BF)
    )
    grad_key_pre = apply_rotation(
        own_key_gradient.astype(F32).reshape(rows, KEY_VALUE_HEADS, HEAD_DIMENSION),
        cosine_lookup,
        -sine_lookup,
    )
    grad_key_pre = grad_key_pre.reshape(rows, key_width).astype(BF)
    grad_qkv_pre = jnp.concatenate(
        [grad_query_pre, grad_key_pre, own_value_gradient], axis=1
    )
    grad_qkv = dot_tn(first_norm, grad_qkv_pre)
    grad_first = dot_nt(grad_qkv_pre, qkv_weight)
    scaled_one = grad_first * gain_one
    grad_gain1 = jnp.sum(grad_first * unit_one, axis=0)
    grad_tokens = grad_residual + inverse_one * (
        scaled_one - unit_one * jnp.mean(scaled_one * unit_one, axis=-1, keepdims=True)
    )
    grad_small = jnp.concatenate(
        [grad_router, grad_gain1[:, None], grad_gain2[:, None]]
        + [jnp.zeros((D, LANES - EXPERTS - 2), F32)],
        axis=1,
    )
    shares = (grad_qkv.astype(BF), grad_out.astype(BF), grad_small.astype(BF))
    if groups == 8:
        *shares, expert_sum = reduce_weights(*shares, y_part, query_width, n, 6)
    else:
        shares = [lax.psum(scatter_rows(share), "group") for share in shares]
        expert_sum = line_scatter(y_part, n, F32, 8, "scatter_outputs")
    mixed = (residual + expert_sum).astype(BF)
    share_qkv, share_out, share_small = [share.astype(F32) for share in shares]

    def sum_over_groups(value):
        if groups != 8:
            value = lax.psum_scatter(value, "group", scatter_dimension=1, tiled=True)
        return widen(lax.all_gather(value, "group", axis=1, tiled=True))

    return (
        mixed,
        grad_tokens,
        share_small[:, EXPERTS],
        share_qkv[:, :query_width],
        share_qkv[:, query_width : query_width + key_width],
        share_qkv[:, query_width + key_width :],
        share_out,
        share_small[:, EXPERTS + 1],
        share_small[:, :EXPERTS],
        sum_over_groups(grad_gate),
        sum_over_groups(grad_up),
        sum_over_groups(grad_down),
    )


def solution(mesh):
    rows = P(("group", "expert"), None)
    vector, matrix, stack = P("expert"), P("expert", None), P("expert", None, None)
    return jax.shard_map(
        per_device,
        mesh=mesh,
        in_specs=(
            rows,
            P("group"),
            rows,
            vector,
            matrix,
            matrix,
            matrix,
            matrix,
            vector,
            matrix,
            stack,
            stack,
            stack,
            rows,
        ),
        out_specs=(
            rows,
            rows,
            vector,
            matrix,
            matrix,
            matrix,
            matrix,
            vector,
            matrix,
            stack,
            stack,
            stack,
        ),
        check_vma=False,
    )
```

```python
import functools

import jax
import jax.numpy as jnp
from jax import lax
from jax.experimental import pallas as pl
from jax.experimental.pallas import tpu as pltpu
from jax.sharding import PartitionSpec as P

D = 1024
QUERY_HEADS = 16
KEY_VALUE_HEADS = 8
HEAD_DIMENSION = 64
EXPERTS = 32
TOP = 8
FF = 512
LANES = 128
STAGES = 4

EPSILON = 1e-05
NEGATIVE_LARGE = -1e30
BF = jnp.bfloat16
F32 = jnp.float32


def rotary_tables(positions, head_size):
    half_width = head_size // 2
    frequency = 10000.0 ** (-2.0 * jnp.arange(half_width).astype(F32) / head_size)
    angles = positions.astype(F32)[:, None] * frequency[None, :]
    return (jnp.cos(angles)[:, None, :], jnp.sin(angles)[:, None, :])


def apply_rotation(tensor_in, cosine_lookup, sine_lookup):
    half_width = tensor_in.shape[-1] // 2
    first_half = tensor_in[..., :half_width]
    second_half = tensor_in[..., half_width:]
    return jnp.concatenate(
        [
            first_half * cosine_lookup - second_half * sine_lookup,
            second_half * cosine_lookup + first_half * sine_lookup,
        ],
        axis=-1,
    )


def dot(a, b):
    return jnp.dot(a, b, preferred_element_type=F32)


def dot_nt(a, b):
    return lax.dot_general(a, b, (((1,), (1,)), ((), ())), preferred_element_type=F32)


def dot_tn(a, b):
    return lax.dot_general(a, b, (((0,), (0,)), ((), ())), preferred_element_type=F32)


MESH = pl.DeviceIdType.MESH
ANY = pl.BlockSpec(memory_space=pl.ANY)
IN_VMEM = pl.BlockSpec(memory_space=pltpu.VMEM)


def remote(source, target, send, receive, device):
    return pltpu.make_async_remote_copy(
        src_ref=source,
        dst_ref=target,
        send_sem=send,
        recv_sem=receive,
        device_id=device,
        device_id_type=MESH,
    )


def greet(devices):
    barrier = pltpu.get_barrier_semaphore()
    count = 0
    for condition, device in devices:
        if condition is None:
            pl.semaphore_signal(barrier, inc=1, device_id=device, device_id_type=MESH)
            count = count + 1
        else:

            @pl.when(condition)
            def _():
                pl.semaphore_signal(barrier, inc=1, device_id=device, device_id_type=MESH)

            count = count + jnp.where(condition, 1, 0)
    pl.semaphore_wait(barrier, count)


def line_gather_kernel(n, count, *refs):
    ins, outs = refs[:count], refs[count : 2 * count]
    local, send, receive = refs[2 * count :]
    group, me = lax.axis_index("group"), lax.axis_index("expert")
    left, right = (group, me - 1), (group, me + 1)
    own = [
        pltpu.make_async_copy(ins[i], outs[i].at[me], local.at[i]) for i in range(count)
    ]
    for copy in own:
        copy.start()
    greet([(me > 0, left), (me < n - 1, right)])

    def hop(i, step, side):
        block = me - step if side == 0 else me + step
        source = ins[i] if step == 0 else outs[i].at[block]
        index = (side, step, i)
        return remote(
            source, outs[i].at[block], send.at[index], receive.at[index], right if side == 0 else left
        )

    def arrival(i, step, side):
        block = me - 1 - step if side == 0 else me + 1 + step
        index = (side, step, i)
        return remote(
            outs[i].at[block], outs[i].at[block], send.at[index], receive.at[index], left if side == 0 else right
        )

    def sends(step, side):
        return (me - step >= 0) & (me < n - 1) if side == 0 else (me + step < n) & (me > 0)

    def arrives(step, side):
        return me - 1 - step >= 0 if side == 0 else me + 1 + step < n

    for step in range(n - 1):
        for side in (0, 1):

            @pl.when(sends(step, side))
            def _():
                for i in range(count):
                    hop(i, step, side).start()

        for side in (0, 1):

            @pl.when(arrives(step, side))
            def _():
                for i in range(count):
                    arrival(i, step, side).wait_recv()

    for step in range(n - 1):
        for side in (0, 1):

            @pl.when(sends(step, side))
            def _():
                for i in range(count):
                    hop(i, step, side).wait_send()

    for copy in own:
        copy.wait()


def line_gather(values, n, collective_id, name):
    count = len(values)
    outs = pl.pallas_call(
        functools.partial(line_gather_kernel, n, count),
        out_shape=[jax.ShapeDtypeStruct((n,) + v.shape, v.dtype) for v in values],
        in_specs=[IN_VMEM] * count,
        out_specs=[ANY] * count,
        scratch_shapes=[
            pltpu.SemaphoreType.DMA((count,)),
            pltpu.SemaphoreType.DMA((2, n - 1, count)),
            pltpu.SemaphoreType.DMA((2, n - 1, count)),
        ],
        compiler_params=pltpu.CompilerParams(collective_id=collective_id, has_side_effects=True),
        cost_estimate=pl.CostEstimate(flops=0, bytes_accessed=100000000, transcendentals=0),
        name=name,
    )(*values)
    return [o.reshape((n * v.shape[0],) + v.shape[1:]) for o, v in zip(outs, values)]


class LineSum:
    def __init__(self, n, part, landing, staging, send, receive):
        self.n, self.part, self.landing, self.staging = n, part, landing, staging
        self.send, self.receive = send, receive
        self.group, self.me = lax.axis_index("group"), lax.axis_index("expert")
        self.rows = part.shape[1]
        self.tile = min(32, self.rows)

    def neighbours(self):
        left, right = (self.group, self.me - 1), (self.group, self.me + 1)
        return [(self.me > 0, left), (self.me < self.n - 1, right)]

    def copy(self, source, step, side):
        index = (side, step)
        device = (self.group, self.me + 1 if side == 0 else self.me - 1)
        return remote(
            source, self.landing.at[index], self.send.at[index], self.receive.at[index], device
        )

    def places(self):
        me, n = self.me, self.n
        for step in range(n - 1):
            for side in (0, 1):
                owner = n - 1 - step if side == 0 else step
                beyond = me < owner if side == 0 else me > owner
                edge = me == 0 if side == 0 else me == n - 1
                yield step, side, owner, beyond, edge

    def start(self):
        for step, side, owner, beyond, edge in self.places():

            @pl.when(beyond & edge)
            def _():
                self.copy(self.part.at[owner], step, side).start()

    def spans(self, body):
        def tile_body(t, carry):
            body(pl.ds(pl.multiple_of(t * self.tile, self.tile), self.tile))
            return carry

        lax.fori_loop(0, self.rows // self.tile, tile_body, 0)

    def forward(self, hop):
        me, n = self.me, self.n
        for side in (0, 1):
            step = hop - me if side == 0 else hop - (n - 1 - me)
            owner = n - 1 - step if side == 0 else step
            inner = me > 0 if side == 0 else me < n - 1
            beyond = me < owner if side == 0 else me > owner

            @pl.when(inner & (step >= 0) & beyond)
            def _():
                self.copy(self.part.at[owner], step, side).wait_recv()

                def add(span):
                    total = self.part[owner, span, :].astype(F32)
                    total = total + self.landing[side, step, span, :].astype(F32)
                    self.staging[side, step, span, :] = total.astype(BF)

                self.spans(add)
                self.copy(self.staging.at[side, step], step, side).start()

    def finish(self, out_ref):
        me, n = self.me, self.n

        @pl.when(me > 0)
        def _():
            self.copy(self.part.at[me], n - 1 - me, 0).wait_recv()

        @pl.when(me < n - 1)
        def _():
            self.copy(self.part.at[me], me, 1).wait_recv()

        def total(span):
            value = self.part[me, span, :].astype(F32)
            from_left = self.landing[0, jnp.minimum(n - 1 - me, n - 2), span, :].astype(F32)
            from_right = self.landing[1, jnp.minimum(me, n - 2), span, :].astype(F32)
            value = value + jnp.where(me > 0, from_left, 0.0)
            value = value + jnp.where(me < n - 1, from_right, 0.0)
            out_ref[span, :] = value.astype(out_ref.dtype)

        self.spans(total)
        for step, side, owner, beyond, edge in self.places():

            @pl.when(beyond)
            def _():
                self.copy(self.part.at[owner], step, side).wait_send()


def line_sum_scratch(n, rows, width):
    return [
        pltpu.VMEM((2, n - 1, rows, width), BF),
        pltpu.VMEM((2, n - 2, rows, width), BF),
        pltpu.SemaphoreType.DMA((2, n - 1)),
        pltpu.SemaphoreType.DMA((2, n - 1)),
    ]


def line_scatter_kernel(n, part_ref, out_ref, *scratch):
    line = LineSum(n, part_ref, *scratch)
    greet(line.neighbours())
    line.start()
    for hop in range(1, n - 1):
        line.forward(hop)
    line.finish(out_ref)


def line_scatter(value, n, dtype, collective_id, name):
    total, width = value.shape
    rows = total // n
    return pl.pallas_call(
        functools.partial(line_scatter_kernel, n),
        out_shape=jax.ShapeDtypeStruct((rows, width), dtype),
        in_specs=[IN_VMEM],
        out_specs=IN_VMEM,
        scratch_shapes=line_sum_scratch(n, rows, width),
        compiler_params=pltpu.CompilerParams(collective_id=collective_id, has_side_effects=True),
        cost_estimate=pl.CostEstimate(flops=0, bytes_accessed=100000000, transcendentals=0),
        name=name,
    )(value.reshape(n, rows, width))


def plane_position():
    group, me = lax.axis_index("group"), lax.axis_index("expert")
    c, x, y = group % 2, (group // 2) % 2, (group // 4) % 2
    by_c, by_x, by_y = (group + 1 - 2 * c, me), (group + 2 - 4 * x, me), (group + 4 - 8 * y, me)
    return group, me, (y, x, c), (by_y, by_x, by_c)


def weights_kernel(n, pieces, widths, *refs):
    wq, wk, wv, wo, small, extra = refs[:6]
    outs, extra_out, owns = refs[6:9], refs[9], refs[10:13]
    load, store, zsend, zrecv, psend, precv, csend, crecv, xsend, xrecv = refs[13:]
    group, me, (y, x, c), (by_y, by_x, by_c) = plane_position()
    left, right = (group, me - 1), (group, me + 1)
    eighth = owns[0].shape[0]
    span = pl.ds(pl.multiple_of((y * 4 + x * 2 + c) * eighth, eighth), eighth)
    query_width, key_width = wq.shape[1], wk.shape[1]
    targets = (
        owns[0].at[:, :query_width],
        owns[0].at[:, query_width : query_width + key_width],
        owns[0].at[:, query_width + key_width :],
        owns[1],
        owns[2],
    )
    loads = [
        pltpu.make_async_copy(source.at[span, :], target, load.at[i])
        for i, (source, target) in enumerate(zip((wq, wk, wv, wo, small), targets))
    ]
    for copy in loads:
        copy.start()
    for copy in loads:
        copy.wait()
    stores = [
        pltpu.make_async_copy(owns[i], outs[i].at[me, y, x, c], store.at[i]) for i in range(3)
    ]
    stores.append(pltpu.make_async_copy(extra, extra_out.at[me], store.at[3]))
    for copy in stores:
        copy.start()
    greet(
        [(me > 0, left), (me < n - 1, right), (None, by_c), (None, by_x), (None, by_y)]
    )

    def hop(i, step, side):
        block = me - step if side == 0 else me + step
        source = owns[i] if step == 0 else outs[i].at[block, y, x, c]
        index = (side, step, i)
        return remote(
            source,
            outs[i].at[block, y, x, c],
            zsend.at[index],
            zrecv.at[index],
            right if side == 0 else left,
        )

    def sends(step, side):
        return (me - step >= 0) & (me < n - 1) if side == 0 else (me + step < n) & (me > 0)

    def extra_hop(step, side):
        block = me - step if side == 0 else me + step
        source = extra if step == 0 else extra_out.at[block]
        return remote(
            source,
            extra_out.at[block],
            xsend.at[side, step],
            xrecv.at[side, step],
            right if side == 0 else left,
        )

    def first(slot, block, p):
        i, start, width, along_x = pieces[p]
        spot = outs[i].at[block, y, x, c, :, start : start + width]
        source = owns[i].at[:, start : start + width] if slot == 0 else spot
        index = (0, slot, p)
        return remote(source, spot, psend.at[index], precv.at[index], by_x if along_x else by_y)

    def second(slot, block, p):
        i, start, width, along_x = pieces[p]
        columns = slice(start, start + width)
        if along_x:
            spot = outs[i].at[block, y, :, c, :, columns]
        else:
            spot = outs[i].at[block, :, x, c, :, columns]
        index = (1, slot, p)
        return remote(spot, spot, psend.at[index], precv.at[index], by_y if along_x else by_x)

    def third(slot, block, i):
        spot = outs[i].at[block, :, :, c]
        index = (slot, i)
        return remote(spot, spot, csend.at[index], crecv.at[index], by_c)

    def held(step):
        if step == 0:
            return [(0, me, me >= 0)]
        return [(step, me - step, me - step >= 0), (n - 1 + step, me + step, me + step < n)]

    count = len(pieces)
    for step in range(n + 2):
        if step < n:
            for slot, block, there in held(step):

                @pl.when(there)
                def _():
                    if step > 0:
                        side = 0 if slot < n else 1
                        for i in range(3):
                            hop(i, step - 1, side).wait_recv()
                    for p in range(count):
                        first(slot, block, p).start()

            if step < n - 1:
                for side in (0, 1):

                    @pl.when(sends(step, side))
                    def _():
                        for i in range(3):
                            hop(i, step, side).start()

        if 1 <= step < n + 1:
            if step == 1:
                for copy in stores:
                    copy.wait()
            for slot, block, there in held(step - 1):

                @pl.when(there)
                def _():
                    for p in range(count):
                        first(slot, block, p).wait_recv()
                    for p in range(count):
                        second(slot, block, p).start()

        if step >= 2:
            for slot, block, there in held(step - 2):

                @pl.when(there)
                def _():
                    for p in range(count):
                        second(slot, block, p).wait_recv()
                    for i in range(3):
                        third(slot, block, i).start()

            for side in (0, 1):
                if step > 2:

                    @pl.when(me - step + 2 >= 0 if side == 0 else me + step - 2 < n)
                    def _():
                        extra_hop(step - 3, side).wait_recv()

                if step < n + 1:

                    @pl.when(sends(step - 2, side))
                    def _():
                        extra_hop(step - 2, side).start()

    for step in range(n):
        for slot, block, there in held(step):

            @pl.when(there)
            def _():
                for p in range(count):
                    first(slot, block, p).wait_send()
                    second(slot, block, p).wait_send()
                for i in range(3):
                    third(slot, block, i).wait()

        if step < n - 1:
            for side in (0, 1):

                @pl.when(sends(step, side))
                def _():
                    for i in range(3):
                        hop(i, step, side).wait_send()
                    extra_hop(step, side).wait_send()


def path_pieces(query_width, key_width, out_width, small_width):
    half = (query_width + 2 * key_width + out_width) // 2
    return (
        (0, 0, half, True),
        (0, half, query_width + 2 * key_width - half, False),
        (1, 0, out_width, False),
        (2, 0, small_width, True),
    )


def gather_weights(wq, wk, wv, wo, small, extra, n, collective_id):
    rows = wq.shape[0]
    eighth = rows // 8
    widths = (wq.shape[1] + wk.shape[1] + wv.shape[1], wo.shape[1], small.shape[1])
    pieces = path_pieces(wq.shape[1], wk.shape[1], wo.shape[1], small.shape[1])
    outs = pl.pallas_call(
        functools.partial(weights_kernel, n, pieces, widths),
        out_shape=[jax.ShapeDtypeStruct((n, 2, 2, 2, eighth, w), BF) for w in widths]
        + [jax.ShapeDtypeStruct((n,) + extra.shape, BF)],
        in_specs=[ANY] * 5 + [IN_VMEM],
        out_specs=[ANY] * 4,
        scratch_shapes=[pltpu.VMEM((eighth, w), BF) for w in widths]
        + [
            pltpu.SemaphoreType.DMA((5,)),
            pltpu.SemaphoreType.DMA((4,)),
            pltpu.SemaphoreType.DMA((2, n - 1, 3)),
            pltpu.SemaphoreType.DMA((2, n - 1, 3)),
            pltpu.SemaphoreType.DMA((2, 2 * n - 1, 4)),
            pltpu.SemaphoreType.DMA((2, 2 * n - 1, 4)),
            pltpu.SemaphoreType.DMA((2 * n - 1, 3)),
            pltpu.SemaphoreType.DMA((2 * n - 1, 3)),
            pltpu.SemaphoreType.DMA((2, n - 1)),
            pltpu.SemaphoreType.DMA((2, n - 1)),
        ],
        compiler_params=pltpu.CompilerParams(collective_id=collective_id, has_side_effects=True),
        cost_estimate=pl.CostEstimate(flops=0, bytes_accessed=100000000, transcendentals=0),
        name="gather_weights",
    )(wq, wk, wv, wo, small, extra)
    weights = [o.reshape(n * rows, w) for o, w in zip(outs, widths)]
    return weights + [outs[3].reshape(-1, extra.shape[1])]


def reduce_kernel(n, pieces, *refs):
    ins, y_part, outs, y_out = refs[:3], refs[3], refs[4:6], refs[6]
    refs = refs[7:]
    pair, one, two, landing, staging = refs[:2], refs[2:4], refs[4:6], refs[6:8], refs[8:10]
    csend, crecv, psend, precv, zsend, zrecv, gsend, grecv = refs[10:18]
    line = LineSum(n, y_part, *refs[18:])
    group, me, (y, x, c), (by_y, by_x, by_c) = plane_position()
    left, right = (group, me - 1), (group, me + 1)
    eighth = pair[0].shape[3]
    greet(
        [(me > 0, left), (me < n - 1, right), (None, by_c), (None, by_x), (None, by_y)]
    )

    places, ends = [], [0, 0]
    for array, start, width, along_x in pieces:
        path = 0 if along_x else 1
        places.append((array, start, width, path, ends[path]))
        ends[path] += width

    def swap(p):
        array, start, width, path, at = places[p]
        return remote(
            ins[array].at[:, :, :, 1 - c, :, start : start + width],
            pair[path].at[:, :, :, :, at : at + width],
            csend.at[p],
            crecv.at[p],
            by_c,
        )

    for p in range(len(places)):
        swap(p).start()
    line.start()
    for p in range(len(places)):
        swap(p).wait_recv()
        array, start, width, path, at = places[p]

        def pair_sum(t, carry):
            z, a, b = t // 4, (t // 2) % 2, t % 2
            mine = ins[array][z, a, b, c, :, start : start + width].astype(F32)
            theirs = pair[path][z, a, b, :, at : at + width].astype(F32)
            pair[path][z, a, b, :, at : at + width] = (mine + theirs).astype(BF)
            return carry

        lax.fori_loop(0, 4 * n, pair_sum, 0)

    def first(path):
        source = pair[0].at[:, :, 1 - x] if path == 0 else pair[1].at[:, 1 - y]
        return remote(
            source, one[path], psend.at[0, path], precv.at[0, path], by_x if path == 0 else by_y
        )

    def second(path):
        source = one[path].at[:, 1 - y] if path == 0 else one[path].at[:, 1 - x]
        return remote(
            source, two[path], psend.at[1, path], precv.at[1, path], by_y if path == 0 else by_x
        )

    for path in (0, 1):
        first(path).start()
    line.forward(1)
    for path in (0, 1):
        first(path).wait_recv()

        def first_sum(t, carry):
            z, a = t // 2, t % 2
            mine = pair[0][z, a, x] if path == 0 else pair[1][z, y, a]
            one[path][z, a] = (mine.astype(F32) + one[path][z, a].astype(F32)).astype(BF)
            return carry

        lax.fori_loop(0, 2 * n, first_sum, 0)
        second(path).start()
    for far in range(2, n - 1):
        line.forward(far)
    for path in (0, 1):
        second(path).wait_recv()

        def second_sum(z, carry):
            mine = one[0][z, y] if path == 0 else one[1][z, x]
            two[path][z] = (mine.astype(F32) + two[path][z].astype(F32)).astype(BF)
            return carry

        lax.fori_loop(0, n, second_sum, 0)

    def hop(source, path, step, side):
        index = (path, side, step)
        return remote(
            source,
            landing[path].at[side, step],
            zsend.at[index],
            zrecv.at[index],
            right if side == 0 else left,
        )

    for step in range(n - 1):
        for side in (0, 1):
            owner = n - 1 - step if side == 0 else step
            beyond = me < owner if side == 0 else me > owner
            edge = me == 0 if side == 0 else me == n - 1

            @pl.when(beyond & edge)
            def _():
                for path in (0, 1):
                    hop(two[path].at[owner], path, step, side).start()

    for far in range(1, n - 1):
        for side in (0, 1):
            step = far - me if side == 0 else far - (n - 1 - me)
            owner = n - 1 - step if side == 0 else step
            inner = me > 0 if side == 0 else me < n - 1
            beyond = me < owner if side == 0 else me > owner

            @pl.when(inner & (step >= 0) & beyond)
            def _():
                for path in (0, 1):
                    hop(two[path].at[owner], path, step, side).wait_recv()
                    staging[path][side, step] = (
                        two[path][owner].astype(F32) + landing[path][side, step].astype(F32)
                    ).astype(BF)
                    hop(staging[path].at[side, step], path, step, side).start()

    @pl.when(me > 0)
    def _():
        for path in (0, 1):
            hop(two[path].at[me], path, n - 1 - me, 0).wait_recv()

    @pl.when(me < n - 1)
    def _():
        for path in (0, 1):
            hop(two[path].at[me], path, me, 1).wait_recv()

    for path in (0, 1):
        total = two[path][me].astype(F32)
        from_left = landing[path][0, jnp.minimum(n - 1 - me, n - 2)].astype(F32)
        from_right = landing[path][1, jnp.minimum(me, n - 2)].astype(F32)
        total = total + jnp.where(me > 0, from_left, 0.0)
        total = total + jnp.where(me < n - 1, from_right, 0.0)
        outs[path][y, x, c] = total.astype(BF)

    def spread(path, stage):
        out = outs[path]
        if stage == 2:
            spot, device = out.at[:, :, c], by_c
        elif stage == 0:
            spot, device = out.at[y, x, c], by_x if path == 0 else by_y
        elif path == 0:
            spot, device = out.at[y, :, c], by_y
        else:
            spot, device = out.at[:, x, c], by_x
        return remote(spot, spot, gsend.at[path, stage], grecv.at[path, stage], device)

    for stage in range(3):
        for path in (0, 1):
            spread(path, stage).start()
        if stage == 0:
            line.finish(y_out)
        for path in (0, 1):
            spread(path, stage).wait_recv()

    for path in (0, 1):
        for stage in range(3):
            spread(path, stage).wait_send()
        first(path).wait_send()
        second(path).wait_send()
    for p in range(len(places)):
        swap(p).wait_send()
    for step in range(n - 1):
        for side in (0, 1):
            owner = n - 1 - step if side == 0 else step
            beyond = me < owner if side == 0 else me > owner

            @pl.when(beyond)
            def _():
                for path in (0, 1):
                    hop(two[path].at[owner], path, step, side).wait_send()


def reduce_weights(grad_qkv, grad_out, grad_small, y_part, query_width, n, collective_id):
    values = (grad_qkv, grad_out, grad_small)
    rows = grad_qkv.shape[0] // n
    eighth = rows // 8
    key_width = (grad_qkv.shape[1] - query_width) // 2
    pieces = path_pieces(query_width, key_width, grad_out.shape[1], grad_small.shape[1])
    widths = [sum(p[2] for p in pieces if p[3]), sum(p[2] for p in pieces if not p[3])]
    scratch = [pltpu.VMEM((n, 2, 2, eighth, w), BF) for w in widths]
    scratch += [pltpu.VMEM((n, 2, eighth, w), BF) for w in widths]
    scratch += [pltpu.VMEM((n, eighth, w), BF) for w in widths]
    scratch += [pltpu.VMEM((2, n - 1, eighth, w), BF) for w in widths] * 2
    sems = [(4,), (4,), (2, 2), (2, 2), (2, 2, n - 1), (2, 2, n - 1), (2, 3), (2, 3)]
    y_rows = y_part.shape[0] // n
    outs = pl.pallas_call(
        functools.partial(reduce_kernel, n, pieces),
        out_shape=[jax.ShapeDtypeStruct((2, 2, 2, eighth, w), BF) for w in widths]
        + [jax.ShapeDtypeStruct((y_rows, y_part.shape[1]), F32)],
        in_specs=[IN_VMEM] * 4,
        out_specs=[IN_VMEM] * 3,
        scratch_shapes=scratch
        + [pltpu.SemaphoreType.DMA(s) for s in sems]
        + line_sum_scratch(n, y_rows, y_part.shape[1]),
        compiler_params=pltpu.CompilerParams(
            collective_id=collective_id, has_side_effects=True, vmem_limit_bytes=48 * 1024 * 1024
        ),
        cost_estimate=pl.CostEstimate(flops=0, bytes_accessed=100000000, transcendentals=0),
        name="reduce_weights",
    )(
        *[v.reshape(n, 2, 2, 2, eighth, v.shape[1]) for v in values],
        y_part.reshape(n, y_rows, y_part.shape[1]),
    )
    first, second = [o.reshape(rows, w) for o, w in zip(outs, widths)]
    cut = pieces[0][2]
    rest = pieces[1][2]
    qkv = jnp.concatenate([first[:, :cut], second[:, :rest]], axis=1)
    return qkv, second[:, rest:], first[:, cut:], outs[2]


def plane_tick(step, local):
    tick = jnp.where(step <= 4, step // 2, jnp.where(step < local - 1, step - 2, step - 3))
    runs = (step != local - 1) & ((step > 4) | (step % 2 == 0))
    return tick, runs


def expert_kernel(sizes, plane, *refs):
    blocks, rows, local, capacity = sizes
    x_ref, ct_low_ref, ct_high_ref, router_t_ref, rank_row_ref, rank_col_ref = refs[:6]
    w_gate_ref, w_up_ref, w_down_ref = refs[6:9]
    y_ref, gs_ref, out_gate_ref, out_up_ref, out_down_ref = refs[9:14]
    xs_ref, g_ref, rank_ref, gate_ref, dots_ref, y_sem = refs[14:20]
    refs = refs[20:]
    slots = local * capacity
    step = pl.program_id(0)
    tick, ticks = plane_tick(step, local)
    base = lax.axis_index("expert") * local
    if plane:
        stage_refs, pair_refs, one_refs, two_refs = refs[:3], refs[3:6], refs[6:10], refs[10:14]
        csend, crecv, psend, precv, qsend, qrecv = refs[14:20]
        gs_part = refs[20]
        line = LineSum(blocks, gs_part, *refs[21:])
        _, _, (y, x, c), (by_y, by_x, by_c) = plane_position()
        half = stage_refs[2].shape[4] // 2

        @pl.when(step == 0)
        def _():
            greet([(None, by_c), (None, by_x), (None, by_y)] + line.neighbours())

    @pl.when(step == 0)
    def _():
        logits = dot_nt(router_t_ref[...], x_ref[...])
        hot = rank_row_ref[...] < 200.0
        top = jnp.max(jnp.where(hot, logits, NEGATIVE_LARGE), axis=0, keepdims=True)
        weight = jnp.where(hot, jnp.exp(jnp.minimum(logits - top, 0.0)), 0.0)
        gates = weight / jnp.sum(weight, axis=0, keepdims=True)
        expert_id = lax.broadcasted_iota(jnp.int32, gates.shape, 0)
        slot_id = lax.broadcasted_iota(jnp.int32, (capacity, rows), 0).astype(F32)
        rank_rows = []
        for e in range(local):
            mine = expert_id == base + e
            rank_rows.append(jnp.sum(jnp.where(mine, rank_row_ref[...], 0.0), 0, keepdims=True))
            rank_ref[e : e + 1, :] = rank_rows[e]
            gate_ref[e : e + 1, :] = jnp.sum(jnp.where(mine, gates, 0.0), 0, keepdims=True)
        for b in range(blocks):
            here = slice(b * rows, (b + 1) * rows)
            pieces = []
            for e in range(local):
                taken = jnp.broadcast_to(rank_rows[e][:, here], (capacity, rows)) == slot_id
                pieces.append(jnp.where(taken, 1.0, 0.0).astype(BF))
            pick = jnp.concatenate(pieces, axis=0)
            xs_ref[b] = dot(pick, x_ref[here, :]).astype(BF)
            middle = ct_low_ref.shape[1]
            g_ref[b, :, :middle] = dot(pick, ct_low_ref[here, :]).astype(BF)
            g_ref[b, :, middle:] = dot(pick, ct_high_ref[here, :]).astype(BF)

    @pl.when(step < local)
    def _():
        here = pl.ds(pl.multiple_of(step * capacity, capacity), capacity)
        xs = jnp.concatenate([xs_ref[b, here, :] for b in range(blocks)], axis=0)
        g = jnp.concatenate([g_ref[b, here, :] for b in range(blocks)], axis=0).astype(F32)
        slot_id = lax.broadcasted_iota(jnp.int32, (capacity, rows), 0).astype(F32)
        rank_row, gate_row = rank_ref[pl.ds(step, 1), :], gate_ref[pl.ds(step, 1), :]
        gates = []
        for b in range(blocks):
            taken = rank_row[:, b * rows : (b + 1) * rows] == slot_id
            gate = jnp.where(taken, gate_row[:, b * rows : (b + 1) * rows], 0.0)
            gates.append(jnp.sum(gate, axis=1, keepdims=True))
        gate_slot = jnp.concatenate(gates, axis=0)
        w_gate, w_up, w_down = w_gate_ref[0], w_up_ref[0], w_down_ref[0]
        gate_pre = dot(xs, w_gate)
        up_pre = dot(xs, w_up)
        sigmoid = jax.nn.sigmoid(gate_pre)
        silu = gate_pre * sigmoid
        activation = (silu * up_pre).astype(BF)
        expert_out = dot(activation, w_down).astype(BF).astype(F32)
        slot_dot = jnp.sum(g * expert_out, axis=1, keepdims=True)
        grad_out = (gate_slot * g).astype(BF)
        scaled_out = (gate_slot * expert_out).astype(BF)
        grad_down = dot_tn(activation, grad_out).astype(BF)
        grad_activation = dot_nt(grad_out, w_down)
        grad_gate_pre = (
            grad_activation * up_pre * sigmoid * (1.0 + gate_pre * (1.0 - sigmoid))
        ).astype(BF)
        grad_up_pre = (grad_activation * silu).astype(BF)
        grad_gate = dot_tn(xs, grad_gate_pre).astype(BF)
        grad_up = dot_tn(xs, grad_up_pre).astype(BF)
        if plane:
            for ref, value in zip(stage_refs, (grad_gate, grad_up, grad_down)):
                ref[step % STAGES] = value.reshape(ref.shape[1:])
        else:
            out_gate_ref[0], out_up_ref[0], out_down_ref[0] = grad_gate, grad_up, grad_down
        grad_in = (dot_nt(grad_gate_pre, w_gate) + dot_nt(grad_up_pre, w_up)).astype(BF)
        lane = lax.broadcasted_iota(jnp.int32, (blocks * capacity, LANES), 1)
        high = slot_dot.astype(BF).astype(F32)
        middle = (slot_dot - high).astype(BF).astype(F32)
        low = slot_dot - high - middle
        mine = base + step
        dots = jnp.where(lane == mine, high, 0.0)
        dots = jnp.where(lane == mine + EXPERTS, middle, dots)
        dots = jnp.where(lane == mine + 2 * EXPERTS, low, dots).astype(BF)
        for b in range(blocks):
            part = slice(b * capacity, (b + 1) * capacity)
            xs_ref[b, here, :] = grad_in[part]
            g_ref[b, here, :] = scaled_out[part]
            dots_ref[b, here, :] = dots[part]

    def store_y(b):
        there = pl.ds(b * rows, rows)
        return pltpu.make_async_copy(g_ref.at[b, :rows, :], y_ref.at[there, :], y_sem.at[b])

    @pl.when(step == local - 1)
    def _():
        slot_expert = lax.broadcasted_iota(jnp.int32, (EXPERTS, slots), 1) // capacity
        spread_row = lax.broadcasted_iota(jnp.int32, (EXPERTS, slots), 0)
        spread = jnp.where(spread_row == slot_expert + base, 1.0, 0.0).astype(BF)
        slot_rank = (lax.broadcasted_iota(jnp.int32, (rows, slots), 1) % capacity).astype(F32)
        for b in range(blocks):
            there = slice(b * rows, (b + 1) * rows)
            ranks = dot(rank_col_ref[there, :], spread)
            put = jnp.where(ranks == slot_rank, 1.0, 0.0).astype(BF)
            g_ref[b, :rows, :] = dot(put, g_ref[b]).astype(BF)
            store_y(b).start()
            back = dot(put, xs_ref[b]).astype(BF), dot(put, dots_ref[b]).astype(BF)
            if plane:
                gs_part[b, :, :D], gs_part[b, :, D:] = back
            else:
                gs_ref[there, :D], gs_ref[there, D:] = back
        if plane:
            line.start()

    @pl.when(step == pl.num_programs(0) - 1)
    def _():
        for b in range(blocks):
            store_y(b).wait()

    if not plane:
        return

    gate, up, low_down, high_down = range(4)
    low_rows, high_rows = slice(0, half), slice(half, 2 * half)

    def swap(e, i):
        return remote(
            stage_refs[i].at[e % STAGES, :, :, 1 - c],
            pair_refs[i].at[e % 3],
            csend.at[e % 2, i],
            crecv.at[e % 3, i],
            by_c,
        )

    def first(e, k):
        slot = e % 3
        source = {
            gate: lambda: pair_refs[0].at[slot, :, 1 - x],
            up: lambda: pair_refs[1].at[slot, 1 - y],
            low_down: lambda: pair_refs[2].at[slot, :, 1 - x, low_rows],
            high_down: lambda: pair_refs[2].at[slot, 1 - y, :, high_rows],
        }[k]()
        device = by_x if k in (gate, low_down) else by_y
        return remote(source, one_refs[k].at[slot], psend.at[slot, k], precv.at[slot, k], device)

    def second(e, k):
        along_x = k in (gate, low_down)
        source = one_refs[k].at[e % 3, 1 - y] if along_x else one_refs[k].at[e % 3, 1 - x]
        slot = e % 2
        return remote(
            source,
            two_refs[k].at[slot],
            qsend.at[slot, k],
            qrecv.at[slot, k],
            by_y if along_x else by_x,
        )

    def add(first_value, second_value):
        return (first_value.astype(F32) + second_value.astype(F32)).astype(BF)

    @pl.when(ticks & (tick >= 3))
    def _():
        e = tick - 3
        for k in range(4):
            second(e, k).wait()
        own = [one_refs[k][e % 3, y if k in (gate, low_down) else x] for k in range(4)]
        out_gate_ref[0] = add(own[gate], two_refs[gate][e % 2])
        out_up_ref[0] = add(own[up], two_refs[up][e % 2])
        out_down_ref[0, low_rows] = add(own[low_down], two_refs[low_down][e % 2])
        out_down_ref[0, high_rows] = add(own[high_down], two_refs[high_down][e % 2])

    @pl.when(ticks & (tick >= 2) & (tick < local + 2))
    def _():
        e = tick - 2
        slot = e % 3
        for k in range(4):
            first(e, k).wait()
            for t in (0, 1):
                mine = {
                    gate: lambda: pair_refs[0][slot, t, x],
                    up: lambda: pair_refs[1][slot, y, t],
                    low_down: lambda: pair_refs[2][slot, t, x, low_rows],
                    high_down: lambda: pair_refs[2][slot, y, t, high_rows],
                }[k]()
                one_refs[k][slot, t] = add(mine, one_refs[k][slot, t])
            second(e, k).start()

    @pl.when(ticks & (tick >= 1) & (tick < local + 1))
    def _():
        e = tick - 1
        slot = e % 3
        for i in range(3):
            swap(e, i).wait()

            def pair_sum(t, carry):
                a, b = t // 2, t % 2
                pair_refs[i][slot, a, b] = add(
                    stage_refs[i][e % STAGES, a, b, c], pair_refs[i][slot, a, b]
                )
                return carry

            lax.fori_loop(0, 4, pair_sum, 0)
        for k in range(4):
            first(e, k).start()

    @pl.when(ticks & (tick < local))
    def _():
        for i in range(3):
            swap(tick, i).start()

    for hop in range(1, blocks - 1):

        @pl.when(step == local + hop)
        def _():
            line.forward(hop)

    @pl.when(step == local + blocks - 1)
    def _():
        line.finish(gs_ref)


def run_experts(
    x_all,
    ct_low,
    ct_high,
    router_t,
    rank_row,
    rank_col,
    w_gate,
    w_up,
    w_down,
    rows,
    capacity,
    plane,
    collective_id,
):
    total = x_all.shape[0]
    blocks, local = total // rows, w_gate.shape[0]
    slots = local * capacity
    sizes = (blocks, rows, local, capacity)
    whole = lambda shape: pl.BlockSpec(
        shape, lambda e: (0,) * len(shape), pipeline_mode=pl.Buffered(1)
    )
    per = lambda shape: pl.BlockSpec((1,) + shape, lambda e: (jnp.minimum(e, local - 1), 0, 0))
    shapes = ((D, FF), (D, FF), (FF, D))
    scratch = [
        pltpu.VMEM((blocks, slots, D), BF),
        pltpu.VMEM((blocks, slots, D), BF),
        pltpu.VMEM((local, total), F32),
        pltpu.VMEM((local, total), F32),
        pltpu.VMEM((blocks, slots, LANES), BF),
        pltpu.SemaphoreType.DMA((blocks,)),
    ]
    params = dict(dimension_semantics=("arbitrary",), vmem_limit_bytes=63 * 1024 * 1024)
    if plane:
        eighths = [(a // 8, b) for a, b in shapes]
        out = lambda shape: pl.BlockSpec(
            (1,) + shape, lambda e: (jnp.maximum(plane_tick(e, local)[0] - 3, 0), 0, 0)
        )
        grad_shapes, grad_specs = eighths, [out(shape) for shape in eighths]
        low = (eighths[2][0] // 2, eighths[2][1])
        passed = (eighths[0], eighths[1], low, low)
        scratch += [pltpu.VMEM((STAGES, 2, 2, 2) + shape, BF) for shape in eighths]
        scratch += [pltpu.VMEM((3, 2, 2) + shape, BF) for shape in eighths]
        scratch += [pltpu.VMEM((3, 2) + shape, BF) for shape in passed]
        scratch += [pltpu.VMEM((2,) + shape, BF) for shape in passed]
        sems = [(2, 3), (3, 3), (3, 4), (3, 4), (2, 4), (2, 4)]
        scratch += [pltpu.SemaphoreType.DMA(shape) for shape in sems]
        scratch += [pltpu.VMEM((blocks, rows, D + LANES), BF)]
        scratch += line_sum_scratch(blocks, rows, D + LANES)
        gs_shape, gs_type = (rows, D + LANES), F32
        params |= dict(collective_id=collective_id, has_side_effects=True)
    else:
        grad_shapes, grad_specs = shapes, [per(shape) for shape in shapes]
        gs_shape, gs_type = (total, D + LANES), BF
    flops = 2 * total * D * slots * 4 // blocks + 18 * blocks * slots * D * FF
    return pl.pallas_call(
        functools.partial(expert_kernel, sizes, plane),
        grid=(local + 6 if plane else local,),
        out_shape=[
            jax.ShapeDtypeStruct((total, D), BF),
            jax.ShapeDtypeStruct(gs_shape, gs_type),
        ]
        + [jax.ShapeDtypeStruct((local,) + shape, BF) for shape in grad_shapes],
        in_specs=[
            whole((total, D)),
            whole(ct_low.shape),
            whole(ct_high.shape),
            whole((EXPERTS, D)),
            whole((EXPERTS, total)),
            whole((total, EXPERTS)),
        ]
        + [per(shape) for shape in shapes],
        out_specs=[ANY, whole(gs_shape)] + grad_specs,
        scratch_shapes=scratch,
        compiler_params=pltpu.CompilerParams(**params),
        cost_estimate=pl.CostEstimate(
            flops=flops, bytes_accessed=2 * (6 * local * D * FF + 4 * total * D), transcendentals=0
        ),
        name="experts",
    )(x_all, ct_low, ct_high, router_t, rank_row, rank_col, w_gate, w_up, w_down)


def mask_bias(bias_ref, length_ref, rows):
    base = lax.axis_index("expert") * rows
    key = lax.broadcasted_iota(jnp.int32, bias_ref.shape, 0)
    query = lax.broadcasted_iota(jnp.int32, bias_ref.shape, 1) + base
    allowed = (key <= query) & (key < length_ref[0])
    bias_ref[...] = jnp.where(allowed, 0.0, NEGATIVE_LARGE)


def head_columns(ref, head):
    start = 2 * HEAD_DIMENSION * head
    middle = start + HEAD_DIMENSION
    return jnp.concatenate([ref[:, start:middle], ref[:, middle : middle + HEAD_DIMENSION]], 0)


def put_heads(ref, head, transposed):
    rows = ref.shape[0]
    value = transposed.T
    start = 2 * HEAD_DIMENSION * head
    middle = start + HEAD_DIMENSION
    ref[:, start:middle] = value[:rows].astype(ref.dtype)
    ref[:, middle : middle + HEAD_DIMENSION] = value[rows:].astype(ref.dtype)


def attention_kernel(
    n, length_ref, q_ref, kv_ref, rank_ref, mixed_ref, log_total_ref, kv_all_ref, rank_all_ref, *scratch
):
    bias_ref, chunk_ref, rank_buffer, send, recv, rank_send, rank_recv = scratch
    pair, pairs = pl.program_id(0), pl.num_programs(0)
    group, me = lax.axis_index("group"), lax.axis_index("expert")
    left, right = (group, me - 1), (group, me + 1)
    rows, width = kv_ref.shape[1:]

    def hop(j, step, side):
        block = me - step if side == 0 else me + step
        source = kv_ref.at[j] if step == 0 else chunk_ref.at[j, block]
        index = (j, side, step)
        return remote(
            source,
            chunk_ref.at[j, block],
            send.at[index],
            recv.at[index],
            right if side == 0 else left,
        )

    def rank_hop(step, side):
        block = me - step if side == 0 else me + step
        source = rank_ref if step == 0 else rank_buffer.at[block]
        index = (side, step)
        return remote(
            source,
            rank_buffer.at[block],
            rank_send.at[index],
            rank_recv.at[index],
            right if side == 0 else left,
        )

    def sends(step, side):
        return (me - step >= 0) & (me < n - 1) if side == 0 else (me + step < n) & (me > 0)

    def arrives(step, side):
        return me - 1 - step >= 0 if side == 0 else me + 1 + step < n

    def launch(make, step):
        for side in (0, 1):

            @pl.when(sends(step, side))
            def _():
                make(step, side).start()

    def await_hop(make, step):
        for side in (0, 1):

            @pl.when(arrives(step, side))
            def _():
                make(step, side).wait_recv()

    def drain(make):
        for step in range(n - 1):
            for side in (0, 1):

                @pl.when(sends(step, side))
                def _():
                    make(step, side).wait_send()

    def chunk(j):
        return lambda step, side: hop(j, step, side)

    @pl.when(pair == 0)
    def _():
        greet([(me > 0, left), (me < n - 1, right)])
        launch(chunk(0), 0)
        rank_buffer[me] = rank_ref[...]
        launch(chunk(1), 0)
        mask_bias(bias_ref, length_ref, rows)
        await_hop(chunk(0), 0)
        launch(chunk(0), 1)

    for step in range(1, n - 1):
        await_hop(chunk(pair), step)
        if step < n - 2:
            launch(chunk(pair), step + 1)

    @pl.when(pair + 1 < pairs)
    def _():
        await_hop(chunk(pair + 1), 0)
        launch(chunk(pair + 1), 1)

    @pl.when(pair + 2 < pairs)
    def _():
        launch(chunk(pair + 2), 0)

    @pl.when(pair == 1)
    def _():
        launch(rank_hop, 0)

    for step in range(n - 1):

        @pl.when(pair == jnp.minimum(2 + step, pairs - 1))
        def _():
            await_hop(rank_hop, step)
            if step < n - 2:
                launch(rank_hop, step + 1)

    chunk_ref[pair, me] = kv_ref[pair]
    kv = chunk_ref[pair].reshape(n * rows, width)
    kv_all_ref[...] = kv
    bias = jnp.concatenate([bias_ref[...]] * 2, axis=1)
    for head in (0, 1):
        start = head * HEAD_DIMENSION
        key = kv[:, start : start + HEAD_DIMENSION]
        value = kv[:, LANES + start : LANES + start + HEAD_DIMENSION]
        query = head_columns(q_ref, head) * jnp.asarray(HEAD_DIMENSION**-0.5, BF)
        scores = dot_nt(key, query) + bias
        top = jnp.max(scores, axis=0, keepdims=True)
        weights = jnp.exp(scores - top)
        total = jnp.sum(weights, axis=0, keepdims=True)
        put_heads(mixed_ref, head, dot_tn(value, weights.astype(BF)) / total)
        log_total_ref[0, head : head + 1, :] = top + jnp.log(total)

    @pl.when(pair == pairs - 1)
    def _():
        drain(rank_hop)
        rank_all_ref[...] = rank_buffer[...]
        for j in range(KEY_VALUE_HEADS // 2):
            drain(chunk(j))


def attention(length, query, kv, rank, n, collective_id):
    rows = query.shape[0]
    keys, width = n * rows, 2 * LANES
    pairs = KEY_VALUE_HEADS // 2
    return pl.pallas_call(
        functools.partial(attention_kernel, n),
        grid=(pairs,),
        out_shape=(
            jax.ShapeDtypeStruct(query.shape, BF),
            jax.ShapeDtypeStruct((pairs, 2, 2 * rows), F32),
            jax.ShapeDtypeStruct((keys, pairs * width), BF),
            jax.ShapeDtypeStruct((n,) + rank.shape, rank.dtype),
        ),
        in_specs=[
            pl.BlockSpec(memory_space=pltpu.SMEM),
            pl.BlockSpec((rows, width), lambda j: (0, j)),
            IN_VMEM,
            IN_VMEM,
        ],
        out_specs=(
            pl.BlockSpec((rows, width), lambda j: (0, j)),
            pl.BlockSpec((1, 2, 2 * rows), lambda j: (j, 0, 0)),
            pl.BlockSpec((keys, width), lambda j: (0, j)),
            IN_VMEM,
        ),
        scratch_shapes=[
            pltpu.VMEM((keys, rows), F32),
            pltpu.VMEM((pairs, n, rows, width), BF),
            pltpu.VMEM((n,) + rank.shape, rank.dtype),
            pltpu.SemaphoreType.DMA((pairs, 2, n - 1)),
            pltpu.SemaphoreType.DMA((pairs, 2, n - 1)),
            pltpu.SemaphoreType.DMA((2, n - 1)),
            pltpu.SemaphoreType.DMA((2, n - 1)),
        ],
        compiler_params=pltpu.CompilerParams(
            dimension_semantics=("arbitrary",),
            vmem_limit_bytes=56 * 1024 * 1024,
            collective_id=collective_id,
            has_side_effects=True,
        ),
        cost_estimate=pl.CostEstimate(
            flops=16 * rows * keys * D, bytes_accessed=100000000, transcendentals=0
        ),
        name="attention",
    )(length, query, kv, rank)


def attention_back_kernel(
    n,
    length_ref,
    q_ref,
    kv_ref,
    grad_ref,
    log_total_ref,
    grad_q_ref,
    grad_kv_ref,
    bias_ref,
    terms_ref,
    landing,
    staging,
    send,
    recv,
):
    step, pairs = pl.program_id(0), pl.num_programs(0) - 1

    def line(j):
        return LineSum(
            n, terms_ref.at[j], landing.at[j], staging.at[j], send.at[j], recv.at[j]
        )

    @pl.when(step == 0)
    def _():
        greet(line(0).neighbours())
        mask_bias(bias_ref, length_ref, q_ref.shape[0])

    @pl.when(step < pairs)
    def _():
        attention_back_pair(
            q_ref, kv_ref, grad_ref, log_total_ref, grad_q_ref, terms_ref.at[step], bias_ref
        )
        line(step).start()

    @pl.when(step > 0)
    def _():
        for hop in range(1, n - 1):
            line(step - 1).forward(hop)
        line(step - 1).finish(grad_kv_ref)


def attention_back_pair(q_ref, kv_ref, grad_ref, log_total_ref, grad_q_ref, grad_kv_ref, bias_ref):
    scale = HEAD_DIMENSION**-0.5
    blocks, rows, _ = grad_kv_ref.shape
    bias = jnp.concatenate([bias_ref[...]] * 2, axis=1)
    for head in (0, 1):
        columns = slice(head * HEAD_DIMENSION, (head + 1) * HEAD_DIMENSION)
        key, value = kv_ref[:, :LANES][:, columns], kv_ref[:, LANES:][:, columns]
        query = head_columns(q_ref, head) * jnp.asarray(scale, BF)
        grad = head_columns(grad_ref, head)
        scores = dot_nt(key, query) + bias
        probs = jnp.exp(scores - log_total_ref[0, head : head + 1, :])
        grad_probs = dot_nt(value, grad)
        delta = jnp.sum(probs * grad_probs, axis=0, keepdims=True)
        grad_scores = (probs * (grad_probs - delta)).astype(BF)
        grad_key = dot(grad_scores, query).astype(BF).reshape(blocks, rows, HEAD_DIMENSION)
        grad_kv_ref[:, :, columns] = grad_key
        grad_value = dot(probs.astype(BF), grad).astype(BF).reshape(blocks, rows, HEAD_DIMENSION)
        start = LANES + head * HEAD_DIMENSION
        grad_kv_ref[:, :, start : start + HEAD_DIMENSION] = grad_value
        put_heads(grad_q_ref, head, dot_tn(key, grad_scores) * scale)


def attention_back(length, query, kv_all, grad_mixed, log_total, n, collective_id):
    rows, keys = query.shape[0], kv_all.shape[0]
    pairs, width = KEY_VALUE_HEADS // 2, 2 * LANES
    now = lambda j: jnp.minimum(j, pairs - 1)
    row_spec = pl.BlockSpec((rows, width), lambda j: (0, now(j)))
    return pl.pallas_call(
        functools.partial(attention_back_kernel, n),
        grid=(pairs + 1,),
        out_shape=(
            jax.ShapeDtypeStruct(query.shape, F32),
            jax.ShapeDtypeStruct((rows, pairs * width), BF),
        ),
        in_specs=[
            pl.BlockSpec(memory_space=pltpu.SMEM),
            row_spec,
            pl.BlockSpec((keys, width), lambda j: (0, now(j))),
            row_spec,
            pl.BlockSpec((1, 2, 2 * rows), lambda j: (now(j), 0, 0)),
        ],
        out_specs=(
            row_spec,
            pl.BlockSpec((rows, width), lambda j: (0, jnp.maximum(j - 1, 0))),
        ),
        scratch_shapes=[
            pltpu.VMEM((keys, rows), F32),
            pltpu.VMEM((pairs, n, rows, width), BF),
            pltpu.VMEM((pairs, 2, n - 1, rows, width), BF),
            pltpu.VMEM((pairs, 2, n - 2, rows, width), BF),
            pltpu.SemaphoreType.DMA((pairs, 2, n - 1)),
            pltpu.SemaphoreType.DMA((pairs, 2, n - 1)),
        ],
        compiler_params=pltpu.CompilerParams(
            dimension_semantics=("arbitrary",),
            vmem_limit_bytes=60 * 1024 * 1024,
            collective_id=collective_id,
            has_side_effects=True,
        ),
        cost_estimate=pl.CostEstimate(
            flops=40 * rows * keys * D, bytes_accessed=100000000, transcendentals=0
        ),
        name="attention_back",
    )(length, query, kv_all, grad_mixed, log_total)


def widen_kernel(value_ref, out_ref):
    out_ref[...] = value_ref[...].astype(F32)


def widen(value):
    block = (1,) + value.shape[1:]
    spec = pl.BlockSpec(block, lambda e: (e, 0, 0))
    return pl.pallas_call(
        widen_kernel,
        grid=(value.shape[0],),
        out_shape=jax.ShapeDtypeStruct(value.shape, F32),
        in_specs=[spec],
        out_specs=spec,
        compiler_params=pltpu.CompilerParams(dimension_semantics=("arbitrary",)),
        cost_estimate=pl.CostEstimate(flops=0, bytes_accessed=6 * value.size, transcendentals=0),
        name="widen",
    )(value)


def unpair_columns(value):
    rows = value.shape[0]
    value = value.reshape(rows, -1, 2, LANES)
    return value[:, :, 0].reshape(rows, -1), value[:, :, 1].reshape(rows, -1)


def gather_rows(value):
    return lax.all_gather(value, "expert", axis=0, tiled=True)


def scatter_rows(value):
    return lax.psum_scatter(value, "expert", scatter_dimension=0, tiled=True)


def per_device(
    tokens,
    lengths,
    routes,
    norm_gain1,
    w_query,
    key_projection,
    value_projection,
    w_out,
    norm_gain2,
    w_router,
    w_gate,
    w_up,
    w_down,
    cotangent,
):
    rows = tokens.shape[0]
    n, groups = lax.axis_size("expert"), lax.axis_size("group")
    my_index = lax.axis_index("expert")
    capacity = 3 * rows * TOP // (2 * EXPERTS)
    query_width, key_width = w_query.shape[1], key_projection.shape[1]
    length = lengths[0]
    positions = my_index * rows + jnp.arange(rows, dtype=jnp.int32)
    valid_rows = (positions < length)[:, None]
    grad_output = jnp.where(valid_rows, cotangent, jnp.zeros_like(cotangent))

    small = jnp.concatenate(
        [w_router, norm_gain1[:, None], norm_gain2[:, None]]
        + [jnp.zeros((w_router.shape[0], LANES - EXPERTS - 2), BF)],
        axis=1,
    )
    middle = D // 2
    qkv_weight, out_weight, small, ct_low = gather_weights(
        w_query, key_projection, value_projection, w_out, small, grad_output[:, :middle], n, 1
    )
    qkv_weight, ct_high = lax.optimization_barrier((qkv_weight, grad_output[:, middle:]))
    ct_high = gather_rows(ct_high)
    router_weight = small[:, :EXPERTS]
    gain_one = small[:, EXPERTS].astype(F32)
    gain_two = small[:, EXPERTS + 1].astype(F32)

    expert_ids = jnp.arange(EXPERTS, dtype=jnp.int32)
    hot = jnp.any(routes[:, :, None] == expert_ids, axis=1)
    row_id = jnp.arange(rows, dtype=jnp.int32)
    earlier = (row_id[:, None] < row_id[None, :]).astype(BF)
    rank = jnp.where(hot.T, dot(hot.T.astype(BF), earlier), 255.0).astype(BF)

    cosine_lookup, sine_lookup = rotary_tables(positions, HEAD_DIMENSION)
    token_f32 = tokens.astype(F32)
    inverse_one = lax.rsqrt(jnp.mean(token_f32 * token_f32, axis=-1, keepdims=True) + EPSILON)
    unit_one = token_f32 * inverse_one
    first_norm = (unit_one * gain_one).astype(BF)
    qkv = dot(first_norm, qkv_weight)
    query_pre = qkv[:, :query_width]
    unrotated_key = qkv[:, query_width : query_width + key_width]
    value_pre = qkv[:, query_width + key_width :]
    query_rows = apply_rotation(
        query_pre.reshape(rows, QUERY_HEADS, HEAD_DIMENSION), cosine_lookup, sine_lookup
    ).astype(BF)
    query_rows = query_rows.reshape(rows, query_width)
    local_keys = apply_rotation(
        unrotated_key.reshape(rows, KEY_VALUE_HEADS, HEAD_DIMENSION), cosine_lookup, sine_lookup
    ).astype(BF)
    local_keys = local_keys.reshape(rows, key_width)
    own_kv = jnp.stack(
        [
            jnp.concatenate([local_keys[:, cut], value_pre[:, cut].astype(BF)], axis=1)
            for cut in [slice(i, i + LANES) for i in range(0, key_width, LANES)]
        ]
    )
    mixed_low, log_total, kv_all, rank_all = attention(lengths, query_rows, own_kv, rank, n, 2)
    rank_row = jnp.transpose(rank_all, (1, 0, 2)).reshape(EXPERTS, n * rows).astype(F32)
    rank_col = jnp.transpose(rank_all, (0, 2, 1)).reshape(n * rows, EXPERTS)
    residual = token_f32 + dot(mixed_low, out_weight)
    inverse_two = lax.rsqrt(jnp.mean(residual * residual, axis=-1, keepdims=True) + EPSILON)
    unit_two = residual * inverse_two
    second_norm = (unit_two * gain_two).astype(BF)
    (x_all,) = line_gather([second_norm], n, 3, "gather_rows")

    y_part, gs, grad_gate, grad_up, grad_down = run_experts(
        x_all,
        ct_low,
        ct_high,
        router_weight.T,
        rank_row,
        rank_col,
        w_gate,
        w_up,
        w_down,
        rows,
        capacity,
        groups == 8,
        7,
    )
    if groups != 8:
        gs = line_scatter(gs, n, F32, 4, "scatter_grads")

    logits = dot(second_norm, router_weight)
    chosen = jnp.where(hot, logits, NEGATIVE_LARGE)
    gate_weights = jnp.where(hot, jnp.exp(chosen - jnp.max(chosen, axis=-1, keepdims=True)), 0.0)
    gate_weights = gate_weights / jnp.sum(gate_weights, axis=-1, keepdims=True)
    grad_gates = gs[:, D : D + EXPERTS] + gs[:, D + EXPERTS : D + 2 * EXPERTS]
    grad_gates = grad_gates + gs[:, D + 2 * EXPERTS : D + 3 * EXPERTS]
    grad_logits = (
        gate_weights * (grad_gates - jnp.sum(gate_weights * grad_gates, axis=-1, keepdims=True))
    ).astype(BF)
    grad_second = gs[:, :D] + dot_nt(grad_logits, router_weight)
    grad_router = dot_tn(second_norm, grad_logits)
    scaled_two = grad_second * gain_two
    grad_gain2 = jnp.sum(grad_second * unit_two, axis=0)
    grad_residual = grad_output.astype(F32) + inverse_two * (
        scaled_two - unit_two * jnp.mean(scaled_two * unit_two, axis=-1, keepdims=True)
    )
    grad_attn = grad_residual.astype(BF)
    grad_out = dot_tn(mixed_low, grad_attn)
    mixed_gradient = dot_nt(grad_attn, out_weight).astype(BF)
    grad_query_acc, kv_gradient = attention_back(
        lengths, query_rows, kv_all, mixed_gradient, log_total, n, 5
    )
    own_key_gradient, own_value_gradient = unpair_columns(kv_gradient)
    grad_query_pre = (
        apply_rotation(
            grad_query_acc.reshape(rows, QUERY_HEADS, HEAD_DIMENSION), cosine_lookup, -sine_lookup
        )
        .reshape(rows, query_width)
        .astype(BF)
    )
    grad_key_pre = apply_rotation(
        own_key_gradient.astype(F32).reshape(rows, KEY_VALUE_HEADS, HEAD_DIMENSION),
        cosine_lookup,
        -sine_lookup,
    )
    grad_key_pre = grad_key_pre.reshape(rows, key_width).astype(BF)
    grad_qkv_pre = jnp.concatenate(
        [grad_query_pre, grad_key_pre, own_value_gradient], axis=1
    )
    grad_qkv = dot_tn(first_norm, grad_qkv_pre)
    grad_first = dot_nt(grad_qkv_pre, qkv_weight)
    scaled_one = grad_first * gain_one
    grad_gain1 = jnp.sum(grad_first * unit_one, axis=0)
    grad_tokens = grad_residual + inverse_one * (
        scaled_one - unit_one * jnp.mean(scaled_one * unit_one, axis=-1, keepdims=True)
    )
    grad_small = jnp.concatenate(
        [grad_router, grad_gain1[:, None], grad_gain2[:, None]]
        + [jnp.zeros((D, LANES - EXPERTS - 2), F32)],
        axis=1,
    )
    shares = (grad_qkv.astype(BF), grad_out.astype(BF), grad_small.astype(BF))
    if groups == 8:
        *shares, expert_sum = reduce_weights(*shares, y_part, query_width, n, 6)
    else:
        shares = [lax.psum(scatter_rows(share), "group") for share in shares]
        expert_sum = line_scatter(y_part, n, F32, 8, "scatter_outputs")
    mixed = (residual + expert_sum).astype(BF)
    share_qkv, share_out, share_small = [share.astype(F32) for share in shares]

    def sum_over_groups(value):
        if groups != 8:
            value = lax.psum_scatter(value, "group", scatter_dimension=1, tiled=True)
        return widen(lax.all_gather(value, "group", axis=1, tiled=True))

    return (
        mixed,
        grad_tokens,
        share_small[:, EXPERTS],
        share_qkv[:, :query_width],
        share_qkv[:, query_width : query_width + key_width],
        share_qkv[:, query_width + key_width :],
        share_out,
        share_small[:, EXPERTS + 1],
        share_small[:, :EXPERTS],
        sum_over_groups(grad_gate),
        sum_over_groups(grad_up),
        sum_over_groups(grad_down),
    )


def solution(mesh):
    rows = P(("group", "expert"), None)
    vector, matrix, stack = P("expert"), P("expert", None), P("expert", None, None)
    return jax.shard_map(
        per_device,
        mesh=mesh,
        in_specs=(
            rows,
            P("group"),
            rows,
            vector,
            matrix,
            matrix,
            matrix,
            matrix,
            vector,
            matrix,
            stack,
            stack,
            stack,
            rows,
        ),
        out_specs=(
            rows,
            rows,
            vector,
            matrix,
            matrix,
            matrix,
            matrix,
            vector,
            matrix,
            stack,
            stack,
            stack,
        ),
        check_vma=False,
    )
```

```python
import functools

import jax
import jax.numpy as jnp
from jax import lax
from jax.experimental import pallas as pl
from jax.experimental.pallas import tpu as pltpu
from jax.sharding import PartitionSpec as P

D = 1024
QUERY_HEADS = 16
KEY_VALUE_HEADS = 8
HEAD_DIMENSION = 64
EXPERTS = 32
TOP = 8
FF = 512
LANES = 128
STAGES = 4

EPSILON = 1e-05
NEGATIVE_LARGE = -1e30
BF = jnp.bfloat16
F32 = jnp.float32


def rotary_tables(positions, head_size):
    half_width = head_size // 2
    frequency = 10000.0 ** (-2.0 * jnp.arange(half_width).astype(F32) / head_size)
    angles = positions.astype(F32)[:, None] * frequency[None, :]
    return (jnp.cos(angles)[:, None, :], jnp.sin(angles)[:, None, :])


def apply_rotation(tensor_in, cosine_lookup, sine_lookup):
    half_width = tensor_in.shape[-1] // 2
    first_half = tensor_in[..., :half_width]
    second_half = tensor_in[..., half_width:]
    return jnp.concatenate(
        [
            first_half * cosine_lookup - second_half * sine_lookup,
            second_half * cosine_lookup + first_half * sine_lookup,
        ],
        axis=-1,
    )


def dot(a, b):
    return jnp.dot(a, b, preferred_element_type=F32)


def dot_nt(a, b):
    return lax.dot_general(a, b, (((1,), (1,)), ((), ())), preferred_element_type=F32)


def dot_tn(a, b):
    return lax.dot_general(a, b, (((0,), (0,)), ((), ())), preferred_element_type=F32)


MESH = pl.DeviceIdType.MESH
ANY = pl.BlockSpec(memory_space=pl.ANY)
IN_VMEM = pl.BlockSpec(memory_space=pltpu.VMEM)


def remote(source, target, send, receive, device):
    return pltpu.make_async_remote_copy(
        src_ref=source,
        dst_ref=target,
        send_sem=send,
        recv_sem=receive,
        device_id=device,
        device_id_type=MESH,
    )


def greet(devices):
    barrier = pltpu.get_barrier_semaphore()
    count = 0
    for condition, device in devices:
        if condition is None:
            pl.semaphore_signal(barrier, inc=1, device_id=device, device_id_type=MESH)
            count = count + 1
        else:

            @pl.when(condition)
            def _():
                pl.semaphore_signal(barrier, inc=1, device_id=device, device_id_type=MESH)

            count = count + jnp.where(condition, 1, 0)
    pl.semaphore_wait(barrier, count)


def line_gather_kernel(n, count, *refs):
    ins, outs = refs[:count], refs[count : 2 * count]
    local, send, receive = refs[2 * count :]
    group, me = lax.axis_index("group"), lax.axis_index("expert")
    left, right = (group, me - 1), (group, me + 1)
    own = [
        pltpu.make_async_copy(ins[i], outs[i].at[me], local.at[i]) for i in range(count)
    ]
    for copy in own:
        copy.start()
    greet([(me > 0, left), (me < n - 1, right)])

    def hop(i, step, side):
        block = me - step if side == 0 else me + step
        source = ins[i] if step == 0 else outs[i].at[block]
        index = (side, step, i)
        return remote(
            source, outs[i].at[block], send.at[index], receive.at[index], right if side == 0 else left
        )

    def arrival(i, step, side):
        block = me - 1 - step if side == 0 else me + 1 + step
        index = (side, step, i)
        return remote(
            outs[i].at[block], outs[i].at[block], send.at[index], receive.at[index], left if side == 0 else right
        )

    def sends(step, side):
        return (me - step >= 0) & (me < n - 1) if side == 0 else (me + step < n) & (me > 0)

    def arrives(step, side):
        return me - 1 - step >= 0 if side == 0 else me + 1 + step < n

    for step in range(n - 1):
        for side in (0, 1):

            @pl.when(sends(step, side))
            def _():
                for i in range(count):
                    hop(i, step, side).start()

        for side in (0, 1):

            @pl.when(arrives(step, side))
            def _():
                for i in range(count):
                    arrival(i, step, side).wait_recv()

    for step in range(n - 1):
        for side in (0, 1):

            @pl.when(sends(step, side))
            def _():
                for i in range(count):
                    hop(i, step, side).wait_send()

    for copy in own:
        copy.wait()


def line_gather(values, n, collective_id, name):
    count = len(values)
    outs = pl.pallas_call(
        functools.partial(line_gather_kernel, n, count),
        out_shape=[jax.ShapeDtypeStruct((n,) + v.shape, v.dtype) for v in values],
        in_specs=[IN_VMEM] * count,
        out_specs=[ANY] * count,
        scratch_shapes=[
            pltpu.SemaphoreType.DMA((count,)),
            pltpu.SemaphoreType.DMA((2, n - 1, count)),
            pltpu.SemaphoreType.DMA((2, n - 1, count)),
        ],
        compiler_params=pltpu.CompilerParams(collective_id=collective_id, has_side_effects=True),
        cost_estimate=pl.CostEstimate(flops=0, bytes_accessed=100000000, transcendentals=0),
        name=name,
    )(*values)
    return [o.reshape((n * v.shape[0],) + v.shape[1:]) for o, v in zip(outs, values)]


class LineSum:
    def __init__(self, n, part, landing, staging, send, receive):
        self.n, self.part, self.landing, self.staging = n, part, landing, staging
        self.send, self.receive = send, receive
        self.group, self.me = lax.axis_index("group"), lax.axis_index("expert")
        self.rows = part.shape[1]
        self.tile = min(32, self.rows)

    def neighbours(self):
        left, right = (self.group, self.me - 1), (self.group, self.me + 1)
        return [(self.me > 0, left), (self.me < self.n - 1, right)]

    def copy(self, source, step, side):
        index = (side, step)
        device = (self.group, self.me + 1 if side == 0 else self.me - 1)
        return remote(
            source, self.landing.at[index], self.send.at[index], self.receive.at[index], device
        )

    def places(self):
        me, n = self.me, self.n
        for step in range(n - 1):
            for side in (0, 1):
                owner = n - 1 - step if side == 0 else step
                beyond = me < owner if side == 0 else me > owner
                edge = me == 0 if side == 0 else me == n - 1
                yield step, side, owner, beyond, edge

    def start(self):
        for step, side, owner, beyond, edge in self.places():

            @pl.when(beyond & edge)
            def _():
                self.copy(self.part.at[owner], step, side).start()

    def spans(self, body):
        def tile_body(t, carry):
            body(pl.ds(pl.multiple_of(t * self.tile, self.tile), self.tile))
            return carry

        lax.fori_loop(0, self.rows // self.tile, tile_body, 0)

    def forward(self, hop):
        me, n = self.me, self.n
        for side in (0, 1):
            step = hop - me if side == 0 else hop - (n - 1 - me)
            owner = n - 1 - step if side == 0 else step
            inner = me > 0 if side == 0 else me < n - 1
            beyond = me < owner if side == 0 else me > owner

            @pl.when(inner & (step >= 0) & beyond)
            def _():
                self.copy(self.part.at[owner], step, side).wait_recv()

                def add(span):
                    total = self.part[owner, span, :].astype(F32)
                    total = total + self.landing[side, step, span, :].astype(F32)
                    self.staging[side, step, span, :] = total.astype(BF)

                self.spans(add)
                self.copy(self.staging.at[side, step], step, side).start()

    def finish(self, out_ref):
        me, n = self.me, self.n

        @pl.when(me > 0)
        def _():
            self.copy(self.part.at[me], n - 1 - me, 0).wait_recv()

        @pl.when(me < n - 1)
        def _():
            self.copy(self.part.at[me], me, 1).wait_recv()

        def total(span):
            value = self.part[me, span, :].astype(F32)
            from_left = self.landing[0, jnp.minimum(n - 1 - me, n - 2), span, :].astype(F32)
            from_right = self.landing[1, jnp.minimum(me, n - 2), span, :].astype(F32)
            value = value + jnp.where(me > 0, from_left, 0.0)
            value = value + jnp.where(me < n - 1, from_right, 0.0)
            out_ref[span, :] = value.astype(out_ref.dtype)

        self.spans(total)
        for step, side, owner, beyond, edge in self.places():

            @pl.when(beyond)
            def _():
                self.copy(self.part.at[owner], step, side).wait_send()


def line_sum_scratch(n, rows, width):
    return [
        pltpu.VMEM((2, n - 1, rows, width), BF),
        pltpu.VMEM((2, n - 2, rows, width), BF),
        pltpu.SemaphoreType.DMA((2, n - 1)),
        pltpu.SemaphoreType.DMA((2, n - 1)),
    ]


def line_scatter_kernel(n, part_ref, out_ref, *scratch):
    line = LineSum(n, part_ref, *scratch)
    greet(line.neighbours())
    line.start()
    for hop in range(1, n - 1):
        line.forward(hop)
    line.finish(out_ref)


def line_scatter(value, n, dtype, collective_id, name):
    total, width = value.shape
    rows = total // n
    return pl.pallas_call(
        functools.partial(line_scatter_kernel, n),
        out_shape=jax.ShapeDtypeStruct((rows, width), dtype),
        in_specs=[IN_VMEM],
        out_specs=IN_VMEM,
        scratch_shapes=line_sum_scratch(n, rows, width),
        compiler_params=pltpu.CompilerParams(collective_id=collective_id, has_side_effects=True),
        cost_estimate=pl.CostEstimate(flops=0, bytes_accessed=100000000, transcendentals=0),
        name=name,
    )(value.reshape(n, rows, width))


def plane_position():
    group, me = lax.axis_index("group"), lax.axis_index("expert")
    c, x, y = group % 2, (group // 2) % 2, (group // 4) % 2
    by_c, by_x, by_y = (group + 1 - 2 * c, me), (group + 2 - 4 * x, me), (group + 4 - 8 * y, me)
    return group, me, (y, x, c), (by_y, by_x, by_c)


def weights_kernel(n, pieces, widths, *refs):
    wq, wk, wv, wo, small, extra = refs[:6]
    outs, extra_out, owns = refs[6:9], refs[9], refs[10:13]
    load, store, zsend, zrecv, psend, precv, csend, crecv, xsend, xrecv = refs[13:]
    group, me, (y, x, c), (by_y, by_x, by_c) = plane_position()
    left, right = (group, me - 1), (group, me + 1)
    eighth = owns[0].shape[0]
    span = pl.ds(pl.multiple_of((y * 4 + x * 2 + c) * eighth, eighth), eighth)
    query_width, key_width = wq.shape[1], wk.shape[1]
    targets = (
        owns[0].at[:, :query_width],
        owns[0].at[:, query_width : query_width + key_width],
        owns[0].at[:, query_width + key_width :],
        owns[1],
        owns[2],
    )
    loads = [
        pltpu.make_async_copy(source.at[span, :], target, load.at[i])
        for i, (source, target) in enumerate(zip((wq, wk, wv, wo, small), targets))
    ]
    for copy in loads:
        copy.start()
    for copy in loads:
        copy.wait()
    stores = [
        pltpu.make_async_copy(owns[i], outs[i].at[me, y, x, c], store.at[i]) for i in range(3)
    ]
    stores.append(pltpu.make_async_copy(extra, extra_out.at[me], store.at[3]))
    for copy in stores:
        copy.start()
    greet(
        [(me > 0, left), (me < n - 1, right), (None, by_c), (None, by_x), (None, by_y)]
    )

    def hop(i, step, side):
        block = me - step if side == 0 else me + step
        source = owns[i] if step == 0 else outs[i].at[block, y, x, c]
        index = (side, step, i)
        return remote(
            source,
            outs[i].at[block, y, x, c],
            zsend.at[index],
            zrecv.at[index],
            right if side == 0 else left,
        )

    def sends(step, side):
        return (me - step >= 0) & (me < n - 1) if side == 0 else (me + step < n) & (me > 0)

    def extra_hop(step, side):
        block = me - step if side == 0 else me + step
        source = extra if step == 0 else extra_out.at[block]
        return remote(
            source,
            extra_out.at[block],
            xsend.at[side, step],
            xrecv.at[side, step],
            right if side == 0 else left,
        )

    def first(slot, block, p):
        i, start, width, along_x = pieces[p]
        spot = outs[i].at[block, y, x, c, :, start : start + width]
        source = owns[i].at[:, start : start + width] if slot == 0 else spot
        index = (0, slot, p)
        return remote(source, spot, psend.at[index], precv.at[index], by_x if along_x else by_y)

    def second(slot, block, p):
        i, start, width, along_x = pieces[p]
        columns = slice(start, start + width)
        if along_x:
            spot = outs[i].at[block, y, :, c, :, columns]
        else:
            spot = outs[i].at[block, :, x, c, :, columns]
        index = (1, slot, p)
        return remote(spot, spot, psend.at[index], precv.at[index], by_y if along_x else by_x)

    def third(slot, block, i):
        spot = outs[i].at[block, :, :, c]
        index = (slot, i)
        return remote(spot, spot, csend.at[index], crecv.at[index], by_c)

    def held(step):
        if step == 0:
            return [(0, me, me >= 0)]
        return [(step, me - step, me - step >= 0), (n - 1 + step, me + step, me + step < n)]

    count = len(pieces)
    for step in range(n + 2):
        if step < n:
            for slot, block, there in held(step):

                @pl.when(there)
                def _():
                    if step > 0:
                        side = 0 if slot < n else 1
                        for i in range(3):
                            hop(i, step - 1, side).wait_recv()
                    for p in range(count):
                        first(slot, block, p).start()

            if step < n - 1:
                for side in (0, 1):

                    @pl.when(sends(step, side))
                    def _():
                        for i in range(3):
                            hop(i, step, side).start()

        if 1 <= step < n + 1:
            if step == 1:
                for copy in stores:
                    copy.wait()
            for slot, block, there in held(step - 1):

                @pl.when(there)
                def _():
                    for p in range(count):
                        first(slot, block, p).wait_recv()
                    for p in range(count):
                        second(slot, block, p).start()

        if step >= 2:
            for slot, block, there in held(step - 2):

                @pl.when(there)
                def _():
                    for p in range(count):
                        second(slot, block, p).wait_recv()
                    for i in range(3):
                        third(slot, block, i).start()

            for side in (0, 1):
                if step > 2:

                    @pl.when(me - step + 2 >= 0 if side == 0 else me + step - 2 < n)
                    def _():
                        extra_hop(step - 3, side).wait_recv()

                if step < n + 1:

                    @pl.when(sends(step - 2, side))
                    def _():
                        extra_hop(step - 2, side).start()

    for step in range(n):
        for slot, block, there in held(step):

            @pl.when(there)
            def _():
                for p in range(count):
                    first(slot, block, p).wait_send()
                    second(slot, block, p).wait_send()
                for i in range(3):
                    third(slot, block, i).wait()

        if step < n - 1:
            for side in (0, 1):

                @pl.when(sends(step, side))
                def _():
                    for i in range(3):
                        hop(i, step, side).wait_send()
                    extra_hop(step, side).wait_send()


def path_pieces(query_width, key_width, out_width, small_width):
    half = (query_width + 2 * key_width + out_width) // 2
    return (
        (0, 0, half, True),
        (0, half, query_width + 2 * key_width - half, False),
        (1, 0, out_width, False),
        (2, 0, small_width, True),
    )


def gather_weights(wq, wk, wv, wo, small, extra, n, collective_id):
    rows = wq.shape[0]
    eighth = rows // 8
    widths = (wq.shape[1] + wk.shape[1] + wv.shape[1], wo.shape[1], small.shape[1])
    pieces = path_pieces(wq.shape[1], wk.shape[1], wo.shape[1], small.shape[1])
    outs = pl.pallas_call(
        functools.partial(weights_kernel, n, pieces, widths),
        out_shape=[jax.ShapeDtypeStruct((n, 2, 2, 2, eighth, w), BF) for w in widths]
        + [jax.ShapeDtypeStruct((n,) + extra.shape, BF)],
        in_specs=[ANY] * 5 + [IN_VMEM],
        out_specs=[ANY] * 4,
        scratch_shapes=[pltpu.VMEM((eighth, w), BF) for w in widths]
        + [
            pltpu.SemaphoreType.DMA((5,)),
            pltpu.SemaphoreType.DMA((4,)),
            pltpu.SemaphoreType.DMA((2, n - 1, 3)),
            pltpu.SemaphoreType.DMA((2, n - 1, 3)),
            pltpu.SemaphoreType.DMA((2, 2 * n - 1, 4)),
            pltpu.SemaphoreType.DMA((2, 2 * n - 1, 4)),
            pltpu.SemaphoreType.DMA((2 * n - 1, 3)),
            pltpu.SemaphoreType.DMA((2 * n - 1, 3)),
            pltpu.SemaphoreType.DMA((2, n - 1)),
            pltpu.SemaphoreType.DMA((2, n - 1)),
        ],
        compiler_params=pltpu.CompilerParams(collective_id=collective_id, has_side_effects=True),
        cost_estimate=pl.CostEstimate(flops=0, bytes_accessed=100000000, transcendentals=0),
        name="gather_weights",
    )(wq, wk, wv, wo, small, extra)
    weights = [o.reshape(n * rows, w) for o, w in zip(outs, widths)]
    return weights + [outs[3].reshape(-1, extra.shape[1])]


def reduce_kernel(n, pieces, *refs):
    (
        grad_q_ref,
        grad_kv_ref,
        tokens_ref,
        gain_ref,
        weight_ref,
        cosine_ref,
        sine_ref,
        mixed_ref,
        grad_attn_ref,
        grad_residual_ref,
        router_ref,
        gain_two_ref,
        y_part,
    ) = refs[:13]
    outs, y_out, grad_tokens_ref = refs[13:15], refs[15], refs[16]
    ins, grad_pre_ref = refs[17:20], refs[20]
    refs = refs[21:]
    pair, one, two, landing, staging = refs[:2], refs[2:4], refs[4:6], refs[6:8], refs[8:10]
    csend, crecv, psend, precv, zsend, zrecv, gsend, grecv = refs[10:18]
    line = LineSum(n, y_part, *refs[18:])
    group, me, (y, x, c), (by_y, by_x, by_c) = plane_position()
    left, right = (group, me - 1), (group, me + 1)
    eighth = pair[0].shape[3]
    greet(
        [(me > 0, left), (me < n - 1, right), (None, by_c), (None, by_x), (None, by_y)]
    )

    places, ends = [], [0, 0]
    for array, start, width, along_x in pieces:
        path = 0 if along_x else 1
        places.append((array, start, width, path, ends[path]))
        ends[path] += width

    def swap(p):
        array, start, width, path, at = places[p]
        return remote(
            ins[array].at[:, :, :, 1 - c, :, start : start + width],
            pair[path].at[:, :, :, :, at : at + width],
            csend.at[p],
            crecv.at[p],
            by_c,
        )

    line.start()
    D_rows = weight_ref.shape[0]
    query_width = grad_q_ref.shape[1]
    key_width = (weight_ref.shape[1] - query_width) // 2

    def put(array, columns, value):
        ins[array][:, :, :, :, :, columns] = value.astype(BF).reshape(
            ins[array].shape[:5] + (value.shape[1],)
        )

    tile = 4 * LANES
    for start in range(0, grad_attn_ref.shape[1], tile):
        columns = slice(start, start + tile)
        put(1, columns, dot_tn(mixed_ref[...], grad_attn_ref[:, columns]))
    swap(2).start()
    unit, inverse = normed(tokens_ref)
    gain = gain_ref[...]
    first_norm = (unit * gain).astype(BF)
    cosine, sine = cosine_ref[...], -sine_ref[...]
    for j in range(query_width // LANES):
        columns = slice(j * LANES, (j + 1) * LANES)
        grad_pre_ref[:, columns] = rotate(grad_q_ref[:, columns], cosine, sine).astype(BF)
    for j in range(key_width // LANES):
        start = 2 * j * LANES
        key = grad_kv_ref[:, start : start + LANES].astype(F32)
        at = query_width + j * LANES
        grad_pre_ref[:, at : at + LANES] = rotate(key, cosine, sine).astype(BF)
        at = at + key_width
        grad_pre_ref[:, at : at + LANES] = grad_kv_ref[:, start + LANES : start + 2 * LANES]
    for start in range(0, weight_ref.shape[1], tile):
        columns = slice(start, start + tile)
        put(0, columns, dot_tn(first_norm, grad_pre_ref[:, columns]))
    swap(0).start()
    swap(1).start()
    grad_first = dot_nt(grad_pre_ref[...], weight_ref[...])
    gain_one_row = jnp.sum(grad_first * unit, axis=0, keepdims=True)
    lane = lax.broadcasted_iota(jnp.int32, (LANES, D_rows), 0)
    gains = jnp.where(lane == EXPERTS, gain_one_row, 0.0)
    gains = jnp.where(lane == EXPERTS + 1, gain_two_ref[...], gains)
    put(2, slice(0, LANES), router_ref[...] + gains.T)
    swap(3).start()
    scaled = grad_first * gain
    mean = jnp.mean(scaled * unit, axis=-1, keepdims=True)
    grad_tokens_ref[...] = grad_residual_ref[...] + inverse * (scaled - unit * mean)
    for p in range(len(places)):
        swap(p).wait_recv()
        array, start, width, path, at = places[p]

        def pair_sum(t, carry):
            z, a, b = t // 4, (t // 2) % 2, t % 2
            mine = ins[array][z, a, b, c, :, start : start + width].astype(F32)
            theirs = pair[path][z, a, b, :, at : at + width].astype(F32)
            pair[path][z, a, b, :, at : at + width] = (mine + theirs).astype(BF)
            return carry

        lax.fori_loop(0, 4 * n, pair_sum, 0)

    def first(path):
        source = pair[0].at[:, :, 1 - x] if path == 0 else pair[1].at[:, 1 - y]
        return remote(
            source, one[path], psend.at[0, path], precv.at[0, path], by_x if path == 0 else by_y
        )

    def second(path):
        source = one[path].at[:, 1 - y] if path == 0 else one[path].at[:, 1 - x]
        return remote(
            source, two[path], psend.at[1, path], precv.at[1, path], by_y if path == 0 else by_x
        )

    for path in (0, 1):
        first(path).start()
    line.forward(1)
    for path in (0, 1):
        first(path).wait_recv()

        def first_sum(t, carry):
            z, a = t // 2, t % 2
            mine = pair[0][z, a, x] if path == 0 else pair[1][z, y, a]
            one[path][z, a] = (mine.astype(F32) + one[path][z, a].astype(F32)).astype(BF)
            return carry

        lax.fori_loop(0, 2 * n, first_sum, 0)
        second(path).start()
    for far in range(2, n - 1):
        line.forward(far)
    for path in (0, 1):
        second(path).wait_recv()

        def second_sum(z, carry):
            mine = one[0][z, y] if path == 0 else one[1][z, x]
            two[path][z] = (mine.astype(F32) + two[path][z].astype(F32)).astype(BF)
            return carry

        lax.fori_loop(0, n, second_sum, 0)

    def hop(source, path, step, side):
        index = (path, side, step)
        return remote(
            source,
            landing[path].at[side, step],
            zsend.at[index],
            zrecv.at[index],
            right if side == 0 else left,
        )

    for step in range(n - 1):
        for side in (0, 1):
            owner = n - 1 - step if side == 0 else step
            beyond = me < owner if side == 0 else me > owner
            edge = me == 0 if side == 0 else me == n - 1

            @pl.when(beyond & edge)
            def _():
                for path in (0, 1):
                    hop(two[path].at[owner], path, step, side).start()

    for far in range(1, n - 1):
        for side in (0, 1):
            step = far - me if side == 0 else far - (n - 1 - me)
            owner = n - 1 - step if side == 0 else step
            inner = me > 0 if side == 0 else me < n - 1
            beyond = me < owner if side == 0 else me > owner

            @pl.when(inner & (step >= 0) & beyond)
            def _():
                for path in (0, 1):
                    hop(two[path].at[owner], path, step, side).wait_recv()
                    staging[path][side, step] = (
                        two[path][owner].astype(F32) + landing[path][side, step].astype(F32)
                    ).astype(BF)
                    hop(staging[path].at[side, step], path, step, side).start()

    @pl.when(me > 0)
    def _():
        for path in (0, 1):
            hop(two[path].at[me], path, n - 1 - me, 0).wait_recv()

    @pl.when(me < n - 1)
    def _():
        for path in (0, 1):
            hop(two[path].at[me], path, me, 1).wait_recv()

    for path in (0, 1):
        total = two[path][me].astype(F32)
        from_left = landing[path][0, jnp.minimum(n - 1 - me, n - 2)].astype(F32)
        from_right = landing[path][1, jnp.minimum(me, n - 2)].astype(F32)
        total = total + jnp.where(me > 0, from_left, 0.0)
        total = total + jnp.where(me < n - 1, from_right, 0.0)
        outs[path][y, x, c] = total.astype(BF)

    def spread(path, stage):
        out = outs[path]
        if stage == 2:
            spot, device = out.at[:, :, c], by_c
        elif stage == 0:
            spot, device = out.at[y, x, c], by_x if path == 0 else by_y
        elif path == 0:
            spot, device = out.at[y, :, c], by_y
        else:
            spot, device = out.at[:, x, c], by_x
        return remote(spot, spot, gsend.at[path, stage], grecv.at[path, stage], device)

    for stage in range(3):
        for path in (0, 1):
            spread(path, stage).start()
        if stage == 0:
            line.finish(y_out)
        for path in (0, 1):
            spread(path, stage).wait_recv()

    for path in (0, 1):
        for stage in range(3):
            spread(path, stage).wait_send()
        first(path).wait_send()
        second(path).wait_send()
    for p in range(len(places)):
        swap(p).wait_send()
    for step in range(n - 1):
        for side in (0, 1):
            owner = n - 1 - step if side == 0 else step
            beyond = me < owner if side == 0 else me > owner

            @pl.when(beyond)
            def _():
                for path in (0, 1):
                    hop(two[path].at[owner], path, step, side).wait_send()


def reduce_weights(
    grad_q,
    grad_kv,
    tokens,
    gain,
    weight,
    cosine,
    sine,
    mixed_low,
    grad_attn,
    grad_residual,
    grad_router,
    gain_two_row,
    y_part,
    n,
    collective_id,
):
    rows_all, width_all = weight.shape
    query_width = grad_q.shape[1]
    key_width = (width_all - query_width) // 2
    array_widths = (width_all, grad_attn.shape[1], LANES)
    rows = rows_all // n
    eighth = rows // 8
    pieces = path_pieces(query_width, key_width, grad_attn.shape[1], LANES)
    widths = [sum(p[2] for p in pieces if p[3]), sum(p[2] for p in pieces if not p[3])]
    scratch = [pltpu.VMEM((n, 2, 2, 2, eighth, w), BF) for w in array_widths]
    scratch += [pltpu.VMEM((grad_q.shape[0], width_all), BF)]
    scratch += [pltpu.VMEM((n, 2, 2, eighth, w), BF) for w in widths]
    scratch += [pltpu.VMEM((n, 2, eighth, w), BF) for w in widths]
    scratch += [pltpu.VMEM((n, eighth, w), BF) for w in widths]
    scratch += [pltpu.VMEM((2, n - 1, eighth, w), BF) for w in widths] * 2
    sems = [(4,), (4,), (2, 2), (2, 2), (2, 2, n - 1), (2, 2, n - 1), (2, 3), (2, 3)]
    y_rows = y_part.shape[0] // n
    outs = pl.pallas_call(
        functools.partial(reduce_kernel, n, pieces),
        out_shape=[jax.ShapeDtypeStruct((2, 2, 2, eighth, w), BF) for w in widths]
        + [jax.ShapeDtypeStruct((y_rows, y_part.shape[1]), F32)]
        + [jax.ShapeDtypeStruct(tokens.shape, F32)],
        in_specs=[IN_VMEM] * 13,
        out_specs=[IN_VMEM] * 4,
        scratch_shapes=scratch
        + [pltpu.SemaphoreType.DMA(s) for s in sems]
        + line_sum_scratch(n, y_rows, y_part.shape[1]),
        compiler_params=pltpu.CompilerParams(
            collective_id=collective_id, has_side_effects=True, vmem_limit_bytes=60 * 1024 * 1024
        ),
        cost_estimate=pl.CostEstimate(flops=0, bytes_accessed=100000000, transcendentals=0),
        name="reduce_weights",
    )(
        grad_q,
        grad_kv,
        tokens,
        gain,
        weight,
        cosine,
        sine,
        mixed_low,
        grad_attn,
        grad_residual,
        grad_router,
        gain_two_row,
        y_part.reshape(n, y_rows, y_part.shape[1]),
    )
    first, second = [o.reshape(rows, w) for o, w in zip(outs, widths)]
    cut = pieces[0][2]
    rest = pieces[1][2]
    qkv = jnp.concatenate([first[:, :cut], second[:, :rest]], axis=1)
    return qkv, second[:, rest:], first[:, cut:], outs[2], outs[3]


def plane_tick(step, local):
    tick = jnp.where(step <= 2, step, jnp.where(step < local, (step + 2) // 2, step - 3))
    runs = (step <= 2) | (step >= local) | (step % 2 == 0)
    return tick, runs


def expert_kernel(sizes, plane, *refs):
    blocks, rows, local, capacity = sizes
    x_ref, ct_low_ref, ct_high_ref, router_t_ref, rank_row_ref, rank_col_ref = refs[:6]
    w_gate_ref, w_up_ref, w_down_ref = refs[6:9]
    y_ref, gs_ref, out_gate_ref, out_up_ref, out_down_ref = refs[9:14]
    xs_ref, g_ref, rank_ref, gate_ref, dots_ref, y_sem = refs[14:20]
    refs = refs[20:]
    slots = local * capacity
    step = pl.program_id(0)
    tick, ticks = plane_tick(step, local)
    base = lax.axis_index("expert") * local
    if plane:
        stage_refs, pair_refs, one_refs, two_refs = refs[:3], refs[3:6], refs[6:10], refs[10:14]
        csend, crecv, psend, precv, qsend, qrecv = refs[14:20]
        gs_part = refs[20]
        line = LineSum(blocks, gs_part, *refs[21:])
        _, _, (y, x, c), (by_y, by_x, by_c) = plane_position()
        half = stage_refs[2].shape[4] // 2

        @pl.when(step == 0)
        def _():
            greet([(None, by_c), (None, by_x), (None, by_y)] + line.neighbours())

    @pl.when(step == 0)
    def _():
        logits = dot_nt(router_t_ref[...], x_ref[...])
        hot = rank_row_ref[...] < 200.0
        top = jnp.max(jnp.where(hot, logits, NEGATIVE_LARGE), axis=0, keepdims=True)
        weight = jnp.where(hot, jnp.exp(jnp.minimum(logits - top, 0.0)), 0.0)
        gates = weight / jnp.sum(weight, axis=0, keepdims=True)
        expert_id = lax.broadcasted_iota(jnp.int32, gates.shape, 0)
        slot_id = lax.broadcasted_iota(jnp.int32, (capacity, rows), 0).astype(F32)
        rank_rows = []
        for e in range(local):
            mine = expert_id == base + e
            rank_rows.append(jnp.sum(jnp.where(mine, rank_row_ref[...], 0.0), 0, keepdims=True))
            rank_ref[e : e + 1, :] = rank_rows[e]
            gate_ref[e : e + 1, :] = jnp.sum(jnp.where(mine, gates, 0.0), 0, keepdims=True)
        for b in range(blocks):
            here = slice(b * rows, (b + 1) * rows)
            pieces = []
            for e in range(local):
                taken = jnp.broadcast_to(rank_rows[e][:, here], (capacity, rows)) == slot_id
                pieces.append(jnp.where(taken, 1.0, 0.0).astype(BF))
            pick = jnp.concatenate(pieces, axis=0)
            xs_ref[b] = dot(pick, x_ref[here, :]).astype(BF)
            middle = ct_low_ref.shape[1]
            g_ref[b, :, :middle] = dot(pick, ct_low_ref[here, :]).astype(BF)
            g_ref[b, :, middle:] = dot(pick, ct_high_ref[here, :]).astype(BF)

    @pl.when(step < local)
    def _():
        here = pl.ds(pl.multiple_of(step * capacity, capacity), capacity)
        xs = jnp.concatenate([xs_ref[b, here, :] for b in range(blocks)], axis=0)
        g = jnp.concatenate([g_ref[b, here, :] for b in range(blocks)], axis=0).astype(F32)
        slot_id = lax.broadcasted_iota(jnp.int32, (capacity, rows), 0).astype(F32)
        rank_row, gate_row = rank_ref[pl.ds(step, 1), :], gate_ref[pl.ds(step, 1), :]
        gates = []
        for b in range(blocks):
            taken = rank_row[:, b * rows : (b + 1) * rows] == slot_id
            gate = jnp.where(taken, gate_row[:, b * rows : (b + 1) * rows], 0.0)
            gates.append(jnp.sum(gate, axis=1, keepdims=True))
        gate_slot = jnp.concatenate(gates, axis=0)
        w_gate, w_up, w_down = w_gate_ref[0], w_up_ref[0], w_down_ref[0]
        gate_pre = dot(xs, w_gate)
        up_pre = dot(xs, w_up)
        sigmoid = jax.nn.sigmoid(gate_pre)
        silu = gate_pre * sigmoid
        activation = (silu * up_pre).astype(BF)
        expert_out = dot(activation, w_down).astype(BF).astype(F32)
        slot_dot = jnp.sum(g * expert_out, axis=1, keepdims=True)
        grad_out = (gate_slot * g).astype(BF)
        scaled_out = (gate_slot * expert_out).astype(BF)
        grad_down = dot_tn(activation, grad_out).astype(BF)
        grad_activation = dot_nt(grad_out, w_down)
        grad_gate_pre = (
            grad_activation * up_pre * sigmoid * (1.0 + gate_pre * (1.0 - sigmoid))
        ).astype(BF)
        grad_up_pre = (grad_activation * silu).astype(BF)
        grad_gate = dot_tn(xs, grad_gate_pre).astype(BF)
        grad_up = dot_tn(xs, grad_up_pre).astype(BF)
        if plane:
            for ref, value in zip(stage_refs, (grad_gate, grad_up, grad_down)):
                ref[step % STAGES] = value.reshape(ref.shape[1:])
        else:
            out_gate_ref[0], out_up_ref[0], out_down_ref[0] = grad_gate, grad_up, grad_down
        grad_in = (dot_nt(grad_gate_pre, w_gate) + dot_nt(grad_up_pre, w_up)).astype(BF)
        lane = lax.broadcasted_iota(jnp.int32, (blocks * capacity, LANES), 1)
        high = slot_dot.astype(BF).astype(F32)
        middle = (slot_dot - high).astype(BF).astype(F32)
        low = slot_dot - high - middle
        mine = base + step
        dots = jnp.where(lane == mine, high, 0.0)
        dots = jnp.where(lane == mine + EXPERTS, middle, dots)
        dots = jnp.where(lane == mine + 2 * EXPERTS, low, dots).astype(BF)
        for b in range(blocks):
            part = slice(b * capacity, (b + 1) * capacity)
            xs_ref[b, here, :] = grad_in[part]
            g_ref[b, here, :] = scaled_out[part]
            dots_ref[b, here, :] = dots[part]

    def store_y(b):
        there = pl.ds(b * rows, rows)
        return pltpu.make_async_copy(g_ref.at[b, :rows, :], y_ref.at[there, :], y_sem.at[b])

    @pl.when(step == local - 1)
    def _():
        slot_expert = lax.broadcasted_iota(jnp.int32, (EXPERTS, slots), 1) // capacity
        spread_row = lax.broadcasted_iota(jnp.int32, (EXPERTS, slots), 0)
        spread = jnp.where(spread_row == slot_expert + base, 1.0, 0.0).astype(BF)
        slot_rank = (lax.broadcasted_iota(jnp.int32, (rows, slots), 1) % capacity).astype(F32)
        for b in range(blocks):
            there = slice(b * rows, (b + 1) * rows)
            ranks = dot(rank_col_ref[there, :], spread)
            put = jnp.where(ranks == slot_rank, 1.0, 0.0).astype(BF)
            g_ref[b, :rows, :] = dot(put, g_ref[b]).astype(BF)
            store_y(b).start()
            back = dot(put, xs_ref[b]).astype(BF), dot(put, dots_ref[b]).astype(BF)
            if plane:
                gs_part[b, :, :D], gs_part[b, :, D:] = back
            else:
                gs_ref[there, :D], gs_ref[there, D:] = back
        if plane:
            line.start()

    @pl.when(step == pl.num_programs(0) - 1)
    def _():
        for b in range(blocks):
            store_y(b).wait()

    if not plane:
        return

    gate, up, low_down, high_down = range(4)
    low_rows, high_rows = slice(0, half), slice(half, 2 * half)

    def swap(e, i):
        return remote(
            stage_refs[i].at[e % STAGES, :, :, 1 - c],
            pair_refs[i].at[e % 3],
            csend.at[e % 2, i],
            crecv.at[e % 3, i],
            by_c,
        )

    def first(e, k):
        slot = e % 3
        source = {
            gate: lambda: pair_refs[0].at[slot, :, 1 - x],
            up: lambda: pair_refs[1].at[slot, 1 - y],
            low_down: lambda: pair_refs[2].at[slot, :, 1 - x, low_rows],
            high_down: lambda: pair_refs[2].at[slot, 1 - y, :, high_rows],
        }[k]()
        device = by_x if k in (gate, low_down) else by_y
        return remote(source, one_refs[k].at[slot], psend.at[slot, k], precv.at[slot, k], device)

    def second(e, k):
        along_x = k in (gate, low_down)
        source = one_refs[k].at[e % 3, 1 - y] if along_x else one_refs[k].at[e % 3, 1 - x]
        slot = e % 2
        return remote(
            source,
            two_refs[k].at[slot],
            qsend.at[slot, k],
            qrecv.at[slot, k],
            by_y if along_x else by_x,
        )

    def add(first_value, second_value):
        return (first_value.astype(F32) + second_value.astype(F32)).astype(BF)

    @pl.when(ticks & (tick >= 3))
    def _():
        e = tick - 3
        for k in range(4):
            second(e, k).wait()
        own = [one_refs[k][e % 3, y if k in (gate, low_down) else x] for k in range(4)]
        out_gate_ref[0] = add(own[gate], two_refs[gate][e % 2])
        out_up_ref[0] = add(own[up], two_refs[up][e % 2])
        out_down_ref[0, low_rows] = add(own[low_down], two_refs[low_down][e % 2])
        out_down_ref[0, high_rows] = add(own[high_down], two_refs[high_down][e % 2])

    @pl.when(ticks & (tick >= 2) & (tick < local + 2))
    def _():
        e = tick - 2
        slot = e % 3
        for k in range(4):
            first(e, k).wait()
            for t in (0, 1):
                mine = {
                    gate: lambda: pair_refs[0][slot, t, x],
                    up: lambda: pair_refs[1][slot, y, t],
                    low_down: lambda: pair_refs[2][slot, t, x, low_rows],
                    high_down: lambda: pair_refs[2][slot, y, t, high_rows],
                }[k]()
                one_refs[k][slot, t] = add(mine, one_refs[k][slot, t])
            second(e, k).start()

    @pl.when(ticks & (tick >= 1) & (tick < local + 1))
    def _():
        e = tick - 1
        slot = e % 3
        for i in range(3):
            swap(e, i).wait()

            def pair_sum(t, carry):
                a, b = t // 2, t % 2
                pair_refs[i][slot, a, b] = add(
                    stage_refs[i][e % STAGES, a, b, c], pair_refs[i][slot, a, b]
                )
                return carry

            lax.fori_loop(0, 4, pair_sum, 0)
        for k in range(4):
            first(e, k).start()

    @pl.when(ticks & (tick < local))
    def _():
        for i in range(3):
            swap(tick, i).start()

    for hop in range(1, blocks - 1):

        @pl.when(step == local + hop)
        def _():
            line.forward(hop)

    @pl.when(step == local + blocks - 1)
    def _():
        line.finish(gs_ref)


def run_experts(
    x_all,
    ct_low,
    ct_high,
    router_t,
    rank_row,
    rank_col,
    w_gate,
    w_up,
    w_down,
    rows,
    capacity,
    plane,
    collective_id,
):
    total = x_all.shape[0]
    blocks, local = total // rows, w_gate.shape[0]
    slots = local * capacity
    sizes = (blocks, rows, local, capacity)
    whole = lambda shape: pl.BlockSpec(
        shape, lambda e: (0,) * len(shape), pipeline_mode=pl.Buffered(1)
    )
    per = lambda shape: pl.BlockSpec((1,) + shape, lambda e: (jnp.minimum(e, local - 1), 0, 0))
    shapes = ((D, FF), (D, FF), (FF, D))
    scratch = [
        pltpu.VMEM((blocks, slots, D), BF),
        pltpu.VMEM((blocks, slots, D), BF),
        pltpu.VMEM((local, total), F32),
        pltpu.VMEM((local, total), F32),
        pltpu.VMEM((blocks, slots, LANES), BF),
        pltpu.SemaphoreType.DMA((blocks,)),
    ]
    params = dict(dimension_semantics=("arbitrary",), vmem_limit_bytes=63 * 1024 * 1024)
    if plane:
        eighths = [(a // 8, b) for a, b in shapes]
        out = lambda shape: pl.BlockSpec(
            (1,) + shape, lambda e: (jnp.maximum(plane_tick(e, local)[0] - 3, 0), 0, 0)
        )
        grad_shapes, grad_specs = eighths, [out(shape) for shape in eighths]
        low = (eighths[2][0] // 2, eighths[2][1])
        passed = (eighths[0], eighths[1], low, low)
        scratch += [pltpu.VMEM((STAGES, 2, 2, 2) + shape, BF) for shape in eighths]
        scratch += [pltpu.VMEM((3, 2, 2) + shape, BF) for shape in eighths]
        scratch += [pltpu.VMEM((3, 2) + shape, BF) for shape in passed]
        scratch += [pltpu.VMEM((2,) + shape, BF) for shape in passed]
        sems = [(2, 3), (3, 3), (3, 4), (3, 4), (2, 4), (2, 4)]
        scratch += [pltpu.SemaphoreType.DMA(shape) for shape in sems]
        scratch += [pltpu.VMEM((blocks, rows, D + LANES), BF)]
        scratch += line_sum_scratch(blocks, rows, D + LANES)
        gs_shape, gs_type = (rows, D + LANES), F32
        params |= dict(collective_id=collective_id, has_side_effects=True)
    else:
        grad_shapes, grad_specs = shapes, [per(shape) for shape in shapes]
        gs_shape, gs_type = (total, D + LANES), BF
    flops = 2 * total * D * slots * 4 // blocks + 18 * blocks * slots * D * FF
    return pl.pallas_call(
        functools.partial(expert_kernel, sizes, plane),
        grid=(local + 6 if plane else local,),
        out_shape=[
            jax.ShapeDtypeStruct((total, D), BF),
            jax.ShapeDtypeStruct(gs_shape, gs_type),
        ]
        + [jax.ShapeDtypeStruct((local,) + shape, BF) for shape in grad_shapes],
        in_specs=[
            whole((total, D)),
            whole(ct_low.shape),
            whole(ct_high.shape),
            whole((EXPERTS, D)),
            whole((EXPERTS, total)),
            whole((total, EXPERTS)),
        ]
        + [per(shape) for shape in shapes],
        out_specs=[ANY, whole(gs_shape)] + grad_specs,
        scratch_shapes=scratch,
        compiler_params=pltpu.CompilerParams(**params),
        cost_estimate=pl.CostEstimate(
            flops=flops, bytes_accessed=2 * (6 * local * D * FF + 4 * total * D), transcendentals=0
        ),
        name="experts",
    )(x_all, ct_low, ct_high, router_t, rank_row, rank_col, w_gate, w_up, w_down)


def rotate(tile, cosine, sine):
    half = HEAD_DIMENSION // 2
    lane = lax.broadcasted_iota(jnp.int32, tile.shape, 1) % HEAD_DIMENSION
    other = jnp.where(lane < half, pltpu.roll(tile, LANES - half, 1), pltpu.roll(tile, half, 1))
    return tile * cosine + other * sine


def normed(tokens_ref):
    value = tokens_ref[...].astype(F32)
    inverse = lax.rsqrt(jnp.mean(value * value, axis=-1, keepdims=True) + EPSILON)
    return value * inverse, inverse


def mask_bias(bias_ref, length_ref, rows):
    base = lax.axis_index("expert") * rows
    key = lax.broadcasted_iota(jnp.int32, bias_ref.shape, 0)
    query = lax.broadcasted_iota(jnp.int32, bias_ref.shape, 1) + base
    allowed = (key <= query) & (key < length_ref[0])
    bias_ref[...] = jnp.where(allowed, 0.0, NEGATIVE_LARGE)


def head_columns(ref, head):
    start = 2 * HEAD_DIMENSION * head
    middle = start + HEAD_DIMENSION
    return jnp.concatenate([ref[:, start:middle], ref[:, middle : middle + HEAD_DIMENSION]], 0)


def put_heads(ref, head, transposed):
    rows = ref.shape[0]
    value = transposed.T
    start = 2 * HEAD_DIMENSION * head
    middle = start + HEAD_DIMENSION
    ref[:, start:middle] = value[:rows].astype(ref.dtype)
    ref[:, middle : middle + HEAD_DIMENSION] = value[rows:].astype(ref.dtype)


def attention_kernel(
    n,
    length_ref,
    tokens_ref,
    gain_ref,
    weight_ref,
    cosine_ref,
    sine_ref,
    rank_ref,
    mixed_ref,
    log_total_ref,
    kv_all_ref,
    query_out_ref,
    rank_all_ref,
    *scratch,
):
    bias_ref, query_ref, kv_ref, chunk_ref, rank_buffer, send, recv, rank_send, rank_recv = scratch
    pair, pairs = pl.program_id(0), pl.num_programs(0)
    group, me = lax.axis_index("group"), lax.axis_index("expert")
    left, right = (group, me - 1), (group, me + 1)
    rows, width = kv_ref.shape[1:]

    def hop(j, step, side):
        block = me - step if side == 0 else me + step
        source = kv_ref.at[j] if step == 0 else chunk_ref.at[j, block]
        index = (j, side, step)
        return remote(
            source,
            chunk_ref.at[j, block],
            send.at[index],
            recv.at[index],
            right if side == 0 else left,
        )

    def rank_hop(step, side):
        block = me - step if side == 0 else me + step
        source = rank_ref if step == 0 else rank_buffer.at[block]
        index = (side, step)
        return remote(
            source,
            rank_buffer.at[block],
            rank_send.at[index],
            rank_recv.at[index],
            right if side == 0 else left,
        )

    def sends(step, side):
        return (me - step >= 0) & (me < n - 1) if side == 0 else (me + step < n) & (me > 0)

    def arrives(step, side):
        return me - 1 - step >= 0 if side == 0 else me + 1 + step < n

    def launch(make, step):
        for side in (0, 1):

            @pl.when(sends(step, side))
            def _():
                make(step, side).start()

    def await_hop(make, step):
        for side in (0, 1):

            @pl.when(arrives(step, side))
            def _():
                make(step, side).wait_recv()

    def drain(make):
        for step in range(n - 1):
            for side in (0, 1):

                @pl.when(sends(step, side))
                def _():
                    make(step, side).wait_send()

    def chunk(j):
        return lambda step, side: hop(j, step, side)

    @pl.when(pair == 0)
    def _():
        unit, _ = normed(tokens_ref)
        first_norm = (unit * gain_ref[...]).astype(BF)
        cosine, sine = cosine_ref[...], sine_ref[...]
        count = kv_ref.shape[0]
        query_width = count * width
        key_width = query_width // 2
        keys = dot(first_norm, weight_ref[:, query_width : query_width + key_width])
        values = dot(first_norm, weight_ref[:, query_width + key_width :])
        for j in range(count):
            columns = slice(j * LANES, (j + 1) * LANES)
            kv_ref[j, :, :LANES] = rotate(keys[:, columns], cosine, sine).astype(BF)
            kv_ref[j, :, LANES:] = values[:, columns].astype(BF)
        rank_buffer[me] = rank_ref[...]
        greet([(me > 0, left), (me < n - 1, right)])
        launch(chunk(0), 0)
        launch(chunk(1), 0)
        queries = dot(first_norm, weight_ref[:, :query_width])
        for j in range(2 * count):
            start = (j % 2) * LANES
            tile = queries[:, j * LANES : (j + 1) * LANES]
            query_ref[j // 2, :, start : start + LANES] = rotate(tile, cosine, sine).astype(BF)
        mask_bias(bias_ref, length_ref, rows)
        await_hop(chunk(0), 0)
        launch(chunk(0), 1)

    for step in range(1, n - 1):
        await_hop(chunk(pair), step)
        if step < n - 2:
            launch(chunk(pair), step + 1)

    @pl.when(pair + 1 < pairs)
    def _():
        await_hop(chunk(pair + 1), 0)
        launch(chunk(pair + 1), 1)

    @pl.when(pair + 2 < pairs)
    def _():
        launch(chunk(pair + 2), 0)

    @pl.when(pair == 1)
    def _():
        launch(rank_hop, 0)

    for step in range(n - 1):

        @pl.when(pair == jnp.minimum(2 + step, pairs - 1))
        def _():
            await_hop(rank_hop, step)
            if step < n - 2:
                launch(rank_hop, step + 1)

    chunk_ref[pair, me] = kv_ref[pair]
    kv = chunk_ref[pair].reshape(n * rows, width)
    kv_all_ref[...] = kv
    query_out_ref[0] = query_ref[pair]
    bias = jnp.concatenate([bias_ref[...]] * 2, axis=1)
    for head in (0, 1):
        start = head * HEAD_DIMENSION
        key = kv[:, start : start + HEAD_DIMENSION]
        value = kv[:, LANES + start : LANES + start + HEAD_DIMENSION]
        query = head_columns(query_ref.at[pair], head) * jnp.asarray(HEAD_DIMENSION**-0.5, BF)
        scores = dot_nt(key, query) + bias
        top = jnp.max(scores, axis=0, keepdims=True)
        weights = jnp.exp(scores - top)
        total = jnp.sum(weights, axis=0, keepdims=True)
        put_heads(mixed_ref, head, dot_tn(value, weights.astype(BF)) / total)
        log_total_ref[0, head : head + 1, :] = top + jnp.log(total)

    @pl.when(pair == pairs - 1)
    def _():
        drain(rank_hop)
        rank_all_ref[...] = rank_buffer[...]
        for j in range(KEY_VALUE_HEADS // 2):
            drain(chunk(j))


def attention(length, tokens, gain, weight, cosine, sine, rank, n, collective_id):
    rows = tokens.shape[0]
    keys, width = n * rows, 2 * LANES
    pairs = KEY_VALUE_HEADS // 2
    return pl.pallas_call(
        functools.partial(attention_kernel, n),
        grid=(pairs,),
        out_shape=(
            jax.ShapeDtypeStruct((rows, pairs * width), BF),
            jax.ShapeDtypeStruct((pairs, 2, 2 * rows), F32),
            jax.ShapeDtypeStruct((keys, pairs * width), BF),
            jax.ShapeDtypeStruct((pairs, rows, width), BF),
            jax.ShapeDtypeStruct((n,) + rank.shape, rank.dtype),
        ),
        in_specs=[pl.BlockSpec(memory_space=pltpu.SMEM)] + [IN_VMEM] * 6,
        out_specs=(
            pl.BlockSpec((rows, width), lambda j: (0, j)),
            pl.BlockSpec((1, 2, 2 * rows), lambda j: (j, 0, 0)),
            pl.BlockSpec((keys, width), lambda j: (0, j)),
            pl.BlockSpec((1, rows, width), lambda j: (j, 0, 0)),
            IN_VMEM,
        ),
        scratch_shapes=[
            pltpu.VMEM((keys, rows), F32),
            pltpu.VMEM((pairs, rows, width), BF),
            pltpu.VMEM((pairs, rows, width), BF),
            pltpu.VMEM((pairs, n, rows, width), BF),
            pltpu.VMEM((n,) + rank.shape, rank.dtype),
            pltpu.SemaphoreType.DMA((pairs, 2, n - 1)),
            pltpu.SemaphoreType.DMA((pairs, 2, n - 1)),
            pltpu.SemaphoreType.DMA((2, n - 1)),
            pltpu.SemaphoreType.DMA((2, n - 1)),
        ],
        compiler_params=pltpu.CompilerParams(
            dimension_semantics=("arbitrary",),
            vmem_limit_bytes=56 * 1024 * 1024,
            collective_id=collective_id,
            has_side_effects=True,
        ),
        cost_estimate=pl.CostEstimate(
            flops=16 * rows * keys * D, bytes_accessed=100000000, transcendentals=0
        ),
        name="attention",
    )(length, tokens, gain, weight, cosine, sine, rank)


def attention_back_kernel(
    n,
    length_ref,
    q_ref,
    kv_ref,
    grad_ref,
    log_total_ref,
    grad_q_ref,
    grad_kv_ref,
    bias_ref,
    terms_ref,
    landing,
    staging,
    send,
    recv,
):
    step, pairs = pl.program_id(0), pl.num_programs(0) - 1

    def line(j):
        return LineSum(
            n, terms_ref.at[j], landing.at[j], staging.at[j], send.at[j], recv.at[j]
        )

    @pl.when(step == 0)
    def _():
        greet(line(0).neighbours())
        mask_bias(bias_ref, length_ref, q_ref.shape[1])

    @pl.when(step < pairs)
    def _():
        attention_back_pair(
            q_ref, kv_ref, grad_ref, log_total_ref, grad_q_ref, terms_ref.at[step], bias_ref
        )
        line(step).start()

    @pl.when(step > 0)
    def _():
        for hop in range(1, n - 1):
            line(step - 1).forward(hop)
        line(step - 1).finish(grad_kv_ref)


def attention_back_pair(q_ref, kv_ref, grad_ref, log_total_ref, grad_q_ref, grad_kv_ref, bias_ref):
    scale = HEAD_DIMENSION**-0.5
    blocks, rows, _ = grad_kv_ref.shape
    q_ref = q_ref.at[0]
    bias = jnp.concatenate([bias_ref[...]] * 2, axis=1)
    for head in (0, 1):
        columns = slice(head * HEAD_DIMENSION, (head + 1) * HEAD_DIMENSION)
        key, value = kv_ref[:, :LANES][:, columns], kv_ref[:, LANES:][:, columns]
        query = head_columns(q_ref, head) * jnp.asarray(scale, BF)
        grad = head_columns(grad_ref, head)
        scores = dot_nt(key, query) + bias
        probs = jnp.exp(scores - log_total_ref[0, head : head + 1, :])
        grad_probs = dot_nt(value, grad)
        delta = jnp.sum(probs * grad_probs, axis=0, keepdims=True)
        grad_scores = (probs * (grad_probs - delta)).astype(BF)
        grad_key = dot(grad_scores, query).astype(BF).reshape(blocks, rows, HEAD_DIMENSION)
        grad_kv_ref[:, :, columns] = grad_key
        grad_value = dot(probs.astype(BF), grad).astype(BF).reshape(blocks, rows, HEAD_DIMENSION)
        start = LANES + head * HEAD_DIMENSION
        grad_kv_ref[:, :, start : start + HEAD_DIMENSION] = grad_value
        put_heads(grad_q_ref, head, dot_tn(key, grad_scores) * scale)


def attention_back(length, query, kv_all, grad_mixed, log_total, n, collective_id):
    rows, keys = query.shape[1], kv_all.shape[0]
    pairs, width = KEY_VALUE_HEADS // 2, 2 * LANES
    now = lambda j: jnp.minimum(j, pairs - 1)
    row_spec = pl.BlockSpec((rows, width), lambda j: (0, now(j)))
    return pl.pallas_call(
        functools.partial(attention_back_kernel, n),
        grid=(pairs + 1,),
        out_shape=(
            jax.ShapeDtypeStruct((rows, pairs * width), F32),
            jax.ShapeDtypeStruct((rows, pairs * width), BF),
        ),
        in_specs=[
            pl.BlockSpec(memory_space=pltpu.SMEM),
            pl.BlockSpec((1, rows, width), lambda j: (now(j), 0, 0)),
            pl.BlockSpec((keys, width), lambda j: (0, now(j))),
            row_spec,
            pl.BlockSpec((1, 2, 2 * rows), lambda j: (now(j), 0, 0)),
        ],
        out_specs=(
            row_spec,
            pl.BlockSpec((rows, width), lambda j: (0, jnp.maximum(j - 1, 0))),
        ),
        scratch_shapes=[
            pltpu.VMEM((keys, rows), F32),
            pltpu.VMEM((pairs, n, rows, width), BF),
            pltpu.VMEM((pairs, 2, n - 1, rows, width), BF),
            pltpu.VMEM((pairs, 2, n - 2, rows, width), BF),
            pltpu.SemaphoreType.DMA((pairs, 2, n - 1)),
            pltpu.SemaphoreType.DMA((pairs, 2, n - 1)),
        ],
        compiler_params=pltpu.CompilerParams(
            dimension_semantics=("arbitrary",),
            vmem_limit_bytes=60 * 1024 * 1024,
            collective_id=collective_id,
            has_side_effects=True,
        ),
        cost_estimate=pl.CostEstimate(
            flops=40 * rows * keys * D, bytes_accessed=100000000, transcendentals=0
        ),
        name="attention_back",
    )(length, query, kv_all, grad_mixed, log_total)


def widen_kernel(value_ref, out_ref):
    out_ref[...] = value_ref[...].astype(F32)


def widen(value):
    block = (1,) + value.shape[1:]
    spec = pl.BlockSpec(block, lambda e: (e, 0, 0))
    return pl.pallas_call(
        widen_kernel,
        grid=(value.shape[0],),
        out_shape=jax.ShapeDtypeStruct(value.shape, F32),
        in_specs=[spec],
        out_specs=spec,
        compiler_params=pltpu.CompilerParams(dimension_semantics=("arbitrary",)),
        cost_estimate=pl.CostEstimate(flops=0, bytes_accessed=6 * value.size, transcendentals=0),
        name="widen",
    )(value)


def unpair_columns(value):
    rows = value.shape[0]
    value = value.reshape(rows, -1, 2, LANES)
    return value[:, :, 0].reshape(rows, -1), value[:, :, 1].reshape(rows, -1)


def gather_rows(value):
    return lax.all_gather(value, "expert", axis=0, tiled=True)


def scatter_rows(value):
    return lax.psum_scatter(value, "expert", scatter_dimension=0, tiled=True)


def per_device(
    tokens,
    lengths,
    routes,
    norm_gain1,
    w_query,
    key_projection,
    value_projection,
    w_out,
    norm_gain2,
    w_router,
    w_gate,
    w_up,
    w_down,
    cotangent,
):
    rows = tokens.shape[0]
    n, groups = lax.axis_size("expert"), lax.axis_size("group")
    plane = groups == 8 and w_gate.shape[0] == 8
    my_index = lax.axis_index("expert")
    capacity = 3 * rows * TOP // (2 * EXPERTS)
    query_width, key_width = w_query.shape[1], key_projection.shape[1]
    length = lengths[0]
    positions = my_index * rows + jnp.arange(rows, dtype=jnp.int32)
    valid_rows = (positions < length)[:, None]
    grad_output = jnp.where(valid_rows, cotangent, jnp.zeros_like(cotangent))

    small = jnp.concatenate(
        [w_router, norm_gain1[:, None], norm_gain2[:, None]]
        + [jnp.zeros((w_router.shape[0], LANES - EXPERTS - 2), BF)],
        axis=1,
    )
    middle = D // 2
    qkv_weight, out_weight, small, ct_low = gather_weights(
        w_query, key_projection, value_projection, w_out, small, grad_output[:, :middle], n, 1
    )
    qkv_weight, ct_high = lax.optimization_barrier((qkv_weight, grad_output[:, middle:]))
    ct_high = gather_rows(ct_high)
    router_weight = small[:, :EXPERTS]
    gain_one = small[:, EXPERTS].astype(F32)
    gain_two = small[:, EXPERTS + 1].astype(F32)

    expert_ids = jnp.arange(EXPERTS, dtype=jnp.int32)
    hot = jnp.any(routes[:, :, None] == expert_ids, axis=1)
    row_id = jnp.arange(rows, dtype=jnp.int32)
    earlier = (row_id[:, None] < row_id[None, :]).astype(BF)
    rank = jnp.where(hot.T, dot(hot.T.astype(BF), earlier), 255.0).astype(BF)

    cosine_lookup, sine_lookup = [table[:, 0] for table in rotary_tables(positions, HEAD_DIMENSION)]
    cosine = jnp.tile(cosine_lookup, (1, 4))
    sine = jnp.tile(jnp.concatenate([-sine_lookup, sine_lookup], axis=1), (1, 2))
    token_f32 = tokens.astype(F32)
    gain_one_row = gain_one[None, :]
    mixed_low, log_total, kv_all, query_pairs, rank_all = attention(
        lengths, tokens, gain_one_row, qkv_weight, cosine, sine, rank, n, 2
    )
    rank_row = jnp.transpose(rank_all, (1, 0, 2)).reshape(EXPERTS, n * rows).astype(F32)
    rank_col = jnp.transpose(rank_all, (0, 2, 1)).reshape(n * rows, EXPERTS)
    residual = token_f32 + dot(mixed_low, out_weight)
    inverse_two = lax.rsqrt(jnp.mean(residual * residual, axis=-1, keepdims=True) + EPSILON)
    unit_two = residual * inverse_two
    second_norm = (unit_two * gain_two).astype(BF)
    (x_all,) = line_gather([second_norm], n, 3, "gather_rows")

    y_part, gs, grad_gate, grad_up, grad_down = run_experts(
        x_all,
        ct_low,
        ct_high,
        router_weight.T,
        rank_row,
        rank_col,
        w_gate,
        w_up,
        w_down,
        rows,
        capacity,
        plane,
        7,
    )
    if not plane:
        gs = line_scatter(gs, n, F32, 4, "scatter_grads")

    logits = dot(second_norm, router_weight)
    chosen = jnp.where(hot, logits, NEGATIVE_LARGE)
    gate_weights = jnp.where(hot, jnp.exp(chosen - jnp.max(chosen, axis=-1, keepdims=True)), 0.0)
    gate_weights = gate_weights / jnp.sum(gate_weights, axis=-1, keepdims=True)
    grad_gates = gs[:, D : D + EXPERTS] + gs[:, D + EXPERTS : D + 2 * EXPERTS]
    grad_gates = grad_gates + gs[:, D + 2 * EXPERTS : D + 3 * EXPERTS]
    grad_logits = (
        gate_weights * (grad_gates - jnp.sum(gate_weights * grad_gates, axis=-1, keepdims=True))
    ).astype(BF)
    grad_second = gs[:, :D] + dot_nt(grad_logits, router_weight)
    grad_router = dot_tn(second_norm, grad_logits)
    scaled_two = grad_second * gain_two
    grad_gain2 = jnp.sum(grad_second * unit_two, axis=0)
    grad_residual = grad_output.astype(F32) + inverse_two * (
        scaled_two - unit_two * jnp.mean(scaled_two * unit_two, axis=-1, keepdims=True)
    )
    grad_attn = grad_residual.astype(BF)
    mixed_gradient = dot_nt(grad_attn, out_weight).astype(BF)
    grad_query_acc, kv_gradient = attention_back(
        lengths, query_pairs, kv_all, mixed_gradient, log_total, n, 5
    )
    pad = jnp.zeros((D, LANES - EXPERTS), F32)
    if plane:
        *shares, expert_sum, grad_tokens = reduce_weights(
            grad_query_acc,
            kv_gradient,
            tokens,
            gain_one_row,
            qkv_weight,
            cosine,
            sine,
            mixed_low,
            grad_attn,
            grad_residual,
            jnp.concatenate([grad_router, pad], axis=1),
            grad_gain2[None, :],
            y_part,
            n,
            6,
        )
    else:
        inverse_one = lax.rsqrt(jnp.mean(token_f32 * token_f32, axis=-1, keepdims=True) + EPSILON)
        unit_one = token_f32 * inverse_one
        first_norm = (unit_one * gain_one).astype(BF)
        own_key_gradient, own_value_gradient = unpair_columns(kv_gradient)
        back = lambda value: apply_rotation(
            value.astype(F32).reshape(rows, -1, HEAD_DIMENSION),
            cosine_lookup[:, None],
            -sine_lookup[:, None],
        )
        grad_query_pre = back(grad_query_acc).reshape(rows, query_width).astype(BF)
        grad_key_pre = back(own_key_gradient).reshape(rows, key_width).astype(BF)
        grad_qkv_pre = jnp.concatenate([grad_query_pre, grad_key_pre, own_value_gradient], axis=1)
        grad_first = dot_nt(grad_qkv_pre, qkv_weight)
        scaled_one = grad_first * gain_one
        grad_gain1 = jnp.sum(grad_first * unit_one, axis=0)
        grad_tokens = grad_residual + inverse_one * (
            scaled_one - unit_one * jnp.mean(scaled_one * unit_one, axis=-1, keepdims=True)
        )
        grad_small = jnp.concatenate(
            [grad_router, grad_gain1[:, None], grad_gain2[:, None], pad[:, 2:]], axis=1
        )
        shares = (dot_tn(first_norm, grad_qkv_pre), dot_tn(mixed_low, grad_attn), grad_small)
        shares = [lax.psum(scatter_rows(share.astype(BF)), "group") for share in shares]
        expert_sum = line_scatter(y_part, n, F32, 8, "scatter_outputs")
    mixed = (residual + expert_sum).astype(BF)
    share_qkv, share_out, share_small = [share.astype(F32) for share in shares]

    def sum_over_groups(value):
        if not plane:
            value = lax.psum_scatter(value, "group", scatter_dimension=1, tiled=True)
        return widen(lax.all_gather(value, "group", axis=1, tiled=True))

    return (
        mixed,
        grad_tokens,
        share_small[:, EXPERTS],
        share_qkv[:, :query_width],
        share_qkv[:, query_width : query_width + key_width],
        share_qkv[:, query_width + key_width :],
        share_out,
        share_small[:, EXPERTS + 1],
        share_small[:, :EXPERTS],
        sum_over_groups(grad_gate),
        sum_over_groups(grad_up),
        sum_over_groups(grad_down),
    )


def solution(mesh):
    rows = P(("group", "expert"), None)
    vector, matrix, stack = P("expert"), P("expert", None), P("expert", None, None)
    return jax.shard_map(
        per_device,
        mesh=mesh,
        in_specs=(
            rows,
            P("group"),
            rows,
            vector,
            matrix,
            matrix,
            matrix,
            matrix,
            vector,
            matrix,
            stack,
            stack,
            stack,
            rows,
        ),
        out_specs=(
            rows,
            rows,
            vector,
            matrix,
            matrix,
            matrix,
            matrix,
            vector,
            matrix,
            stack,
            stack,
            stack,
        ),
        check_vma=False,
    )
```

```python
import functools

import jax
import jax.numpy as jnp
from jax import lax
from jax.experimental import pallas as pl
from jax.experimental.pallas import tpu as pltpu
from jax.sharding import PartitionSpec as P

D = 1024
QUERY_HEADS = 16
KEY_VALUE_HEADS = 8
HEAD_DIMENSION = 64
EXPERTS = 32
TOP = 8
FF = 512
LANES = 128
STAGES = 4

EPSILON = 1e-05
NEGATIVE_LARGE = -1e30
BF = jnp.bfloat16
F32 = jnp.float32


def rotary_tables(positions, head_size):
    half_width = head_size // 2
    frequency = 10000.0 ** (-2.0 * jnp.arange(half_width).astype(F32) / head_size)
    angles = positions.astype(F32)[:, None] * frequency[None, :]
    return (jnp.cos(angles)[:, None, :], jnp.sin(angles)[:, None, :])


def apply_rotation(tensor_in, cosine_lookup, sine_lookup):
    half_width = tensor_in.shape[-1] // 2
    first_half = tensor_in[..., :half_width]
    second_half = tensor_in[..., half_width:]
    return jnp.concatenate(
        [
            first_half * cosine_lookup - second_half * sine_lookup,
            second_half * cosine_lookup + first_half * sine_lookup,
        ],
        axis=-1,
    )


def dot(a, b):
    return jnp.dot(a, b, preferred_element_type=F32)


def dot_nt(a, b):
    return lax.dot_general(a, b, (((1,), (1,)), ((), ())), preferred_element_type=F32)


def dot_tn(a, b):
    return lax.dot_general(a, b, (((0,), (0,)), ((), ())), preferred_element_type=F32)


MESH = pl.DeviceIdType.MESH
ANY = pl.BlockSpec(memory_space=pl.ANY)
IN_VMEM = pl.BlockSpec(memory_space=pltpu.VMEM)


def remote(source, target, send, receive, device):
    return pltpu.make_async_remote_copy(
        src_ref=source,
        dst_ref=target,
        send_sem=send,
        recv_sem=receive,
        device_id=device,
        device_id_type=MESH,
    )


def greet(devices):
    barrier = pltpu.get_barrier_semaphore()
    count = 0
    for condition, device in devices:
        if condition is None:
            pl.semaphore_signal(barrier, inc=1, device_id=device, device_id_type=MESH)
            count = count + 1
        else:

            @pl.when(condition)
            def _():
                pl.semaphore_signal(barrier, inc=1, device_id=device, device_id_type=MESH)

            count = count + jnp.where(condition, 1, 0)
    pl.semaphore_wait(barrier, count)


def line_gather_kernel(n, count, *refs):
    ins, outs = refs[:count], refs[count : 2 * count]
    local, send, receive = refs[2 * count :]
    group, me = lax.axis_index("group"), lax.axis_index("expert")
    left, right = (group, me - 1), (group, me + 1)
    own = [
        pltpu.make_async_copy(ins[i], outs[i].at[me], local.at[i]) for i in range(count)
    ]
    for copy in own:
        copy.start()
    greet([(me > 0, left), (me < n - 1, right)])

    def hop(i, step, side):
        block = me - step if side == 0 else me + step
        source = ins[i] if step == 0 else outs[i].at[block]
        index = (side, step, i)
        return remote(
            source, outs[i].at[block], send.at[index], receive.at[index], right if side == 0 else left
        )

    def arrival(i, step, side):
        block = me - 1 - step if side == 0 else me + 1 + step
        index = (side, step, i)
        return remote(
            outs[i].at[block], outs[i].at[block], send.at[index], receive.at[index], left if side == 0 else right
        )

    def sends(step, side):
        return (me - step >= 0) & (me < n - 1) if side == 0 else (me + step < n) & (me > 0)

    def arrives(step, side):
        return me - 1 - step >= 0 if side == 0 else me + 1 + step < n

    for step in range(n - 1):
        for side in (0, 1):

            @pl.when(sends(step, side))
            def _():
                for i in range(count):
                    hop(i, step, side).start()

        for side in (0, 1):

            @pl.when(arrives(step, side))
            def _():
                for i in range(count):
                    arrival(i, step, side).wait_recv()

    for step in range(n - 1):
        for side in (0, 1):

            @pl.when(sends(step, side))
            def _():
                for i in range(count):
                    hop(i, step, side).wait_send()

    for copy in own:
        copy.wait()


def line_gather(values, n, collective_id, name):
    count = len(values)
    outs = pl.pallas_call(
        functools.partial(line_gather_kernel, n, count),
        out_shape=[jax.ShapeDtypeStruct((n,) + v.shape, v.dtype) for v in values],
        in_specs=[IN_VMEM] * count,
        out_specs=[ANY] * count,
        scratch_shapes=[
            pltpu.SemaphoreType.DMA((count,)),
            pltpu.SemaphoreType.DMA((2, n - 1, count)),
            pltpu.SemaphoreType.DMA((2, n - 1, count)),
        ],
        compiler_params=pltpu.CompilerParams(collective_id=collective_id, has_side_effects=True),
        cost_estimate=pl.CostEstimate(flops=0, bytes_accessed=100000000, transcendentals=0),
        name=name,
    )(*values)
    return [o.reshape((n * v.shape[0],) + v.shape[1:]) for o, v in zip(outs, values)]


class LineSum:
    def __init__(self, n, part, landing, staging, send, receive):
        self.n, self.part, self.landing, self.staging = n, part, landing, staging
        self.send, self.receive = send, receive
        self.group, self.me = lax.axis_index("group"), lax.axis_index("expert")
        self.rows = part.shape[1]
        self.tile = min(32, self.rows)

    def neighbours(self):
        left, right = (self.group, self.me - 1), (self.group, self.me + 1)
        return [(self.me > 0, left), (self.me < self.n - 1, right)]

    def copy(self, source, step, side):
        index = (side, step)
        device = (self.group, self.me + 1 if side == 0 else self.me - 1)
        return remote(
            source, self.landing.at[index], self.send.at[index], self.receive.at[index], device
        )

    def places(self):
        me, n = self.me, self.n
        for step in range(n - 1):
            for side in (0, 1):
                owner = n - 1 - step if side == 0 else step
                beyond = me < owner if side == 0 else me > owner
                edge = me == 0 if side == 0 else me == n - 1
                yield step, side, owner, beyond, edge

    def start(self):
        for step, side, owner, beyond, edge in self.places():

            @pl.when(beyond & edge)
            def _():
                self.copy(self.part.at[owner], step, side).start()

    def spans(self, body):
        def tile_body(t, carry):
            body(pl.ds(pl.multiple_of(t * self.tile, self.tile), self.tile))
            return carry

        lax.fori_loop(0, self.rows // self.tile, tile_body, 0)

    def forward(self, hop):
        me, n = self.me, self.n
        for side in (0, 1):
            step = hop - me if side == 0 else hop - (n - 1 - me)
            owner = n - 1 - step if side == 0 else step
            inner = me > 0 if side == 0 else me < n - 1
            beyond = me < owner if side == 0 else me > owner

            @pl.when(inner & (step >= 0) & beyond)
            def _():
                self.copy(self.part.at[owner], step, side).wait_recv()

                def add(span):
                    total = self.part[owner, span, :].astype(F32)
                    total = total + self.landing[side, step, span, :].astype(F32)
                    self.staging[side, step, span, :] = total.astype(BF)

                self.spans(add)
                self.copy(self.staging.at[side, step], step, side).start()

    def finish(self, out_ref):
        me, n = self.me, self.n

        @pl.when(me > 0)
        def _():
            self.copy(self.part.at[me], n - 1 - me, 0).wait_recv()

        @pl.when(me < n - 1)
        def _():
            self.copy(self.part.at[me], me, 1).wait_recv()

        def total(span):
            value = self.part[me, span, :].astype(F32)
            from_left = self.landing[0, jnp.minimum(n - 1 - me, n - 2), span, :].astype(F32)
            from_right = self.landing[1, jnp.minimum(me, n - 2), span, :].astype(F32)
            value = value + jnp.where(me > 0, from_left, 0.0)
            value = value + jnp.where(me < n - 1, from_right, 0.0)
            out_ref[span, :] = value.astype(out_ref.dtype)

        self.spans(total)
        for step, side, owner, beyond, edge in self.places():

            @pl.when(beyond)
            def _():
                self.copy(self.part.at[owner], step, side).wait_send()


def line_sum_scratch(n, rows, width):
    return [
        pltpu.VMEM((2, n - 1, rows, width), BF),
        pltpu.VMEM((2, n - 2, rows, width), BF),
        pltpu.SemaphoreType.DMA((2, n - 1)),
        pltpu.SemaphoreType.DMA((2, n - 1)),
    ]


def line_scatter_kernel(n, part_ref, out_ref, *scratch):
    line = LineSum(n, part_ref, *scratch)
    greet(line.neighbours())
    line.start()
    for hop in range(1, n - 1):
        line.forward(hop)
    line.finish(out_ref)


def line_scatter(value, n, dtype, collective_id, name):
    total, width = value.shape
    rows = total // n
    return pl.pallas_call(
        functools.partial(line_scatter_kernel, n),
        out_shape=jax.ShapeDtypeStruct((rows, width), dtype),
        in_specs=[IN_VMEM],
        out_specs=IN_VMEM,
        scratch_shapes=line_sum_scratch(n, rows, width),
        compiler_params=pltpu.CompilerParams(collective_id=collective_id, has_side_effects=True),
        cost_estimate=pl.CostEstimate(flops=0, bytes_accessed=100000000, transcendentals=0),
        name=name,
    )(value.reshape(n, rows, width))


def plane_position():
    group, me = lax.axis_index("group"), lax.axis_index("expert")
    c, x, y = group % 2, (group // 2) % 2, (group // 4) % 2
    by_c, by_x, by_y = (group + 1 - 2 * c, me), (group + 2 - 4 * x, me), (group + 4 - 8 * y, me)
    return group, me, (y, x, c), (by_y, by_x, by_c)


def weights_kernel(n, pieces, widths, *refs):
    wq, wk, wv, wo, small, extra = refs[:6]
    outs, extra_out, owns = refs[6:9], refs[9], refs[10:13]
    load, store, zsend, zrecv, psend, precv, csend, crecv, xsend, xrecv = refs[13:]
    group, me, (y, x, c), (by_y, by_x, by_c) = plane_position()
    left, right = (group, me - 1), (group, me + 1)
    eighth = owns[0].shape[0]
    span = pl.ds(pl.multiple_of((y * 4 + x * 2 + c) * eighth, eighth), eighth)
    query_width, key_width = wq.shape[1], wk.shape[1]
    targets = (
        owns[0].at[:, :query_width],
        owns[0].at[:, query_width : query_width + key_width],
        owns[0].at[:, query_width + key_width :],
        owns[1],
        owns[2],
    )
    loads = [
        pltpu.make_async_copy(source.at[span, :], target, load.at[i])
        for i, (source, target) in enumerate(zip((wq, wk, wv, wo, small), targets))
    ]
    for copy in loads:
        copy.start()
    for copy in loads:
        copy.wait()
    stores = [
        pltpu.make_async_copy(owns[i], outs[i].at[me, y, x, c], store.at[i]) for i in range(3)
    ]
    stores.append(pltpu.make_async_copy(extra, extra_out.at[me], store.at[3]))
    for copy in stores:
        copy.start()
    greet(
        [(me > 0, left), (me < n - 1, right), (None, by_c), (None, by_x), (None, by_y)]
    )

    def hop(i, step, side):
        block = me - step if side == 0 else me + step
        source = owns[i] if step == 0 else outs[i].at[block, y, x, c]
        index = (side, step, i)
        return remote(
            source,
            outs[i].at[block, y, x, c],
            zsend.at[index],
            zrecv.at[index],
            right if side == 0 else left,
        )

    def sends(step, side):
        return (me - step >= 0) & (me < n - 1) if side == 0 else (me + step < n) & (me > 0)

    def extra_hop(step, side):
        block = me - step if side == 0 else me + step
        source = extra if step == 0 else extra_out.at[block]
        return remote(
            source,
            extra_out.at[block],
            xsend.at[side, step],
            xrecv.at[side, step],
            right if side == 0 else left,
        )

    def first(slot, block, p):
        i, start, width, along_x = pieces[p]
        spot = outs[i].at[block, y, x, c, :, start : start + width]
        source = owns[i].at[:, start : start + width] if slot == 0 else spot
        index = (0, slot, p)
        return remote(source, spot, psend.at[index], precv.at[index], by_x if along_x else by_y)

    def second(slot, block, p):
        i, start, width, along_x = pieces[p]
        columns = slice(start, start + width)
        if along_x:
            spot = outs[i].at[block, y, :, c, :, columns]
        else:
            spot = outs[i].at[block, :, x, c, :, columns]
        index = (1, slot, p)
        return remote(spot, spot, psend.at[index], precv.at[index], by_y if along_x else by_x)

    def third(slot, block, i):
        spot = outs[i].at[block, :, :, c]
        index = (slot, i)
        return remote(spot, spot, csend.at[index], crecv.at[index], by_c)

    def held(step):
        if step == 0:
            return [(0, me, me >= 0)]
        return [(step, me - step, me - step >= 0), (n - 1 + step, me + step, me + step < n)]

    count = len(pieces)
    for step in range(n + 2):
        if step < n:
            for slot, block, there in held(step):

                @pl.when(there)
                def _():
                    if step > 0:
                        side = 0 if slot < n else 1
                        for i in range(3):
                            hop(i, step - 1, side).wait_recv()
                    for p in range(count):
                        first(slot, block, p).start()

            if step < n - 1:
                for side in (0, 1):

                    @pl.when(sends(step, side))
                    def _():
                        for i in range(3):
                            hop(i, step, side).start()

        if 1 <= step < n + 1:
            if step == 1:
                for copy in stores:
                    copy.wait()
            for slot, block, there in held(step - 1):

                @pl.when(there)
                def _():
                    for p in range(count):
                        first(slot, block, p).wait_recv()
                    for p in range(count):
                        second(slot, block, p).start()

        if step >= 2:
            for slot, block, there in held(step - 2):

                @pl.when(there)
                def _():
                    for p in range(count):
                        second(slot, block, p).wait_recv()
                    for i in range(3):
                        third(slot, block, i).start()

            for side in (0, 1):
                if step > 2:

                    @pl.when(me - step + 2 >= 0 if side == 0 else me + step - 2 < n)
                    def _():
                        extra_hop(step - 3, side).wait_recv()

                if step < n + 1:

                    @pl.when(sends(step - 2, side))
                    def _():
                        extra_hop(step - 2, side).start()

    for step in range(n):
        for slot, block, there in held(step):

            @pl.when(there)
            def _():
                for p in range(count):
                    first(slot, block, p).wait_send()
                    second(slot, block, p).wait_send()
                for i in range(3):
                    third(slot, block, i).wait()

        if step < n - 1:
            for side in (0, 1):

                @pl.when(sends(step, side))
                def _():
                    for i in range(3):
                        hop(i, step, side).wait_send()
                    extra_hop(step, side).wait_send()


def path_pieces(query_width, key_width, out_width, small_width):
    half = (query_width + 2 * key_width + out_width) // 2
    return (
        (0, 0, half, True),
        (0, half, query_width + 2 * key_width - half, False),
        (1, 0, out_width, False),
        (2, 0, small_width, True),
    )


def gather_weights(wq, wk, wv, wo, small, extra, n, collective_id):
    rows = wq.shape[0]
    eighth = rows // 8
    widths = (wq.shape[1] + wk.shape[1] + wv.shape[1], wo.shape[1], small.shape[1])
    pieces = path_pieces(wq.shape[1], wk.shape[1], wo.shape[1], small.shape[1])
    outs = pl.pallas_call(
        functools.partial(weights_kernel, n, pieces, widths),
        out_shape=[jax.ShapeDtypeStruct((n, 2, 2, 2, eighth, w), BF) for w in widths]
        + [jax.ShapeDtypeStruct((n,) + extra.shape, BF)],
        in_specs=[ANY] * 5 + [IN_VMEM],
        out_specs=[ANY] * 4,
        scratch_shapes=[pltpu.VMEM((eighth, w), BF) for w in widths]
        + [
            pltpu.SemaphoreType.DMA((5,)),
            pltpu.SemaphoreType.DMA((4,)),
            pltpu.SemaphoreType.DMA((2, n - 1, 3)),
            pltpu.SemaphoreType.DMA((2, n - 1, 3)),
            pltpu.SemaphoreType.DMA((2, 2 * n - 1, 4)),
            pltpu.SemaphoreType.DMA((2, 2 * n - 1, 4)),
            pltpu.SemaphoreType.DMA((2 * n - 1, 3)),
            pltpu.SemaphoreType.DMA((2 * n - 1, 3)),
            pltpu.SemaphoreType.DMA((2, n - 1)),
            pltpu.SemaphoreType.DMA((2, n - 1)),
        ],
        compiler_params=pltpu.CompilerParams(collective_id=collective_id, has_side_effects=True),
        cost_estimate=pl.CostEstimate(flops=0, bytes_accessed=100000000, transcendentals=0),
        name="gather_weights",
    )(wq, wk, wv, wo, small, extra)
    weights = [o.reshape(n * rows, w) for o, w in zip(outs, widths)]
    return weights + [outs[3].reshape(-1, extra.shape[1])]


def reduce_kernel(n, pieces, *refs):
    (
        grad_q_ref,
        grad_kv_ref,
        tokens_ref,
        gain_ref,
        weight_ref,
        cosine_ref,
        sine_ref,
        mixed_ref,
        grad_attn_ref,
        grad_residual_ref,
        router_ref,
        gain_two_ref,
        y_part,
    ) = refs[:13]
    outs, y_out, grad_tokens_ref = refs[13:15], refs[15], refs[16]
    ins, grad_pre_ref = refs[17:20], refs[20]
    refs = refs[21:]
    pair, one, two, landing, staging = refs[:2], refs[2:4], refs[4:6], refs[6:8], refs[8:10]
    csend, crecv, psend, precv, zsend, zrecv, gsend, grecv = refs[10:18]
    line = LineSum(n, y_part, *refs[18:])
    group, me, (y, x, c), (by_y, by_x, by_c) = plane_position()
    left, right = (group, me - 1), (group, me + 1)
    eighth = pair[0].shape[3]
    greet(
        [(me > 0, left), (me < n - 1, right), (None, by_c), (None, by_x), (None, by_y)]
    )

    places, ends = [], [0, 0]
    for array, start, width, along_x in pieces:
        path = 0 if along_x else 1
        places.append((array, start, width, path, ends[path]))
        ends[path] += width

    def swap(p):
        array, start, width, path, at = places[p]
        return remote(
            ins[array].at[:, :, :, 1 - c, :, start : start + width],
            pair[path].at[:, :, :, :, at : at + width],
            csend.at[p],
            crecv.at[p],
            by_c,
        )

    line.start()
    D_rows = weight_ref.shape[0]
    query_width = grad_q_ref.shape[1]
    key_width = (weight_ref.shape[1] - query_width) // 2

    def put(array, columns, value):
        ins[array][:, :, :, :, :, columns] = value.astype(BF).reshape(
            ins[array].shape[:5] + (value.shape[1],)
        )

    tile = 4 * LANES
    for start in range(0, grad_attn_ref.shape[1], tile):
        columns = slice(start, start + tile)
        put(1, columns, dot_tn(mixed_ref[...], grad_attn_ref[:, columns]))
    swap(2).start()
    unit, inverse = normed(tokens_ref)
    gain = gain_ref[...]
    first_norm = (unit * gain).astype(BF)
    cosine, sine = cosine_ref[...], -sine_ref[...]
    for j in range(query_width // LANES):
        columns = slice(j * LANES, (j + 1) * LANES)
        grad_pre_ref[:, columns] = rotate(grad_q_ref[:, columns], cosine, sine).astype(BF)
    for j in range(key_width // LANES):
        start = 2 * j * LANES
        key = grad_kv_ref[:, start : start + LANES].astype(F32)
        at = query_width + j * LANES
        grad_pre_ref[:, at : at + LANES] = rotate(key, cosine, sine).astype(BF)
        at = at + key_width
        grad_pre_ref[:, at : at + LANES] = grad_kv_ref[:, start + LANES : start + 2 * LANES]
    for start in range(0, weight_ref.shape[1], tile):
        columns = slice(start, start + tile)
        put(0, columns, dot_tn(first_norm, grad_pre_ref[:, columns]))
    swap(0).start()
    swap(1).start()
    grad_first = dot_nt(grad_pre_ref[...], weight_ref[...])
    gain_one_row = jnp.sum(grad_first * unit, axis=0, keepdims=True)
    lane = lax.broadcasted_iota(jnp.int32, (LANES, D_rows), 0)
    gains = jnp.where(lane == EXPERTS, gain_one_row, 0.0)
    gains = jnp.where(lane == EXPERTS + 1, gain_two_ref[...], gains)
    put(2, slice(0, LANES), router_ref[...] + gains.T)
    swap(3).start()
    scaled = grad_first * gain
    mean = jnp.mean(scaled * unit, axis=-1, keepdims=True)
    grad_tokens_ref[...] = grad_residual_ref[...] + inverse * (scaled - unit * mean)
    for p in range(len(places)):
        swap(p).wait_recv()
        array, start, width, path, at = places[p]

        def pair_sum(t, carry):
            z, a, b = t // 4, (t // 2) % 2, t % 2
            mine = ins[array][z, a, b, c, :, start : start + width].astype(F32)
            theirs = pair[path][z, a, b, :, at : at + width].astype(F32)
            pair[path][z, a, b, :, at : at + width] = (mine + theirs).astype(BF)
            return carry

        lax.fori_loop(0, 4 * n, pair_sum, 0)

    def first(path):
        source = pair[0].at[:, :, 1 - x] if path == 0 else pair[1].at[:, 1 - y]
        return remote(
            source, one[path], psend.at[0, path], precv.at[0, path], by_x if path == 0 else by_y
        )

    def second(path):
        source = one[path].at[:, 1 - y] if path == 0 else one[path].at[:, 1 - x]
        return remote(
            source, two[path], psend.at[1, path], precv.at[1, path], by_y if path == 0 else by_x
        )

    for path in (0, 1):
        first(path).start()
    line.forward(1)
    for path in (0, 1):
        first(path).wait_recv()

        def first_sum(t, carry):
            z, a = t // 2, t % 2
            mine = pair[0][z, a, x] if path == 0 else pair[1][z, y, a]
            one[path][z, a] = (mine.astype(F32) + one[path][z, a].astype(F32)).astype(BF)
            return carry

        lax.fori_loop(0, 2 * n, first_sum, 0)
        second(path).start()
    for far in range(2, n - 1):
        line.forward(far)
    for path in (0, 1):
        second(path).wait_recv()

        def second_sum(z, carry):
            mine = one[0][z, y] if path == 0 else one[1][z, x]
            two[path][z] = (mine.astype(F32) + two[path][z].astype(F32)).astype(BF)
            return carry

        lax.fori_loop(0, n, second_sum, 0)

    def hop(source, path, step, side):
        index = (path, side, step)
        return remote(
            source,
            landing[path].at[side, step],
            zsend.at[index],
            zrecv.at[index],
            right if side == 0 else left,
        )

    for step in range(n - 1):
        for side in (0, 1):
            owner = n - 1 - step if side == 0 else step
            beyond = me < owner if side == 0 else me > owner
            edge = me == 0 if side == 0 else me == n - 1

            @pl.when(beyond & edge)
            def _():
                for path in (0, 1):
                    hop(two[path].at[owner], path, step, side).start()

    for far in range(1, n - 1):
        for side in (0, 1):
            step = far - me if side == 0 else far - (n - 1 - me)
            owner = n - 1 - step if side == 0 else step
            inner = me > 0 if side == 0 else me < n - 1
            beyond = me < owner if side == 0 else me > owner

            @pl.when(inner & (step >= 0) & beyond)
            def _():
                for path in (0, 1):
                    hop(two[path].at[owner], path, step, side).wait_recv()
                    staging[path][side, step] = (
                        two[path][owner].astype(F32) + landing[path][side, step].astype(F32)
                    ).astype(BF)
                    hop(staging[path].at[side, step], path, step, side).start()

    @pl.when(me > 0)
    def _():
        for path in (0, 1):
            hop(two[path].at[me], path, n - 1 - me, 0).wait_recv()

    @pl.when(me < n - 1)
    def _():
        for path in (0, 1):
            hop(two[path].at[me], path, me, 1).wait_recv()

    for path in (0, 1):
        total = two[path][me].astype(F32)
        from_left = landing[path][0, jnp.minimum(n - 1 - me, n - 2)].astype(F32)
        from_right = landing[path][1, jnp.minimum(me, n - 2)].astype(F32)
        total = total + jnp.where(me > 0, from_left, 0.0)
        total = total + jnp.where(me < n - 1, from_right, 0.0)
        outs[path][y, x, c] = total.astype(BF)

    def spread(path, stage):
        out = outs[path]
        if stage == 2:
            spot, device = out.at[:, :, c], by_c
        elif stage == 0:
            spot, device = out.at[y, x, c], by_x if path == 0 else by_y
        elif path == 0:
            spot, device = out.at[y, :, c], by_y
        else:
            spot, device = out.at[:, x, c], by_x
        return remote(spot, spot, gsend.at[path, stage], grecv.at[path, stage], device)

    for stage in range(3):
        for path in (0, 1):
            spread(path, stage).start()
        if stage == 0:
            line.finish(y_out)
        for path in (0, 1):
            spread(path, stage).wait_recv()

    for path in (0, 1):
        for stage in range(3):
            spread(path, stage).wait_send()
        first(path).wait_send()
        second(path).wait_send()
    for p in range(len(places)):
        swap(p).wait_send()
    for step in range(n - 1):
        for side in (0, 1):
            owner = n - 1 - step if side == 0 else step
            beyond = me < owner if side == 0 else me > owner

            @pl.when(beyond)
            def _():
                for path in (0, 1):
                    hop(two[path].at[owner], path, step, side).wait_send()


def reduce_weights(
    grad_q,
    grad_kv,
    tokens,
    gain,
    weight,
    cosine,
    sine,
    mixed_low,
    grad_attn,
    grad_residual,
    grad_router,
    gain_two_row,
    y_part,
    n,
    collective_id,
):
    rows_all, width_all = weight.shape
    query_width = grad_q.shape[1]
    key_width = (width_all - query_width) // 2
    array_widths = (width_all, grad_attn.shape[1], LANES)
    rows = rows_all // n
    eighth = rows // 8
    pieces = path_pieces(query_width, key_width, grad_attn.shape[1], LANES)
    widths = [sum(p[2] for p in pieces if p[3]), sum(p[2] for p in pieces if not p[3])]
    scratch = [pltpu.VMEM((n, 2, 2, 2, eighth, w), BF) for w in array_widths]
    scratch += [pltpu.VMEM((grad_q.shape[0], width_all), BF)]
    scratch += [pltpu.VMEM((n, 2, 2, eighth, w), BF) for w in widths]
    scratch += [pltpu.VMEM((n, 2, eighth, w), BF) for w in widths]
    scratch += [pltpu.VMEM((n, eighth, w), BF) for w in widths]
    scratch += [pltpu.VMEM((2, n - 1, eighth, w), BF) for w in widths] * 2
    sems = [(4,), (4,), (2, 2), (2, 2), (2, 2, n - 1), (2, 2, n - 1), (2, 3), (2, 3)]
    y_rows = y_part.shape[0] // n
    outs = pl.pallas_call(
        functools.partial(reduce_kernel, n, pieces),
        out_shape=[jax.ShapeDtypeStruct((2, 2, 2, eighth, w), BF) for w in widths]
        + [jax.ShapeDtypeStruct((y_rows, y_part.shape[1]), F32)]
        + [jax.ShapeDtypeStruct(tokens.shape, F32)],
        in_specs=[IN_VMEM] * 13,
        out_specs=[IN_VMEM] * 4,
        scratch_shapes=scratch
        + [pltpu.SemaphoreType.DMA(s) for s in sems]
        + line_sum_scratch(n, y_rows, y_part.shape[1]),
        compiler_params=pltpu.CompilerParams(
            collective_id=collective_id, has_side_effects=True, vmem_limit_bytes=60 * 1024 * 1024
        ),
        cost_estimate=pl.CostEstimate(flops=0, bytes_accessed=100000000, transcendentals=0),
        name="reduce_weights",
    )(
        grad_q,
        grad_kv,
        tokens,
        gain,
        weight,
        cosine,
        sine,
        mixed_low,
        grad_attn,
        grad_residual,
        grad_router,
        gain_two_row,
        y_part.reshape(n, y_rows, y_part.shape[1]),
    )
    first, second = [o.reshape(rows, w) for o, w in zip(outs, widths)]
    cut = pieces[0][2]
    rest = pieces[1][2]
    qkv = jnp.concatenate([first[:, :cut], second[:, :rest]], axis=1)
    return qkv, second[:, rest:], first[:, cut:], outs[2], outs[3]


def plane_tick(step, local):
    tick = jnp.where(step <= 2, step, jnp.where(step < local, (step + 2) // 2, step - 3))
    runs = (step <= 2) | (step >= local) | (step % 2 == 0)
    return tick, runs


def expert_kernel(sizes, plane, *refs):
    blocks, rows, local, capacity = sizes
    if plane:
        mixed_in, tokens_in, out_weight_in, gain_ref = refs[:4]
        refs = refs[4:]
    else:
        x_ref = refs[0]
        refs = refs[1:]
    ct_low_ref, ct_high_ref, router_t_ref, rank_all_ref = refs[:4]
    w_gate_ref, w_up_ref, w_down_ref = refs[4:7]
    y_ref, gs_ref, out_gate_ref, out_up_ref, out_down_ref = refs[7:12]
    refs = refs[12:]
    if plane:
        second_ref, residual_ref = refs[:2]
        refs = refs[2:]
    xs_ref, g_ref, rank_ref, gate_ref, dots_ref, y_sem = refs[:6]
    refs = refs[6:]
    slots = local * capacity
    step = pl.program_id(0)
    tick, ticks = plane_tick(step, local)
    me = lax.axis_index("expert")
    base = me * local
    if plane:
        stage_refs, pair_refs, one_refs, two_refs = refs[:3], refs[3:6], refs[6:10], refs[10:14]
        csend, crecv, psend, precv, qsend, qrecv = refs[14:20]
        gs_part = refs[20]
        line = LineSum(blocks, gs_part, *refs[21:25])
        x_ref, xsend, xrecv, in_sem, out_sem = refs[25:]
        group, _, (y, x, c), (by_y, by_x, by_c) = plane_position()
        half = stage_refs[2].shape[4] // 2

    def expert_id():
        return lax.broadcasted_iota(jnp.int32, (EXPERTS, rows), 0)

    def note_ranks(b):
        ranks = rank_all_ref[b].astype(F32)
        for e in range(local):
            mine = jnp.where(expert_id() == base + e, ranks, 0.0)
            rank_ref[b, e : e + 1, :] = jnp.sum(mine, axis=0, keepdims=True)

    def pick(b):
        slot_id = lax.broadcasted_iota(jnp.int32, (capacity, rows), 0).astype(F32)
        pieces = [
            jnp.where(rank_ref[b, e : e + 1, :] == slot_id, 1.0, 0.0).astype(BF)
            for e in range(local)
        ]
        return jnp.concatenate(pieces, axis=0)

    def dispatch_grads(b):
        picked = pick(b)
        middle = ct_low_ref.shape[2]
        g_ref[b, :, :middle] = dot(picked, ct_low_ref[b]).astype(BF)
        g_ref[b, :, middle:] = dot(picked, ct_high_ref[b]).astype(BF)

    def dispatch_rows(b):
        logits = dot_nt(router_t_ref[...], x_ref[b])
        hot = rank_all_ref[b].astype(F32) < 200.0
        top = jnp.max(jnp.where(hot, logits, NEGATIVE_LARGE), axis=0, keepdims=True)
        weight = jnp.where(hot, jnp.exp(jnp.minimum(logits - top, 0.0)), 0.0)
        gates = weight / jnp.sum(weight, axis=0, keepdims=True)
        for e in range(local):
            mine = jnp.where(expert_id() == base + e, gates, 0.0)
            gate_ref[b, e : e + 1, :] = jnp.sum(mine, axis=0, keepdims=True)
        xs_ref[b] = dot(pick(b), x_ref[b]).astype(BF)

    if plane:
        n = blocks
        leave_second = pltpu.make_async_copy(x_ref.at[me], second_ref, out_sem.at[0])
        leave_residual = pltpu.make_async_copy(gs_ref.at[:, :D], residual_ref, out_sem.at[1])

        def hop(far, side):
            block = me - far if side == 0 else me + far
            device = (group, me + 1 if side == 0 else me - 1)
            index = (side, far)
            return remote(
                x_ref.at[block], x_ref.at[block], xsend.at[index], xrecv.at[index], device
            )

        def sends(far, side):
            if side == 0:
                return (far < n - 1) & (me - far >= 0) & (me < n - 1)
            return (far < n - 1) & (me + far < n) & (me > 0)

        def arrives(far, side):
            return me - 1 - far >= 0 if side == 0 else me + 1 + far < n

        @pl.when(step == 0)
        def _():
            loads = [
                pltpu.make_async_copy(out_weight_in, stage_refs[2].at[2:4], in_sem.at[0]),
                pltpu.make_async_copy(tokens_in, xs_ref.at[0, :rows, :], in_sem.at[1]),
                pltpu.make_async_copy(mixed_in, xs_ref.at[1, :rows, :], in_sem.at[2]),
            ]
            for copy in loads:
                copy.start()
            for b in range(blocks):
                note_ranks(b)
            for copy in loads:
                copy.wait()
            out_weight = stage_refs[2][2:4].reshape(D, D)
            residual = xs_ref[0, :rows, :].astype(F32) + dot(xs_ref[1, :rows, :], out_weight)
            inverse = lax.rsqrt(jnp.mean(residual * residual, axis=-1, keepdims=True) + EPSILON)
            x_ref[me] = (residual * inverse * gain_ref[...]).astype(BF)
            gs_ref[:, :D] = residual
            greet([(None, by_c), (None, by_x), (None, by_y)] + line.neighbours())
            for side in (0, 1):

                @pl.when(sends(0, side))
                def _():
                    hop(0, side).start()

            leave_second.start()
            leave_residual.start()
            for b in range(blocks):
                dispatch_grads(b)
            dispatch_rows(me)

            def arrived(far, carry):
                for side in (0, 1):

                    @pl.when(arrives(far, side))
                    def _():
                        hop(far, side).wait_recv()

                    @pl.when(sends(far + 1, side))
                    def _():
                        hop(far + 1, side).start()

                for side in (0, 1):

                    @pl.when(arrives(far, side))
                    def _():
                        dispatch_rows(me - 1 - far if side == 0 else me + 1 + far)

                return carry

            lax.fori_loop(0, n - 1, arrived, 0)

        @pl.when(step == 1)
        def _():
            leave_second.wait()
            leave_residual.wait()
            for far in range(n - 1):
                for side in (0, 1):

                    @pl.when(sends(far, side))
                    def _():
                        hop(far, side).wait_send()

    else:

        @pl.when(step == 0)
        def _():
            for b in range(blocks):
                note_ranks(b)
                dispatch_grads(b)
                dispatch_rows(b)

    @pl.when(step < local)
    def _():
        here = pl.ds(pl.multiple_of(step * capacity, capacity), capacity)
        xs = jnp.concatenate([xs_ref[b, here, :] for b in range(blocks)], axis=0)
        g = jnp.concatenate([g_ref[b, here, :] for b in range(blocks)], axis=0).astype(F32)
        slot_id = lax.broadcasted_iota(jnp.int32, (capacity, rows), 0).astype(F32)
        gates = []
        for b in range(blocks):
            taken = rank_ref[b, pl.ds(step, 1), :] == slot_id
            gate = jnp.where(taken, gate_ref[b, pl.ds(step, 1), :], 0.0)
            gates.append(jnp.sum(gate, axis=1, keepdims=True))
        gate_slot = jnp.concatenate(gates, axis=0)
        w_gate, w_up, w_down = w_gate_ref[0], w_up_ref[0], w_down_ref[0]
        gate_pre = dot(xs, w_gate)
        up_pre = dot(xs, w_up)
        sigmoid = jax.nn.sigmoid(gate_pre)
        silu = gate_pre * sigmoid
        activation = (silu * up_pre).astype(BF)
        expert_out = dot(activation, w_down).astype(BF).astype(F32)
        slot_dot = jnp.sum(g * expert_out, axis=1, keepdims=True)
        grad_out = (gate_slot * g).astype(BF)
        scaled_out = (gate_slot * expert_out).astype(BF)
        grad_down = dot_tn(activation, grad_out).astype(BF)
        grad_activation = dot_nt(grad_out, w_down)
        grad_gate_pre = (
            grad_activation * up_pre * sigmoid * (1.0 + gate_pre * (1.0 - sigmoid))
        ).astype(BF)
        grad_up_pre = (grad_activation * silu).astype(BF)
        grad_gate = dot_tn(xs, grad_gate_pre).astype(BF)
        grad_up = dot_tn(xs, grad_up_pre).astype(BF)
        if plane:
            for ref, value in zip(stage_refs, (grad_gate, grad_up, grad_down)):
                ref[step % STAGES] = value.reshape(ref.shape[1:])
        else:
            out_gate_ref[0], out_up_ref[0], out_down_ref[0] = grad_gate, grad_up, grad_down
        grad_in = (dot_nt(grad_gate_pre, w_gate) + dot_nt(grad_up_pre, w_up)).astype(BF)
        lane = lax.broadcasted_iota(jnp.int32, (blocks * capacity, LANES), 1)
        high = slot_dot.astype(BF).astype(F32)
        middle = (slot_dot - high).astype(BF).astype(F32)
        low = slot_dot - high - middle
        mine = base + step
        dots = jnp.where(lane == mine, high, 0.0)
        dots = jnp.where(lane == mine + EXPERTS, middle, dots)
        dots = jnp.where(lane == mine + 2 * EXPERTS, low, dots).astype(BF)
        for b in range(blocks):
            part = slice(b * capacity, (b + 1) * capacity)
            xs_ref[b, here, :] = grad_in[part]
            g_ref[b, here, :] = scaled_out[part]
            dots_ref[b, here, :] = dots[part]

    def store_y(b):
        there = pl.ds(b * rows, rows)
        return pltpu.make_async_copy(g_ref.at[b, :rows, :], y_ref.at[there, :], y_sem.at[b])

    @pl.when(step == local - 1)
    def _():
        slot_expert = lax.broadcasted_iota(jnp.int32, (EXPERTS, slots), 1) // capacity
        spread_row = lax.broadcasted_iota(jnp.int32, (EXPERTS, slots), 0)
        spread = jnp.where(spread_row == slot_expert + base, 1.0, 0.0).astype(BF)
        slot_rank = (lax.broadcasted_iota(jnp.int32, (rows, slots), 1) % capacity).astype(F32)
        for b in range(blocks):
            there = slice(b * rows, (b + 1) * rows)
            ranks = dot_tn(rank_all_ref[b], spread)
            put = jnp.where(ranks == slot_rank, 1.0, 0.0).astype(BF)
            g_ref[b, :rows, :] = dot(put, g_ref[b]).astype(BF)
            store_y(b).start()
            back = dot(put, xs_ref[b]).astype(BF), dot(put, dots_ref[b]).astype(BF)
            if plane:
                gs_part[b, :, :D], gs_part[b, :, D:] = back
            else:
                gs_ref[there, :D], gs_ref[there, D:] = back
        if plane:
            line.start()

    @pl.when(step == pl.num_programs(0) - 1)
    def _():
        for b in range(blocks):
            store_y(b).wait()

    if not plane:
        return

    gate, up, low_down, high_down = range(4)
    low_rows, high_rows = slice(0, half), slice(half, 2 * half)

    def swap(e, i):
        return remote(
            stage_refs[i].at[e % STAGES, :, :, 1 - c],
            pair_refs[i].at[e % 3],
            csend.at[e % 2, i],
            crecv.at[e % 3, i],
            by_c,
        )

    def first(e, k):
        slot = e % 3
        source = {
            gate: lambda: pair_refs[0].at[slot, :, 1 - x],
            up: lambda: pair_refs[1].at[slot, 1 - y],
            low_down: lambda: pair_refs[2].at[slot, :, 1 - x, low_rows],
            high_down: lambda: pair_refs[2].at[slot, 1 - y, :, high_rows],
        }[k]()
        device = by_x if k in (gate, low_down) else by_y
        return remote(source, one_refs[k].at[slot], psend.at[slot, k], precv.at[slot, k], device)

    def second(e, k):
        along_x = k in (gate, low_down)
        source = one_refs[k].at[e % 3, 1 - y] if along_x else one_refs[k].at[e % 3, 1 - x]
        slot = e % 2
        return remote(
            source,
            two_refs[k].at[slot],
            qsend.at[slot, k],
            qrecv.at[slot, k],
            by_y if along_x else by_x,
        )

    def add(first_value, second_value):
        return (first_value.astype(F32) + second_value.astype(F32)).astype(BF)

    @pl.when(ticks & (tick >= 3))
    def _():
        e = tick - 3
        for k in range(4):
            second(e, k).wait()
        own = [one_refs[k][e % 3, y if k in (gate, low_down) else x] for k in range(4)]
        out_gate_ref[0] = add(own[gate], two_refs[gate][e % 2])
        out_up_ref[0] = add(own[up], two_refs[up][e % 2])
        out_down_ref[0, low_rows] = add(own[low_down], two_refs[low_down][e % 2])
        out_down_ref[0, high_rows] = add(own[high_down], two_refs[high_down][e % 2])

    @pl.when(ticks & (tick >= 2) & (tick < local + 2))
    def _():
        e = tick - 2
        slot = e % 3
        for k in range(4):
            first(e, k).wait()
            for t in (0, 1):
                mine = {
                    gate: lambda: pair_refs[0][slot, t, x],
                    up: lambda: pair_refs[1][slot, y, t],
                    low_down: lambda: pair_refs[2][slot, t, x, low_rows],
                    high_down: lambda: pair_refs[2][slot, y, t, high_rows],
                }[k]()
                one_refs[k][slot, t] = add(mine, one_refs[k][slot, t])
            second(e, k).start()

    @pl.when(ticks & (tick >= 1) & (tick < local + 1))
    def _():
        e = tick - 1
        slot = e % 3
        for i in range(3):
            swap(e, i).wait()

            def pair_sum(t, carry):
                a, b = t // 2, t % 2
                pair_refs[i][slot, a, b] = add(
                    stage_refs[i][e % STAGES, a, b, c], pair_refs[i][slot, a, b]
                )
                return carry

            lax.fori_loop(0, 4, pair_sum, 0)
        for k in range(4):
            first(e, k).start()

    @pl.when(ticks & (tick < local))
    def _():
        for i in range(3):
            swap(tick, i).start()

    for hop in range(1, blocks - 1):

        @pl.when(step == local + hop)
        def _():
            line.forward(hop)

    @pl.when(step == local + blocks - 1)
    def _():
        line.finish(gs_ref)


def run_experts(
    sources, ct_low, ct_high, router_t, rank_all, w_gate, w_up, w_down, capacity, plane, collective_id
):
    blocks, _, rows = rank_all.shape
    total, local = blocks * rows, w_gate.shape[0]
    slots = local * capacity
    sizes = (blocks, rows, local, capacity)
    whole = lambda shape: pl.BlockSpec(
        shape, lambda e: (0,) * len(shape), pipeline_mode=pl.Buffered(1)
    )
    per = lambda shape: pl.BlockSpec((1,) + shape, lambda e: (jnp.minimum(e, local - 1), 0, 0))
    shapes = ((D, FF), (D, FF), (FF, D))
    ct_low, ct_high = [ct.reshape(blocks, rows, -1) for ct in (ct_low, ct_high)]
    scratch = [
        pltpu.VMEM((blocks, slots, D), BF),
        pltpu.VMEM((blocks, slots, D), BF),
        pltpu.VMEM((blocks, local, rows), F32),
        pltpu.VMEM((blocks, local, rows), F32),
        pltpu.VMEM((blocks, slots, LANES), BF),
        pltpu.SemaphoreType.DMA((blocks,)),
    ]
    params = dict(dimension_semantics=("arbitrary",), vmem_limit_bytes=63 * 1024 * 1024)
    if plane:
        eighths = [(a // 8, b) for a, b in shapes]
        out = lambda shape: pl.BlockSpec(
            (1,) + shape, lambda e: (jnp.maximum(plane_tick(e, local)[0] - 3, 0), 0, 0)
        )
        grad_shapes, grad_specs = eighths, [out(shape) for shape in eighths]
        low = (eighths[2][0] // 2, eighths[2][1])
        passed = (eighths[0], eighths[1], low, low)
        scratch += [pltpu.VMEM((STAGES, 2, 2, 2) + shape, BF) for shape in eighths]
        scratch += [pltpu.VMEM((3, 2, 2) + shape, BF) for shape in eighths]
        scratch += [pltpu.VMEM((3, 2) + shape, BF) for shape in passed]
        scratch += [pltpu.VMEM((2,) + shape, BF) for shape in passed]
        sems = [(2, 3), (3, 3), (3, 4), (3, 4), (2, 4), (2, 4)]
        scratch += [pltpu.SemaphoreType.DMA(shape) for shape in sems]
        scratch += [pltpu.VMEM((blocks, rows, D + LANES), BF)]
        scratch += line_sum_scratch(blocks, rows, D + LANES)
        scratch += [pltpu.VMEM((blocks, rows, D), BF)]
        sems = [(2, blocks - 1), (2, blocks - 1), (3,), (2,)]
        scratch += [pltpu.SemaphoreType.DMA(shape) for shape in sems]
        mixed_low, tokens, out_weight, gain = sources
        sources = [mixed_low, tokens, out_weight.reshape((2, 2, 2, 2) + eighths[2]), gain]
        source_specs = [ANY] * 3 + [whole(gain.shape)]
        more_shapes = [
            jax.ShapeDtypeStruct((rows, D), BF),
            jax.ShapeDtypeStruct((rows, D), F32),
        ]
        gs_shape, gs_type = (rows, D + LANES), F32
        params |= dict(collective_id=collective_id, has_side_effects=True)
    else:
        grad_shapes, grad_specs = shapes, [per(shape) for shape in shapes]
        gs_shape, gs_type = (total, D + LANES), BF
        sources = [sources[0].reshape(blocks, rows, D)]
        source_specs = [whole(sources[0].shape)]
        more_shapes = []
    flops = 2 * total * D * slots * 4 // blocks + 18 * blocks * slots * D * FF
    return pl.pallas_call(
        functools.partial(expert_kernel, sizes, plane),
        grid=(local + 6 if plane else local,),
        out_shape=[
            jax.ShapeDtypeStruct((total, D), BF),
            jax.ShapeDtypeStruct(gs_shape, gs_type),
        ]
        + [jax.ShapeDtypeStruct((local,) + shape, BF) for shape in grad_shapes]
        + more_shapes,
        in_specs=source_specs
        + [
            whole(ct_low.shape),
            whole(ct_high.shape),
            whole((EXPERTS, D)),
            whole(rank_all.shape),
        ]
        + [per(shape) for shape in shapes],
        out_specs=[ANY, whole(gs_shape)] + grad_specs + [ANY] * len(more_shapes),
        scratch_shapes=scratch,
        compiler_params=pltpu.CompilerParams(**params),
        cost_estimate=pl.CostEstimate(
            flops=flops, bytes_accessed=2 * (6 * local * D * FF + 4 * total * D), transcendentals=0
        ),
        name="experts",
    )(*sources, ct_low, ct_high, router_t, rank_all, w_gate, w_up, w_down)


def rotate(tile, cosine, sine):
    half = HEAD_DIMENSION // 2
    lane = lax.broadcasted_iota(jnp.int32, tile.shape, 1) % HEAD_DIMENSION
    other = jnp.where(lane < half, pltpu.roll(tile, LANES - half, 1), pltpu.roll(tile, half, 1))
    return tile * cosine + other * sine


def normed(tokens_ref):
    value = tokens_ref[...].astype(F32)
    inverse = lax.rsqrt(jnp.mean(value * value, axis=-1, keepdims=True) + EPSILON)
    return value * inverse, inverse


def mask_bias(bias_ref, length_ref, rows):
    base = lax.axis_index("expert") * rows
    key = lax.broadcasted_iota(jnp.int32, bias_ref.shape, 0)
    query = lax.broadcasted_iota(jnp.int32, bias_ref.shape, 1) + base
    allowed = (key <= query) & (key < length_ref[0])
    bias_ref[...] = jnp.where(allowed, 0.0, NEGATIVE_LARGE)


def head_columns(ref, head):
    start = 2 * HEAD_DIMENSION * head
    middle = start + HEAD_DIMENSION
    return jnp.concatenate([ref[:, start:middle], ref[:, middle : middle + HEAD_DIMENSION]], 0)


def put_heads(ref, head, transposed):
    rows = ref.shape[0]
    value = transposed.T
    start = 2 * HEAD_DIMENSION * head
    middle = start + HEAD_DIMENSION
    ref[:, start:middle] = value[:rows].astype(ref.dtype)
    ref[:, middle : middle + HEAD_DIMENSION] = value[rows:].astype(ref.dtype)


def attention_kernel(
    n,
    length_ref,
    tokens_ref,
    gain_ref,
    weight_ref,
    cosine_ref,
    sine_ref,
    rank_ref,
    mixed_ref,
    log_total_ref,
    kv_all_ref,
    query_out_ref,
    rank_all_ref,
    *scratch,
):
    bias_ref, query_ref, kv_ref, chunk_ref, rank_buffer, send, recv, rank_send, rank_recv = scratch
    pair, pairs = pl.program_id(0), pl.num_programs(0)
    group, me = lax.axis_index("group"), lax.axis_index("expert")
    left, right = (group, me - 1), (group, me + 1)
    rows, width = kv_ref.shape[1:]

    def hop(j, step, side):
        block = me - step if side == 0 else me + step
        source = kv_ref.at[j] if step == 0 else chunk_ref.at[j, block]
        index = (j, side, step)
        return remote(
            source,
            chunk_ref.at[j, block],
            send.at[index],
            recv.at[index],
            right if side == 0 else left,
        )

    def rank_hop(step, side):
        block = me - step if side == 0 else me + step
        source = rank_ref if step == 0 else rank_buffer.at[block]
        index = (side, step)
        return remote(
            source,
            rank_buffer.at[block],
            rank_send.at[index],
            rank_recv.at[index],
            right if side == 0 else left,
        )

    def sends(step, side):
        return (me - step >= 0) & (me < n - 1) if side == 0 else (me + step < n) & (me > 0)

    def arrives(step, side):
        return me - 1 - step >= 0 if side == 0 else me + 1 + step < n

    def launch(make, step):
        for side in (0, 1):

            @pl.when(sends(step, side))
            def _():
                make(step, side).start()

    def await_hop(make, step):
        for side in (0, 1):

            @pl.when(arrives(step, side))
            def _():
                make(step, side).wait_recv()

    def drain(make):
        for step in range(n - 1):
            for side in (0, 1):

                @pl.when(sends(step, side))
                def _():
                    make(step, side).wait_send()

    def chunk(j):
        return lambda step, side: hop(j, step, side)

    @pl.when(pair == 0)
    def _():
        unit, _ = normed(tokens_ref)
        first_norm = (unit * gain_ref[...]).astype(BF)
        cosine, sine = cosine_ref[...], sine_ref[...]
        count = kv_ref.shape[0]
        query_width = count * width
        key_width = query_width // 2
        keys = dot(first_norm, weight_ref[:, query_width : query_width + key_width])
        values = dot(first_norm, weight_ref[:, query_width + key_width :])
        for j in range(count):
            columns = slice(j * LANES, (j + 1) * LANES)
            kv_ref[j, :, :LANES] = rotate(keys[:, columns], cosine, sine).astype(BF)
            kv_ref[j, :, LANES:] = values[:, columns].astype(BF)
        rank_buffer[me] = rank_ref[...]
        greet([(me > 0, left), (me < n - 1, right)])
        launch(chunk(0), 0)
        launch(chunk(1), 0)
        queries = dot(first_norm, weight_ref[:, :query_width])
        for j in range(2 * count):
            start = (j % 2) * LANES
            tile = queries[:, j * LANES : (j + 1) * LANES]
            query_ref[j // 2, :, start : start + LANES] = rotate(tile, cosine, sine).astype(BF)
        mask_bias(bias_ref, length_ref, rows)
        await_hop(chunk(0), 0)
        launch(chunk(0), 1)

    for step in range(1, n - 1):
        await_hop(chunk(pair), step)
        if step < n - 2:
            launch(chunk(pair), step + 1)

    @pl.when(pair + 1 < pairs)
    def _():
        await_hop(chunk(pair + 1), 0)
        launch(chunk(pair + 1), 1)

    @pl.when(pair + 2 < pairs)
    def _():
        launch(chunk(pair + 2), 0)

    @pl.when(pair == 1)
    def _():
        launch(rank_hop, 0)

    for step in range(n - 1):

        @pl.when(pair == jnp.minimum(2 + step, pairs - 1))
        def _():
            await_hop(rank_hop, step)
            if step < n - 2:
                launch(rank_hop, step + 1)

    chunk_ref[pair, me] = kv_ref[pair]
    kv = chunk_ref[pair].reshape(n * rows, width)
    kv_all_ref[...] = kv
    query_out_ref[0] = query_ref[pair]
    bias = jnp.concatenate([bias_ref[...]] * 2, axis=1)
    for head in (0, 1):
        start = head * HEAD_DIMENSION
        key = kv[:, start : start + HEAD_DIMENSION]
        value = kv[:, LANES + start : LANES + start + HEAD_DIMENSION]
        query = head_columns(query_ref.at[pair], head) * jnp.asarray(HEAD_DIMENSION**-0.5, BF)
        scores = dot_nt(key, query) + bias
        top = jnp.max(scores, axis=0, keepdims=True)
        weights = jnp.exp(scores - top)
        total = jnp.sum(weights, axis=0, keepdims=True)
        put_heads(mixed_ref, head, dot_tn(value, weights.astype(BF)) / total)
        log_total_ref[0, head : head + 1, :] = top + jnp.log(total)

    @pl.when(pair == pairs - 1)
    def _():
        drain(rank_hop)
        rank_all_ref[...] = rank_buffer[...]
        for j in range(KEY_VALUE_HEADS // 2):
            drain(chunk(j))


def attention(length, tokens, gain, weight, cosine, sine, rank, n, collective_id):
    rows = tokens.shape[0]
    keys, width = n * rows, 2 * LANES
    pairs = KEY_VALUE_HEADS // 2
    return pl.pallas_call(
        functools.partial(attention_kernel, n),
        grid=(pairs,),
        out_shape=(
            jax.ShapeDtypeStruct((rows, pairs * width), BF),
            jax.ShapeDtypeStruct((pairs, 2, 2 * rows), F32),
            jax.ShapeDtypeStruct((keys, pairs * width), BF),
            jax.ShapeDtypeStruct((pairs, rows, width), BF),
            jax.ShapeDtypeStruct((n,) + rank.shape, rank.dtype),
        ),
        in_specs=[pl.BlockSpec(memory_space=pltpu.SMEM)] + [IN_VMEM] * 6,
        out_specs=(
            pl.BlockSpec((rows, width), lambda j: (0, j)),
            pl.BlockSpec((1, 2, 2 * rows), lambda j: (j, 0, 0)),
            pl.BlockSpec((keys, width), lambda j: (0, j)),
            pl.BlockSpec((1, rows, width), lambda j: (j, 0, 0)),
            IN_VMEM,
        ),
        scratch_shapes=[
            pltpu.VMEM((keys, rows), F32),
            pltpu.VMEM((pairs, rows, width), BF),
            pltpu.VMEM((pairs, rows, width), BF),
            pltpu.VMEM((pairs, n, rows, width), BF),
            pltpu.VMEM((n,) + rank.shape, rank.dtype),
            pltpu.SemaphoreType.DMA((pairs, 2, n - 1)),
            pltpu.SemaphoreType.DMA((pairs, 2, n - 1)),
            pltpu.SemaphoreType.DMA((2, n - 1)),
            pltpu.SemaphoreType.DMA((2, n - 1)),
        ],
        compiler_params=pltpu.CompilerParams(
            dimension_semantics=("arbitrary",),
            vmem_limit_bytes=56 * 1024 * 1024,
            collective_id=collective_id,
            has_side_effects=True,
        ),
        cost_estimate=pl.CostEstimate(
            flops=16 * rows * keys * D, bytes_accessed=100000000, transcendentals=0
        ),
        name="attention",
    )(length, tokens, gain, weight, cosine, sine, rank)


def attention_back_kernel(
    n,
    length_ref,
    q_ref,
    kv_ref,
    grad_ref,
    log_total_ref,
    grad_q_ref,
    grad_kv_ref,
    bias_ref,
    terms_ref,
    landing,
    staging,
    send,
    recv,
):
    step, pairs = pl.program_id(0), pl.num_programs(0) - 1

    def line(j):
        return LineSum(
            n, terms_ref.at[j], landing.at[j], staging.at[j], send.at[j], recv.at[j]
        )

    @pl.when(step == 0)
    def _():
        greet(line(0).neighbours())
        mask_bias(bias_ref, length_ref, q_ref.shape[1])

    @pl.when(step < pairs)
    def _():
        attention_back_pair(
            q_ref, kv_ref, grad_ref, log_total_ref, grad_q_ref, terms_ref.at[step], bias_ref
        )
        line(step).start()

    @pl.when(step > 0)
    def _():
        for hop in range(1, n - 1):
            line(step - 1).forward(hop)
        line(step - 1).finish(grad_kv_ref)


def attention_back_pair(q_ref, kv_ref, grad_ref, log_total_ref, grad_q_ref, grad_kv_ref, bias_ref):
    scale = HEAD_DIMENSION**-0.5
    blocks, rows, _ = grad_kv_ref.shape
    q_ref = q_ref.at[0]
    bias = jnp.concatenate([bias_ref[...]] * 2, axis=1)
    for head in (0, 1):
        columns = slice(head * HEAD_DIMENSION, (head + 1) * HEAD_DIMENSION)
        key, value = kv_ref[:, :LANES][:, columns], kv_ref[:, LANES:][:, columns]
        query = head_columns(q_ref, head) * jnp.asarray(scale, BF)
        grad = head_columns(grad_ref, head)
        scores = dot_nt(key, query) + bias
        probs = jnp.exp(scores - log_total_ref[0, head : head + 1, :])
        grad_probs = dot_nt(value, grad)
        delta = jnp.sum(probs * grad_probs, axis=0, keepdims=True)
        grad_scores = (probs * (grad_probs - delta)).astype(BF)
        grad_key = dot(grad_scores, query).astype(BF).reshape(blocks, rows, HEAD_DIMENSION)
        grad_kv_ref[:, :, columns] = grad_key
        grad_value = dot(probs.astype(BF), grad).astype(BF).reshape(blocks, rows, HEAD_DIMENSION)
        start = LANES + head * HEAD_DIMENSION
        grad_kv_ref[:, :, start : start + HEAD_DIMENSION] = grad_value
        put_heads(grad_q_ref, head, dot_tn(key, grad_scores) * scale)


def attention_back(length, query, kv_all, grad_mixed, log_total, n, collective_id):
    rows, keys = query.shape[1], kv_all.shape[0]
    pairs, width = KEY_VALUE_HEADS // 2, 2 * LANES
    now = lambda j: jnp.minimum(j, pairs - 1)
    row_spec = pl.BlockSpec((rows, width), lambda j: (0, now(j)))
    return pl.pallas_call(
        functools.partial(attention_back_kernel, n),
        grid=(pairs + 1,),
        out_shape=(
            jax.ShapeDtypeStruct((rows, pairs * width), F32),
            jax.ShapeDtypeStruct((rows, pairs * width), BF),
        ),
        in_specs=[
            pl.BlockSpec(memory_space=pltpu.SMEM),
            pl.BlockSpec((1, rows, width), lambda j: (now(j), 0, 0)),
            pl.BlockSpec((keys, width), lambda j: (0, now(j))),
            row_spec,
            pl.BlockSpec((1, 2, 2 * rows), lambda j: (now(j), 0, 0)),
        ],
        out_specs=(
            row_spec,
            pl.BlockSpec((rows, width), lambda j: (0, jnp.maximum(j - 1, 0))),
        ),
        scratch_shapes=[
            pltpu.VMEM((keys, rows), F32),
            pltpu.VMEM((pairs, n, rows, width), BF),
            pltpu.VMEM((pairs, 2, n - 1, rows, width), BF),
            pltpu.VMEM((pairs, 2, n - 2, rows, width), BF),
            pltpu.SemaphoreType.DMA((pairs, 2, n - 1)),
            pltpu.SemaphoreType.DMA((pairs, 2, n - 1)),
        ],
        compiler_params=pltpu.CompilerParams(
            dimension_semantics=("arbitrary",),
            vmem_limit_bytes=60 * 1024 * 1024,
            collective_id=collective_id,
            has_side_effects=True,
        ),
        cost_estimate=pl.CostEstimate(
            flops=40 * rows * keys * D, bytes_accessed=100000000, transcendentals=0
        ),
        name="attention_back",
    )(length, query, kv_all, grad_mixed, log_total)


def widen_kernel(value_ref, out_ref):
    out_ref[...] = value_ref[...].astype(F32)


def widen(value):
    block = (1,) + value.shape[1:]
    spec = pl.BlockSpec(block, lambda e: (e, 0, 0))
    return pl.pallas_call(
        widen_kernel,
        grid=(value.shape[0],),
        out_shape=jax.ShapeDtypeStruct(value.shape, F32),
        in_specs=[spec],
        out_specs=spec,
        compiler_params=pltpu.CompilerParams(dimension_semantics=("arbitrary",)),
        cost_estimate=pl.CostEstimate(flops=0, bytes_accessed=6 * value.size, transcendentals=0),
        name="widen",
    )(value)


def unpair_columns(value):
    rows = value.shape[0]
    value = value.reshape(rows, -1, 2, LANES)
    return value[:, :, 0].reshape(rows, -1), value[:, :, 1].reshape(rows, -1)


def gather_rows(value):
    return lax.all_gather(value, "expert", axis=0, tiled=True)


def scatter_rows(value):
    return lax.psum_scatter(value, "expert", scatter_dimension=0, tiled=True)


def per_device(
    tokens,
    lengths,
    routes,
    norm_gain1,
    w_query,
    key_projection,
    value_projection,
    w_out,
    norm_gain2,
    w_router,
    w_gate,
    w_up,
    w_down,
    cotangent,
):
    rows = tokens.shape[0]
    n, groups = lax.axis_size("expert"), lax.axis_size("group")
    plane = groups == 8 and w_gate.shape[0] == 8
    my_index = lax.axis_index("expert")
    capacity = 3 * rows * TOP // (2 * EXPERTS)
    query_width, key_width = w_query.shape[1], key_projection.shape[1]
    length = lengths[0]
    positions = my_index * rows + jnp.arange(rows, dtype=jnp.int32)
    valid_rows = (positions < length)[:, None]
    grad_output = jnp.where(valid_rows, cotangent, jnp.zeros_like(cotangent))

    small = jnp.concatenate(
        [w_router, norm_gain1[:, None], norm_gain2[:, None]]
        + [jnp.zeros((w_router.shape[0], LANES - EXPERTS - 2), BF)],
        axis=1,
    )
    middle = D // 2
    qkv_weight, out_weight, small, ct_low = gather_weights(
        w_query, key_projection, value_projection, w_out, small, grad_output[:, :middle], n, 1
    )
    qkv_weight, ct_high = lax.optimization_barrier((qkv_weight, grad_output[:, middle:]))
    ct_high = gather_rows(ct_high)
    router_weight = small[:, :EXPERTS]
    gain_one = small[:, EXPERTS].astype(F32)
    gain_two = small[:, EXPERTS + 1].astype(F32)

    expert_ids = jnp.arange(EXPERTS, dtype=jnp.int32)
    hot = jnp.any(routes[:, :, None] == expert_ids, axis=1)
    row_id = jnp.arange(rows, dtype=jnp.int32)
    earlier = (row_id[:, None] < row_id[None, :]).astype(BF)
    rank = jnp.where(hot.T, dot(hot.T.astype(BF), earlier), 255.0).astype(BF)

    cosine_lookup, sine_lookup = [table[:, 0] for table in rotary_tables(positions, HEAD_DIMENSION)]
    cosine = jnp.tile(cosine_lookup, (1, 4))
    sine = jnp.tile(jnp.concatenate([-sine_lookup, sine_lookup], axis=1), (1, 2))
    token_f32 = tokens.astype(F32)
    gain_one_row = gain_one[None, :]
    mixed_low, log_total, kv_all, query_pairs, rank_all = attention(
        lengths, tokens, gain_one_row, qkv_weight, cosine, sine, rank, n, 2
    )
    expert_args = (ct_low, ct_high, router_weight.T, rank_all, w_gate, w_up, w_down, capacity)
    if plane:
        sources = (mixed_low, tokens, out_weight, gain_two[None, :])
        y_part, gs, grad_gate, grad_up, grad_down, second_norm, residual = run_experts(
            sources, *expert_args, plane, 7
        )
    else:
        residual = token_f32 + dot(mixed_low, out_weight)
    inverse_two = lax.rsqrt(jnp.mean(residual * residual, axis=-1, keepdims=True) + EPSILON)
    unit_two = residual * inverse_two
    if not plane:
        second_norm = (unit_two * gain_two).astype(BF)
        sources = line_gather([second_norm], n, 3, "gather_rows")
        y_part, gs, grad_gate, grad_up, grad_down = run_experts(sources, *expert_args, plane, 7)
        gs = line_scatter(gs, n, F32, 4, "scatter_grads")

    logits = dot(second_norm, router_weight)
    chosen = jnp.where(hot, logits, NEGATIVE_LARGE)
    gate_weights = jnp.where(hot, jnp.exp(chosen - jnp.max(chosen, axis=-1, keepdims=True)), 0.0)
    gate_weights = gate_weights / jnp.sum(gate_weights, axis=-1, keepdims=True)
    grad_gates = gs[:, D : D + EXPERTS] + gs[:, D + EXPERTS : D + 2 * EXPERTS]
    grad_gates = grad_gates + gs[:, D + 2 * EXPERTS : D + 3 * EXPERTS]
    grad_logits = (
        gate_weights * (grad_gates - jnp.sum(gate_weights * grad_gates, axis=-1, keepdims=True))
    ).astype(BF)
    grad_second = gs[:, :D] + dot_nt(grad_logits, router_weight)
    grad_router = dot_tn(second_norm, grad_logits)
    scaled_two = grad_second * gain_two
    grad_gain2 = jnp.sum(grad_second * unit_two, axis=0)
    grad_residual = grad_output.astype(F32) + inverse_two * (
        scaled_two - unit_two * jnp.mean(scaled_two * unit_two, axis=-1, keepdims=True)
    )
    grad_attn = grad_residual.astype(BF)
    mixed_gradient = dot_nt(grad_attn, out_weight).astype(BF)
    grad_query_acc, kv_gradient = attention_back(
        lengths, query_pairs, kv_all, mixed_gradient, log_total, n, 5
    )
    pad = jnp.zeros((D, LANES - EXPERTS), F32)
    if plane:
        *shares, expert_sum, grad_tokens = reduce_weights(
            grad_query_acc,
            kv_gradient,
            tokens,
            gain_one_row,
            qkv_weight,
            cosine,
            sine,
            mixed_low,
            grad_attn,
            grad_residual,
            jnp.concatenate([grad_router, pad], axis=1),
            grad_gain2[None, :],
            y_part,
            n,
            6,
        )
    else:
        inverse_one = lax.rsqrt(jnp.mean(token_f32 * token_f32, axis=-1, keepdims=True) + EPSILON)
        unit_one = token_f32 * inverse_one
        first_norm = (unit_one * gain_one).astype(BF)
        own_key_gradient, own_value_gradient = unpair_columns(kv_gradient)
        back = lambda value: apply_rotation(
            value.astype(F32).reshape(rows, -1, HEAD_DIMENSION),
            cosine_lookup[:, None],
            -sine_lookup[:, None],
        )
        grad_query_pre = back(grad_query_acc).reshape(rows, query_width).astype(BF)
        grad_key_pre = back(own_key_gradient).reshape(rows, key_width).astype(BF)
        grad_qkv_pre = jnp.concatenate([grad_query_pre, grad_key_pre, own_value_gradient], axis=1)
        grad_first = dot_nt(grad_qkv_pre, qkv_weight)
        scaled_one = grad_first * gain_one
        grad_gain1 = jnp.sum(grad_first * unit_one, axis=0)
        grad_tokens = grad_residual + inverse_one * (
            scaled_one - unit_one * jnp.mean(scaled_one * unit_one, axis=-1, keepdims=True)
        )
        grad_small = jnp.concatenate(
            [grad_router, grad_gain1[:, None], grad_gain2[:, None], pad[:, 2:]], axis=1
        )
        shares = (dot_tn(first_norm, grad_qkv_pre), dot_tn(mixed_low, grad_attn), grad_small)
        shares = [lax.psum(scatter_rows(share.astype(BF)), "group") for share in shares]
        expert_sum = line_scatter(y_part, n, F32, 8, "scatter_outputs")
    mixed = (residual + expert_sum).astype(BF)
    share_qkv, share_out, share_small = [share.astype(F32) for share in shares]

    def sum_over_groups(value):
        if not plane:
            value = lax.psum_scatter(value, "group", scatter_dimension=1, tiled=True)
        return widen(lax.all_gather(value, "group", axis=1, tiled=True))

    return (
        mixed,
        grad_tokens,
        share_small[:, EXPERTS],
        share_qkv[:, :query_width],
        share_qkv[:, query_width : query_width + key_width],
        share_qkv[:, query_width + key_width :],
        share_out,
        share_small[:, EXPERTS + 1],
        share_small[:, :EXPERTS],
        sum_over_groups(grad_gate),
        sum_over_groups(grad_up),
        sum_over_groups(grad_down),
    )


def solution(mesh):
    rows = P(("group", "expert"), None)
    vector, matrix, stack = P("expert"), P("expert", None), P("expert", None, None)
    return jax.shard_map(
        per_device,
        mesh=mesh,
        in_specs=(
            rows,
            P("group"),
            rows,
            vector,
            matrix,
            matrix,
            matrix,
            matrix,
            vector,
            matrix,
            stack,
            stack,
            stack,
            rows,
        ),
        out_specs=(
            rows,
            rows,
            vector,
            matrix,
            matrix,
            matrix,
            matrix,
            vector,
            matrix,
            stack,
            stack,
            stack,
        ),
        check_vma=False,
    )
```

```python
import functools
import itertools

import jax
import jax.numpy as jnp
from jax import lax
from jax.experimental import pallas as pl
from jax.experimental.pallas import tpu as pltpu
from jax.sharding import PartitionSpec as P

D = 1024
QUERY_HEADS = 16
KEY_VALUE_HEADS = 8
HEAD_DIMENSION = 64
EXPERTS = 32
TOP = 8
FF = 512
LANES = 128
STAGES = 4

EPSILON = 1e-05
NEGATIVE_LARGE = -1e30
BF = jnp.bfloat16
F32 = jnp.float32


def rotary_tables(positions, head_size):
    half_width = head_size // 2
    frequency = 10000.0 ** (-2.0 * jnp.arange(half_width).astype(F32) / head_size)
    angles = positions.astype(F32)[:, None] * frequency[None, :]
    return (jnp.cos(angles)[:, None, :], jnp.sin(angles)[:, None, :])


def apply_rotation(tensor_in, cosine_lookup, sine_lookup):
    half_width = tensor_in.shape[-1] // 2
    first_half = tensor_in[..., :half_width]
    second_half = tensor_in[..., half_width:]
    return jnp.concatenate(
        [
            first_half * cosine_lookup - second_half * sine_lookup,
            second_half * cosine_lookup + first_half * sine_lookup,
        ],
        axis=-1,
    )


def dot(a, b):
    return jnp.dot(a, b, preferred_element_type=F32)


def dot_nt(a, b):
    return lax.dot_general(a, b, (((1,), (1,)), ((), ())), preferred_element_type=F32)


def dot_tn(a, b):
    return lax.dot_general(a, b, (((0,), (0,)), ((), ())), preferred_element_type=F32)


MESH = pl.DeviceIdType.MESH
ANY = pl.BlockSpec(memory_space=pl.ANY)
IN_VMEM = pl.BlockSpec(memory_space=pltpu.VMEM)


def remote(source, target, send, receive, device):
    return pltpu.make_async_remote_copy(
        src_ref=source,
        dst_ref=target,
        send_sem=send,
        recv_sem=receive,
        device_id=device,
        device_id_type=MESH,
    )


def greet(devices):
    barrier = pltpu.get_barrier_semaphore()
    count = 0
    for condition, device in devices:
        if condition is None:
            pl.semaphore_signal(barrier, inc=1, device_id=device, device_id_type=MESH)
            count = count + 1
        else:

            @pl.when(condition)
            def _():
                pl.semaphore_signal(barrier, inc=1, device_id=device, device_id_type=MESH)

            count = count + jnp.where(condition, 1, 0)
    pl.semaphore_wait(barrier, count)


def line_gather_kernel(n, count, *refs):
    ins, outs = refs[:count], refs[count : 2 * count]
    local, send, receive = refs[2 * count :]
    group, me = lax.axis_index("group"), lax.axis_index("expert")
    left, right = (group, me - 1), (group, me + 1)
    own = [
        pltpu.make_async_copy(ins[i], outs[i].at[me], local.at[i]) for i in range(count)
    ]
    for copy in own:
        copy.start()
    greet([(me > 0, left), (me < n - 1, right)])

    def hop(i, step, side):
        block = me - step if side == 0 else me + step
        source = ins[i] if step == 0 else outs[i].at[block]
        index = (side, step, i)
        return remote(
            source, outs[i].at[block], send.at[index], receive.at[index], right if side == 0 else left
        )

    def arrival(i, step, side):
        block = me - 1 - step if side == 0 else me + 1 + step
        index = (side, step, i)
        return remote(
            outs[i].at[block], outs[i].at[block], send.at[index], receive.at[index], left if side == 0 else right
        )

    def sends(step, side):
        return (me - step >= 0) & (me < n - 1) if side == 0 else (me + step < n) & (me > 0)

    def arrives(step, side):
        return me - 1 - step >= 0 if side == 0 else me + 1 + step < n

    for step in range(n - 1):
        for side in (0, 1):

            @pl.when(sends(step, side))
            def _():
                for i in range(count):
                    hop(i, step, side).start()

        for side in (0, 1):

            @pl.when(arrives(step, side))
            def _():
                for i in range(count):
                    arrival(i, step, side).wait_recv()

    for step in range(n - 1):
        for side in (0, 1):

            @pl.when(sends(step, side))
            def _():
                for i in range(count):
                    hop(i, step, side).wait_send()

    for copy in own:
        copy.wait()


def line_gather(values, n, collective_id, name):
    count = len(values)
    outs = pl.pallas_call(
        functools.partial(line_gather_kernel, n, count),
        out_shape=[jax.ShapeDtypeStruct((n,) + v.shape, v.dtype) for v in values],
        in_specs=[IN_VMEM] * count,
        out_specs=[ANY] * count,
        scratch_shapes=[
            pltpu.SemaphoreType.DMA((count,)),
            pltpu.SemaphoreType.DMA((2, n - 1, count)),
            pltpu.SemaphoreType.DMA((2, n - 1, count)),
        ],
        compiler_params=pltpu.CompilerParams(collective_id=collective_id, has_side_effects=True),
        cost_estimate=pl.CostEstimate(flops=0, bytes_accessed=100000000, transcendentals=0),
        name=name,
    )(*values)
    return [o.reshape((n * v.shape[0],) + v.shape[1:]) for o, v in zip(outs, values)]


class LineSum:
    def __init__(self, n, part, landing, staging, send, receive):
        self.n, self.part, self.landing, self.staging = n, part, landing, staging
        self.send, self.receive = send, receive
        self.group, self.me = lax.axis_index("group"), lax.axis_index("expert")
        self.rows = part.shape[1]
        self.tile = min(32, self.rows)

    def neighbours(self):
        left, right = (self.group, self.me - 1), (self.group, self.me + 1)
        return [(self.me > 0, left), (self.me < self.n - 1, right)]

    def copy(self, source, step, side):
        index = (side, step)
        device = (self.group, self.me + 1 if side == 0 else self.me - 1)
        return remote(
            source, self.landing.at[index], self.send.at[index], self.receive.at[index], device
        )

    def places(self):
        me, n = self.me, self.n
        for step in range(n - 1):
            for side in (0, 1):
                owner = n - 1 - step if side == 0 else step
                beyond = me < owner if side == 0 else me > owner
                edge = me == 0 if side == 0 else me == n - 1
                yield step, side, owner, beyond, edge

    def start(self):
        for step, side, owner, beyond, edge in self.places():

            @pl.when(beyond & edge)
            def _():
                self.copy(self.part.at[owner], step, side).start()

    def spans(self, body):
        def tile_body(t, carry):
            body(pl.ds(pl.multiple_of(t * self.tile, self.tile), self.tile))
            return carry

        lax.fori_loop(0, self.rows // self.tile, tile_body, 0)

    def forward(self, hop):
        me, n = self.me, self.n
        for side in (0, 1):
            step = hop - me if side == 0 else hop - (n - 1 - me)
            owner = n - 1 - step if side == 0 else step
            inner = me > 0 if side == 0 else me < n - 1
            beyond = me < owner if side == 0 else me > owner

            @pl.when(inner & (step >= 0) & beyond)
            def _():
                self.copy(self.part.at[owner], step, side).wait_recv()

                def add(span):
                    total = self.part[owner, span, :].astype(F32)
                    total = total + self.landing[side, step, span, :].astype(F32)
                    self.staging[side, step, span, :] = total.astype(BF)

                self.spans(add)
                self.copy(self.staging.at[side, step], step, side).start()

    def finish(self, out_ref):
        me, n = self.me, self.n

        @pl.when(me > 0)
        def _():
            self.copy(self.part.at[me], n - 1 - me, 0).wait_recv()

        @pl.when(me < n - 1)
        def _():
            self.copy(self.part.at[me], me, 1).wait_recv()

        def total(span):
            value = self.part[me, span, :].astype(F32)
            from_left = self.landing[0, jnp.minimum(n - 1 - me, n - 2), span, :].astype(F32)
            from_right = self.landing[1, jnp.minimum(me, n - 2), span, :].astype(F32)
            value = value + jnp.where(me > 0, from_left, 0.0)
            value = value + jnp.where(me < n - 1, from_right, 0.0)
            out_ref[span, :] = value.astype(out_ref.dtype)

        self.spans(total)
        for step, side, owner, beyond, edge in self.places():

            @pl.when(beyond)
            def _():
                self.copy(self.part.at[owner], step, side).wait_send()


def line_sum_scratch(n, rows, width):
    return [
        pltpu.VMEM((2, n - 1, rows, width), BF),
        pltpu.VMEM((2, n - 2, rows, width), BF),
        pltpu.SemaphoreType.DMA((2, n - 1)),
        pltpu.SemaphoreType.DMA((2, n - 1)),
    ]


def line_scatter_kernel(n, part_ref, out_ref, *scratch):
    line = LineSum(n, part_ref, *scratch)
    greet(line.neighbours())
    line.start()
    for hop in range(1, n - 1):
        line.forward(hop)
    line.finish(out_ref)


def line_scatter(value, n, dtype, collective_id, name):
    total, width = value.shape
    rows = total // n
    return pl.pallas_call(
        functools.partial(line_scatter_kernel, n),
        out_shape=jax.ShapeDtypeStruct((rows, width), dtype),
        in_specs=[IN_VMEM],
        out_specs=IN_VMEM,
        scratch_shapes=line_sum_scratch(n, rows, width),
        compiler_params=pltpu.CompilerParams(collective_id=collective_id, has_side_effects=True),
        cost_estimate=pl.CostEstimate(flops=0, bytes_accessed=100000000, transcendentals=0),
        name=name,
    )(value.reshape(n, rows, width))


def plane_position():
    group, me = lax.axis_index("group"), lax.axis_index("expert")
    c, x, y = group % 2, (group // 2) % 2, (group // 4) % 2
    by_c, by_x, by_y = (group + 1 - 2 * c, me), (group + 2 - 4 * x, me), (group + 4 - 8 * y, me)
    return group, me, (y, x, c), (by_y, by_x, by_c)


def weights_kernel(n, pieces, widths, *refs):
    wq, wk, wv, wo, small, extra = refs[:6]
    outs, extra_out, owns = refs[6:9], refs[9], refs[10:13]
    load, store, zsend, zrecv, psend, precv, csend, crecv, xsend, xrecv = refs[13:]
    group, me, (y, x, c), (by_y, by_x, by_c) = plane_position()
    left, right = (group, me - 1), (group, me + 1)
    eighth = owns[0].shape[0]
    span = pl.ds(pl.multiple_of((y * 4 + x * 2 + c) * eighth, eighth), eighth)
    query_width, key_width = wq.shape[1], wk.shape[1]
    targets = (
        owns[0].at[:, :query_width],
        owns[0].at[:, query_width : query_width + key_width],
        owns[0].at[:, query_width + key_width :],
        owns[1],
        owns[2],
    )
    loads = [
        pltpu.make_async_copy(source.at[span, :], target, load.at[i])
        for i, (source, target) in enumerate(zip((wq, wk, wv, wo, small), targets))
    ]
    for copy in loads:
        copy.start()
    for copy in loads:
        copy.wait()
    stores = [
        pltpu.make_async_copy(owns[i], outs[i].at[me, y, x, c], store.at[i]) for i in range(3)
    ]
    stores.append(pltpu.make_async_copy(extra, extra_out.at[me], store.at[3]))
    for copy in stores:
        copy.start()
    greet(
        [(me > 0, left), (me < n - 1, right), (None, by_c), (None, by_x), (None, by_y)]
    )

    def hop(i, step, side):
        block = me - step if side == 0 else me + step
        source = owns[i] if step == 0 else outs[i].at[block, y, x, c]
        index = (side, step, i)
        return remote(
            source,
            outs[i].at[block, y, x, c],
            zsend.at[index],
            zrecv.at[index],
            right if side == 0 else left,
        )

    def sends(step, side):
        return (me - step >= 0) & (me < n - 1) if side == 0 else (me + step < n) & (me > 0)

    def extra_hop(step, side):
        block = me - step if side == 0 else me + step
        source = extra if step == 0 else extra_out.at[block]
        return remote(
            source,
            extra_out.at[block],
            xsend.at[side, step],
            xrecv.at[side, step],
            right if side == 0 else left,
        )

    def first(slot, block, p):
        i, start, width, along_x = pieces[p]
        spot = outs[i].at[block, y, x, c, :, start : start + width]
        source = owns[i].at[:, start : start + width] if slot == 0 else spot
        index = (0, slot, p)
        return remote(source, spot, psend.at[index], precv.at[index], by_x if along_x else by_y)

    def second(slot, block, p):
        i, start, width, along_x = pieces[p]
        columns = slice(start, start + width)
        if along_x:
            spot = outs[i].at[block, y, :, c, :, columns]
        else:
            spot = outs[i].at[block, :, x, c, :, columns]
        index = (1, slot, p)
        return remote(spot, spot, psend.at[index], precv.at[index], by_y if along_x else by_x)

    def third(slot, block, i):
        spot = outs[i].at[block, :, :, c]
        index = (slot, i)
        return remote(spot, spot, csend.at[index], crecv.at[index], by_c)

    def held(step):
        if step == 0:
            return [(0, me, me >= 0)]
        return [(step, me - step, me - step >= 0), (n - 1 + step, me + step, me + step < n)]

    count = len(pieces)
    for step in range(n + 2):
        if step < n:
            for slot, block, there in held(step):

                @pl.when(there)
                def _():
                    if step > 0:
                        side = 0 if slot < n else 1
                        for i in range(3):
                            hop(i, step - 1, side).wait_recv()
                    for p in range(count):
                        first(slot, block, p).start()

            if step < n - 1:
                for side in (0, 1):

                    @pl.when(sends(step, side))
                    def _():
                        for i in range(3):
                            hop(i, step, side).start()

        if 1 <= step < n + 1:
            if step == 1:
                for copy in stores:
                    copy.wait()
            for slot, block, there in held(step - 1):

                @pl.when(there)
                def _():
                    for p in range(count):
                        first(slot, block, p).wait_recv()
                    for p in range(count):
                        second(slot, block, p).start()

        if step >= 2:
            for slot, block, there in held(step - 2):

                @pl.when(there)
                def _():
                    for p in range(count):
                        second(slot, block, p).wait_recv()
                    for i in range(3):
                        third(slot, block, i).start()

        for side in (0, 1):
            if 2 <= step < n + 1:

                @pl.when(me - step + 1 >= 0 if side == 0 else me + step - 1 < n)
                def _():
                    extra_hop(step - 2, side).wait_recv()

        for side in (0, 1):
            if 1 <= step < n:

                @pl.when(sends(step - 1, side))
                def _():
                    extra_hop(step - 1, side).start()

    for step in range(n):
        for slot, block, there in held(step):

            @pl.when(there)
            def _():
                for p in range(count):
                    first(slot, block, p).wait_send()
                    second(slot, block, p).wait_send()
                for i in range(3):
                    third(slot, block, i).wait()

        if step < n - 1:
            for side in (0, 1):

                @pl.when(sends(step, side))
                def _():
                    for i in range(3):
                        hop(i, step, side).wait_send()
                    extra_hop(step, side).wait_send()


def path_pieces(query_width, key_width, out_width, small_width):
    half = query_width + key_width
    return (
        (0, 0, half, True),
        (0, half, query_width + 2 * key_width - half, False),
        (1, 0, out_width, False),
        (2, 0, small_width, True),
    )


def gather_weights(wq, wk, wv, wo, small, extra, n, collective_id):
    rows = wq.shape[0]
    eighth = rows // 8
    widths = (wq.shape[1] + wk.shape[1] + wv.shape[1], wo.shape[1], small.shape[1])
    pieces = path_pieces(wq.shape[1], wk.shape[1], wo.shape[1], small.shape[1])
    outs = pl.pallas_call(
        functools.partial(weights_kernel, n, pieces, widths),
        out_shape=[jax.ShapeDtypeStruct((n, 2, 2, 2, eighth, w), BF) for w in widths]
        + [jax.ShapeDtypeStruct((n,) + extra.shape, BF)],
        in_specs=[ANY] * 5 + [IN_VMEM],
        out_specs=[ANY] * 4,
        scratch_shapes=[pltpu.VMEM((eighth, w), BF) for w in widths]
        + [
            pltpu.SemaphoreType.DMA((5,)),
            pltpu.SemaphoreType.DMA((4,)),
            pltpu.SemaphoreType.DMA((2, n - 1, 3)),
            pltpu.SemaphoreType.DMA((2, n - 1, 3)),
            pltpu.SemaphoreType.DMA((2, 2 * n - 1, 4)),
            pltpu.SemaphoreType.DMA((2, 2 * n - 1, 4)),
            pltpu.SemaphoreType.DMA((2 * n - 1, 3)),
            pltpu.SemaphoreType.DMA((2 * n - 1, 3)),
            pltpu.SemaphoreType.DMA((2, n - 1)),
            pltpu.SemaphoreType.DMA((2, n - 1)),
        ],
        compiler_params=pltpu.CompilerParams(collective_id=collective_id, has_side_effects=True),
        cost_estimate=pl.CostEstimate(flops=0, bytes_accessed=100000000, transcendentals=0),
        name="gather_weights",
    )(wq, wk, wv, wo, small, extra)
    weights = [o.reshape(n * rows, w) for o, w in zip(outs, widths)]
    return weights + [outs[3].reshape(-1, extra.shape[1])]


def reduce_kernel(n, pieces, *refs):
    (
        grad_q_ref,
        grad_kv_ref,
        tokens_ref,
        gain_ref,
        weight_ref,
        cosine_ref,
        sine_ref,
        mixed_ref,
        grad_attn_ref,
        grad_residual_ref,
        router_ref,
        gain_two_ref,
        residual_ref,
        y_part,
    ) = refs[:14]
    q_out, k_out, v_out, o_out, small_out, mixed_out, grad_tokens_ref = refs[14:21]
    ins, grad_pre_ref, outs, y_out = refs[21:24], refs[24], refs[25:27], refs[27]
    refs = refs[28:]
    pair, one, two, landing, staging = refs[:2], refs[2:4], refs[4:6], refs[6:8], refs[8:10]
    csend, crecv, psend, precv, zsend, zrecv, gsend, grecv = refs[10:18]
    line = LineSum(n, y_part, *refs[18:])
    group, me, (y, x, c), (by_y, by_x, by_c) = plane_position()
    left, right = (group, me - 1), (group, me + 1)
    eighth = pair[0].shape[3]
    greet(
        [(me > 0, left), (me < n - 1, right), (None, by_c), (None, by_x), (None, by_y)]
    )

    places, ends = [], [0, 0]
    for array, start, width, along_x in pieces:
        path = 0 if along_x else 1
        places.append((array, start, width, path, ends[path]))
        ends[path] += width

    def swap(p):
        array, start, width, path, at = places[p]
        return remote(
            ins[array].at[:, :, :, 1 - c, :, start : start + width],
            pair[path].at[:, :, :, :, at : at + width],
            csend.at[p],
            crecv.at[p],
            by_c,
        )

    line.start()
    D_rows = weight_ref.shape[0]
    query_width = grad_q_ref.shape[1]
    key_width = (weight_ref.shape[1] - query_width) // 2

    def put(array, columns, value):
        ins[array][:, :, :, :, :, columns] = value.astype(BF).reshape(
            ins[array].shape[:5] + (value.shape[1],)
        )

    tile = 4 * LANES
    for start in range(0, grad_attn_ref.shape[1], tile):
        columns = slice(start, start + tile)
        put(1, columns, dot_tn(mixed_ref[...], grad_attn_ref[:, columns]))
    swap(2).start()
    unit, inverse = normed(tokens_ref)
    gain = gain_ref[...]
    first_norm = (unit * gain).astype(BF)
    cosine, sine = cosine_ref[...], -sine_ref[...]
    for j in range(query_width // LANES):
        columns = slice(j * LANES, (j + 1) * LANES)
        grad_pre_ref[:, columns] = rotate(grad_q_ref[:, columns], cosine, sine).astype(BF)
    for j in range(key_width // LANES):
        start = 2 * j * LANES
        key = grad_kv_ref[:, start : start + LANES].astype(F32)
        at = query_width + j * LANES
        grad_pre_ref[:, at : at + LANES] = rotate(key, cosine, sine).astype(BF)
        at = at + key_width
        grad_pre_ref[:, at : at + LANES] = grad_kv_ref[:, start + LANES : start + 2 * LANES]
    for start in range(0, weight_ref.shape[1], tile):
        columns = slice(start, start + tile)
        put(0, columns, dot_tn(first_norm, grad_pre_ref[:, columns]))
    swap(0).start()
    swap(1).start()
    grad_first = dot_nt(grad_pre_ref[...], weight_ref[...])
    gain_one_row = jnp.sum(grad_first * unit, axis=0, keepdims=True)
    lane = lax.broadcasted_iota(jnp.int32, (LANES, D_rows), 0)
    gains = jnp.where(lane == EXPERTS, gain_one_row, 0.0)
    gains = jnp.where(lane == EXPERTS + 1, gain_two_ref[...], gains)
    put(2, slice(0, LANES), router_ref[...] + gains.T)
    swap(3).start()
    scaled = grad_first * gain
    mean = jnp.mean(scaled * unit, axis=-1, keepdims=True)
    grad_tokens_ref[...] = grad_residual_ref[...] + inverse * (scaled - unit * mean)
    for p in range(len(places)):
        swap(p).wait_recv()
        array, start, width, path, at = places[p]

        def pair_sum(t, carry):
            z, a, b = t // 4, (t // 2) % 2, t % 2
            mine = ins[array][z, a, b, c, :, start : start + width].astype(F32)
            theirs = pair[path][z, a, b, :, at : at + width].astype(F32)
            pair[path][z, a, b, :, at : at + width] = (mine + theirs).astype(BF)
            return carry

        lax.fori_loop(0, 4 * n, pair_sum, 0)

    def first(path):
        source = pair[0].at[:, :, 1 - x] if path == 0 else pair[1].at[:, 1 - y]
        return remote(
            source, one[path], psend.at[0, path], precv.at[0, path], by_x if path == 0 else by_y
        )

    def second(path):
        source = one[path].at[:, 1 - y] if path == 0 else one[path].at[:, 1 - x]
        return remote(
            source, two[path], psend.at[1, path], precv.at[1, path], by_y if path == 0 else by_x
        )

    for path in (0, 1):
        first(path).start()
    line.forward(1)
    for path in (0, 1):
        first(path).wait_recv()

        def first_sum(t, carry):
            z, a = t // 2, t % 2
            mine = pair[0][z, a, x] if path == 0 else pair[1][z, y, a]
            one[path][z, a] = (mine.astype(F32) + one[path][z, a].astype(F32)).astype(BF)
            return carry

        lax.fori_loop(0, 2 * n, first_sum, 0)
        second(path).start()
    for far in range(2, n - 1):
        line.forward(far)
    for path in (0, 1):
        second(path).wait_recv()

        def second_sum(z, carry):
            mine = one[0][z, y] if path == 0 else one[1][z, x]
            two[path][z] = (mine.astype(F32) + two[path][z].astype(F32)).astype(BF)
            return carry

        lax.fori_loop(0, n, second_sum, 0)

    def hop(source, path, step, side):
        index = (path, side, step)
        return remote(
            source,
            landing[path].at[side, step],
            zsend.at[index],
            zrecv.at[index],
            right if side == 0 else left,
        )

    for step in range(n - 1):
        for side in (0, 1):
            owner = n - 1 - step if side == 0 else step
            beyond = me < owner if side == 0 else me > owner
            edge = me == 0 if side == 0 else me == n - 1

            @pl.when(beyond & edge)
            def _():
                for path in (0, 1):
                    hop(two[path].at[owner], path, step, side).start()

    for far in range(1, n - 1):
        for side in (0, 1):
            step = far - me if side == 0 else far - (n - 1 - me)
            owner = n - 1 - step if side == 0 else step
            inner = me > 0 if side == 0 else me < n - 1
            beyond = me < owner if side == 0 else me > owner

            @pl.when(inner & (step >= 0) & beyond)
            def _():
                for path in (0, 1):
                    hop(two[path].at[owner], path, step, side).wait_recv()
                    staging[path][side, step] = (
                        two[path][owner].astype(F32) + landing[path][side, step].astype(F32)
                    ).astype(BF)
                    hop(staging[path].at[side, step], path, step, side).start()

    @pl.when(me > 0)
    def _():
        for path in (0, 1):
            hop(two[path].at[me], path, n - 1 - me, 0).wait_recv()

    @pl.when(me < n - 1)
    def _():
        for path in (0, 1):
            hop(two[path].at[me], path, me, 1).wait_recv()

    for path in (0, 1):
        total = two[path][me].astype(F32)
        from_left = landing[path][0, jnp.minimum(n - 1 - me, n - 2)].astype(F32)
        from_right = landing[path][1, jnp.minimum(me, n - 2)].astype(F32)
        total = total + jnp.where(me > 0, from_left, 0.0)
        total = total + jnp.where(me < n - 1, from_right, 0.0)
        outs[path][y, x, c] = total.astype(BF)

    def spread(path, stage):
        out = outs[path]
        if stage == 2:
            spot, device = out.at[:, :, c], by_c
        elif stage == 0:
            spot, device = out.at[y, x, c], by_x if path == 0 else by_y
        elif path == 0:
            spot, device = out.at[y, :, c], by_y
        else:
            spot, device = out.at[:, x, c], by_x
        return remote(spot, spot, gsend.at[path, stage], grecv.at[path, stage], device)

    for stage in range(3):
        for path in (0, 1):
            spread(path, stage).start()
        if stage == 0:
            line.finish(y_out)
            mixed_out[...] = (residual_ref[...] + y_out[...]).astype(BF)
        for path in (0, 1):
            spread(path, stage).wait_recv()

    flat = [out[...].reshape(-1, out.shape[4]).astype(F32) for out in outs]
    columns = ([(0, q_out), (0, k_out)], [(1, v_out), (1, o_out)], [(0, small_out)])
    starts = [0, 0]
    for path, target in itertools.chain(*columns):
        width = target.shape[1]
        target[...] = flat[path][:, starts[path] : starts[path] + width]
        starts[path] += width

    for path in (0, 1):
        for stage in range(3):
            spread(path, stage).wait_send()
        first(path).wait_send()
        second(path).wait_send()
    for p in range(len(places)):
        swap(p).wait_send()
    for step in range(n - 1):
        for side in (0, 1):
            owner = n - 1 - step if side == 0 else step
            beyond = me < owner if side == 0 else me > owner

            @pl.when(beyond)
            def _():
                for path in (0, 1):
                    hop(two[path].at[owner], path, step, side).wait_send()


def reduce_weights(
    grad_q,
    grad_kv,
    tokens,
    gain,
    weight,
    cosine,
    sine,
    mixed_low,
    grad_attn,
    grad_residual,
    grad_router,
    gain_two_row,
    residual,
    y_part,
    n,
    collective_id,
):
    rows_all, width_all = weight.shape
    query_width = grad_q.shape[1]
    key_width = (width_all - query_width) // 2
    array_widths = (width_all, grad_attn.shape[1], LANES)
    rows = rows_all // n
    eighth = rows // 8
    pieces = path_pieces(query_width, key_width, grad_attn.shape[1], LANES)
    widths = [sum(p[2] for p in pieces if p[3]), sum(p[2] for p in pieces if not p[3])]
    scratch = [pltpu.VMEM((n, 2, 2, 2, eighth, w), BF) for w in array_widths]
    scratch += [pltpu.VMEM((grad_q.shape[0], width_all), BF)]
    scratch += [pltpu.VMEM((2, 2, 2, eighth, w), BF) for w in widths]
    scratch += [pltpu.VMEM((y_part.shape[0] // n, y_part.shape[1]), F32)]
    scratch += [pltpu.VMEM((n, 2, 2, eighth, w), BF) for w in widths]
    scratch += [pltpu.VMEM((n, 2, eighth, w), BF) for w in widths]
    scratch += [pltpu.VMEM((n, eighth, w), BF) for w in widths]
    scratch += [pltpu.VMEM((2, n - 1, eighth, w), BF) for w in widths] * 2
    sems = [(4,), (4,), (2, 2), (2, 2), (2, 2, n - 1), (2, 2, n - 1), (2, 3), (2, 3)]
    y_rows = y_part.shape[0] // n
    out_widths = (query_width, key_width, key_width, grad_attn.shape[1], LANES)
    return pl.pallas_call(
        functools.partial(reduce_kernel, n, pieces),
        out_shape=[jax.ShapeDtypeStruct((rows, w), F32) for w in out_widths]
        + [jax.ShapeDtypeStruct(tokens.shape, BF), jax.ShapeDtypeStruct(tokens.shape, F32)],
        in_specs=[IN_VMEM] * 14,
        out_specs=[IN_VMEM] * 7,
        scratch_shapes=scratch
        + [pltpu.SemaphoreType.DMA(s) for s in sems]
        + line_sum_scratch(n, y_rows, y_part.shape[1]),
        compiler_params=pltpu.CompilerParams(
            collective_id=collective_id, has_side_effects=True, vmem_limit_bytes=60 * 1024 * 1024
        ),
        cost_estimate=pl.CostEstimate(flops=0, bytes_accessed=100000000, transcendentals=0),
        name="reduce_weights",
    )(
        grad_q,
        grad_kv,
        tokens,
        gain,
        weight,
        cosine,
        sine,
        mixed_low,
        grad_attn,
        grad_residual,
        grad_router,
        gain_two_row,
        residual,
        y_part.reshape(n, y_rows, y_part.shape[1]),
    )


def plane_tick(step, local):
    tick = jnp.where(step <= 2, step, jnp.where(step < local, (step + 2) // 2, step - 3))
    runs = (step <= 2) | (step >= local) | (step % 2 == 0)
    return tick, runs


def expert_kernel(sizes, plane, *refs):
    blocks, rows, local, capacity = sizes
    if plane:
        mixed_in, tokens_in, out_weight_in, gain_ref = refs[:4]
        refs = refs[4:]
    else:
        x_ref = refs[0]
        refs = refs[1:]
    ct_ref, router_t_ref, rank_all_ref = refs[:3]
    w_gate_ref, w_up_ref, w_down_ref = refs[3:6]
    y_ref, gs_ref, out_gate_ref, out_up_ref, out_down_ref = refs[6:11]
    refs = refs[11:]
    if plane:
        second_ref, residual_ref = refs[:2]
        refs = refs[2:]
    xs_ref, g_ref, rank_ref, gate_ref, dots_ref, y_sem = refs[:6]
    refs = refs[6:]
    slots = local * capacity
    step = pl.program_id(0)
    tick, ticks = plane_tick(step, local)
    me = lax.axis_index("expert")
    base = me * local
    if plane:
        stage_refs, pair_refs, one_refs, two_refs = refs[:3], refs[3:6], refs[6:10], refs[10:14]
        csend, crecv, psend, precv, qsend, qrecv = refs[14:20]
        gs_part = refs[20]
        line = LineSum(blocks, gs_part, *refs[21:25])
        x_ref, xsend, xrecv, in_sem, out_sem = refs[25:]
        group, _, (y, x, c), (by_y, by_x, by_c) = plane_position()
        half = stage_refs[2].shape[4] // 2

    def expert_id():
        return lax.broadcasted_iota(jnp.int32, (EXPERTS, rows), 0)

    def note_ranks(b):
        ranks = rank_all_ref[b].astype(F32)
        for e in range(local):
            mine = jnp.where(expert_id() == base + e, ranks, 0.0)
            rank_ref[b, e : e + 1, :] = jnp.sum(mine, axis=0, keepdims=True)

    def pick(b):
        slot_id = lax.broadcasted_iota(jnp.int32, (capacity, rows), 0).astype(F32)
        pieces = [
            jnp.where(rank_ref[b, e : e + 1, :] == slot_id, 1.0, 0.0).astype(BF)
            for e in range(local)
        ]
        return jnp.concatenate(pieces, axis=0)

    def dispatch_grads(b):
        g_ref[b] = dot(pick(b), ct_ref[b]).astype(BF)

    def dispatch_rows(b):
        logits = dot_nt(router_t_ref[...], x_ref[b])
        hot = rank_all_ref[b].astype(F32) < 200.0
        top = jnp.max(jnp.where(hot, logits, NEGATIVE_LARGE), axis=0, keepdims=True)
        weight = jnp.where(hot, jnp.exp(jnp.minimum(logits - top, 0.0)), 0.0)
        gates = weight / jnp.sum(weight, axis=0, keepdims=True)
        for e in range(local):
            mine = jnp.where(expert_id() == base + e, gates, 0.0)
            gate_ref[b, e : e + 1, :] = jnp.sum(mine, axis=0, keepdims=True)
        xs_ref[b] = dot(pick(b), x_ref[b]).astype(BF)

    if plane:
        n = blocks
        leave_second = pltpu.make_async_copy(x_ref.at[me], second_ref, out_sem.at[0])
        leave_residual = pltpu.make_async_copy(gs_ref.at[:, :D], residual_ref, out_sem.at[1])

        def hop(far, side):
            block = me - far if side == 0 else me + far
            device = (group, me + 1 if side == 0 else me - 1)
            index = (side, far)
            return remote(
                x_ref.at[block], x_ref.at[block], xsend.at[index], xrecv.at[index], device
            )

        def sends(far, side):
            if side == 0:
                return (far < n - 1) & (me - far >= 0) & (me < n - 1)
            return (far < n - 1) & (me + far < n) & (me > 0)

        def arrives(far, side):
            return me - 1 - far >= 0 if side == 0 else me + 1 + far < n

        @pl.when(step == 0)
        def _():
            loads = [
                pltpu.make_async_copy(out_weight_in, stage_refs[2].at[2:4], in_sem.at[0]),
                pltpu.make_async_copy(tokens_in, xs_ref.at[0, :rows, :], in_sem.at[1]),
                pltpu.make_async_copy(mixed_in, xs_ref.at[1, :rows, :], in_sem.at[2]),
            ]
            for copy in loads:
                copy.start()
            for b in range(blocks):
                note_ranks(b)
            for copy in loads:
                copy.wait()
            out_weight = stage_refs[2][2:4].reshape(D, D)
            residual = xs_ref[0, :rows, :].astype(F32) + dot(xs_ref[1, :rows, :], out_weight)
            inverse = lax.rsqrt(jnp.mean(residual * residual, axis=-1, keepdims=True) + EPSILON)
            x_ref[me] = (residual * inverse * gain_ref[...]).astype(BF)
            gs_ref[:, :D] = residual
            greet([(None, by_c), (None, by_x), (None, by_y)] + line.neighbours())
            for side in (0, 1):

                @pl.when(sends(0, side))
                def _():
                    hop(0, side).start()

            leave_second.start()
            leave_residual.start()
            for b in range(blocks):
                dispatch_grads(b)
            dispatch_rows(me)

            def arrived(far, carry):
                for side in (0, 1):

                    @pl.when(arrives(far, side))
                    def _():
                        hop(far, side).wait_recv()

                    @pl.when(sends(far + 1, side))
                    def _():
                        hop(far + 1, side).start()

                for side in (0, 1):

                    @pl.when(arrives(far, side))
                    def _():
                        dispatch_rows(me - 1 - far if side == 0 else me + 1 + far)

                return carry

            lax.fori_loop(0, n - 1, arrived, 0)

        @pl.when(step == 1)
        def _():
            leave_second.wait()
            leave_residual.wait()
            for far in range(n - 1):
                for side in (0, 1):

                    @pl.when(sends(far, side))
                    def _():
                        hop(far, side).wait_send()

    else:

        @pl.when(step == 0)
        def _():
            for b in range(blocks):
                note_ranks(b)
                dispatch_grads(b)
                dispatch_rows(b)

    @pl.when(step < local)
    def _():
        here = pl.ds(pl.multiple_of(step * capacity, capacity), capacity)
        xs = jnp.concatenate([xs_ref[b, here, :] for b in range(blocks)], axis=0)
        g = jnp.concatenate([g_ref[b, here, :] for b in range(blocks)], axis=0).astype(F32)
        slot_id = lax.broadcasted_iota(jnp.int32, (capacity, rows), 0).astype(F32)
        gates = []
        for b in range(blocks):
            taken = rank_ref[b, pl.ds(step, 1), :] == slot_id
            gate = jnp.where(taken, gate_ref[b, pl.ds(step, 1), :], 0.0)
            gates.append(jnp.sum(gate, axis=1, keepdims=True))
        gate_slot = jnp.concatenate(gates, axis=0)
        w_gate, w_up, w_down = w_gate_ref[0], w_up_ref[0], w_down_ref[0]
        gate_pre = dot(xs, w_gate)
        up_pre = dot(xs, w_up)
        sigmoid = jax.nn.sigmoid(gate_pre)
        silu = gate_pre * sigmoid
        activation = (silu * up_pre).astype(BF)
        expert_out = dot(activation, w_down).astype(BF).astype(F32)
        slot_dot = jnp.sum(g * expert_out, axis=1, keepdims=True)
        grad_out = (gate_slot * g).astype(BF)
        scaled_out = (gate_slot * expert_out).astype(BF)
        grad_down = dot_tn(activation, grad_out).astype(BF)
        grad_activation = dot_nt(grad_out, w_down)
        grad_gate_pre = (
            grad_activation * up_pre * sigmoid * (1.0 + gate_pre * (1.0 - sigmoid))
        ).astype(BF)
        grad_up_pre = (grad_activation * silu).astype(BF)
        grad_gate = dot_tn(xs, grad_gate_pre).astype(BF)
        grad_up = dot_tn(xs, grad_up_pre).astype(BF)
        if plane:
            for ref, value in zip(stage_refs, (grad_gate, grad_up, grad_down)):
                ref[step % STAGES] = value.reshape(ref.shape[1:])
        else:
            out_gate_ref[0], out_up_ref[0], out_down_ref[0] = grad_gate, grad_up, grad_down
        grad_in = (dot_nt(grad_gate_pre, w_gate) + dot_nt(grad_up_pre, w_up)).astype(BF)
        lane = lax.broadcasted_iota(jnp.int32, (blocks * capacity, LANES), 1)
        high = slot_dot.astype(BF).astype(F32)
        middle = (slot_dot - high).astype(BF).astype(F32)
        low = slot_dot - high - middle
        mine = base + step
        dots = jnp.where(lane == mine, high, 0.0)
        dots = jnp.where(lane == mine + EXPERTS, middle, dots)
        dots = jnp.where(lane == mine + 2 * EXPERTS, low, dots).astype(BF)
        for b in range(blocks):
            part = slice(b * capacity, (b + 1) * capacity)
            xs_ref[b, here, :] = grad_in[part]
            g_ref[b, here, :] = scaled_out[part]
            dots_ref[b, here, :] = dots[part]

    def store_y(b):
        there = pl.ds(b * rows, rows)
        return pltpu.make_async_copy(g_ref.at[b, :rows, :], y_ref.at[there, :], y_sem.at[b])

    @pl.when(step == local - 1)
    def _():
        slot_expert = lax.broadcasted_iota(jnp.int32, (EXPERTS, slots), 1) // capacity
        spread_row = lax.broadcasted_iota(jnp.int32, (EXPERTS, slots), 0)
        spread = jnp.where(spread_row == slot_expert + base, 1.0, 0.0).astype(BF)
        slot_rank = (lax.broadcasted_iota(jnp.int32, (rows, slots), 1) % capacity).astype(F32)
        for b in range(blocks):
            there = slice(b * rows, (b + 1) * rows)
            ranks = dot_tn(rank_all_ref[b], spread)
            put = jnp.where(ranks == slot_rank, 1.0, 0.0).astype(BF)
            g_ref[b, :rows, :] = dot(put, g_ref[b]).astype(BF)
            store_y(b).start()
            back = dot(put, xs_ref[b]).astype(BF), dot(put, dots_ref[b]).astype(BF)
            if plane:
                gs_part[b, :, :D], gs_part[b, :, D:] = back
            else:
                gs_ref[there, :D], gs_ref[there, D:] = back
        if plane:
            line.start()

    @pl.when(step == pl.num_programs(0) - 1)
    def _():
        for b in range(blocks):
            store_y(b).wait()

    if not plane:
        return

    gate, up, low_down, high_down = range(4)
    low_rows, high_rows = slice(0, half), slice(half, 2 * half)

    def swap(e, i):
        return remote(
            stage_refs[i].at[e % STAGES, :, :, 1 - c],
            pair_refs[i].at[e % 3],
            csend.at[e % 2, i],
            crecv.at[e % 3, i],
            by_c,
        )

    def first(e, k):
        slot = e % 3
        source = {
            gate: lambda: pair_refs[0].at[slot, :, 1 - x],
            up: lambda: pair_refs[1].at[slot, 1 - y],
            low_down: lambda: pair_refs[2].at[slot, :, 1 - x, low_rows],
            high_down: lambda: pair_refs[2].at[slot, 1 - y, :, high_rows],
        }[k]()
        device = by_x if k in (gate, low_down) else by_y
        return remote(source, one_refs[k].at[slot], psend.at[slot, k], precv.at[slot, k], device)

    def second(e, k):
        along_x = k in (gate, low_down)
        source = one_refs[k].at[e % 3, 1 - y] if along_x else one_refs[k].at[e % 3, 1 - x]
        slot = e % 2
        return remote(
            source,
            two_refs[k].at[slot],
            qsend.at[slot, k],
            qrecv.at[slot, k],
            by_y if along_x else by_x,
        )

    def add(first_value, second_value):
        return (first_value.astype(F32) + second_value.astype(F32)).astype(BF)

    @pl.when(ticks & (tick >= 3))
    def _():
        e = tick - 3
        for k in range(4):
            second(e, k).wait()
        own = [one_refs[k][e % 3, y if k in (gate, low_down) else x] for k in range(4)]
        out_gate_ref[0] = add(own[gate], two_refs[gate][e % 2])
        out_up_ref[0] = add(own[up], two_refs[up][e % 2])
        out_down_ref[0, low_rows] = add(own[low_down], two_refs[low_down][e % 2])
        out_down_ref[0, high_rows] = add(own[high_down], two_refs[high_down][e % 2])

    @pl.when(ticks & (tick >= 2) & (tick < local + 2))
    def _():
        e = tick - 2
        slot = e % 3
        for k in range(4):
            first(e, k).wait()
            for t in (0, 1):
                mine = {
                    gate: lambda: pair_refs[0][slot, t, x],
                    up: lambda: pair_refs[1][slot, y, t],
                    low_down: lambda: pair_refs[2][slot, t, x, low_rows],
                    high_down: lambda: pair_refs[2][slot, y, t, high_rows],
                }[k]()
                one_refs[k][slot, t] = add(mine, one_refs[k][slot, t])
            second(e, k).start()

    @pl.when(ticks & (tick >= 1) & (tick < local + 1))
    def _():
        e = tick - 1
        slot = e % 3
        for i in range(3):
            swap(e, i).wait()

            def pair_sum(t, carry):
                a, b = t // 2, t % 2
                pair_refs[i][slot, a, b] = add(
                    stage_refs[i][e % STAGES, a, b, c], pair_refs[i][slot, a, b]
                )
                return carry

            lax.fori_loop(0, 4, pair_sum, 0)
        for k in range(4):
            first(e, k).start()

    @pl.when(ticks & (tick < local))
    def _():
        for i in range(3):
            swap(tick, i).start()

    for hop in range(1, blocks - 1):

        @pl.when(step == local + hop)
        def _():
            line.forward(hop)

    @pl.when(step == local + blocks - 1)
    def _():
        line.finish(gs_ref)


def run_experts(
    sources, ct_all, router_t, rank_all, w_gate, w_up, w_down, capacity, plane, collective_id
):
    blocks, _, rows = rank_all.shape
    total, local = blocks * rows, w_gate.shape[0]
    slots = local * capacity
    sizes = (blocks, rows, local, capacity)
    whole = lambda shape: pl.BlockSpec(
        shape, lambda e: (0,) * len(shape), pipeline_mode=pl.Buffered(1)
    )
    per = lambda shape: pl.BlockSpec((1,) + shape, lambda e: (jnp.minimum(e, local - 1), 0, 0))
    shapes = ((D, FF), (D, FF), (FF, D))
    ct_all = ct_all.reshape(blocks, rows, D)
    scratch = [
        pltpu.VMEM((blocks, slots, D), BF),
        pltpu.VMEM((blocks, slots, D), BF),
        pltpu.VMEM((blocks, local, rows), F32),
        pltpu.VMEM((blocks, local, rows), F32),
        pltpu.VMEM((blocks, slots, LANES), BF),
        pltpu.SemaphoreType.DMA((blocks,)),
    ]
    params = dict(dimension_semantics=("arbitrary",), vmem_limit_bytes=63 * 1024 * 1024)
    if plane:
        eighths = [(a // 8, b) for a, b in shapes]
        out = lambda shape: pl.BlockSpec(
            (1,) + shape, lambda e: (jnp.maximum(plane_tick(e, local)[0] - 3, 0), 0, 0)
        )
        grad_shapes, grad_specs = eighths, [out(shape) for shape in eighths]
        low = (eighths[2][0] // 2, eighths[2][1])
        passed = (eighths[0], eighths[1], low, low)
        scratch += [pltpu.VMEM((STAGES, 2, 2, 2) + shape, BF) for shape in eighths]
        scratch += [pltpu.VMEM((3, 2, 2) + shape, BF) for shape in eighths]
        scratch += [pltpu.VMEM((3, 2) + shape, BF) for shape in passed]
        scratch += [pltpu.VMEM((2,) + shape, BF) for shape in passed]
        sems = [(2, 3), (3, 3), (3, 4), (3, 4), (2, 4), (2, 4)]
        scratch += [pltpu.SemaphoreType.DMA(shape) for shape in sems]
        scratch += [pltpu.VMEM((blocks, rows, D + LANES), BF)]
        scratch += line_sum_scratch(blocks, rows, D + LANES)
        scratch += [pltpu.VMEM((blocks, rows, D), BF)]
        sems = [(2, blocks - 1), (2, blocks - 1), (3,), (2,)]
        scratch += [pltpu.SemaphoreType.DMA(shape) for shape in sems]
        mixed_low, tokens, out_weight, gain = sources
        sources = [mixed_low, tokens, out_weight.reshape((2, 2, 2, 2) + eighths[2]), gain]
        source_specs = [ANY] * 3 + [whole(gain.shape)]
        more_shapes = [
            jax.ShapeDtypeStruct((rows, D), BF),
            jax.ShapeDtypeStruct((rows, D), F32),
        ]
        gs_shape, gs_type = (rows, D + LANES), F32
        params |= dict(collective_id=collective_id, has_side_effects=True)
    else:
        grad_shapes, grad_specs = shapes, [per(shape) for shape in shapes]
        gs_shape, gs_type = (total, D + LANES), BF
        sources = [sources[0].reshape(blocks, rows, D)]
        source_specs = [whole(sources[0].shape)]
        more_shapes = []
    flops = 2 * total * D * slots * 4 // blocks + 18 * blocks * slots * D * FF
    return pl.pallas_call(
        functools.partial(expert_kernel, sizes, plane),
        grid=(local + 6 if plane else local,),
        out_shape=[
            jax.ShapeDtypeStruct((total, D), BF),
            jax.ShapeDtypeStruct(gs_shape, gs_type),
        ]
        + [jax.ShapeDtypeStruct((local,) + shape, BF) for shape in grad_shapes]
        + more_shapes,
        in_specs=source_specs
        + [
            whole(ct_all.shape),
            whole((EXPERTS, D)),
            whole(rank_all.shape),
        ]
        + [per(shape) for shape in shapes],
        out_specs=[ANY, whole(gs_shape)] + grad_specs + [ANY] * len(more_shapes),
        scratch_shapes=scratch,
        compiler_params=pltpu.CompilerParams(**params),
        cost_estimate=pl.CostEstimate(
            flops=flops, bytes_accessed=2 * (6 * local * D * FF + 4 * total * D), transcendentals=0
        ),
        name="experts",
    )(*sources, ct_all, router_t, rank_all, w_gate, w_up, w_down)


def rotate(tile, cosine, sine):
    half = HEAD_DIMENSION // 2
    lane = lax.broadcasted_iota(jnp.int32, tile.shape, 1) % HEAD_DIMENSION
    other = jnp.where(lane < half, pltpu.roll(tile, LANES - half, 1), pltpu.roll(tile, half, 1))
    return tile * cosine + other * sine


def normed(tokens_ref):
    value = tokens_ref[...].astype(F32)
    inverse = lax.rsqrt(jnp.mean(value * value, axis=-1, keepdims=True) + EPSILON)
    return value * inverse, inverse


def mask_bias(bias_ref, length_ref, rows):
    base = lax.axis_index("expert") * rows
    key = lax.broadcasted_iota(jnp.int32, bias_ref.shape, 0)
    query = lax.broadcasted_iota(jnp.int32, bias_ref.shape, 1) + base
    allowed = (key <= query) & (key < length_ref[0])
    bias_ref[...] = jnp.where(allowed, 0.0, NEGATIVE_LARGE)


def head_columns(ref, head):
    start = 2 * HEAD_DIMENSION * head
    middle = start + HEAD_DIMENSION
    return jnp.concatenate([ref[:, start:middle], ref[:, middle : middle + HEAD_DIMENSION]], 0)


def put_heads(ref, head, transposed):
    rows = ref.shape[0]
    value = transposed.T
    start = 2 * HEAD_DIMENSION * head
    middle = start + HEAD_DIMENSION
    ref[:, start:middle] = value[:rows].astype(ref.dtype)
    ref[:, middle : middle + HEAD_DIMENSION] = value[rows:].astype(ref.dtype)


def attention_kernel(
    n,
    length_ref,
    tokens_ref,
    gain_ref,
    weight_ref,
    cosine_ref,
    sine_ref,
    rank_ref,
    mixed_ref,
    log_total_ref,
    kv_all_ref,
    query_out_ref,
    rank_all_ref,
    *scratch,
):
    bias_ref, query_ref, kv_ref, chunk_ref, rank_buffer, send, recv, rank_send, rank_recv = scratch
    pair, pairs = pl.program_id(0), pl.num_programs(0)
    group, me = lax.axis_index("group"), lax.axis_index("expert")
    left, right = (group, me - 1), (group, me + 1)
    rows, width = kv_ref.shape[1:]

    def hop(j, step, side):
        block = me - step if side == 0 else me + step
        source = kv_ref.at[j] if step == 0 else chunk_ref.at[j, block]
        index = (j, side, step)
        return remote(
            source,
            chunk_ref.at[j, block],
            send.at[index],
            recv.at[index],
            right if side == 0 else left,
        )

    def rank_hop(step, side):
        block = me - step if side == 0 else me + step
        source = rank_ref if step == 0 else rank_buffer.at[block]
        index = (side, step)
        return remote(
            source,
            rank_buffer.at[block],
            rank_send.at[index],
            rank_recv.at[index],
            right if side == 0 else left,
        )

    def sends(step, side):
        return (me - step >= 0) & (me < n - 1) if side == 0 else (me + step < n) & (me > 0)

    def arrives(step, side):
        return me - 1 - step >= 0 if side == 0 else me + 1 + step < n

    def launch(make, step):
        for side in (0, 1):

            @pl.when(sends(step, side))
            def _():
                make(step, side).start()

    def await_hop(make, step):
        for side in (0, 1):

            @pl.when(arrives(step, side))
            def _():
                make(step, side).wait_recv()

    def drain(make):
        for step in range(n - 1):
            for side in (0, 1):

                @pl.when(sends(step, side))
                def _():
                    make(step, side).wait_send()

    def chunk(j):
        return lambda step, side: hop(j, step, side)

    @pl.when(pair == 0)
    def _():
        unit, _ = normed(tokens_ref)
        first_norm = (unit * gain_ref[...]).astype(BF)
        cosine, sine = cosine_ref[...], sine_ref[...]
        count = kv_ref.shape[0]
        query_width = count * width
        key_width = query_width // 2
        keys = dot(first_norm, weight_ref[:, query_width : query_width + key_width])
        values = dot(first_norm, weight_ref[:, query_width + key_width :])
        for j in range(count):
            columns = slice(j * LANES, (j + 1) * LANES)
            kv_ref[j, :, :LANES] = rotate(keys[:, columns], cosine, sine).astype(BF)
            kv_ref[j, :, LANES:] = values[:, columns].astype(BF)
        rank_buffer[me] = rank_ref[...]
        greet([(me > 0, left), (me < n - 1, right)])
        launch(chunk(0), 0)
        launch(chunk(1), 0)
        queries = dot(first_norm, weight_ref[:, :query_width])
        for j in range(2 * count):
            start = (j % 2) * LANES
            tile = queries[:, j * LANES : (j + 1) * LANES]
            query_ref[j // 2, :, start : start + LANES] = rotate(tile, cosine, sine).astype(BF)
        mask_bias(bias_ref, length_ref, rows)
        await_hop(chunk(0), 0)
        launch(chunk(0), 1)

    for step in range(1, n - 1):
        await_hop(chunk(pair), step)
        if step < n - 2:
            launch(chunk(pair), step + 1)

    @pl.when(pair + 1 < pairs)
    def _():
        await_hop(chunk(pair + 1), 0)
        launch(chunk(pair + 1), 1)

    @pl.when(pair + 2 < pairs)
    def _():
        launch(chunk(pair + 2), 0)

    @pl.when(pair == 1)
    def _():
        launch(rank_hop, 0)

    for step in range(n - 1):

        @pl.when(pair == jnp.minimum(2 + step, pairs - 1))
        def _():
            await_hop(rank_hop, step)
            if step < n - 2:
                launch(rank_hop, step + 1)

    chunk_ref[pair, me] = kv_ref[pair]
    kv = chunk_ref[pair].reshape(n * rows, width)
    kv_all_ref[...] = kv
    query_out_ref[0] = query_ref[pair]
    bias = jnp.concatenate([bias_ref[...]] * 2, axis=1)
    for head in (0, 1):
        start = head * HEAD_DIMENSION
        key = kv[:, start : start + HEAD_DIMENSION]
        value = kv[:, LANES + start : LANES + start + HEAD_DIMENSION]
        query = head_columns(query_ref.at[pair], head) * jnp.asarray(HEAD_DIMENSION**-0.5, BF)
        scores = dot_nt(key, query) + bias
        top = jnp.max(scores, axis=0, keepdims=True)
        weights = jnp.exp(scores - top)
        total = jnp.sum(weights, axis=0, keepdims=True)
        put_heads(mixed_ref, head, dot_tn(value, weights.astype(BF)) / total)
        log_total_ref[0, head : head + 1, :] = top + jnp.log(total)

    @pl.when(pair == pairs - 1)
    def _():
        drain(rank_hop)
        rank_all_ref[...] = rank_buffer[...]
        for j in range(KEY_VALUE_HEADS // 2):
            drain(chunk(j))


def attention(length, tokens, gain, weight, cosine, sine, rank, n, collective_id):
    rows = tokens.shape[0]
    keys, width = n * rows, 2 * LANES
    pairs = KEY_VALUE_HEADS // 2
    return pl.pallas_call(
        functools.partial(attention_kernel, n),
        grid=(pairs,),
        out_shape=(
            jax.ShapeDtypeStruct((rows, pairs * width), BF),
            jax.ShapeDtypeStruct((pairs, 2, 2 * rows), F32),
            jax.ShapeDtypeStruct((keys, pairs * width), BF),
            jax.ShapeDtypeStruct((pairs, rows, width), BF),
            jax.ShapeDtypeStruct((n,) + rank.shape, rank.dtype),
        ),
        in_specs=[pl.BlockSpec(memory_space=pltpu.SMEM)] + [IN_VMEM] * 6,
        out_specs=(
            pl.BlockSpec((rows, width), lambda j: (0, j)),
            pl.BlockSpec((1, 2, 2 * rows), lambda j: (j, 0, 0)),
            pl.BlockSpec((keys, width), lambda j: (0, j)),
            pl.BlockSpec((1, rows, width), lambda j: (j, 0, 0)),
            IN_VMEM,
        ),
        scratch_shapes=[
            pltpu.VMEM((keys, rows), F32),
            pltpu.VMEM((pairs, rows, width), BF),
            pltpu.VMEM((pairs, rows, width), BF),
            pltpu.VMEM((pairs, n, rows, width), BF),
            pltpu.VMEM((n,) + rank.shape, rank.dtype),
            pltpu.SemaphoreType.DMA((pairs, 2, n - 1)),
            pltpu.SemaphoreType.DMA((pairs, 2, n - 1)),
            pltpu.SemaphoreType.DMA((2, n - 1)),
            pltpu.SemaphoreType.DMA((2, n - 1)),
        ],
        compiler_params=pltpu.CompilerParams(
            dimension_semantics=("arbitrary",),
            vmem_limit_bytes=56 * 1024 * 1024,
            collective_id=collective_id,
            has_side_effects=True,
        ),
        cost_estimate=pl.CostEstimate(
            flops=16 * rows * keys * D, bytes_accessed=100000000, transcendentals=0
        ),
        name="attention",
    )(length, tokens, gain, weight, cosine, sine, rank)


def attention_back_kernel(
    n,
    length_ref,
    q_ref,
    kv_ref,
    log_total_ref,
    gs_ref,
    residual_ref,
    second_ref,
    ct_ref,
    hot_ref,
    gain_ref,
    router_ref,
    out_weight_ref,
    grad_q_ref,
    grad_kv_ref,
    grad_residual_ref,
    grad_attn_ref,
    grad_router_ref,
    grad_gain_ref,
    bias_ref,
    grad_ref,
    terms_ref,
    landing,
    staging,
    send,
    recv,
):
    step, pairs = pl.program_id(0), pl.num_programs(0) - 1

    def line(j):
        return LineSum(
            n, terms_ref.at[j], landing.at[j], staging.at[j], send.at[j], recv.at[j]
        )

    @pl.when(step == 0)
    def _():
        greet(line(0).neighbours())
        mask_bias(bias_ref, length_ref, q_ref.shape[1])
        hot = hot_ref[...] > 0.5
        second, router = second_ref[...], router_ref[...]
        logits = dot(second, router)
        top = jnp.max(jnp.where(hot, logits, NEGATIVE_LARGE), axis=-1, keepdims=True)
        weight = jnp.where(hot, jnp.exp(jnp.minimum(logits - top, 0.0)), 0.0)
        gates = weight / jnp.sum(weight, axis=-1, keepdims=True)
        grad_gates = gs_ref[:, D : D + EXPERTS] + gs_ref[:, D + EXPERTS : D + 2 * EXPERTS]
        grad_gates = grad_gates + gs_ref[:, D + 2 * EXPERTS : D + 3 * EXPERTS]
        mean = jnp.sum(gates * grad_gates, axis=-1, keepdims=True)
        grad_logits = (gates * (grad_gates - mean)).astype(BF)
        grad_second = gs_ref[:, :D] + dot_nt(grad_logits, router)
        grad_router_ref[...] = jnp.zeros_like(grad_router_ref)
        grad_router_ref[:, :EXPERTS] = dot_tn(second, grad_logits)
        unit, inverse = normed(residual_ref)
        grad_gain_ref[...] = jnp.sum(grad_second * unit, axis=0, keepdims=True)
        scaled = grad_second * gain_ref[...]
        mean = jnp.mean(scaled * unit, axis=-1, keepdims=True)
        grad_residual = ct_ref[...].astype(F32) + inverse * (scaled - unit * mean)
        grad_residual_ref[...] = grad_residual
        grad_attn_ref[...] = grad_residual.astype(BF)
        grad_mixed = dot_nt(grad_residual.astype(BF), out_weight_ref[...]).astype(BF)
        width = grad_ref.shape[2]
        for j in range(grad_ref.shape[0]):
            grad_ref[j] = grad_mixed[:, j * width : (j + 1) * width]

    @pl.when(step < pairs)
    def _():
        attention_back_pair(
            q_ref, kv_ref, grad_ref.at[step], log_total_ref, grad_q_ref, terms_ref.at[step], bias_ref
        )
        line(step).start()

    @pl.when(step > 0)
    def _():
        for hop in range(1, n - 1):
            line(step - 1).forward(hop)
        line(step - 1).finish(grad_kv_ref)


def attention_back_pair(q_ref, kv_ref, grad_ref, log_total_ref, grad_q_ref, grad_kv_ref, bias_ref):
    scale = HEAD_DIMENSION**-0.5
    blocks, rows, _ = grad_kv_ref.shape
    q_ref = q_ref.at[0]
    bias = jnp.concatenate([bias_ref[...]] * 2, axis=1)
    for head in (0, 1):
        columns = slice(head * HEAD_DIMENSION, (head + 1) * HEAD_DIMENSION)
        key, value = kv_ref[:, :LANES][:, columns], kv_ref[:, LANES:][:, columns]
        query = head_columns(q_ref, head) * jnp.asarray(scale, BF)
        grad = head_columns(grad_ref, head)
        scores = dot_nt(key, query) + bias
        probs = jnp.exp(scores - log_total_ref[0, head : head + 1, :])
        grad_probs = dot_nt(value, grad)
        delta = jnp.sum(probs * grad_probs, axis=0, keepdims=True)
        grad_scores = (probs * (grad_probs - delta)).astype(BF)
        grad_key = dot(grad_scores, query).astype(BF).reshape(blocks, rows, HEAD_DIMENSION)
        grad_kv_ref[:, :, columns] = grad_key
        grad_value = dot(probs.astype(BF), grad).astype(BF).reshape(blocks, rows, HEAD_DIMENSION)
        start = LANES + head * HEAD_DIMENSION
        grad_kv_ref[:, :, start : start + HEAD_DIMENSION] = grad_value
        put_heads(grad_q_ref, head, dot_tn(key, grad_scores) * scale)


def attention_back(length, query, kv_all, log_total, sources, n, collective_id):
    rows, keys = query.shape[1], kv_all.shape[0]
    pairs, width = KEY_VALUE_HEADS // 2, 2 * LANES
    now = lambda j: jnp.minimum(j, pairs - 1)
    row_spec = pl.BlockSpec((rows, width), lambda j: (0, now(j)))
    return pl.pallas_call(
        functools.partial(attention_back_kernel, n),
        grid=(pairs + 1,),
        out_shape=(
            jax.ShapeDtypeStruct((rows, pairs * width), F32),
            jax.ShapeDtypeStruct((rows, pairs * width), BF),
            jax.ShapeDtypeStruct((rows, D), F32),
            jax.ShapeDtypeStruct((rows, D), BF),
            jax.ShapeDtypeStruct((D, LANES), F32),
            jax.ShapeDtypeStruct((1, D), F32),
        ),
        in_specs=[
            pl.BlockSpec(memory_space=pltpu.SMEM),
            pl.BlockSpec((1, rows, width), lambda j: (now(j), 0, 0)),
            pl.BlockSpec((keys, width), lambda j: (0, now(j))),
            pl.BlockSpec((1, 2, 2 * rows), lambda j: (now(j), 0, 0)),
        ]
        + [IN_VMEM] * len(sources),
        out_specs=(
            row_spec,
            pl.BlockSpec((rows, width), lambda j: (0, jnp.maximum(j - 1, 0))),
        )
        + (IN_VMEM,) * 4,
        scratch_shapes=[
            pltpu.VMEM((keys, rows), F32),
            pltpu.VMEM((pairs, rows, width), BF),
            pltpu.VMEM((pairs, n, rows, width), BF),
            pltpu.VMEM((pairs, 2, n - 1, rows, width), BF),
            pltpu.VMEM((pairs, 2, n - 2, rows, width), BF),
            pltpu.SemaphoreType.DMA((pairs, 2, n - 1)),
            pltpu.SemaphoreType.DMA((pairs, 2, n - 1)),
        ],
        compiler_params=pltpu.CompilerParams(
            dimension_semantics=("arbitrary",),
            vmem_limit_bytes=60 * 1024 * 1024,
            collective_id=collective_id,
            has_side_effects=True,
        ),
        cost_estimate=pl.CostEstimate(
            flops=40 * rows * keys * D, bytes_accessed=100000000, transcendentals=0
        ),
        name="attention_back",
    )(length, query, kv_all, log_total, *sources)


def widen_kernel(value_ref, out_ref):
    out_ref[...] = value_ref[...].astype(F32)


def widen(value):
    block = (1,) + value.shape[1:]
    spec = pl.BlockSpec(block, lambda e: (e, 0, 0))
    return pl.pallas_call(
        widen_kernel,
        grid=(value.shape[0],),
        out_shape=jax.ShapeDtypeStruct(value.shape, F32),
        in_specs=[spec],
        out_specs=spec,
        compiler_params=pltpu.CompilerParams(dimension_semantics=("arbitrary",)),
        cost_estimate=pl.CostEstimate(flops=0, bytes_accessed=6 * value.size, transcendentals=0),
        name="widen",
    )(value)


def unpair_columns(value):
    rows = value.shape[0]
    value = value.reshape(rows, -1, 2, LANES)
    return value[:, :, 0].reshape(rows, -1), value[:, :, 1].reshape(rows, -1)


def gather_rows(value):
    return lax.all_gather(value, "expert", axis=0, tiled=True)


def scatter_rows(value):
    return lax.psum_scatter(value, "expert", scatter_dimension=0, tiled=True)


def per_device(
    tokens,
    lengths,
    routes,
    norm_gain1,
    w_query,
    key_projection,
    value_projection,
    w_out,
    norm_gain2,
    w_router,
    w_gate,
    w_up,
    w_down,
    cotangent,
):
    rows = tokens.shape[0]
    n, groups = lax.axis_size("expert"), lax.axis_size("group")
    plane = groups == 8 and w_gate.shape[0] == 8
    my_index = lax.axis_index("expert")
    capacity = 3 * rows * TOP // (2 * EXPERTS)
    query_width, key_width = w_query.shape[1], key_projection.shape[1]
    length = lengths[0]
    positions = my_index * rows + jnp.arange(rows, dtype=jnp.int32)
    valid_rows = (positions < length)[:, None]
    grad_output = jnp.where(valid_rows, cotangent, jnp.zeros_like(cotangent))

    small = jnp.concatenate(
        [w_router, norm_gain1[:, None], norm_gain2[:, None]]
        + [jnp.zeros((w_router.shape[0], LANES - EXPERTS - 2), BF)],
        axis=1,
    )
    qkv_weight, out_weight, small, ct_all = gather_weights(
        w_query, key_projection, value_projection, w_out, small, grad_output, n, 1
    )
    router_weight = small[:, :EXPERTS]
    gain_one = small[:, EXPERTS].astype(F32)
    gain_two = small[:, EXPERTS + 1].astype(F32)

    expert_ids = jnp.arange(EXPERTS, dtype=jnp.int32)
    hot = jnp.any(routes[:, :, None] == expert_ids, axis=1)
    row_id = jnp.arange(rows, dtype=jnp.int32)
    earlier = (row_id[:, None] < row_id[None, :]).astype(BF)
    rank = jnp.where(hot.T, dot(hot.T.astype(BF), earlier), 255.0).astype(BF)

    cosine_lookup, sine_lookup = [table[:, 0] for table in rotary_tables(positions, HEAD_DIMENSION)]
    cosine = jnp.tile(cosine_lookup, (1, 4))
    sine = jnp.tile(jnp.concatenate([-sine_lookup, sine_lookup], axis=1), (1, 2))
    token_f32 = tokens.astype(F32)
    gain_one_row = gain_one[None, :]
    mixed_low, log_total, kv_all, query_pairs, rank_all = attention(
        lengths, tokens, gain_one_row, qkv_weight, cosine, sine, rank, n, 2
    )
    expert_args = (ct_all, router_weight.T, rank_all, w_gate, w_up, w_down, capacity)
    if plane:
        sources = (mixed_low, tokens, out_weight, gain_two[None, :])
        y_part, gs, grad_gate, grad_up, grad_down, second_norm, residual = run_experts(
            sources, *expert_args, plane, 7
        )
    else:
        residual = token_f32 + dot(mixed_low, out_weight)
        inverse_two = lax.rsqrt(jnp.mean(residual * residual, axis=-1, keepdims=True) + EPSILON)
        second_norm = (residual * inverse_two * gain_two).astype(BF)
        sources = line_gather([second_norm], n, 3, "gather_rows")
        y_part, gs, grad_gate, grad_up, grad_down = run_experts(sources, *expert_args, plane, 7)
        gs = line_scatter(gs, n, F32, 4, "scatter_grads")

    sources = (
        gs,
        residual,
        second_norm,
        grad_output,
        hot.astype(F32),
        gain_two[None, :],
        router_weight,
        out_weight,
    )
    grad_query_acc, kv_gradient, grad_residual, grad_attn, grad_router, gain_two_row = (
        attention_back(lengths, query_pairs, kv_all, log_total, sources, n, 5)
    )
    if plane:
        *shares, mixed, grad_tokens = reduce_weights(
            grad_query_acc,
            kv_gradient,
            tokens,
            gain_one_row,
            qkv_weight,
            cosine,
            sine,
            mixed_low,
            grad_attn,
            grad_residual,
            grad_router,
            gain_two_row,
            residual,
            y_part,
            n,
            6,
        )
    else:
        inverse_one = lax.rsqrt(jnp.mean(token_f32 * token_f32, axis=-1, keepdims=True) + EPSILON)
        unit_one = token_f32 * inverse_one
        first_norm = (unit_one * gain_one).astype(BF)
        own_key_gradient, own_value_gradient = unpair_columns(kv_gradient)
        back = lambda value: apply_rotation(
            value.astype(F32).reshape(rows, -1, HEAD_DIMENSION),
            cosine_lookup[:, None],
            -sine_lookup[:, None],
        )
        grad_query_pre = back(grad_query_acc).reshape(rows, query_width).astype(BF)
        grad_key_pre = back(own_key_gradient).reshape(rows, key_width).astype(BF)
        grad_qkv_pre = jnp.concatenate([grad_query_pre, grad_key_pre, own_value_gradient], axis=1)
        grad_first = dot_nt(grad_qkv_pre, qkv_weight)
        scaled_one = grad_first * gain_one
        grad_gain1 = jnp.sum(grad_first * unit_one, axis=0)
        grad_tokens = grad_residual + inverse_one * (
            scaled_one - unit_one * jnp.mean(scaled_one * unit_one, axis=-1, keepdims=True)
        )
        gains = [grad_gain1[:, None], gain_two_row.T]
        rest = grad_router[:, EXPERTS + 2 :]
        grad_small = jnp.concatenate([grad_router[:, :EXPERTS]] + gains + [rest], axis=1)
        shares = (dot_tn(first_norm, grad_qkv_pre), dot_tn(mixed_low, grad_attn), grad_small)
        shares = [lax.psum(scatter_rows(share.astype(BF)), "group") for share in shares]
        share_qkv, share_out, share_small = [share.astype(F32) for share in shares]
        split = (query_width, query_width + key_width)
        shares = jnp.split(share_qkv, split, axis=1) + [share_out, share_small]
        expert_sum = line_scatter(y_part, n, F32, 8, "scatter_outputs")
        mixed = (residual + expert_sum).astype(BF)
    share_query, share_key, share_value, share_out, share_small = shares

    def sum_over_groups(value):
        if not plane:
            value = lax.psum_scatter(value, "group", scatter_dimension=1, tiled=True)
        return widen(lax.all_gather(value, "group", axis=1, tiled=True))

    return (
        mixed,
        grad_tokens,
        share_small[:, EXPERTS],
        share_query,
        share_key,
        share_value,
        share_out,
        share_small[:, EXPERTS + 1],
        share_small[:, :EXPERTS],
        sum_over_groups(grad_gate),
        sum_over_groups(grad_up),
        sum_over_groups(grad_down),
    )


def solution(mesh):
    rows = P(("group", "expert"), None)
    vector, matrix, stack = P("expert"), P("expert", None), P("expert", None, None)
    return jax.shard_map(
        per_device,
        mesh=mesh,
        in_specs=(
            rows,
            P("group"),
            rows,
            vector,
            matrix,
            matrix,
            matrix,
            matrix,
            vector,
            matrix,
            stack,
            stack,
            stack,
            rows,
        ),
        out_specs=(
            rows,
            rows,
            vector,
            matrix,
            matrix,
            matrix,
            matrix,
            vector,
            matrix,
            stack,
            stack,
            stack,
        ),
        check_vma=False,
    )
```

```python
import functools
import itertools

import jax
import jax.numpy as jnp
from jax import lax
from jax.experimental import pallas as pl
from jax.experimental.pallas import tpu as pltpu
from jax.sharding import PartitionSpec as P

D = 1024
QUERY_HEADS = 16
KEY_VALUE_HEADS = 8
HEAD_DIMENSION = 64
EXPERTS = 32
TOP = 8
FF = 512
LANES = 128
STAGES = 4

EPSILON = 1e-05
NEGATIVE_LARGE = -1e30
BF = jnp.bfloat16
F32 = jnp.float32


def rotary_tables(positions, head_size):
    half_width = head_size // 2
    frequency = 10000.0 ** (-2.0 * jnp.arange(half_width).astype(F32) / head_size)
    angles = positions.astype(F32)[:, None] * frequency[None, :]
    return (jnp.cos(angles)[:, None, :], jnp.sin(angles)[:, None, :])


def apply_rotation(tensor_in, cosine_lookup, sine_lookup):
    half_width = tensor_in.shape[-1] // 2
    first_half = tensor_in[..., :half_width]
    second_half = tensor_in[..., half_width:]
    return jnp.concatenate(
        [
            first_half * cosine_lookup - second_half * sine_lookup,
            second_half * cosine_lookup + first_half * sine_lookup,
        ],
        axis=-1,
    )


def dot(a, b):
    return jnp.dot(a, b, preferred_element_type=F32)


def dot_nt(a, b):
    return lax.dot_general(a, b, (((1,), (1,)), ((), ())), preferred_element_type=F32)


def dot_tn(a, b):
    return lax.dot_general(a, b, (((0,), (0,)), ((), ())), preferred_element_type=F32)


MESH = pl.DeviceIdType.MESH
ANY = pl.BlockSpec(memory_space=pl.ANY)
IN_VMEM = pl.BlockSpec(memory_space=pltpu.VMEM)


def remote(source, target, send, receive, device):
    return pltpu.make_async_remote_copy(
        src_ref=source,
        dst_ref=target,
        send_sem=send,
        recv_sem=receive,
        device_id=device,
        device_id_type=MESH,
    )


def greet(devices):
    barrier = pltpu.get_barrier_semaphore()
    count = 0
    for condition, device in devices:
        if condition is None:
            pl.semaphore_signal(barrier, inc=1, device_id=device, device_id_type=MESH)
            count = count + 1
        else:

            @pl.when(condition)
            def _():
                pl.semaphore_signal(barrier, inc=1, device_id=device, device_id_type=MESH)

            count = count + jnp.where(condition, 1, 0)
    pl.semaphore_wait(barrier, count)


def line_gather_kernel(n, count, *refs):
    ins, outs = refs[:count], refs[count : 2 * count]
    local, send, receive = refs[2 * count :]
    group, me = lax.axis_index("group"), lax.axis_index("expert")
    left, right = (group, me - 1), (group, me + 1)
    own = [
        pltpu.make_async_copy(ins[i], outs[i].at[me], local.at[i]) for i in range(count)
    ]
    for copy in own:
        copy.start()
    greet([(me > 0, left), (me < n - 1, right)])

    def hop(i, step, side):
        block = me - step if side == 0 else me + step
        source = ins[i] if step == 0 else outs[i].at[block]
        index = (side, step, i)
        return remote(
            source, outs[i].at[block], send.at[index], receive.at[index], right if side == 0 else left
        )

    def arrival(i, step, side):
        block = me - 1 - step if side == 0 else me + 1 + step
        index = (side, step, i)
        return remote(
            outs[i].at[block], outs[i].at[block], send.at[index], receive.at[index], left if side == 0 else right
        )

    def sends(step, side):
        return (me - step >= 0) & (me < n - 1) if side == 0 else (me + step < n) & (me > 0)

    def arrives(step, side):
        return me - 1 - step >= 0 if side == 0 else me + 1 + step < n

    for step in range(n - 1):
        for side in (0, 1):

            @pl.when(sends(step, side))
            def _():
                for i in range(count):
                    hop(i, step, side).start()

        for side in (0, 1):

            @pl.when(arrives(step, side))
            def _():
                for i in range(count):
                    arrival(i, step, side).wait_recv()

    for step in range(n - 1):
        for side in (0, 1):

            @pl.when(sends(step, side))
            def _():
                for i in range(count):
                    hop(i, step, side).wait_send()

    for copy in own:
        copy.wait()


def line_gather(values, n, collective_id, name):
    count = len(values)
    outs = pl.pallas_call(
        functools.partial(line_gather_kernel, n, count),
        out_shape=[jax.ShapeDtypeStruct((n,) + v.shape, v.dtype) for v in values],
        in_specs=[IN_VMEM] * count,
        out_specs=[ANY] * count,
        scratch_shapes=[
            pltpu.SemaphoreType.DMA((count,)),
            pltpu.SemaphoreType.DMA((2, n - 1, count)),
            pltpu.SemaphoreType.DMA((2, n - 1, count)),
        ],
        compiler_params=pltpu.CompilerParams(collective_id=collective_id, has_side_effects=True),
        cost_estimate=pl.CostEstimate(flops=0, bytes_accessed=100000000, transcendentals=0),
        name=name,
    )(*values)
    return [o.reshape((n * v.shape[0],) + v.shape[1:]) for o, v in zip(outs, values)]


class LineSum:
    def __init__(self, n, part, landing, staging, send, receive):
        self.n, self.part, self.landing, self.staging = n, part, landing, staging
        self.send, self.receive = send, receive
        self.group, self.me = lax.axis_index("group"), lax.axis_index("expert")
        self.rows = part.shape[1]
        self.tile = min(32, self.rows)

    def neighbours(self):
        left, right = (self.group, self.me - 1), (self.group, self.me + 1)
        return [(self.me > 0, left), (self.me < self.n - 1, right)]

    def copy(self, source, step, side):
        index = (side, step)
        device = (self.group, self.me + 1 if side == 0 else self.me - 1)
        return remote(
            source, self.landing.at[index], self.send.at[index], self.receive.at[index], device
        )

    def places(self):
        me, n = self.me, self.n
        for step in range(n - 1):
            for side in (0, 1):
                owner = n - 1 - step if side == 0 else step
                beyond = me < owner if side == 0 else me > owner
                edge = me == 0 if side == 0 else me == n - 1
                yield step, side, owner, beyond, edge

    def start(self):
        for step, side, owner, beyond, edge in self.places():

            @pl.when(beyond & edge)
            def _():
                self.copy(self.part.at[owner], step, side).start()

    def spans(self, body):
        def tile_body(t, carry):
            body(pl.ds(pl.multiple_of(t * self.tile, self.tile), self.tile))
            return carry

        lax.fori_loop(0, self.rows // self.tile, tile_body, 0)

    def forward(self, hop):
        me, n = self.me, self.n
        for side in (0, 1):
            step = hop - me if side == 0 else hop - (n - 1 - me)
            owner = n - 1 - step if side == 0 else step
            inner = me > 0 if side == 0 else me < n - 1
            beyond = me < owner if side == 0 else me > owner

            @pl.when(inner & (step >= 0) & beyond)
            def _():
                self.copy(self.part.at[owner], step, side).wait_recv()

                def add(span):
                    total = self.part[owner, span, :].astype(F32)
                    total = total + self.landing[side, step, span, :].astype(F32)
                    self.staging[side, step, span, :] = total.astype(BF)

                self.spans(add)
                self.copy(self.staging.at[side, step], step, side).start()

    def finish(self, out_ref):
        me, n = self.me, self.n

        @pl.when(me > 0)
        def _():
            self.copy(self.part.at[me], n - 1 - me, 0).wait_recv()

        @pl.when(me < n - 1)
        def _():
            self.copy(self.part.at[me], me, 1).wait_recv()

        def total(span):
            value = self.part[me, span, :].astype(F32)
            from_left = self.landing[0, jnp.minimum(n - 1 - me, n - 2), span, :].astype(F32)
            from_right = self.landing[1, jnp.minimum(me, n - 2), span, :].astype(F32)
            value = value + jnp.where(me > 0, from_left, 0.0)
            value = value + jnp.where(me < n - 1, from_right, 0.0)
            out_ref[span, :] = value.astype(out_ref.dtype)

        self.spans(total)
        for step, side, owner, beyond, edge in self.places():

            @pl.when(beyond)
            def _():
                self.copy(self.part.at[owner], step, side).wait_send()


def line_sum_scratch(n, rows, width):
    return [
        pltpu.VMEM((2, n - 1, rows, width), BF),
        pltpu.VMEM((2, n - 2, rows, width), BF),
        pltpu.SemaphoreType.DMA((2, n - 1)),
        pltpu.SemaphoreType.DMA((2, n - 1)),
    ]


def line_scatter_kernel(n, part_ref, out_ref, *scratch):
    line = LineSum(n, part_ref, *scratch)
    greet(line.neighbours())
    line.start()
    for hop in range(1, n - 1):
        line.forward(hop)
    line.finish(out_ref)


def line_scatter(value, n, dtype, collective_id, name):
    total, width = value.shape
    rows = total // n
    return pl.pallas_call(
        functools.partial(line_scatter_kernel, n),
        out_shape=jax.ShapeDtypeStruct((rows, width), dtype),
        in_specs=[IN_VMEM],
        out_specs=IN_VMEM,
        scratch_shapes=line_sum_scratch(n, rows, width),
        compiler_params=pltpu.CompilerParams(collective_id=collective_id, has_side_effects=True),
        cost_estimate=pl.CostEstimate(flops=0, bytes_accessed=100000000, transcendentals=0),
        name=name,
    )(value.reshape(n, rows, width))


def plane_position():
    group, me = lax.axis_index("group"), lax.axis_index("expert")
    c, x, y = group % 2, (group // 2) % 2, (group // 4) % 2
    by_c, by_x, by_y = (group + 1 - 2 * c, me), (group + 2 - 4 * x, me), (group + 4 - 8 * y, me)
    return group, me, (y, x, c), (by_y, by_x, by_c)


def weights_kernel(n, pieces, widths, *refs):
    wq, wk, wv, wo, small, extra = refs[:6]
    outs, extra_out, owns = refs[6:9], refs[9], refs[10:13]
    load, store, zsend, zrecv, psend, precv, csend, crecv, xsend, xrecv = refs[13:]
    group, me, (y, x, c), (by_y, by_x, by_c) = plane_position()
    left, right = (group, me - 1), (group, me + 1)
    eighth = owns[0].shape[0]
    span = pl.ds(pl.multiple_of((y * 4 + x * 2 + c) * eighth, eighth), eighth)
    query_width, key_width = wq.shape[1], wk.shape[1]
    targets = (
        owns[0].at[:, :query_width],
        owns[0].at[:, query_width : query_width + key_width],
        owns[0].at[:, query_width + key_width :],
        owns[1],
        owns[2],
    )
    loads = [
        pltpu.make_async_copy(source.at[span, :], target, load.at[i])
        for i, (source, target) in enumerate(zip((wq, wk, wv, wo, small), targets))
    ]
    for copy in loads:
        copy.start()
    for copy in loads:
        copy.wait()
    stores = [
        pltpu.make_async_copy(owns[i], outs[i].at[me, y, x, c], store.at[i]) for i in range(3)
    ]
    stores.append(pltpu.make_async_copy(extra, extra_out.at[me], store.at[3]))
    for copy in stores:
        copy.start()
    greet(
        [(me > 0, left), (me < n - 1, right), (None, by_c), (None, by_x), (None, by_y)]
    )

    def hop(i, step, side):
        block = me - step if side == 0 else me + step
        source = owns[i] if step == 0 else outs[i].at[block, y, x, c]
        index = (side, step, i)
        return remote(
            source,
            outs[i].at[block, y, x, c],
            zsend.at[index],
            zrecv.at[index],
            right if side == 0 else left,
        )

    def sends(step, side):
        return (me - step >= 0) & (me < n - 1) if side == 0 else (me + step < n) & (me > 0)

    def extra_hop(step, side):
        block = me - step if side == 0 else me + step
        source = extra if step == 0 else extra_out.at[block]
        return remote(
            source,
            extra_out.at[block],
            xsend.at[side, step],
            xrecv.at[side, step],
            right if side == 0 else left,
        )

    def first(slot, block, p):
        i, start, width, along_x = pieces[p]
        spot = outs[i].at[block, y, x, c, :, start : start + width]
        source = owns[i].at[:, start : start + width] if slot == 0 else spot
        index = (0, slot, p)
        return remote(source, spot, psend.at[index], precv.at[index], by_x if along_x else by_y)

    def second(slot, block, p):
        i, start, width, along_x = pieces[p]
        columns = slice(start, start + width)
        if along_x:
            spot = outs[i].at[block, y, :, c, :, columns]
        else:
            spot = outs[i].at[block, :, x, c, :, columns]
        index = (1, slot, p)
        return remote(spot, spot, psend.at[index], precv.at[index], by_y if along_x else by_x)

    def third(slot, block, i):
        spot = outs[i].at[block, :, :, c]
        index = (slot, i)
        return remote(spot, spot, csend.at[index], crecv.at[index], by_c)

    def held(step):
        if step == 0:
            return [(0, me, me >= 0)]
        return [(step, me - step, me - step >= 0), (n - 1 + step, me + step, me + step < n)]

    def extra_step(far):
        for side in (0, 1):
            if far > 0:

                @pl.when(me - far >= 0 if side == 0 else me + far < n)
                def _():
                    extra_hop(far - 1, side).wait_recv()

        for side in (0, 1):
            if far < n - 1:

                @pl.when(sends(far, side))
                def _():
                    extra_hop(far, side).start()

    count = len(pieces)
    for step in range(n + 2):
        if step < n:
            for slot, block, there in held(step):

                @pl.when(there)
                def _():
                    if step > 0:
                        side = 0 if slot < n else 1
                        for i in range(3):
                            hop(i, step - 1, side).wait_recv()
                    for p in range(count):
                        first(slot, block, p).start()

            if step < n - 1:
                for side in (0, 1):

                    @pl.when(sends(step, side))
                    def _():
                        for i in range(3):
                            hop(i, step, side).start()

        if 1 <= step < n + 1:
            if step == 1:
                for copy in stores:
                    copy.wait()
            for slot, block, there in held(step - 1):

                @pl.when(there)
                def _():
                    for p in range(count):
                        first(slot, block, p).wait_recv()
                    for p in range(count):
                        second(slot, block, p).start()

        if step >= 2:
            for slot, block, there in held(step - 2):

                @pl.when(there)
                def _():
                    for p in range(count):
                        second(slot, block, p).wait_recv()
                    for i in range(3):
                        third(slot, block, i).start()

        if step == 1:
            extra_step(0)
        elif step >= n:
            extra_step(step - n + 1)
    for far in range(3, n):
        extra_step(far)

    for step in range(n):
        for slot, block, there in held(step):

            @pl.when(there)
            def _():
                for p in range(count):
                    first(slot, block, p).wait_send()
                    second(slot, block, p).wait_send()
                for i in range(3):
                    third(slot, block, i).wait()

        if step < n - 1:
            for side in (0, 1):

                @pl.when(sends(step, side))
                def _():
                    for i in range(3):
                        hop(i, step, side).wait_send()
                    extra_hop(step, side).wait_send()


def path_pieces(query_width, key_width, out_width, small_width):
    half = query_width + key_width
    return (
        (0, 0, half, True),
        (0, half, query_width + 2 * key_width - half, False),
        (1, 0, out_width, False),
        (2, 0, small_width, True),
    )


def gather_weights(wq, wk, wv, wo, small, extra, n, collective_id):
    rows = wq.shape[0]
    eighth = rows // 8
    widths = (wq.shape[1] + wk.shape[1] + wv.shape[1], wo.shape[1], small.shape[1])
    pieces = path_pieces(wq.shape[1], wk.shape[1], wo.shape[1], small.shape[1])
    outs = pl.pallas_call(
        functools.partial(weights_kernel, n, pieces, widths),
        out_shape=[jax.ShapeDtypeStruct((n, 2, 2, 2, eighth, w), BF) for w in widths]
        + [jax.ShapeDtypeStruct((n,) + extra.shape, BF)],
        in_specs=[ANY] * 5 + [IN_VMEM],
        out_specs=[ANY] * 4,
        scratch_shapes=[pltpu.VMEM((eighth, w), BF) for w in widths]
        + [
            pltpu.SemaphoreType.DMA((5,)),
            pltpu.SemaphoreType.DMA((4,)),
            pltpu.SemaphoreType.DMA((2, n - 1, 3)),
            pltpu.SemaphoreType.DMA((2, n - 1, 3)),
            pltpu.SemaphoreType.DMA((2, 2 * n - 1, 4)),
            pltpu.SemaphoreType.DMA((2, 2 * n - 1, 4)),
            pltpu.SemaphoreType.DMA((2 * n - 1, 3)),
            pltpu.SemaphoreType.DMA((2 * n - 1, 3)),
            pltpu.SemaphoreType.DMA((2, n - 1)),
            pltpu.SemaphoreType.DMA((2, n - 1)),
        ],
        compiler_params=pltpu.CompilerParams(collective_id=collective_id, has_side_effects=True),
        cost_estimate=pl.CostEstimate(flops=0, bytes_accessed=100000000, transcendentals=0),
        name="gather_weights",
    )(wq, wk, wv, wo, small, extra)
    weights = [o.reshape(n * rows, w) for o, w in zip(outs, widths)]
    return weights + [outs[3].reshape(-1, extra.shape[1])]


def reduce_kernel(n, pieces, *refs):
    (
        grad_q_ref,
        grad_kv_ref,
        tokens_ref,
        gain_ref,
        weight_ref,
        cosine_ref,
        sine_ref,
        mixed_ref,
        grad_attn_ref,
        router_ref,
        gain_two_ref,
        y_part,
    ) = refs[:12]
    outs, y_out, grad_tokens_ref = refs[12:14], refs[14], refs[15]
    ins, grad_pre_ref = refs[16:19], refs[19]
    refs = refs[20:]
    pair, one, two, landing, staging = refs[:2], refs[2:4], refs[4:6], refs[6:8], refs[8:10]
    csend, crecv, psend, precv, zsend, zrecv, gsend, grecv = refs[10:18]
    line = LineSum(n, y_part, *refs[18:])
    group, me, (y, x, c), (by_y, by_x, by_c) = plane_position()
    left, right = (group, me - 1), (group, me + 1)
    eighth = pair[0].shape[3]
    greet(
        [(me > 0, left), (me < n - 1, right), (None, by_c), (None, by_x), (None, by_y)]
    )

    places, ends = [], [0, 0]
    for array, start, width, along_x in pieces:
        path = 0 if along_x else 1
        places.append((array, start, width, path, ends[path]))
        ends[path] += width

    def swap(p):
        array, start, width, path, at = places[p]
        return remote(
            ins[array].at[:, :, :, 1 - c, :, start : start + width],
            pair[path].at[:, :, :, :, at : at + width],
            csend.at[p],
            crecv.at[p],
            by_c,
        )

    line.start()
    D_rows = weight_ref.shape[0]
    query_width = grad_q_ref.shape[1]
    key_width = (weight_ref.shape[1] - query_width) // 2

    def put(array, columns, value):
        ins[array][:, :, :, :, :, columns] = value.astype(BF).reshape(
            ins[array].shape[:5] + (value.shape[1],)
        )

    tile = 4 * LANES
    for start in range(0, grad_attn_ref.shape[1], tile):
        columns = slice(start, start + tile)
        put(1, columns, dot_tn(mixed_ref[...], grad_attn_ref[:, columns]))
    swap(2).start()
    unit, inverse = normed(tokens_ref)
    gain = gain_ref[0:1, :]
    first_norm = (unit * gain).astype(BF)
    cosine, sine = cosine_ref[...], -sine_ref[...]
    for j in range(query_width // LANES):
        columns = slice(j * LANES, (j + 1) * LANES)
        grad_pre_ref[:, columns] = rotate(grad_q_ref[:, columns], cosine, sine).astype(BF)
    for j in range(key_width // LANES):
        start = 2 * j * LANES
        key = grad_kv_ref[:, start : start + LANES].astype(F32)
        at = query_width + j * LANES
        grad_pre_ref[:, at : at + LANES] = rotate(key, cosine, sine).astype(BF)
        at = at + key_width
        grad_pre_ref[:, at : at + LANES] = grad_kv_ref[:, start + LANES : start + 2 * LANES]
    for start in range(0, weight_ref.shape[1], tile):
        columns = slice(start, start + tile)
        put(0, columns, dot_tn(first_norm, grad_pre_ref[:, columns]))
    swap(0).start()
    swap(1).start()
    grad_first = dot_nt(grad_pre_ref[...], weight_ref[...])
    gain_one_row = jnp.sum(grad_first * unit, axis=0, keepdims=True)
    lane = lax.broadcasted_iota(jnp.int32, (LANES, D_rows), 0)
    gains = jnp.where(lane == EXPERTS, gain_one_row, 0.0)
    gains = jnp.where(lane == EXPERTS + 1, gain_two_ref[...], gains)
    put(2, slice(0, LANES), router_ref[...] + gains.T)
    swap(3).start()
    scaled = grad_first * gain
    mean = jnp.mean(scaled * unit, axis=-1, keepdims=True)
    grad_tokens_ref[...] = inverse * (scaled - unit * mean)
    for p in range(len(places)):
        swap(p).wait_recv()
        array, start, width, path, at = places[p]

        def pair_sum(t, carry):
            z, a, b = t // 4, (t // 2) % 2, t % 2
            mine = ins[array][z, a, b, c, :, start : start + width].astype(F32)
            theirs = pair[path][z, a, b, :, at : at + width].astype(F32)
            pair[path][z, a, b, :, at : at + width] = (mine + theirs).astype(BF)
            return carry

        lax.fori_loop(0, 4 * n, pair_sum, 0)

    def first(path):
        source = pair[0].at[:, :, 1 - x] if path == 0 else pair[1].at[:, 1 - y]
        return remote(
            source, one[path], psend.at[0, path], precv.at[0, path], by_x if path == 0 else by_y
        )

    def second(path):
        source = one[path].at[:, 1 - y] if path == 0 else one[path].at[:, 1 - x]
        return remote(
            source, two[path], psend.at[1, path], precv.at[1, path], by_y if path == 0 else by_x
        )

    for path in (0, 1):
        first(path).start()
    line.forward(1)
    for path in (0, 1):
        first(path).wait_recv()

        def first_sum(t, carry):
            z, a = t // 2, t % 2
            mine = pair[0][z, a, x] if path == 0 else pair[1][z, y, a]
            one[path][z, a] = (mine.astype(F32) + one[path][z, a].astype(F32)).astype(BF)
            return carry

        lax.fori_loop(0, 2 * n, first_sum, 0)
        second(path).start()
    for far in range(2, n - 1):
        line.forward(far)
    for path in (0, 1):
        second(path).wait_recv()

        def second_sum(z, carry):
            mine = one[0][z, y] if path == 0 else one[1][z, x]
            two[path][z] = (mine.astype(F32) + two[path][z].astype(F32)).astype(BF)
            return carry

        lax.fori_loop(0, n, second_sum, 0)

    def hop(source, path, step, side):
        index = (path, side, step)
        return remote(
            source,
            landing[path].at[side, step],
            zsend.at[index],
            zrecv.at[index],
            right if side == 0 else left,
        )

    for step in range(n - 1):
        for side in (0, 1):
            owner = n - 1 - step if side == 0 else step
            beyond = me < owner if side == 0 else me > owner
            edge = me == 0 if side == 0 else me == n - 1

            @pl.when(beyond & edge)
            def _():
                for path in (0, 1):
                    hop(two[path].at[owner], path, step, side).start()

    for far in range(1, n - 1):
        for side in (0, 1):
            step = far - me if side == 0 else far - (n - 1 - me)
            owner = n - 1 - step if side == 0 else step
            inner = me > 0 if side == 0 else me < n - 1
            beyond = me < owner if side == 0 else me > owner

            @pl.when(inner & (step >= 0) & beyond)
            def _():
                for path in (0, 1):
                    hop(two[path].at[owner], path, step, side).wait_recv()
                    staging[path][side, step] = (
                        two[path][owner].astype(F32) + landing[path][side, step].astype(F32)
                    ).astype(BF)
                    hop(staging[path].at[side, step], path, step, side).start()

    @pl.when(me > 0)
    def _():
        for path in (0, 1):
            hop(two[path].at[me], path, n - 1 - me, 0).wait_recv()

    @pl.when(me < n - 1)
    def _():
        for path in (0, 1):
            hop(two[path].at[me], path, me, 1).wait_recv()

    for path in (0, 1):
        total = two[path][me].astype(F32)
        from_left = landing[path][0, jnp.minimum(n - 1 - me, n - 2)].astype(F32)
        from_right = landing[path][1, jnp.minimum(me, n - 2)].astype(F32)
        total = total + jnp.where(me > 0, from_left, 0.0)
        total = total + jnp.where(me < n - 1, from_right, 0.0)
        outs[path][y, x, c] = total.astype(BF)

    def spread(path, stage):
        out = outs[path]
        if stage == 2:
            spot, device = out.at[:, :, c], by_c
        elif stage == 0:
            spot, device = out.at[y, x, c], by_x if path == 0 else by_y
        elif path == 0:
            spot, device = out.at[y, :, c], by_y
        else:
            spot, device = out.at[:, x, c], by_x
        return remote(spot, spot, gsend.at[path, stage], grecv.at[path, stage], device)

    for stage in range(3):
        for path in (0, 1):
            spread(path, stage).start()
        if stage == 0:
            line.finish(y_out)
        for path in (0, 1):
            spread(path, stage).wait_recv()

    for path in (0, 1):
        for stage in range(3):
            spread(path, stage).wait_send()
        first(path).wait_send()
        second(path).wait_send()
    for p in range(len(places)):
        swap(p).wait_send()
    for step in range(n - 1):
        for side in (0, 1):
            owner = n - 1 - step if side == 0 else step
            beyond = me < owner if side == 0 else me > owner

            @pl.when(beyond)
            def _():
                for path in (0, 1):
                    hop(two[path].at[owner], path, step, side).wait_send()


def reduce_weights(
    grad_q,
    grad_kv,
    tokens,
    gain,
    weight,
    cosine,
    sine,
    mixed_low,
    grad_attn,
    grad_router,
    gain_two_row,
    y_part,
    n,
    collective_id,
):
    rows_all, width_all = weight.shape
    query_width = grad_q.shape[1]
    key_width = (width_all - query_width) // 2
    array_widths = (width_all, grad_attn.shape[1], LANES)
    rows = rows_all // n
    eighth = rows // 8
    pieces = path_pieces(query_width, key_width, grad_attn.shape[1], LANES)
    widths = [sum(p[2] for p in pieces if p[3]), sum(p[2] for p in pieces if not p[3])]
    scratch = [pltpu.VMEM((n, 2, 2, 2, eighth, w), BF) for w in array_widths]
    scratch += [pltpu.VMEM((grad_q.shape[0], width_all), BF)]
    scratch += [pltpu.VMEM((n, 2, 2, eighth, w), BF) for w in widths]
    scratch += [pltpu.VMEM((n, 2, eighth, w), BF) for w in widths]
    scratch += [pltpu.VMEM((n, eighth, w), BF) for w in widths]
    scratch += [pltpu.VMEM((2, n - 1, eighth, w), BF) for w in widths] * 2
    sems = [(4,), (4,), (2, 2), (2, 2), (2, 2, n - 1), (2, 2, n - 1), (2, 3), (2, 3)]
    y_rows = y_part.shape[0] // n
    first, second, y_sum, grad_rest = pl.pallas_call(
        functools.partial(reduce_kernel, n, pieces),
        out_shape=[jax.ShapeDtypeStruct((2, 2, 2, eighth, w), BF) for w in widths]
        + [jax.ShapeDtypeStruct(tokens.shape, F32)] * 2,
        in_specs=[IN_VMEM] * 12,
        out_specs=[IN_VMEM] * 4,
        scratch_shapes=scratch
        + [pltpu.SemaphoreType.DMA(s) for s in sems]
        + line_sum_scratch(n, y_rows, y_part.shape[1]),
        compiler_params=pltpu.CompilerParams(
            collective_id=collective_id, has_side_effects=True, vmem_limit_bytes=60 * 1024 * 1024
        ),
        cost_estimate=pl.CostEstimate(flops=0, bytes_accessed=100000000, transcendentals=0),
        name="reduce_weights",
    )(
        grad_q,
        grad_kv,
        tokens,
        gain,
        weight,
        cosine,
        sine,
        mixed_low,
        grad_attn,
        grad_router,
        gain_two_row,
        y_part.reshape(n, y_rows, y_part.shape[1]),
    )
    first, second = [o.reshape(rows, w) for o, w in zip((first, second), widths)]
    first = jnp.split(first, (query_width, query_width + key_width), axis=1)
    second = jnp.split(second, (key_width,), axis=1)
    return first[0], first[1], second[0], second[1], first[2], y_sum, grad_rest


def plane_tick(step, local):
    tick = jnp.where(step <= 2, step, jnp.where(step < local, (step + 2) // 2, step - 3))
    runs = (step <= 2) | (step >= local) | (step % 2 == 0)
    return tick, runs


def expert_kernel(sizes, plane, *refs):
    blocks, rows, local, capacity = sizes
    if plane:
        mixed_in, tokens_in, out_weight_in, gain_ref = refs[:4]
        refs = refs[4:]
    else:
        x_ref = refs[0]
        refs = refs[1:]
    ct_ref, router_ref, rank_all_ref = refs[:3]
    w_gate_ref, w_up_ref, w_down_ref = refs[3:6]
    y_ref, gs_ref, out_gate_ref, out_up_ref, out_down_ref = refs[6:11]
    refs = refs[11:]
    if plane:
        second_ref, residual_ref = refs[:2]
        refs = refs[2:]
    xs_ref, g_ref, rank_ref, gate_ref, dots_ref, y_sem = refs[:6]
    refs = refs[6:]
    slots = local * capacity
    step = pl.program_id(0)
    tick, ticks = plane_tick(step, local)
    me = lax.axis_index("expert")
    base = me * local
    if plane:
        stage_refs, pair_refs, one_refs, two_refs = refs[:3], refs[3:6], refs[6:10], refs[10:14]
        csend, crecv, psend, precv, qsend, qrecv = refs[14:20]
        gs_part = refs[20]
        line = LineSum(blocks, gs_part, *refs[21:25])
        x_ref, xsend, xrecv, in_sem, out_sem = refs[25:]
        group, _, (y, x, c), (by_y, by_x, by_c) = plane_position()
        half = stage_refs[2].shape[4] // 2

    def expert_id():
        return lax.broadcasted_iota(jnp.int32, (EXPERTS, rows), 0)

    def note_ranks(b):
        ranks = rank_all_ref[b].astype(F32)
        for e in range(local):
            mine = jnp.where(expert_id() == base + e, ranks, 0.0)
            rank_ref[b, e : e + 1, :] = jnp.sum(mine, axis=0, keepdims=True)

    def pick(b):
        slot_id = lax.broadcasted_iota(jnp.int32, (capacity, rows), 0).astype(F32)
        pieces = [
            jnp.where(rank_ref[b, e : e + 1, :] == slot_id, 1.0, 0.0).astype(BF)
            for e in range(local)
        ]
        return jnp.concatenate(pieces, axis=0)

    def dispatch_grads(b):
        g_ref[b] = dot(pick(b), ct_ref[b, :rows, :]).astype(BF)

    def dispatch_rows(b):
        logits = lax.dot_general(
            router_ref[...], x_ref[b], (((0,), (1,)), ((), ())), preferred_element_type=F32
        )[:EXPERTS]
        hot = rank_all_ref[b].astype(F32) < 200.0
        top = jnp.max(jnp.where(hot, logits, NEGATIVE_LARGE), axis=0, keepdims=True)
        weight = jnp.where(hot, jnp.exp(jnp.minimum(logits - top, 0.0)), 0.0)
        gates = weight / jnp.sum(weight, axis=0, keepdims=True)
        for e in range(local):
            mine = jnp.where(expert_id() == base + e, gates, 0.0)
            gate_ref[b, e : e + 1, :] = jnp.sum(mine, axis=0, keepdims=True)
        xs_ref[b] = dot(pick(b), x_ref[b]).astype(BF)

    if plane:
        n = blocks
        leave_second = pltpu.make_async_copy(x_ref.at[me], second_ref, out_sem.at[0])
        leave_residual = pltpu.make_async_copy(gs_ref.at[:, :D], residual_ref, out_sem.at[1])

        def hop(far, side):
            block = me - far if side == 0 else me + far
            device = (group, me + 1 if side == 0 else me - 1)
            index = (side, far)
            return remote(
                x_ref.at[block], x_ref.at[block], xsend.at[index], xrecv.at[index], device
            )

        def sends(far, side):
            if side == 0:
                return (far < n - 1) & (me - far >= 0) & (me < n - 1)
            return (far < n - 1) & (me + far < n) & (me > 0)

        def arrives(far, side):
            return me - 1 - far >= 0 if side == 0 else me + 1 + far < n

        @pl.when(step == 0)
        def _():
            loads = [
                pltpu.make_async_copy(out_weight_in, stage_refs[2].at[2:4], in_sem.at[0]),
                pltpu.make_async_copy(tokens_in, xs_ref.at[0, :rows, :], in_sem.at[1]),
                pltpu.make_async_copy(mixed_in, xs_ref.at[1, :rows, :], in_sem.at[2]),
            ]
            for copy in loads:
                copy.start()
            for b in range(blocks):
                note_ranks(b)
            for copy in loads:
                copy.wait()
            out_weight = stage_refs[2][2:4].reshape(D, D)
            residual = xs_ref[0, :rows, :].astype(F32) + dot(xs_ref[1, :rows, :], out_weight)
            inverse = lax.rsqrt(jnp.mean(residual * residual, axis=-1, keepdims=True) + EPSILON)
            x_ref[me] = (residual * inverse * gain_ref[1:2, :]).astype(BF)
            gs_ref[:, :D] = residual
            greet([(None, by_c), (None, by_x), (None, by_y)] + line.neighbours())
            for side in (0, 1):

                @pl.when(sends(0, side))
                def _():
                    hop(0, side).start()

            leave_second.start()
            leave_residual.start()
            for b in range(blocks):
                dispatch_grads(b)
            dispatch_rows(me)

            def arrived(far, carry):
                for side in (0, 1):

                    @pl.when(arrives(far, side))
                    def _():
                        hop(far, side).wait_recv()

                    @pl.when(sends(far + 1, side))
                    def _():
                        hop(far + 1, side).start()

                for side in (0, 1):

                    @pl.when(arrives(far, side))
                    def _():
                        dispatch_rows(me - 1 - far if side == 0 else me + 1 + far)

                return carry

            lax.fori_loop(0, n - 1, arrived, 0)

        @pl.when(step == 1)
        def _():
            leave_second.wait()
            leave_residual.wait()
            for far in range(n - 1):
                for side in (0, 1):

                    @pl.when(sends(far, side))
                    def _():
                        hop(far, side).wait_send()

    else:

        @pl.when(step == 0)
        def _():
            for b in range(blocks):
                note_ranks(b)
                dispatch_grads(b)
                dispatch_rows(b)

    @pl.when(step < local)
    def _():
        here = pl.ds(pl.multiple_of(step * capacity, capacity), capacity)
        xs = jnp.concatenate([xs_ref[b, here, :] for b in range(blocks)], axis=0)
        g = jnp.concatenate([g_ref[b, here, :] for b in range(blocks)], axis=0).astype(F32)
        slot_id = lax.broadcasted_iota(jnp.int32, (capacity, rows), 0).astype(F32)
        gates = []
        for b in range(blocks):
            taken = rank_ref[b, pl.ds(step, 1), :] == slot_id
            gate = jnp.where(taken, gate_ref[b, pl.ds(step, 1), :], 0.0)
            gates.append(jnp.sum(gate, axis=1, keepdims=True))
        gate_slot = jnp.concatenate(gates, axis=0)
        w_gate, w_up, w_down = w_gate_ref[0], w_up_ref[0], w_down_ref[0]
        gate_pre = dot(xs, w_gate)
        up_pre = dot(xs, w_up)
        sigmoid = jax.nn.sigmoid(gate_pre)
        silu = gate_pre * sigmoid
        activation = (silu * up_pre).astype(BF)
        expert_out = dot(activation, w_down).astype(BF).astype(F32)
        slot_dot = jnp.sum(g * expert_out, axis=1, keepdims=True)
        grad_out = (gate_slot * g).astype(BF)
        scaled_out = (gate_slot * expert_out).astype(BF)
        grad_down = dot_tn(activation, grad_out).astype(BF)
        grad_activation = dot_nt(grad_out, w_down)
        grad_gate_pre = (
            grad_activation * up_pre * sigmoid * (1.0 + gate_pre * (1.0 - sigmoid))
        ).astype(BF)
        grad_up_pre = (grad_activation * silu).astype(BF)
        grad_gate = dot_tn(xs, grad_gate_pre).astype(BF)
        grad_up = dot_tn(xs, grad_up_pre).astype(BF)
        if plane:
            for ref, value in zip(stage_refs, (grad_gate, grad_up, grad_down)):
                ref[step % STAGES] = value.reshape(ref.shape[1:])
        else:
            out_gate_ref[0], out_up_ref[0], out_down_ref[0] = grad_gate, grad_up, grad_down
        grad_in = (dot_nt(grad_gate_pre, w_gate) + dot_nt(grad_up_pre, w_up)).astype(BF)
        lane = lax.broadcasted_iota(jnp.int32, (blocks * capacity, LANES), 1)
        high = slot_dot.astype(BF).astype(F32)
        middle = (slot_dot - high).astype(BF).astype(F32)
        low = slot_dot - high - middle
        mine = base + step
        dots = jnp.where(lane == mine, high, 0.0)
        dots = jnp.where(lane == mine + EXPERTS, middle, dots)
        dots = jnp.where(lane == mine + 2 * EXPERTS, low, dots).astype(BF)
        for b in range(blocks):
            part = slice(b * capacity, (b + 1) * capacity)
            xs_ref[b, here, :] = grad_in[part]
            g_ref[b, here, :] = scaled_out[part]
            dots_ref[b, here, :] = dots[part]

    def store_y(b):
        there = pl.ds(b * rows, rows)
        return pltpu.make_async_copy(g_ref.at[b, :rows, :], y_ref.at[there, :], y_sem.at[b])

    @pl.when(step == local - 1)
    def _():
        slot_expert = lax.broadcasted_iota(jnp.int32, (EXPERTS, slots), 1) // capacity
        spread_row = lax.broadcasted_iota(jnp.int32, (EXPERTS, slots), 0)
        spread = jnp.where(spread_row == slot_expert + base, 1.0, 0.0).astype(BF)
        slot_rank = (lax.broadcasted_iota(jnp.int32, (rows, slots), 1) % capacity).astype(F32)
        for b in range(blocks):
            there = slice(b * rows, (b + 1) * rows)
            ranks = dot_tn(rank_all_ref[b], spread)
            put = jnp.where(ranks == slot_rank, 1.0, 0.0).astype(BF)
            g_ref[b, :rows, :] = dot(put, g_ref[b]).astype(BF)
            store_y(b).start()
            back = dot(put, xs_ref[b]).astype(BF), dot(put, dots_ref[b]).astype(BF)
            if plane:
                gs_part[b, :, :D], gs_part[b, :, D:] = back
            else:
                gs_ref[there, :D], gs_ref[there, D:] = back
        if plane:
            line.start()

    @pl.when(step == pl.num_programs(0) - 1)
    def _():
        for b in range(blocks):
            store_y(b).wait()

    if not plane:
        return

    gate, up, low_down, high_down = range(4)
    low_rows, high_rows = slice(0, half), slice(half, 2 * half)

    def swap(e, i):
        return remote(
            stage_refs[i].at[e % STAGES, :, :, 1 - c],
            pair_refs[i].at[e % 3],
            csend.at[e % 2, i],
            crecv.at[e % 3, i],
            by_c,
        )

    def first(e, k):
        slot = e % 3
        source = {
            gate: lambda: pair_refs[0].at[slot, :, 1 - x],
            up: lambda: pair_refs[1].at[slot, 1 - y],
            low_down: lambda: pair_refs[2].at[slot, :, 1 - x, low_rows],
            high_down: lambda: pair_refs[2].at[slot, 1 - y, :, high_rows],
        }[k]()
        device = by_x if k in (gate, low_down) else by_y
        return remote(source, one_refs[k].at[slot], psend.at[slot, k], precv.at[slot, k], device)

    def second(e, k):
        along_x = k in (gate, low_down)
        source = one_refs[k].at[e % 3, 1 - y] if along_x else one_refs[k].at[e % 3, 1 - x]
        slot = e % 2
        return remote(
            source,
            two_refs[k].at[slot],
            qsend.at[slot, k],
            qrecv.at[slot, k],
            by_y if along_x else by_x,
        )

    def add(first_value, second_value):
        return (first_value.astype(F32) + second_value.astype(F32)).astype(BF)

    @pl.when(ticks & (tick >= 3))
    def _():
        e = tick - 3
        for k in range(4):
            second(e, k).wait()
        own = [one_refs[k][e % 3, y if k in (gate, low_down) else x] for k in range(4)]
        out_gate_ref[0] = add(own[gate], two_refs[gate][e % 2])
        out_up_ref[0] = add(own[up], two_refs[up][e % 2])
        out_down_ref[0, low_rows] = add(own[low_down], two_refs[low_down][e % 2])
        out_down_ref[0, high_rows] = add(own[high_down], two_refs[high_down][e % 2])

    @pl.when(ticks & (tick >= 2) & (tick < local + 2))
    def _():
        e = tick - 2
        slot = e % 3
        for k in range(4):
            first(e, k).wait()
            for t in (0, 1):
                mine = {
                    gate: lambda: pair_refs[0][slot, t, x],
                    up: lambda: pair_refs[1][slot, y, t],
                    low_down: lambda: pair_refs[2][slot, t, x, low_rows],
                    high_down: lambda: pair_refs[2][slot, y, t, high_rows],
                }[k]()
                one_refs[k][slot, t] = add(mine, one_refs[k][slot, t])
            second(e, k).start()

    @pl.when(ticks & (tick >= 1) & (tick < local + 1))
    def _():
        e = tick - 1
        slot = e % 3
        for i in range(3):
            swap(e, i).wait()

            def pair_sum(t, carry):
                a, b = t // 2, t % 2
                pair_refs[i][slot, a, b] = add(
                    stage_refs[i][e % STAGES, a, b, c], pair_refs[i][slot, a, b]
                )
                return carry

            lax.fori_loop(0, 4, pair_sum, 0)
        for k in range(4):
            first(e, k).start()

    @pl.when(ticks & (tick < local))
    def _():
        for i in range(3):
            swap(tick, i).start()

    for hop in range(1, blocks - 1):

        @pl.when(step == local + hop)
        def _():
            line.forward(hop)

    @pl.when(step == local + blocks - 1)
    def _():
        line.finish(gs_ref)


def run_experts(
    sources, ct_all, router, rank_all, w_gate, w_up, w_down, capacity, plane, collective_id
):
    blocks, _, rows = rank_all.shape
    total, local = blocks * rows, w_gate.shape[0]
    slots = local * capacity
    sizes = (blocks, rows, local, capacity)
    whole = lambda shape: pl.BlockSpec(
        shape, lambda e: (0,) * len(shape), pipeline_mode=pl.Buffered(1)
    )
    per = lambda shape: pl.BlockSpec((1,) + shape, lambda e: (jnp.minimum(e, local - 1), 0, 0))
    shapes = ((D, FF), (D, FF), (FF, D))
    scratch = [
        pltpu.VMEM((blocks, slots, D), BF),
        pltpu.VMEM((blocks, slots, D), BF),
        pltpu.VMEM((blocks, local, rows), F32),
        pltpu.VMEM((blocks, local, rows), F32),
        pltpu.VMEM((blocks, slots, LANES), BF),
        pltpu.SemaphoreType.DMA((blocks,)),
    ]
    params = dict(dimension_semantics=("arbitrary",), vmem_limit_bytes=63 * 1024 * 1024)
    if plane:
        eighths = [(a // 8, b) for a, b in shapes]
        out = lambda shape: pl.BlockSpec(
            (1,) + shape, lambda e: (jnp.maximum(plane_tick(e, local)[0] - 3, 0), 0, 0)
        )
        grad_shapes, grad_specs = eighths, [out(shape) for shape in eighths]
        low = (eighths[2][0] // 2, eighths[2][1])
        passed = (eighths[0], eighths[1], low, low)
        scratch += [pltpu.VMEM((STAGES, 2, 2, 2) + shape, BF) for shape in eighths]
        scratch += [pltpu.VMEM((3, 2, 2) + shape, BF) for shape in eighths]
        scratch += [pltpu.VMEM((3, 2) + shape, BF) for shape in passed]
        scratch += [pltpu.VMEM((2,) + shape, BF) for shape in passed]
        sems = [(2, 3), (3, 3), (3, 4), (3, 4), (2, 4), (2, 4)]
        scratch += [pltpu.SemaphoreType.DMA(shape) for shape in sems]
        scratch += [pltpu.VMEM((blocks, rows, D + LANES), BF)]
        scratch += line_sum_scratch(blocks, rows, D + LANES)
        scratch += [pltpu.VMEM((blocks, rows, D), BF)]
        sems = [(2, blocks - 1), (2, blocks - 1), (3,), (2,)]
        scratch += [pltpu.SemaphoreType.DMA(shape) for shape in sems]
        mixed_low, tokens, out_weight, gain = sources
        sources = [mixed_low, tokens, out_weight.reshape((2, 2, 2, 2) + eighths[2]), gain]
        source_specs = [ANY] * 3 + [whole(gain.shape)]
        more_shapes = [
            jax.ShapeDtypeStruct((rows, D), BF),
            jax.ShapeDtypeStruct((rows, D), F32),
        ]
        gs_shape, gs_type = (rows, D + LANES), F32
        params |= dict(collective_id=collective_id, has_side_effects=True)
    else:
        grad_shapes, grad_specs = shapes, [per(shape) for shape in shapes]
        gs_shape, gs_type = (total, D + LANES), BF
        sources = [sources[0].reshape(blocks, rows, D)]
        source_specs = [whole(sources[0].shape)]
        more_shapes = []
    flops = 2 * total * D * slots * 4 // blocks + 18 * blocks * slots * D * FF
    return pl.pallas_call(
        functools.partial(expert_kernel, sizes, plane),
        grid=(local + 6 if plane else local,),
        out_shape=[
            jax.ShapeDtypeStruct((total, D), BF),
            jax.ShapeDtypeStruct(gs_shape, gs_type),
        ]
        + [jax.ShapeDtypeStruct((local,) + shape, BF) for shape in grad_shapes]
        + more_shapes,
        in_specs=source_specs
        + [
            whole(ct_all.shape),
            whole(router.shape),
            whole(rank_all.shape),
        ]
        + [per(shape) for shape in shapes],
        out_specs=[ANY, whole(gs_shape)] + grad_specs + [ANY] * len(more_shapes),
        scratch_shapes=scratch,
        compiler_params=pltpu.CompilerParams(**params),
        cost_estimate=pl.CostEstimate(
            flops=flops, bytes_accessed=2 * (6 * local * D * FF + 4 * total * D), transcendentals=0
        ),
        name="experts",
    )(*sources, ct_all, router, rank_all, w_gate, w_up, w_down)


def rotate(tile, cosine, sine):
    half = HEAD_DIMENSION // 2
    lane = lax.broadcasted_iota(jnp.int32, tile.shape, 1) % HEAD_DIMENSION
    other = jnp.where(lane < half, pltpu.roll(tile, LANES - half, 1), pltpu.roll(tile, half, 1))
    return tile * cosine + other * sine


def normed(tokens_ref):
    value = tokens_ref[...].astype(F32)
    inverse = lax.rsqrt(jnp.mean(value * value, axis=-1, keepdims=True) + EPSILON)
    return value * inverse, inverse


def mask_bias(bias_ref, length_ref, rows):
    base = lax.axis_index("expert") * rows
    key = lax.broadcasted_iota(jnp.int32, bias_ref.shape, 0)
    query = lax.broadcasted_iota(jnp.int32, bias_ref.shape, 1) + base
    allowed = (key <= query) & (key < length_ref[0])
    bias_ref[...] = jnp.where(allowed, 0.0, NEGATIVE_LARGE)


def head_columns(ref, head):
    start = 2 * HEAD_DIMENSION * head
    middle = start + HEAD_DIMENSION
    return jnp.concatenate([ref[:, start:middle], ref[:, middle : middle + HEAD_DIMENSION]], 0)


def put_heads(ref, head, transposed):
    rows = ref.shape[0]
    value = transposed.T
    start = 2 * HEAD_DIMENSION * head
    middle = start + HEAD_DIMENSION
    ref[:, start:middle] = value[:rows].astype(ref.dtype)
    ref[:, middle : middle + HEAD_DIMENSION] = value[rows:].astype(ref.dtype)


def attention_kernel(
    n,
    length_ref,
    tokens_ref,
    gain_ref,
    weight_ref,
    cosine_ref,
    sine_ref,
    routes_ref,
    mixed_ref,
    log_total_ref,
    kv_all_ref,
    query_out_ref,
    rank_all_ref,
    *scratch,
):
    bias_ref, query_ref, kv_ref, chunk_ref, rank_buffer, send, recv, rank_send, rank_recv = scratch
    pair, pairs = pl.program_id(0), pl.num_programs(0)
    group, me = lax.axis_index("group"), lax.axis_index("expert")
    left, right = (group, me - 1), (group, me + 1)
    rows, width = kv_ref.shape[1:]

    def hop(j, step, side):
        block = me - step if side == 0 else me + step
        source = kv_ref.at[j] if step == 0 else chunk_ref.at[j, block]
        index = (j, side, step)
        return remote(
            source,
            chunk_ref.at[j, block],
            send.at[index],
            recv.at[index],
            right if side == 0 else left,
        )

    def rank_hop(step, side):
        block = me - step if side == 0 else me + step
        source = rank_buffer.at[block]
        index = (side, step)
        return remote(
            source,
            rank_buffer.at[block],
            rank_send.at[index],
            rank_recv.at[index],
            right if side == 0 else left,
        )

    def sends(step, side):
        return (me - step >= 0) & (me < n - 1) if side == 0 else (me + step < n) & (me > 0)

    def arrives(step, side):
        return me - 1 - step >= 0 if side == 0 else me + 1 + step < n

    def launch(make, step):
        for side in (0, 1):

            @pl.when(sends(step, side))
            def _():
                make(step, side).start()

    def await_hop(make, step):
        for side in (0, 1):

            @pl.when(arrives(step, side))
            def _():
                make(step, side).wait_recv()

    def drain(make):
        for step in range(n - 1):
            for side in (0, 1):

                @pl.when(sends(step, side))
                def _():
                    make(step, side).wait_send()

    def chunk(j):
        return lambda step, side: hop(j, step, side)

    @pl.when(pair == 0)
    def _():
        unit, _ = normed(tokens_ref)
        first_norm = (unit * gain_ref[0:1, :]).astype(BF)
        cosine, sine = cosine_ref[...], sine_ref[...]
        count = kv_ref.shape[0]
        query_width = count * width
        key_width = query_width // 2
        keys = dot(first_norm, weight_ref[:, query_width : query_width + key_width])
        values = dot(first_norm, weight_ref[:, query_width + key_width :])
        for j in range(count):
            columns = slice(j * LANES, (j + 1) * LANES)
            kv_ref[j, :, :LANES] = rotate(keys[:, columns], cosine, sine).astype(BF)
            kv_ref[j, :, LANES:] = values[:, columns].astype(BF)
        greet([(me > 0, left), (me < n - 1, right)])
        launch(chunk(0), 0)
        launch(chunk(1), 0)
        routes = routes_ref[...].astype(F32).T
        expert_id = lax.broadcasted_iota(jnp.int32, (EXPERTS, rows), 0).astype(F32)
        hot = jnp.zeros((EXPERTS, rows), F32)
        for k in range(TOP):
            hot = jnp.where(routes[k : k + 1, :] == expert_id, 1.0, hot)
        row_id = lax.broadcasted_iota(jnp.int32, (rows, rows), 0)
        earlier = jnp.where(row_id < lax.broadcasted_iota(jnp.int32, (rows, rows), 1), 1.0, 0.0)
        rank = dot(hot.astype(BF), earlier.astype(BF))
        rank_buffer[me] = jnp.where(hot > 0.5, rank, 255.0).astype(BF)
        queries = dot(first_norm, weight_ref[:, :query_width])
        for j in range(2 * count):
            start = (j % 2) * LANES
            tile = queries[:, j * LANES : (j + 1) * LANES]
            query_ref[j // 2, :, start : start + LANES] = rotate(tile, cosine, sine).astype(BF)
        mask_bias(bias_ref, length_ref, rows)
        await_hop(chunk(0), 0)
        launch(chunk(0), 1)

    for step in range(1, n - 1):
        await_hop(chunk(pair), step)
        if step < n - 2:
            launch(chunk(pair), step + 1)

    @pl.when(pair + 1 < pairs)
    def _():
        await_hop(chunk(pair + 1), 0)
        launch(chunk(pair + 1), 1)

    @pl.when(pair + 2 < pairs)
    def _():
        launch(chunk(pair + 2), 0)

    @pl.when(pair == 1)
    def _():
        launch(rank_hop, 0)

    for step in range(n - 1):

        @pl.when(pair == jnp.minimum(2 + step, pairs - 1))
        def _():
            await_hop(rank_hop, step)
            if step < n - 2:
                launch(rank_hop, step + 1)

    chunk_ref[pair, me] = kv_ref[pair]
    kv = chunk_ref[pair].reshape(n * rows, width)
    kv_all_ref[...] = kv
    query_out_ref[0] = query_ref[pair]
    bias = jnp.concatenate([bias_ref[...]] * 2, axis=1)
    for head in (0, 1):
        start = head * HEAD_DIMENSION
        key = kv[:, start : start + HEAD_DIMENSION]
        value = kv[:, LANES + start : LANES + start + HEAD_DIMENSION]
        query = head_columns(query_ref.at[pair], head) * jnp.asarray(HEAD_DIMENSION**-0.5, BF)
        scores = dot_nt(key, query) + bias
        top = jnp.max(scores, axis=0, keepdims=True)
        weights = jnp.exp(scores - top)
        total = jnp.sum(weights, axis=0, keepdims=True)
        put_heads(mixed_ref, head, dot_tn(value, weights.astype(BF)) / total)
        log_total_ref[0, head : head + 1, :] = top + jnp.log(total)

    @pl.when(pair == pairs - 1)
    def _():
        drain(rank_hop)
        rank_all_ref[...] = rank_buffer[...]
        for j in range(KEY_VALUE_HEADS // 2):
            drain(chunk(j))


def attention(length, tokens, gain, weight, cosine, sine, routes, n, collective_id):
    rows = tokens.shape[0]
    rank = jax.ShapeDtypeStruct((EXPERTS, rows), BF)
    keys, width = n * rows, 2 * LANES
    pairs = KEY_VALUE_HEADS // 2
    return pl.pallas_call(
        functools.partial(attention_kernel, n),
        grid=(pairs,),
        out_shape=(
            jax.ShapeDtypeStruct((rows, pairs * width), BF),
            jax.ShapeDtypeStruct((pairs, 2, 2 * rows), F32),
            jax.ShapeDtypeStruct((keys, pairs * width), BF),
            jax.ShapeDtypeStruct((pairs, rows, width), BF),
            jax.ShapeDtypeStruct((n,) + rank.shape, rank.dtype),
        ),
        in_specs=[pl.BlockSpec(memory_space=pltpu.SMEM)] + [IN_VMEM] * 6,
        out_specs=(
            pl.BlockSpec((rows, width), lambda j: (0, j)),
            pl.BlockSpec((1, 2, 2 * rows), lambda j: (j, 0, 0)),
            pl.BlockSpec((keys, width), lambda j: (0, j)),
            pl.BlockSpec((1, rows, width), lambda j: (j, 0, 0)),
            IN_VMEM,
        ),
        scratch_shapes=[
            pltpu.VMEM((keys, rows), F32),
            pltpu.VMEM((pairs, rows, width), BF),
            pltpu.VMEM((pairs, rows, width), BF),
            pltpu.VMEM((pairs, n, rows, width), BF),
            pltpu.VMEM((n,) + rank.shape, rank.dtype),
            pltpu.SemaphoreType.DMA((pairs, 2, n - 1)),
            pltpu.SemaphoreType.DMA((pairs, 2, n - 1)),
            pltpu.SemaphoreType.DMA((2, n - 1)),
            pltpu.SemaphoreType.DMA((2, n - 1)),
        ],
        compiler_params=pltpu.CompilerParams(
            dimension_semantics=("arbitrary",),
            vmem_limit_bytes=56 * 1024 * 1024,
            collective_id=collective_id,
            has_side_effects=True,
        ),
        cost_estimate=pl.CostEstimate(
            flops=16 * rows * keys * D, bytes_accessed=100000000, transcendentals=0
        ),
        name="attention",
    )(length, tokens, gain, weight, cosine, sine, routes)


def attention_back_kernel(
    n,
    length_ref,
    q_ref,
    kv_ref,
    log_total_ref,
    gs_ref,
    residual_ref,
    second_ref,
    ct_ref,
    routes_ref,
    gain_ref,
    router_ref,
    out_weight_ref,
    grad_q_ref,
    grad_kv_ref,
    grad_residual_ref,
    grad_attn_ref,
    grad_router_ref,
    grad_gain_ref,
    bias_ref,
    grad_ref,
    terms_ref,
    landing,
    staging,
    send,
    recv,
):
    step, pairs = pl.program_id(0), pl.num_programs(0) - 1

    def line(j):
        return LineSum(
            n, terms_ref.at[j], landing.at[j], staging.at[j], send.at[j], recv.at[j]
        )

    @pl.when(step == 0)
    def _():
        greet(line(0).neighbours())
        mask_bias(bias_ref, length_ref, q_ref.shape[1])
        routes = routes_ref[...]
        expert_id = lax.broadcasted_iota(jnp.int32, (routes.shape[0], EXPERTS), 1)
        hot = expert_id == routes[:, 0:1]
        for k in range(1, TOP):
            hot = hot | (expert_id == routes[:, k : k + 1])
        second, router = second_ref[...], router_ref[:, :EXPERTS]
        logits = dot(second, router)
        top = jnp.max(jnp.where(hot, logits, NEGATIVE_LARGE), axis=-1, keepdims=True)
        weight = jnp.where(hot, jnp.exp(jnp.minimum(logits - top, 0.0)), 0.0)
        gates = weight / jnp.sum(weight, axis=-1, keepdims=True)
        grad_gates = gs_ref[:, D : D + EXPERTS] + gs_ref[:, D + EXPERTS : D + 2 * EXPERTS]
        grad_gates = grad_gates + gs_ref[:, D + 2 * EXPERTS : D + 3 * EXPERTS]
        mean = jnp.sum(gates * grad_gates, axis=-1, keepdims=True)
        grad_logits = (gates * (grad_gates - mean)).astype(BF)
        grad_second = gs_ref[:, :D] + dot_nt(grad_logits, router)
        grad_router_ref[...] = jnp.zeros_like(grad_router_ref)
        grad_router_ref[:, :EXPERTS] = dot_tn(second, grad_logits)
        unit, inverse = normed(residual_ref)
        grad_gain_ref[...] = jnp.sum(grad_second * unit, axis=0, keepdims=True)
        scaled = grad_second * gain_ref[1:2, :]
        mean = jnp.mean(scaled * unit, axis=-1, keepdims=True)
        grad_residual = ct_ref[...].astype(F32) + inverse * (scaled - unit * mean)
        grad_residual_ref[...] = grad_residual
        grad_attn_ref[...] = grad_residual.astype(BF)
        grad_mixed = dot_nt(grad_residual.astype(BF), out_weight_ref[...]).astype(BF)
        width = grad_ref.shape[2]
        for j in range(grad_ref.shape[0]):
            grad_ref[j] = grad_mixed[:, j * width : (j + 1) * width]

    @pl.when(step < pairs)
    def _():
        attention_back_pair(
            q_ref, kv_ref, grad_ref.at[step], log_total_ref, grad_q_ref, terms_ref.at[step], bias_ref
        )
        line(step).start()

    @pl.when(step > 0)
    def _():
        for hop in range(1, n - 1):
            line(step - 1).forward(hop)
        line(step - 1).finish(grad_kv_ref)


def attention_back_pair(q_ref, kv_ref, grad_ref, log_total_ref, grad_q_ref, grad_kv_ref, bias_ref):
    scale = HEAD_DIMENSION**-0.5
    blocks, rows, _ = grad_kv_ref.shape
    q_ref = q_ref.at[0]
    bias = jnp.concatenate([bias_ref[...]] * 2, axis=1)
    for head in (0, 1):
        columns = slice(head * HEAD_DIMENSION, (head + 1) * HEAD_DIMENSION)
        key, value = kv_ref[:, :LANES][:, columns], kv_ref[:, LANES:][:, columns]
        query = head_columns(q_ref, head) * jnp.asarray(scale, BF)
        grad = head_columns(grad_ref, head)
        scores = dot_nt(key, query) + bias
        probs = jnp.exp(scores - log_total_ref[0, head : head + 1, :])
        grad_probs = dot_nt(value, grad)
        delta = jnp.sum(probs * grad_probs, axis=0, keepdims=True)
        grad_scores = (probs * (grad_probs - delta)).astype(BF)
        grad_key = dot(grad_scores, query).astype(BF).reshape(blocks, rows, HEAD_DIMENSION)
        grad_kv_ref[:, :, columns] = grad_key
        grad_value = dot(probs.astype(BF), grad).astype(BF).reshape(blocks, rows, HEAD_DIMENSION)
        start = LANES + head * HEAD_DIMENSION
        grad_kv_ref[:, :, start : start + HEAD_DIMENSION] = grad_value
        put_heads(grad_q_ref, head, dot_tn(key, grad_scores) * scale)


def attention_back(length, query, kv_all, log_total, sources, n, collective_id):
    rows, keys = query.shape[1], kv_all.shape[0]
    pairs, width = KEY_VALUE_HEADS // 2, 2 * LANES
    now = lambda j: jnp.minimum(j, pairs - 1)
    row_spec = pl.BlockSpec((rows, width), lambda j: (0, now(j)))
    return pl.pallas_call(
        functools.partial(attention_back_kernel, n),
        grid=(pairs + 1,),
        out_shape=(
            jax.ShapeDtypeStruct((rows, pairs * width), F32),
            jax.ShapeDtypeStruct((rows, pairs * width), BF),
            jax.ShapeDtypeStruct((rows, D), F32),
            jax.ShapeDtypeStruct((rows, D), BF),
            jax.ShapeDtypeStruct((D, LANES), F32),
            jax.ShapeDtypeStruct((1, D), F32),
        ),
        in_specs=[
            pl.BlockSpec(memory_space=pltpu.SMEM),
            pl.BlockSpec((1, rows, width), lambda j: (now(j), 0, 0)),
            pl.BlockSpec((keys, width), lambda j: (0, now(j))),
            pl.BlockSpec((1, 2, 2 * rows), lambda j: (now(j), 0, 0)),
        ]
        + [IN_VMEM] * len(sources),
        out_specs=(
            row_spec,
            pl.BlockSpec((rows, width), lambda j: (0, jnp.maximum(j - 1, 0))),
        )
        + (IN_VMEM,) * 4,
        scratch_shapes=[
            pltpu.VMEM((keys, rows), F32),
            pltpu.VMEM((pairs, rows, width), BF),
            pltpu.VMEM((pairs, n, rows, width), BF),
            pltpu.VMEM((pairs, 2, n - 1, rows, width), BF),
            pltpu.VMEM((pairs, 2, n - 2, rows, width), BF),
            pltpu.SemaphoreType.DMA((pairs, 2, n - 1)),
            pltpu.SemaphoreType.DMA((pairs, 2, n - 1)),
        ],
        compiler_params=pltpu.CompilerParams(
            dimension_semantics=("arbitrary",),
            vmem_limit_bytes=60 * 1024 * 1024,
            collective_id=collective_id,
            has_side_effects=True,
        ),
        cost_estimate=pl.CostEstimate(
            flops=40 * rows * keys * D, bytes_accessed=100000000, transcendentals=0
        ),
        name="attention_back",
    )(length, query, kv_all, log_total, *sources)


def widen_kernel(value_ref, out_ref):
    out_ref[...] = value_ref[...].astype(F32)


def widen(value):
    block = (1,) + value.shape[1:]
    spec = pl.BlockSpec(block, lambda e: (e, 0, 0))
    return pl.pallas_call(
        widen_kernel,
        grid=(value.shape[0],),
        out_shape=jax.ShapeDtypeStruct(value.shape, F32),
        in_specs=[spec],
        out_specs=spec,
        compiler_params=pltpu.CompilerParams(dimension_semantics=("arbitrary",)),
        cost_estimate=pl.CostEstimate(flops=0, bytes_accessed=6 * value.size, transcendentals=0),
        name="widen",
    )(value)


def unpair_columns(value):
    rows = value.shape[0]
    value = value.reshape(rows, -1, 2, LANES)
    return value[:, :, 0].reshape(rows, -1), value[:, :, 1].reshape(rows, -1)


def gather_rows(value):
    return lax.all_gather(value, "expert", axis=0, tiled=True)


def scatter_rows(value):
    return lax.psum_scatter(value, "expert", scatter_dimension=0, tiled=True)


def per_device(
    tokens,
    lengths,
    routes,
    norm_gain1,
    w_query,
    key_projection,
    value_projection,
    w_out,
    norm_gain2,
    w_router,
    w_gate,
    w_up,
    w_down,
    cotangent,
):
    rows = tokens.shape[0]
    n, groups = lax.axis_size("expert"), lax.axis_size("group")
    plane = groups == 8 and w_gate.shape[0] == 8
    my_index = lax.axis_index("expert")
    capacity = 3 * rows * TOP // (2 * EXPERTS)
    query_width, key_width = w_query.shape[1], key_projection.shape[1]
    length = lengths[0]
    positions = my_index * rows + jnp.arange(rows, dtype=jnp.int32)
    valid_rows = (positions < length)[:, None]
    grad_output = jnp.where(valid_rows, cotangent, jnp.zeros_like(cotangent))

    small = jnp.pad(w_router, ((0, 0), (0, LANES - EXPERTS)))
    gains = jnp.pad(jnp.concatenate([norm_gain1, norm_gain2]), (0, D - 2 * norm_gain1.shape[0]))
    below = jnp.broadcast_to(gains, (16, D))
    qkv_weight, out_weight, router, extra_all = gather_weights(
        w_query,
        key_projection,
        value_projection,
        w_out,
        small,
        jnp.concatenate([grad_output, below], axis=0),
        n,
        1,
    )
    extra_all = extra_all.reshape(n, rows + 16, D)
    gains = extra_all[:, rows, : 2 * norm_gain1.shape[0]].reshape(n, 2, -1)
    gains = jnp.transpose(gains, (1, 0, 2)).reshape(2, D).astype(F32)

    cosine_lookup, sine_lookup = [table[:, 0] for table in rotary_tables(positions, HEAD_DIMENSION)]
    cosine = jnp.tile(cosine_lookup, (1, 4))
    sine = jnp.tile(jnp.concatenate([-sine_lookup, sine_lookup], axis=1), (1, 2))
    token_f32 = tokens.astype(F32)
    mixed_low, log_total, kv_all, query_pairs, rank_all = attention(
        lengths, tokens, gains, qkv_weight, cosine, sine, routes, n, 2
    )
    expert_args = (extra_all, router, rank_all, w_gate, w_up, w_down, capacity)
    if plane:
        sources = (mixed_low, tokens, out_weight, gains)
        y_part, gs, grad_gate, grad_up, grad_down, second_norm, residual = run_experts(
            sources, *expert_args, plane, 7
        )
    else:
        residual = token_f32 + dot(mixed_low, out_weight)
        inverse_two = lax.rsqrt(jnp.mean(residual * residual, axis=-1, keepdims=True) + EPSILON)
        second_norm = (residual * inverse_two * gains[1]).astype(BF)
        sources = line_gather([second_norm], n, 3, "gather_rows")
        y_part, gs, grad_gate, grad_up, grad_down = run_experts(sources, *expert_args, plane, 7)
        gs = line_scatter(gs, n, F32, 4, "scatter_grads")

    sources = (
        gs,
        residual,
        second_norm,
        grad_output,
        routes,
        gains,
        router,
        out_weight,
    )
    grad_query_acc, kv_gradient, grad_residual, grad_attn, grad_router, gain_two_row = (
        attention_back(lengths, query_pairs, kv_all, log_total, sources, n, 5)
    )
    if plane:
        *shares, expert_sum, grad_rest = reduce_weights(
            grad_query_acc,
            kv_gradient,
            tokens,
            gains,
            qkv_weight,
            cosine,
            sine,
            mixed_low,
            grad_attn,
            grad_router,
            gain_two_row,
            y_part,
            n,
            6,
        )
        grad_tokens = grad_residual + grad_rest
    else:
        inverse_one = lax.rsqrt(jnp.mean(token_f32 * token_f32, axis=-1, keepdims=True) + EPSILON)
        unit_one = token_f32 * inverse_one
        first_norm = (unit_one * gains[0]).astype(BF)
        own_key_gradient, own_value_gradient = unpair_columns(kv_gradient)
        back = lambda value: apply_rotation(
            value.astype(F32).reshape(rows, -1, HEAD_DIMENSION),
            cosine_lookup[:, None],
            -sine_lookup[:, None],
        )
        grad_query_pre = back(grad_query_acc).reshape(rows, query_width).astype(BF)
        grad_key_pre = back(own_key_gradient).reshape(rows, key_width).astype(BF)
        grad_qkv_pre = jnp.concatenate([grad_query_pre, grad_key_pre, own_value_gradient], axis=1)
        grad_first = dot_nt(grad_qkv_pre, qkv_weight)
        scaled_one = grad_first * gains[0]
        grad_gain1 = jnp.sum(grad_first * unit_one, axis=0)
        grad_tokens = grad_residual + inverse_one * (
            scaled_one - unit_one * jnp.mean(scaled_one * unit_one, axis=-1, keepdims=True)
        )
        gains = [grad_gain1[:, None], gain_two_row.T]
        rest = grad_router[:, EXPERTS + 2 :]
        grad_small = jnp.concatenate([grad_router[:, :EXPERTS]] + gains + [rest], axis=1)
        shares = (dot_tn(first_norm, grad_qkv_pre), dot_tn(mixed_low, grad_attn), grad_small)
        shares = [lax.psum(scatter_rows(share.astype(BF)), "group") for share in shares]
        share_qkv, share_out, share_small = shares
        split = (query_width, query_width + key_width)
        shares = jnp.split(share_qkv, split, axis=1) + [share_out, share_small]
        expert_sum = line_scatter(y_part, n, F32, 8, "scatter_outputs")
    mixed = (residual + expert_sum).astype(BF)
    shares = [share.astype(F32) for share in shares]
    share_query, share_key, share_value, share_out, share_small = shares

    def sum_over_groups(value):
        if not plane:
            value = lax.psum_scatter(value, "group", scatter_dimension=1, tiled=True)
        return widen(lax.all_gather(value, "group", axis=1, tiled=True))

    return (
        mixed,
        grad_tokens,
        share_small[:, EXPERTS],
        share_query,
        share_key,
        share_value,
        share_out,
        share_small[:, EXPERTS + 1],
        share_small[:, :EXPERTS],
        sum_over_groups(grad_gate),
        sum_over_groups(grad_up),
        sum_over_groups(grad_down),
    )


def solution(mesh):
    rows = P(("group", "expert"), None)
    vector, matrix, stack = P("expert"), P("expert", None), P("expert", None, None)
    return jax.shard_map(
        per_device,
        mesh=mesh,
        in_specs=(
            rows,
            P("group"),
            rows,
            vector,
            matrix,
            matrix,
            matrix,
            matrix,
            vector,
            matrix,
            stack,
            stack,
            stack,
            rows,
        ),
        out_specs=(
            rows,
            rows,
            vector,
            matrix,
            matrix,
            matrix,
            matrix,
            vector,
            matrix,
            stack,
            stack,
            stack,
        ),
        check_vma=False,
    )
```

```python
import functools
import itertools

import jax
import jax.numpy as jnp
from jax import lax
from jax.experimental import pallas as pl
from jax.experimental.pallas import tpu as pltpu
from jax.sharding import PartitionSpec as P

D = 1024
QUERY_HEADS = 16
KEY_VALUE_HEADS = 8
HEAD_DIMENSION = 64
EXPERTS = 32
TOP = 8
FF = 512
LANES = 128
STAGES = 4

EPSILON = 1e-05
NEGATIVE_LARGE = -1e30
BF = jnp.bfloat16
F32 = jnp.float32


def rotary_tables(positions, head_size):
    half_width = head_size // 2
    frequency = 10000.0 ** (-2.0 * jnp.arange(half_width).astype(F32) / head_size)
    angles = positions.astype(F32)[:, None] * frequency[None, :]
    return (jnp.cos(angles)[:, None, :], jnp.sin(angles)[:, None, :])


def apply_rotation(tensor_in, cosine_lookup, sine_lookup):
    half_width = tensor_in.shape[-1] // 2
    first_half = tensor_in[..., :half_width]
    second_half = tensor_in[..., half_width:]
    return jnp.concatenate(
        [
            first_half * cosine_lookup - second_half * sine_lookup,
            second_half * cosine_lookup + first_half * sine_lookup,
        ],
        axis=-1,
    )


def dot(a, b):
    return jnp.dot(a, b, preferred_element_type=F32)


def dot_nt(a, b):
    return lax.dot_general(a, b, (((1,), (1,)), ((), ())), preferred_element_type=F32)


def dot_tn(a, b):
    return lax.dot_general(a, b, (((0,), (0,)), ((), ())), preferred_element_type=F32)


MESH = pl.DeviceIdType.MESH
ANY = pl.BlockSpec(memory_space=pl.ANY)
IN_VMEM = pl.BlockSpec(memory_space=pltpu.VMEM)


def remote(source, target, send, receive, device):
    return pltpu.make_async_remote_copy(
        src_ref=source,
        dst_ref=target,
        send_sem=send,
        recv_sem=receive,
        device_id=device,
        device_id_type=MESH,
    )


def greet(devices):
    barrier = pltpu.get_barrier_semaphore()
    count = 0
    for condition, device in devices:
        if condition is None:
            pl.semaphore_signal(barrier, inc=1, device_id=device, device_id_type=MESH)
            count = count + 1
        else:

            @pl.when(condition)
            def _():
                pl.semaphore_signal(barrier, inc=1, device_id=device, device_id_type=MESH)

            count = count + jnp.where(condition, 1, 0)
    pl.semaphore_wait(barrier, count)


def line_gather_kernel(n, count, *refs):
    ins, outs = refs[:count], refs[count : 2 * count]
    local, send, receive = refs[2 * count :]
    group, me = lax.axis_index("group"), lax.axis_index("expert")
    left, right = (group, me - 1), (group, me + 1)
    own = [
        pltpu.make_async_copy(ins[i], outs[i].at[me], local.at[i]) for i in range(count)
    ]
    for copy in own:
        copy.start()
    greet([(me > 0, left), (me < n - 1, right)])

    def hop(i, step, side):
        block = me - step if side == 0 else me + step
        source = ins[i] if step == 0 else outs[i].at[block]
        index = (side, step, i)
        return remote(
            source, outs[i].at[block], send.at[index], receive.at[index], right if side == 0 else left
        )

    def arrival(i, step, side):
        block = me - 1 - step if side == 0 else me + 1 + step
        index = (side, step, i)
        return remote(
            outs[i].at[block], outs[i].at[block], send.at[index], receive.at[index], left if side == 0 else right
        )

    def sends(step, side):
        return (me - step >= 0) & (me < n - 1) if side == 0 else (me + step < n) & (me > 0)

    def arrives(step, side):
        return me - 1 - step >= 0 if side == 0 else me + 1 + step < n

    for step in range(n - 1):
        for side in (0, 1):

            @pl.when(sends(step, side))
            def _():
                for i in range(count):
                    hop(i, step, side).start()

        for side in (0, 1):

            @pl.when(arrives(step, side))
            def _():
                for i in range(count):
                    arrival(i, step, side).wait_recv()

    for step in range(n - 1):
        for side in (0, 1):

            @pl.when(sends(step, side))
            def _():
                for i in range(count):
                    hop(i, step, side).wait_send()

    for copy in own:
        copy.wait()


def line_gather(values, n, collective_id, name):
    count = len(values)
    outs = pl.pallas_call(
        functools.partial(line_gather_kernel, n, count),
        out_shape=[jax.ShapeDtypeStruct((n,) + v.shape, v.dtype) for v in values],
        in_specs=[IN_VMEM] * count,
        out_specs=[ANY] * count,
        scratch_shapes=[
            pltpu.SemaphoreType.DMA((count,)),
            pltpu.SemaphoreType.DMA((2, n - 1, count)),
            pltpu.SemaphoreType.DMA((2, n - 1, count)),
        ],
        compiler_params=pltpu.CompilerParams(collective_id=collective_id, has_side_effects=True),
        cost_estimate=pl.CostEstimate(flops=0, bytes_accessed=100000000, transcendentals=0),
        name=name,
    )(*values)
    return [o.reshape((n * v.shape[0],) + v.shape[1:]) for o, v in zip(outs, values)]


class LineSum:
    def __init__(self, n, part, landing, staging, send, receive):
        self.n, self.part, self.landing, self.staging = n, part, landing, staging
        self.send, self.receive = send, receive
        self.group, self.me = lax.axis_index("group"), lax.axis_index("expert")
        self.rows = part.shape[1]
        self.tile = min(32, self.rows)

    def neighbours(self):
        left, right = (self.group, self.me - 1), (self.group, self.me + 1)
        return [(self.me > 0, left), (self.me < self.n - 1, right)]

    def copy(self, source, step, side):
        index = (side, step)
        device = (self.group, self.me + 1 if side == 0 else self.me - 1)
        return remote(
            source, self.landing.at[index], self.send.at[index], self.receive.at[index], device
        )

    def places(self):
        me, n = self.me, self.n
        for step in range(n - 1):
            for side in (0, 1):
                owner = n - 1 - step if side == 0 else step
                beyond = me < owner if side == 0 else me > owner
                edge = me == 0 if side == 0 else me == n - 1
                yield step, side, owner, beyond, edge

    def start(self):
        for step, side, owner, beyond, edge in self.places():

            @pl.when(beyond & edge)
            def _():
                self.copy(self.part.at[owner], step, side).start()

    def spans(self, body):
        def tile_body(t, carry):
            body(pl.ds(pl.multiple_of(t * self.tile, self.tile), self.tile))
            return carry

        lax.fori_loop(0, self.rows // self.tile, tile_body, 0)

    def forward(self, hop):
        me, n = self.me, self.n
        for side in (0, 1):
            step = hop - me if side == 0 else hop - (n - 1 - me)
            owner = n - 1 - step if side == 0 else step
            inner = me > 0 if side == 0 else me < n - 1
            beyond = me < owner if side == 0 else me > owner

            @pl.when(inner & (step >= 0) & beyond)
            def _():
                self.copy(self.part.at[owner], step, side).wait_recv()

                def add(span):
                    total = self.part[owner, span, :].astype(F32)
                    total = total + self.landing[side, step, span, :].astype(F32)
                    self.staging[side, step, span, :] = total.astype(BF)

                self.spans(add)
                self.copy(self.staging.at[side, step], step, side).start()

    def finish(self, out_ref):
        me, n = self.me, self.n

        @pl.when(me > 0)
        def _():
            self.copy(self.part.at[me], n - 1 - me, 0).wait_recv()

        @pl.when(me < n - 1)
        def _():
            self.copy(self.part.at[me], me, 1).wait_recv()

        def total(span):
            value = self.part[me, span, :].astype(F32)
            from_left = self.landing[0, jnp.minimum(n - 1 - me, n - 2), span, :].astype(F32)
            from_right = self.landing[1, jnp.minimum(me, n - 2), span, :].astype(F32)
            value = value + jnp.where(me > 0, from_left, 0.0)
            value = value + jnp.where(me < n - 1, from_right, 0.0)
            out_ref[span, :] = value.astype(out_ref.dtype)

        self.spans(total)
        for step, side, owner, beyond, edge in self.places():

            @pl.when(beyond)
            def _():
                self.copy(self.part.at[owner], step, side).wait_send()


def line_sum_scratch(n, rows, width):
    return [
        pltpu.VMEM((2, n - 1, rows, width), BF),
        pltpu.VMEM((2, n - 2, rows, width), BF),
        pltpu.SemaphoreType.DMA((2, n - 1)),
        pltpu.SemaphoreType.DMA((2, n - 1)),
    ]


def line_scatter_kernel(n, part_ref, out_ref, *scratch):
    line = LineSum(n, part_ref, *scratch)
    greet(line.neighbours())
    line.start()
    for hop in range(1, n - 1):
        line.forward(hop)
    line.finish(out_ref)


def line_scatter(value, n, dtype, collective_id, name):
    total, width = value.shape
    rows = total // n
    return pl.pallas_call(
        functools.partial(line_scatter_kernel, n),
        out_shape=jax.ShapeDtypeStruct((rows, width), dtype),
        in_specs=[IN_VMEM],
        out_specs=IN_VMEM,
        scratch_shapes=line_sum_scratch(n, rows, width),
        compiler_params=pltpu.CompilerParams(collective_id=collective_id, has_side_effects=True),
        cost_estimate=pl.CostEstimate(flops=0, bytes_accessed=100000000, transcendentals=0),
        name=name,
    )(value.reshape(n, rows, width))


def plane_position():
    group, me = lax.axis_index("group"), lax.axis_index("expert")
    c, x, y = group % 2, (group // 2) % 2, (group // 4) % 2
    by_c, by_x, by_y = (group + 1 - 2 * c, me), (group + 2 - 4 * x, me), (group + 4 - 8 * y, me)
    return group, me, (y, x, c), (by_y, by_x, by_c)


class PlaneGather:
    def __init__(self, owns, outs, start, local, send, receive):
        self.owns, self.outs, self.first_expert = owns, outs, start
        self.local, self.send, self.receive = local, send, receive
        _, _, (self.y, self.x, self.c), self.partners = plane_position()
        self.part = outs[0].shape[0] // 2

    def copy(self, i, path, stage):
        y, x, c = self.y, self.x, self.c
        by_y, by_x, by_c = self.partners
        span = slice(path * self.part, (path + 1) * self.part)
        out = self.outs[i]
        near = out.at[span, y, :, c] if path == 0 else out.at[span, :, x, c]
        far = out.at[span, 1 - y, :, c] if path == 0 else out.at[span, :, 1 - x, c]
        if stage == 0:
            start = self.first_expert + path * self.part
            source, target = self.owns[i].at[start : start + self.part], out.at[span, y, x, c]
        else:
            source = far if stage == 3 else near
            target = source
        device = (by_x, by_y, by_c, by_c)[stage] if path == 0 else (by_y, by_x, by_c, by_c)[stage]
        index = (i, path, stage)
        return remote(source, target, self.send.at[index], self.receive.at[index], device)

    def all(self, stage):
        return [self.copy(i, path, stage) for i in range(len(self.outs)) for path in (0, 1)]

    def stores(self):
        span = slice(self.first_expert, self.first_expert + 2 * self.part)
        return [
            pltpu.make_async_copy(
                own.at[span], out.at[:, self.y, self.x, self.c], self.local.at[i]
            )
            for i, (own, out) in enumerate(zip(self.owns, self.outs))
        ]

    def begin(self):
        for copy in self.all(0) + self.stores():
            copy.start()

    def second(self):
        for copy in self.stores():
            copy.wait()
        for copy in self.all(0):
            copy.wait_recv()
        for copy in self.all(1) + self.all(2):
            copy.start()

    def third(self):
        for copy in self.all(1):
            copy.wait_recv()
        for copy in self.all(3):
            copy.start()

    def finish(self):
        for copy in self.all(0) + self.all(1):
            copy.wait_send()
        for copy in self.all(2) + self.all(3):
            copy.wait()


def plane_gather_sems():
    return [pltpu.SemaphoreType.DMA((3,))] + [pltpu.SemaphoreType.DMA((3, 2, 4))] * 2


def plane_gather_shapes(owns):
    half = owns[0].shape[0] // 2
    return [jax.ShapeDtypeStruct((half, 2, 2, 2) + own.shape[1:], own.dtype) for own in owns]


def weights_kernel(n, pieces, widths, *refs):
    wq, wk, wv, wo, small, extra = refs[:6]
    outs, extra_out, owns = refs[6:9], refs[9], refs[10:13]
    load, store, zsend, zrecv, psend, precv, csend, crecv, xsend, xrecv = refs[13:]
    group, me, (y, x, c), (by_y, by_x, by_c) = plane_position()
    left, right = (group, me - 1), (group, me + 1)
    eighth = owns[0].shape[0]
    span = pl.ds(pl.multiple_of((y * 4 + x * 2 + c) * eighth, eighth), eighth)
    query_width, key_width = wq.shape[1], wk.shape[1]
    targets = (
        owns[0].at[:, :query_width],
        owns[0].at[:, query_width : query_width + key_width],
        owns[0].at[:, query_width + key_width :],
        owns[1],
        owns[2],
    )
    loads = [
        pltpu.make_async_copy(source.at[span, :], target, load.at[i])
        for i, (source, target) in enumerate(zip((wq, wk, wv, wo, small), targets))
    ]
    for copy in loads:
        copy.start()
    for copy in loads:
        copy.wait()
    stores = [
        pltpu.make_async_copy(owns[i], outs[i].at[me, y, x, c], store.at[i]) for i in range(3)
    ]
    stores.append(pltpu.make_async_copy(extra, extra_out.at[me], store.at[3]))
    for copy in stores:
        copy.start()
    greet(
        [(me > 0, left), (me < n - 1, right), (None, by_c), (None, by_x), (None, by_y)]
    )

    def hop(i, step, side):
        block = me - step if side == 0 else me + step
        source = owns[i] if step == 0 else outs[i].at[block, y, x, c]
        index = (side, step, i)
        return remote(
            source,
            outs[i].at[block, y, x, c],
            zsend.at[index],
            zrecv.at[index],
            right if side == 0 else left,
        )

    def sends(step, side):
        return (me - step >= 0) & (me < n - 1) if side == 0 else (me + step < n) & (me > 0)

    def extra_hop(step, side):
        block = me - step if side == 0 else me + step
        source = extra if step == 0 else extra_out.at[block]
        return remote(
            source,
            extra_out.at[block],
            xsend.at[side, step],
            xrecv.at[side, step],
            right if side == 0 else left,
        )

    def first(slot, block, p):
        i, start, width, along_x = pieces[p]
        spot = outs[i].at[block, y, x, c, :, start : start + width]
        source = owns[i].at[:, start : start + width] if slot == 0 else spot
        index = (0, slot, p)
        return remote(source, spot, psend.at[index], precv.at[index], by_x if along_x else by_y)

    def second(slot, block, p):
        i, start, width, along_x = pieces[p]
        columns = slice(start, start + width)
        if along_x:
            spot = outs[i].at[block, y, :, c, :, columns]
        else:
            spot = outs[i].at[block, :, x, c, :, columns]
        index = (1, slot, p)
        return remote(spot, spot, psend.at[index], precv.at[index], by_y if along_x else by_x)

    def third(slot, block, i):
        spot = outs[i].at[block, :, :, c]
        index = (slot, i)
        return remote(spot, spot, csend.at[index], crecv.at[index], by_c)

    def held(step):
        if step == 0:
            return [(0, me, me >= 0)]
        return [(step, me - step, me - step >= 0), (n - 1 + step, me + step, me + step < n)]

    def extra_step(far):
        for side in (0, 1):
            if far > 0:

                @pl.when(me - far >= 0 if side == 0 else me + far < n)
                def _():
                    extra_hop(far - 1, side).wait_recv()

        for side in (0, 1):
            if far < n - 1:

                @pl.when(sends(far, side))
                def _():
                    extra_hop(far, side).start()

    count = len(pieces)
    for step in range(n + 2):
        if step < n:
            for slot, block, there in held(step):

                @pl.when(there)
                def _():
                    if step > 0:
                        side = 0 if slot < n else 1
                        for i in range(3):
                            hop(i, step - 1, side).wait_recv()
                    for p in range(count):
                        first(slot, block, p).start()

            if step < n - 1:
                for side in (0, 1):

                    @pl.when(sends(step, side))
                    def _():
                        for i in range(3):
                            hop(i, step, side).start()

        if 1 <= step < n + 1:
            if step == 1:
                for copy in stores:
                    copy.wait()
            for slot, block, there in held(step - 1):

                @pl.when(there)
                def _():
                    for p in range(count):
                        first(slot, block, p).wait_recv()
                    for p in range(count):
                        second(slot, block, p).start()

        if step >= 2:
            for slot, block, there in held(step - 2):

                @pl.when(there)
                def _():
                    for p in range(count):
                        second(slot, block, p).wait_recv()
                    for i in range(3):
                        third(slot, block, i).start()

        if step == 1:
            extra_step(0)
        elif step >= n:
            extra_step(step - n + 1)
    for far in range(3, n):
        extra_step(far)

    for step in range(n):
        for slot, block, there in held(step):

            @pl.when(there)
            def _():
                for p in range(count):
                    first(slot, block, p).wait_send()
                    second(slot, block, p).wait_send()
                for i in range(3):
                    third(slot, block, i).wait()

        if step < n - 1:
            for side in (0, 1):

                @pl.when(sends(step, side))
                def _():
                    for i in range(3):
                        hop(i, step, side).wait_send()
                    extra_hop(step, side).wait_send()


def path_pieces(query_width, key_width, out_width, small_width):
    half = query_width + key_width
    return (
        (0, 0, half, True),
        (0, half, query_width + 2 * key_width - half, False),
        (1, 0, out_width, False),
        (2, 0, small_width, True),
    )


def gather_weights(wq, wk, wv, wo, small, extra, n, collective_id):
    rows = wq.shape[0]
    eighth = rows // 8
    widths = (wq.shape[1] + wk.shape[1] + wv.shape[1], wo.shape[1], small.shape[1])
    pieces = path_pieces(wq.shape[1], wk.shape[1], wo.shape[1], small.shape[1])
    outs = pl.pallas_call(
        functools.partial(weights_kernel, n, pieces, widths),
        out_shape=[jax.ShapeDtypeStruct((n, 2, 2, 2, eighth, w), BF) for w in widths]
        + [jax.ShapeDtypeStruct((n,) + extra.shape, BF)],
        in_specs=[ANY] * 5 + [IN_VMEM],
        out_specs=[ANY] * 4,
        scratch_shapes=[pltpu.VMEM((eighth, w), BF) for w in widths]
        + [
            pltpu.SemaphoreType.DMA((5,)),
            pltpu.SemaphoreType.DMA((4,)),
            pltpu.SemaphoreType.DMA((2, n - 1, 3)),
            pltpu.SemaphoreType.DMA((2, n - 1, 3)),
            pltpu.SemaphoreType.DMA((2, 2 * n - 1, 4)),
            pltpu.SemaphoreType.DMA((2, 2 * n - 1, 4)),
            pltpu.SemaphoreType.DMA((2 * n - 1, 3)),
            pltpu.SemaphoreType.DMA((2 * n - 1, 3)),
            pltpu.SemaphoreType.DMA((2, n - 1)),
            pltpu.SemaphoreType.DMA((2, n - 1)),
        ],
        compiler_params=pltpu.CompilerParams(collective_id=collective_id, has_side_effects=True),
        cost_estimate=pl.CostEstimate(flops=0, bytes_accessed=100000000, transcendentals=0),
        name="gather_weights",
    )(wq, wk, wv, wo, small, extra)
    weights = [o.reshape(n * rows, w) for o, w in zip(outs, widths)]
    return weights + [outs[3].reshape(-1, extra.shape[1])]


def reduce_kernel(n, pieces, *refs):
    (
        grad_q_ref,
        grad_kv_ref,
        tokens_ref,
        gain_ref,
        weight_ref,
        cosine_ref,
        sine_ref,
        mixed_ref,
        grad_attn_ref,
        router_ref,
        gain_two_ref,
        y_part,
    ) = refs[:12]
    owns, outs, y_out, grad_tokens_ref, wholes = refs[12:15], refs[15:17], refs[17], refs[18], refs[19:22]
    ins, grad_pre_ref = refs[22:25], refs[25]
    gather = PlaneGather(owns, wholes, owns[0].shape[0] // 2, *refs[26:29])
    refs = refs[29:]
    pair, one, two, landing, staging = refs[:2], refs[2:4], refs[4:6], refs[6:8], refs[8:10]
    csend, crecv, psend, precv, zsend, zrecv, gsend, grecv = refs[10:18]
    line = LineSum(n, y_part, *refs[18:])
    group, me, (y, x, c), (by_y, by_x, by_c) = plane_position()
    left, right = (group, me - 1), (group, me + 1)
    eighth = pair[0].shape[3]
    greet(
        [(me > 0, left), (me < n - 1, right), (None, by_c), (None, by_x), (None, by_y)]
    )

    places, ends = [], [0, 0]
    for array, start, width, along_x in pieces:
        path = 0 if along_x else 1
        places.append((array, start, width, path, ends[path]))
        ends[path] += width

    def swap(p):
        array, start, width, path, at = places[p]
        return remote(
            ins[array].at[:, :, :, 1 - c, :, start : start + width],
            pair[path].at[:, :, :, :, at : at + width],
            csend.at[p],
            crecv.at[p],
            by_c,
        )

    line.start()
    gather.begin()
    D_rows = weight_ref.shape[0]
    query_width = grad_q_ref.shape[1]
    key_width = (weight_ref.shape[1] - query_width) // 2

    def put(array, columns, value):
        ins[array][:, :, :, :, :, columns] = value.astype(BF).reshape(
            ins[array].shape[:5] + (value.shape[1],)
        )

    tile = 4 * LANES
    for start in range(0, grad_attn_ref.shape[1], tile):
        columns = slice(start, start + tile)
        put(1, columns, dot_tn(mixed_ref[...], grad_attn_ref[:, columns]))
    swap(2).start()
    unit, inverse = normed(tokens_ref)
    gain = gain_ref[0:1, :]
    first_norm = (unit * gain).astype(BF)
    cosine, sine = cosine_ref[...], -sine_ref[...]
    for j in range(query_width // LANES):
        columns = slice(j * LANES, (j + 1) * LANES)
        grad_pre_ref[:, columns] = rotate(grad_q_ref[:, columns], cosine, sine).astype(BF)
    for j in range(key_width // LANES):
        start = 2 * j * LANES
        key = grad_kv_ref[:, start : start + LANES].astype(F32)
        at = query_width + j * LANES
        grad_pre_ref[:, at : at + LANES] = rotate(key, cosine, sine).astype(BF)
        at = at + key_width
        grad_pre_ref[:, at : at + LANES] = grad_kv_ref[:, start + LANES : start + 2 * LANES]
    for start in range(0, weight_ref.shape[1], tile):
        columns = slice(start, start + tile)
        put(0, columns, dot_tn(first_norm, grad_pre_ref[:, columns]))
    swap(0).start()
    swap(1).start()
    grad_first = dot_nt(grad_pre_ref[...], weight_ref[...])
    gain_one_row = jnp.sum(grad_first * unit, axis=0, keepdims=True)
    lane = lax.broadcasted_iota(jnp.int32, (LANES, D_rows), 0)
    gains = jnp.where(lane == EXPERTS, gain_one_row, 0.0)
    gains = jnp.where(lane == EXPERTS + 1, gain_two_ref[...], gains)
    put(2, slice(0, LANES), router_ref[...] + gains.T)
    swap(3).start()
    scaled = grad_first * gain
    mean = jnp.mean(scaled * unit, axis=-1, keepdims=True)
    grad_tokens_ref[...] = inverse * (scaled - unit * mean)
    for p in range(len(places)):
        swap(p).wait_recv()
        array, start, width, path, at = places[p]

        def pair_sum(t, carry):
            z, a, b = t // 4, (t // 2) % 2, t % 2
            mine = ins[array][z, a, b, c, :, start : start + width].astype(F32)
            theirs = pair[path][z, a, b, :, at : at + width].astype(F32)
            pair[path][z, a, b, :, at : at + width] = (mine + theirs).astype(BF)
            return carry

        lax.fori_loop(0, 4 * n, pair_sum, 0)

    def first(path):
        source = pair[0].at[:, :, 1 - x] if path == 0 else pair[1].at[:, 1 - y]
        return remote(
            source, one[path], psend.at[0, path], precv.at[0, path], by_x if path == 0 else by_y
        )

    def second(path):
        source = one[path].at[:, 1 - y] if path == 0 else one[path].at[:, 1 - x]
        return remote(
            source, two[path], psend.at[1, path], precv.at[1, path], by_y if path == 0 else by_x
        )

    for path in (0, 1):
        first(path).start()
    line.forward(1)
    for path in (0, 1):
        first(path).wait_recv()
        if path == 1:
            gather.second()

        def first_sum(t, carry):
            z, a = t // 2, t % 2
            mine = pair[0][z, a, x] if path == 0 else pair[1][z, y, a]
            one[path][z, a] = (mine.astype(F32) + one[path][z, a].astype(F32)).astype(BF)
            return carry

        lax.fori_loop(0, 2 * n, first_sum, 0)
        second(path).start()
    for far in range(2, n - 1):
        line.forward(far)
    for path in (0, 1):
        second(path).wait_recv()

        def second_sum(z, carry):
            mine = one[0][z, y] if path == 0 else one[1][z, x]
            two[path][z] = (mine.astype(F32) + two[path][z].astype(F32)).astype(BF)
            return carry

        lax.fori_loop(0, n, second_sum, 0)

    def hop(source, path, step, side):
        index = (path, side, step)
        return remote(
            source,
            landing[path].at[side, step],
            zsend.at[index],
            zrecv.at[index],
            right if side == 0 else left,
        )

    for step in range(n - 1):
        for side in (0, 1):
            owner = n - 1 - step if side == 0 else step
            beyond = me < owner if side == 0 else me > owner
            edge = me == 0 if side == 0 else me == n - 1

            @pl.when(beyond & edge)
            def _():
                for path in (0, 1):
                    hop(two[path].at[owner], path, step, side).start()

    for far in range(1, n - 1):
        for side in (0, 1):
            step = far - me if side == 0 else far - (n - 1 - me)
            owner = n - 1 - step if side == 0 else step
            inner = me > 0 if side == 0 else me < n - 1
            beyond = me < owner if side == 0 else me > owner

            @pl.when(inner & (step >= 0) & beyond)
            def _():
                for path in (0, 1):
                    hop(two[path].at[owner], path, step, side).wait_recv()
                    staging[path][side, step] = (
                        two[path][owner].astype(F32) + landing[path][side, step].astype(F32)
                    ).astype(BF)
                    hop(staging[path].at[side, step], path, step, side).start()

    @pl.when(me > 0)
    def _():
        for path in (0, 1):
            hop(two[path].at[me], path, n - 1 - me, 0).wait_recv()

    @pl.when(me < n - 1)
    def _():
        for path in (0, 1):
            hop(two[path].at[me], path, me, 1).wait_recv()

    for path in (0, 1):
        total = two[path][me].astype(F32)
        from_left = landing[path][0, jnp.minimum(n - 1 - me, n - 2)].astype(F32)
        from_right = landing[path][1, jnp.minimum(me, n - 2)].astype(F32)
        total = total + jnp.where(me > 0, from_left, 0.0)
        total = total + jnp.where(me < n - 1, from_right, 0.0)
        outs[path][y, x, c] = total.astype(BF)

    def spread(path, stage):
        out = outs[path]
        if stage == 2:
            spot, device = out.at[:, :, c], by_c
        elif stage == 0:
            spot, device = out.at[y, x, c], by_x if path == 0 else by_y
        elif path == 0:
            spot, device = out.at[y, :, c], by_y
        else:
            spot, device = out.at[:, x, c], by_x
        return remote(spot, spot, gsend.at[path, stage], grecv.at[path, stage], device)

    for stage in range(3):
        for path in (0, 1):
            spread(path, stage).start()
        if stage == 0:
            line.finish(y_out)
        for path in (0, 1):
            spread(path, stage).wait_recv()

    gather.third()
    gather.finish()
    for path in (0, 1):
        for stage in range(3):
            spread(path, stage).wait_send()
        first(path).wait_send()
        second(path).wait_send()
    for p in range(len(places)):
        swap(p).wait_send()
    for step in range(n - 1):
        for side in (0, 1):
            owner = n - 1 - step if side == 0 else step
            beyond = me < owner if side == 0 else me > owner

            @pl.when(beyond)
            def _():
                for path in (0, 1):
                    hop(two[path].at[owner], path, step, side).wait_send()


def reduce_weights(
    grad_q,
    grad_kv,
    tokens,
    gain,
    weight,
    cosine,
    sine,
    mixed_low,
    grad_attn,
    grad_router,
    gain_two_row,
    y_part,
    sums,
    n,
    collective_id,
):
    rows_all, width_all = weight.shape
    query_width = grad_q.shape[1]
    key_width = (width_all - query_width) // 2
    array_widths = (width_all, grad_attn.shape[1], LANES)
    rows = rows_all // n
    eighth = rows // 8
    pieces = path_pieces(query_width, key_width, grad_attn.shape[1], LANES)
    widths = [sum(p[2] for p in pieces if p[3]), sum(p[2] for p in pieces if not p[3])]
    scratch = [pltpu.VMEM((n, 2, 2, 2, eighth, w), BF) for w in array_widths]
    scratch += [pltpu.VMEM((grad_q.shape[0], width_all), BF)]
    scratch += plane_gather_sems()
    scratch += [pltpu.VMEM((n, 2, 2, eighth, w), BF) for w in widths]
    scratch += [pltpu.VMEM((n, 2, eighth, w), BF) for w in widths]
    scratch += [pltpu.VMEM((n, eighth, w), BF) for w in widths]
    scratch += [pltpu.VMEM((2, n - 1, eighth, w), BF) for w in widths] * 2
    sems = [(4,), (4,), (2, 2), (2, 2), (2, 2, n - 1), (2, 2, n - 1), (2, 3), (2, 3)]
    y_rows = y_part.shape[0] // n
    first, second, y_sum, grad_rest, *wholes = pl.pallas_call(
        functools.partial(reduce_kernel, n, pieces),
        out_shape=[jax.ShapeDtypeStruct((2, 2, 2, eighth, w), BF) for w in widths]
        + [jax.ShapeDtypeStruct(tokens.shape, F32)] * 2
        + plane_gather_shapes(sums),
        in_specs=[IN_VMEM] * 15,
        out_specs=[IN_VMEM] * 4 + [ANY] * 3,
        scratch_shapes=scratch
        + [pltpu.SemaphoreType.DMA(s) for s in sems]
        + line_sum_scratch(n, y_rows, y_part.shape[1]),
        compiler_params=pltpu.CompilerParams(
            collective_id=collective_id, has_side_effects=True, vmem_limit_bytes=60 * 1024 * 1024
        ),
        cost_estimate=pl.CostEstimate(flops=0, bytes_accessed=100000000, transcendentals=0),
        name="reduce_weights",
    )(
        grad_q,
        grad_kv,
        tokens,
        gain,
        weight,
        cosine,
        sine,
        mixed_low,
        grad_attn,
        grad_router,
        gain_two_row,
        y_part.reshape(n, y_rows, y_part.shape[1]),
        *sums,
    )
    first, second = [o.reshape(rows, w) for o, w in zip((first, second), widths)]
    first = jnp.split(first, (query_width, query_width + key_width), axis=1)
    second = jnp.split(second, (key_width,), axis=1)
    return first[0], first[1], second[0], second[1], first[2], y_sum, grad_rest, wholes


def plane_tick(step, local):
    tick = jnp.where(step <= 2, step, jnp.where(step < local, (step + 2) // 2, step - 3))
    runs = (step <= 2) | (step >= local) | (step % 2 == 0)
    return tick, runs


def expert_kernel(sizes, plane, *refs):
    blocks, rows, local, capacity = sizes
    if plane:
        mixed_in, tokens_in, out_weight_in, gain_ref = refs[:4]
        refs = refs[4:]
    else:
        x_ref = refs[0]
        refs = refs[1:]
    ct_ref, router_ref, rank_all_ref = refs[:3]
    w_gate_ref, w_up_ref, w_down_ref = refs[3:6]
    y_ref, gs_ref, out_gate_ref, out_up_ref, out_down_ref = refs[6:11]
    refs = refs[11:]
    if plane:
        second_ref, residual_ref = refs[:2]
        refs = refs[2:]
    xs_ref, g_ref, rank_ref, gate_ref, dots_ref, y_sem = refs[:6]
    refs = refs[6:]
    slots = local * capacity
    step = pl.program_id(0)
    tick, ticks = plane_tick(step, local)
    me = lax.axis_index("expert")
    base = me * local
    if plane:
        stage_refs, pair_refs, one_refs, two_refs = refs[:3], refs[3:6], refs[6:10], refs[10:14]
        csend, crecv, psend, precv, qsend, qrecv = refs[14:20]
        gs_part = refs[20]
        line = LineSum(blocks, gs_part, *refs[21:25])
        x_ref, xsend, xrecv, in_sem, out_sem = refs[25:]
        group, _, (y, x, c), (by_y, by_x, by_c) = plane_position()
        half = stage_refs[2].shape[4] // 2

    def expert_id():
        return lax.broadcasted_iota(jnp.int32, (EXPERTS, rows), 0)

    def note_ranks(b):
        ranks = rank_all_ref[b].astype(F32)
        for e in range(local):
            mine = jnp.where(expert_id() == base + e, ranks, 0.0)
            rank_ref[b, e : e + 1, :] = jnp.sum(mine, axis=0, keepdims=True)

    def pick(b):
        slot_id = lax.broadcasted_iota(jnp.int32, (capacity, rows), 0).astype(F32)
        pieces = [
            jnp.where(rank_ref[b, e : e + 1, :] == slot_id, 1.0, 0.0).astype(BF)
            for e in range(local)
        ]
        return jnp.concatenate(pieces, axis=0)

    def dispatch_grads(b):
        g_ref[b] = dot(pick(b), ct_ref[b, :rows, :]).astype(BF)

    def dispatch_rows(b):
        logits = lax.dot_general(
            router_ref[...], x_ref[b], (((0,), (1,)), ((), ())), preferred_element_type=F32
        )[:EXPERTS]
        hot = rank_all_ref[b].astype(F32) < 200.0
        top = jnp.max(jnp.where(hot, logits, NEGATIVE_LARGE), axis=0, keepdims=True)
        weight = jnp.where(hot, jnp.exp(jnp.minimum(logits - top, 0.0)), 0.0)
        gates = weight / jnp.sum(weight, axis=0, keepdims=True)
        for e in range(local):
            mine = jnp.where(expert_id() == base + e, gates, 0.0)
            gate_ref[b, e : e + 1, :] = jnp.sum(mine, axis=0, keepdims=True)
        xs_ref[b] = dot(pick(b), x_ref[b]).astype(BF)

    if plane:
        n = blocks
        leave_second = pltpu.make_async_copy(x_ref.at[me], second_ref, out_sem.at[0])
        leave_residual = pltpu.make_async_copy(gs_ref.at[:, :D], residual_ref, out_sem.at[1])

        def hop(far, side):
            block = me - far if side == 0 else me + far
            device = (group, me + 1 if side == 0 else me - 1)
            index = (side, far)
            return remote(
                x_ref.at[block], x_ref.at[block], xsend.at[index], xrecv.at[index], device
            )

        def sends(far, side):
            if side == 0:
                return (far < n - 1) & (me - far >= 0) & (me < n - 1)
            return (far < n - 1) & (me + far < n) & (me > 0)

        def arrives(far, side):
            return me - 1 - far >= 0 if side == 0 else me + 1 + far < n

        @pl.when(step == 0)
        def _():
            loads = [
                pltpu.make_async_copy(out_weight_in, stage_refs[2].at[2:4], in_sem.at[0]),
                pltpu.make_async_copy(tokens_in, xs_ref.at[0, :rows, :], in_sem.at[1]),
                pltpu.make_async_copy(mixed_in, xs_ref.at[1, :rows, :], in_sem.at[2]),
            ]
            for copy in loads:
                copy.start()
            for b in range(blocks):
                note_ranks(b)
            for copy in loads:
                copy.wait()
            out_weight = stage_refs[2][2:4].reshape(D, D)
            residual = xs_ref[0, :rows, :].astype(F32) + dot(xs_ref[1, :rows, :], out_weight)
            inverse = lax.rsqrt(jnp.mean(residual * residual, axis=-1, keepdims=True) + EPSILON)
            x_ref[me] = (residual * inverse * gain_ref[1:2, :]).astype(BF)
            gs_ref[:, :D] = residual
            greet([(None, by_c), (None, by_x), (None, by_y)] + line.neighbours())
            for side in (0, 1):

                @pl.when(sends(0, side))
                def _():
                    hop(0, side).start()

            leave_second.start()
            leave_residual.start()
            for b in range(blocks):
                dispatch_grads(b)
            dispatch_rows(me)

            def arrived(far, carry):
                for side in (0, 1):

                    @pl.when(arrives(far, side))
                    def _():
                        hop(far, side).wait_recv()

                    @pl.when(sends(far + 1, side))
                    def _():
                        hop(far + 1, side).start()

                for side in (0, 1):

                    @pl.when(arrives(far, side))
                    def _():
                        dispatch_rows(me - 1 - far if side == 0 else me + 1 + far)

                return carry

            lax.fori_loop(0, n - 1, arrived, 0)

        @pl.when(step == 1)
        def _():
            leave_second.wait()
            leave_residual.wait()
            for far in range(n - 1):
                for side in (0, 1):

                    @pl.when(sends(far, side))
                    def _():
                        hop(far, side).wait_send()

    else:

        @pl.when(step == 0)
        def _():
            for b in range(blocks):
                note_ranks(b)
                dispatch_grads(b)
                dispatch_rows(b)

    @pl.when(step < local)
    def _():
        here = pl.ds(pl.multiple_of(step * capacity, capacity), capacity)
        xs = jnp.concatenate([xs_ref[b, here, :] for b in range(blocks)], axis=0)
        g = jnp.concatenate([g_ref[b, here, :] for b in range(blocks)], axis=0).astype(F32)
        slot_id = lax.broadcasted_iota(jnp.int32, (capacity, rows), 0).astype(F32)
        gates = []
        for b in range(blocks):
            taken = rank_ref[b, pl.ds(step, 1), :] == slot_id
            gate = jnp.where(taken, gate_ref[b, pl.ds(step, 1), :], 0.0)
            gates.append(jnp.sum(gate, axis=1, keepdims=True))
        gate_slot = jnp.concatenate(gates, axis=0)
        w_gate, w_up, w_down = w_gate_ref[0], w_up_ref[0], w_down_ref[0]
        gate_pre = dot(xs, w_gate)
        up_pre = dot(xs, w_up)
        sigmoid = jax.nn.sigmoid(gate_pre)
        silu = gate_pre * sigmoid
        activation = (silu * up_pre).astype(BF)
        expert_out = dot(activation, w_down).astype(BF).astype(F32)
        slot_dot = jnp.sum(g * expert_out, axis=1, keepdims=True)
        grad_out = (gate_slot * g).astype(BF)
        scaled_out = (gate_slot * expert_out).astype(BF)
        grad_down = dot_tn(activation, grad_out).astype(BF)
        grad_activation = dot_nt(grad_out, w_down)
        grad_gate_pre = (
            grad_activation * up_pre * sigmoid * (1.0 + gate_pre * (1.0 - sigmoid))
        ).astype(BF)
        grad_up_pre = (grad_activation * silu).astype(BF)
        grad_gate = dot_tn(xs, grad_gate_pre).astype(BF)
        grad_up = dot_tn(xs, grad_up_pre).astype(BF)
        if plane:
            for ref, value in zip(stage_refs, (grad_gate, grad_up, grad_down)):
                ref[step % STAGES] = value.reshape(ref.shape[1:])
        else:
            out_gate_ref[0], out_up_ref[0], out_down_ref[0] = grad_gate, grad_up, grad_down
        grad_in = (dot_nt(grad_gate_pre, w_gate) + dot_nt(grad_up_pre, w_up)).astype(BF)
        lane = lax.broadcasted_iota(jnp.int32, (blocks * capacity, LANES), 1)
        high = slot_dot.astype(BF).astype(F32)
        middle = (slot_dot - high).astype(BF).astype(F32)
        low = slot_dot - high - middle
        mine = base + step
        dots = jnp.where(lane == mine, high, 0.0)
        dots = jnp.where(lane == mine + EXPERTS, middle, dots)
        dots = jnp.where(lane == mine + 2 * EXPERTS, low, dots).astype(BF)
        for b in range(blocks):
            part = slice(b * capacity, (b + 1) * capacity)
            xs_ref[b, here, :] = grad_in[part]
            g_ref[b, here, :] = scaled_out[part]
            dots_ref[b, here, :] = dots[part]

    def store_y(b):
        there = pl.ds(b * rows, rows)
        return pltpu.make_async_copy(g_ref.at[b, :rows, :], y_ref.at[there, :], y_sem.at[b])

    @pl.when(step == local - 1)
    def _():
        slot_expert = lax.broadcasted_iota(jnp.int32, (EXPERTS, slots), 1) // capacity
        spread_row = lax.broadcasted_iota(jnp.int32, (EXPERTS, slots), 0)
        spread = jnp.where(spread_row == slot_expert + base, 1.0, 0.0).astype(BF)
        slot_rank = (lax.broadcasted_iota(jnp.int32, (rows, slots), 1) % capacity).astype(F32)
        for b in range(blocks):
            there = slice(b * rows, (b + 1) * rows)
            ranks = dot_tn(rank_all_ref[b], spread)
            put = jnp.where(ranks == slot_rank, 1.0, 0.0).astype(BF)
            g_ref[b, :rows, :] = dot(put, g_ref[b]).astype(BF)
            store_y(b).start()
            back = dot(put, xs_ref[b]).astype(BF), dot(put, dots_ref[b]).astype(BF)
            if plane:
                gs_part[b, :, :D], gs_part[b, :, D:] = back
            else:
                gs_ref[there, :D], gs_ref[there, D:] = back
        if plane:
            line.start()

    @pl.when(step == pl.num_programs(0) - 1)
    def _():
        for b in range(blocks):
            store_y(b).wait()

    if not plane:
        return

    gate, up, low_down, high_down = range(4)
    low_rows, high_rows = slice(0, half), slice(half, 2 * half)

    def swap(e, i):
        return remote(
            stage_refs[i].at[e % STAGES, :, :, 1 - c],
            pair_refs[i].at[e % 3],
            csend.at[e % 2, i],
            crecv.at[e % 3, i],
            by_c,
        )

    def first(e, k):
        slot = e % 3
        source = {
            gate: lambda: pair_refs[0].at[slot, :, 1 - x],
            up: lambda: pair_refs[1].at[slot, 1 - y],
            low_down: lambda: pair_refs[2].at[slot, :, 1 - x, low_rows],
            high_down: lambda: pair_refs[2].at[slot, 1 - y, :, high_rows],
        }[k]()
        device = by_x if k in (gate, low_down) else by_y
        return remote(source, one_refs[k].at[slot], psend.at[slot, k], precv.at[slot, k], device)

    def second(e, k):
        along_x = k in (gate, low_down)
        source = one_refs[k].at[e % 3, 1 - y] if along_x else one_refs[k].at[e % 3, 1 - x]
        slot = e % 2
        return remote(
            source,
            two_refs[k].at[slot],
            qsend.at[slot, k],
            qrecv.at[slot, k],
            by_y if along_x else by_x,
        )

    def add(first_value, second_value):
        return (first_value.astype(F32) + second_value.astype(F32)).astype(BF)

    @pl.when(ticks & (tick >= 3))
    def _():
        e = tick - 3
        for k in range(4):
            second(e, k).wait()
        own = [one_refs[k][e % 3, y if k in (gate, low_down) else x] for k in range(4)]
        out_gate_ref[0] = add(own[gate], two_refs[gate][e % 2])
        out_up_ref[0] = add(own[up], two_refs[up][e % 2])
        out_down_ref[0, low_rows] = add(own[low_down], two_refs[low_down][e % 2])
        out_down_ref[0, high_rows] = add(own[high_down], two_refs[high_down][e % 2])

    @pl.when(ticks & (tick >= 2) & (tick < local + 2))
    def _():
        e = tick - 2
        slot = e % 3
        for k in range(4):
            first(e, k).wait()
            for t in (0, 1):
                mine = {
                    gate: lambda: pair_refs[0][slot, t, x],
                    up: lambda: pair_refs[1][slot, y, t],
                    low_down: lambda: pair_refs[2][slot, t, x, low_rows],
                    high_down: lambda: pair_refs[2][slot, y, t, high_rows],
                }[k]()
                one_refs[k][slot, t] = add(mine, one_refs[k][slot, t])
            second(e, k).start()

    @pl.when(ticks & (tick >= 1) & (tick < local + 1))
    def _():
        e = tick - 1
        slot = e % 3
        for i in range(3):
            swap(e, i).wait()

            def pair_sum(t, carry):
                a, b = t // 2, t % 2
                pair_refs[i][slot, a, b] = add(
                    stage_refs[i][e % STAGES, a, b, c], pair_refs[i][slot, a, b]
                )
                return carry

            lax.fori_loop(0, 4, pair_sum, 0)
        for k in range(4):
            first(e, k).start()

    @pl.when(ticks & (tick < local))
    def _():
        for i in range(3):
            swap(tick, i).start()

    for hop in range(1, blocks - 1):

        @pl.when(step == local + hop)
        def _():
            line.forward(hop)

    @pl.when(step == local + blocks - 1)
    def _():
        line.finish(gs_ref)


def run_experts(
    sources, ct_all, router, rank_all, w_gate, w_up, w_down, capacity, plane, collective_id
):
    blocks, _, rows = rank_all.shape
    total, local = blocks * rows, w_gate.shape[0]
    slots = local * capacity
    sizes = (blocks, rows, local, capacity)
    whole = lambda shape: pl.BlockSpec(
        shape, lambda e: (0,) * len(shape), pipeline_mode=pl.Buffered(1)
    )
    per = lambda shape: pl.BlockSpec((1,) + shape, lambda e: (jnp.minimum(e, local - 1), 0, 0))
    shapes = ((D, FF), (D, FF), (FF, D))
    scratch = [
        pltpu.VMEM((blocks, slots, D), BF),
        pltpu.VMEM((blocks, slots, D), BF),
        pltpu.VMEM((blocks, local, rows), F32),
        pltpu.VMEM((blocks, local, rows), F32),
        pltpu.VMEM((blocks, slots, LANES), BF),
        pltpu.SemaphoreType.DMA((blocks,)),
    ]
    params = dict(dimension_semantics=("arbitrary",), vmem_limit_bytes=63 * 1024 * 1024)
    if plane:
        eighths = [(a // 8, b) for a, b in shapes]
        out = lambda shape: pl.BlockSpec(
            (1,) + shape, lambda e: (jnp.maximum(plane_tick(e, local)[0] - 3, 0), 0, 0)
        )
        grad_shapes, grad_specs = eighths, [out(shape) for shape in eighths]
        low = (eighths[2][0] // 2, eighths[2][1])
        passed = (eighths[0], eighths[1], low, low)
        scratch += [pltpu.VMEM((STAGES, 2, 2, 2) + shape, BF) for shape in eighths]
        scratch += [pltpu.VMEM((3, 2, 2) + shape, BF) for shape in eighths]
        scratch += [pltpu.VMEM((3, 2) + shape, BF) for shape in passed]
        scratch += [pltpu.VMEM((2,) + shape, BF) for shape in passed]
        sems = [(2, 3), (3, 3), (3, 4), (3, 4), (2, 4), (2, 4)]
        scratch += [pltpu.SemaphoreType.DMA(shape) for shape in sems]
        scratch += [pltpu.VMEM((blocks, rows, D + LANES), BF)]
        scratch += line_sum_scratch(blocks, rows, D + LANES)
        scratch += [pltpu.VMEM((blocks, rows, D), BF)]
        sems = [(2, blocks - 1), (2, blocks - 1), (3,), (2,)]
        scratch += [pltpu.SemaphoreType.DMA(shape) for shape in sems]
        mixed_low, tokens, out_weight, gain = sources
        sources = [mixed_low, tokens, out_weight.reshape((2, 2, 2, 2) + eighths[2]), gain]
        source_specs = [ANY] * 3 + [whole(gain.shape)]
        more_shapes = [
            jax.ShapeDtypeStruct((rows, D), BF),
            jax.ShapeDtypeStruct((rows, D), F32),
        ]
        gs_shape, gs_type = (rows, D + LANES), F32
        params |= dict(collective_id=collective_id, has_side_effects=True)
    else:
        grad_shapes, grad_specs = shapes, [per(shape) for shape in shapes]
        gs_shape, gs_type = (total, D + LANES), BF
        sources = [sources[0].reshape(blocks, rows, D)]
        source_specs = [whole(sources[0].shape)]
        more_shapes = []
    flops = 2 * total * D * slots * 4 // blocks + 18 * blocks * slots * D * FF
    return pl.pallas_call(
        functools.partial(expert_kernel, sizes, plane),
        grid=(local + 6 if plane else local,),
        out_shape=[
            jax.ShapeDtypeStruct((total, D), BF),
            jax.ShapeDtypeStruct(gs_shape, gs_type),
        ]
        + [jax.ShapeDtypeStruct((local,) + shape, BF) for shape in grad_shapes]
        + more_shapes,
        in_specs=source_specs
        + [
            whole(ct_all.shape),
            whole(router.shape),
            whole(rank_all.shape),
        ]
        + [per(shape) for shape in shapes],
        out_specs=[ANY, whole(gs_shape)] + grad_specs + [ANY] * len(more_shapes),
        scratch_shapes=scratch,
        compiler_params=pltpu.CompilerParams(**params),
        cost_estimate=pl.CostEstimate(
            flops=flops, bytes_accessed=2 * (6 * local * D * FF + 4 * total * D), transcendentals=0
        ),
        name="experts",
    )(*sources, ct_all, router, rank_all, w_gate, w_up, w_down)


def rotate(tile, cosine, sine):
    half = HEAD_DIMENSION // 2
    lane = lax.broadcasted_iota(jnp.int32, tile.shape, 1) % HEAD_DIMENSION
    other = jnp.where(lane < half, pltpu.roll(tile, LANES - half, 1), pltpu.roll(tile, half, 1))
    return tile * cosine + other * sine


def normed(tokens_ref):
    value = tokens_ref[...].astype(F32)
    inverse = lax.rsqrt(jnp.mean(value * value, axis=-1, keepdims=True) + EPSILON)
    return value * inverse, inverse


def mask_bias(bias_ref, length_ref, rows):
    base = lax.axis_index("expert") * rows
    key = lax.broadcasted_iota(jnp.int32, bias_ref.shape, 0)
    query = lax.broadcasted_iota(jnp.int32, bias_ref.shape, 1) + base
    allowed = (key <= query) & (key < length_ref[0])
    bias_ref[...] = jnp.where(allowed, 0.0, NEGATIVE_LARGE)


def head_columns(ref, head):
    start = 2 * HEAD_DIMENSION * head
    middle = start + HEAD_DIMENSION
    return jnp.concatenate([ref[:, start:middle], ref[:, middle : middle + HEAD_DIMENSION]], 0)


def put_heads(ref, head, transposed):
    rows = ref.shape[0]
    value = transposed.T
    start = 2 * HEAD_DIMENSION * head
    middle = start + HEAD_DIMENSION
    ref[:, start:middle] = value[:rows].astype(ref.dtype)
    ref[:, middle : middle + HEAD_DIMENSION] = value[rows:].astype(ref.dtype)


def attention_kernel(
    n,
    length_ref,
    tokens_ref,
    gain_ref,
    weight_ref,
    cosine_ref,
    sine_ref,
    routes_ref,
    mixed_ref,
    log_total_ref,
    kv_all_ref,
    query_out_ref,
    rank_all_ref,
    *scratch,
):
    bias_ref, query_ref, kv_ref, chunk_ref, rank_buffer, send, recv, rank_send, rank_recv = scratch
    pair, pairs = pl.program_id(0), pl.num_programs(0)
    group, me = lax.axis_index("group"), lax.axis_index("expert")
    left, right = (group, me - 1), (group, me + 1)
    rows, width = kv_ref.shape[1:]

    def hop(j, step, side):
        block = me - step if side == 0 else me + step
        source = kv_ref.at[j] if step == 0 else chunk_ref.at[j, block]
        index = (j, side, step)
        return remote(
            source,
            chunk_ref.at[j, block],
            send.at[index],
            recv.at[index],
            right if side == 0 else left,
        )

    def rank_hop(step, side):
        block = me - step if side == 0 else me + step
        source = rank_buffer.at[block]
        index = (side, step)
        return remote(
            source,
            rank_buffer.at[block],
            rank_send.at[index],
            rank_recv.at[index],
            right if side == 0 else left,
        )

    def sends(step, side):
        return (me - step >= 0) & (me < n - 1) if side == 0 else (me + step < n) & (me > 0)

    def arrives(step, side):
        return me - 1 - step >= 0 if side == 0 else me + 1 + step < n

    def launch(make, step):
        for side in (0, 1):

            @pl.when(sends(step, side))
            def _():
                make(step, side).start()

    def await_hop(make, step):
        for side in (0, 1):

            @pl.when(arrives(step, side))
            def _():
                make(step, side).wait_recv()

    def drain(make):
        for step in range(n - 1):
            for side in (0, 1):

                @pl.when(sends(step, side))
                def _():
                    make(step, side).wait_send()

    def chunk(j):
        return lambda step, side: hop(j, step, side)

    @pl.when(pair == 0)
    def _():
        unit, _ = normed(tokens_ref)
        first_norm = (unit * gain_ref[0:1, :]).astype(BF)
        cosine, sine = cosine_ref[...], sine_ref[...]
        count = kv_ref.shape[0]
        query_width = count * width
        key_width = query_width // 2
        keys = dot(first_norm, weight_ref[:, query_width : query_width + key_width])
        values = dot(first_norm, weight_ref[:, query_width + key_width :])
        for j in range(count):
            columns = slice(j * LANES, (j + 1) * LANES)
            kv_ref[j, :, :LANES] = rotate(keys[:, columns], cosine, sine).astype(BF)
            kv_ref[j, :, LANES:] = values[:, columns].astype(BF)
        greet([(me > 0, left), (me < n - 1, right)])
        launch(chunk(0), 0)
        launch(chunk(1), 0)
        routes = routes_ref[...].astype(F32).T
        expert_id = lax.broadcasted_iota(jnp.int32, (EXPERTS, rows), 0).astype(F32)
        hot = jnp.zeros((EXPERTS, rows), F32)
        for k in range(TOP):
            hot = jnp.where(routes[k : k + 1, :] == expert_id, 1.0, hot)
        row_id = lax.broadcasted_iota(jnp.int32, (rows, rows), 0)
        earlier = jnp.where(row_id < lax.broadcasted_iota(jnp.int32, (rows, rows), 1), 1.0, 0.0)
        rank = dot(hot.astype(BF), earlier.astype(BF))
        rank_buffer[me] = jnp.where(hot > 0.5, rank, 255.0).astype(BF)
        queries = dot(first_norm, weight_ref[:, :query_width])
        for j in range(2 * count):
            start = (j % 2) * LANES
            tile = queries[:, j * LANES : (j + 1) * LANES]
            query_ref[j // 2, :, start : start + LANES] = rotate(tile, cosine, sine).astype(BF)
        mask_bias(bias_ref, length_ref, rows)
        await_hop(chunk(0), 0)
        launch(chunk(0), 1)

    for step in range(1, n - 1):
        await_hop(chunk(pair), step)
        if step < n - 2:
            launch(chunk(pair), step + 1)

    @pl.when(pair + 1 < pairs)
    def _():
        await_hop(chunk(pair + 1), 0)
        launch(chunk(pair + 1), 1)

    @pl.when(pair + 2 < pairs)
    def _():
        launch(chunk(pair + 2), 0)

    @pl.when(pair == 1)
    def _():
        launch(rank_hop, 0)

    for step in range(n - 1):

        @pl.when(pair == jnp.minimum(2 + step, pairs - 1))
        def _():
            await_hop(rank_hop, step)
            if step < n - 2:
                launch(rank_hop, step + 1)

    chunk_ref[pair, me] = kv_ref[pair]
    kv = chunk_ref[pair].reshape(n * rows, width)
    kv_all_ref[...] = kv
    query_out_ref[0] = query_ref[pair]
    bias = jnp.concatenate([bias_ref[...]] * 2, axis=1)
    for head in (0, 1):
        start = head * HEAD_DIMENSION
        key = kv[:, start : start + HEAD_DIMENSION]
        value = kv[:, LANES + start : LANES + start + HEAD_DIMENSION]
        query = head_columns(query_ref.at[pair], head) * jnp.asarray(HEAD_DIMENSION**-0.5, BF)
        scores = dot_nt(key, query) + bias
        top = jnp.max(scores, axis=0, keepdims=True)
        weights = jnp.exp(scores - top)
        total = jnp.sum(weights, axis=0, keepdims=True)
        put_heads(mixed_ref, head, dot_tn(value, weights.astype(BF)) / total)
        log_total_ref[0, head : head + 1, :] = top + jnp.log(total)

    @pl.when(pair == pairs - 1)
    def _():
        drain(rank_hop)
        rank_all_ref[...] = rank_buffer[...]
        for j in range(KEY_VALUE_HEADS // 2):
            drain(chunk(j))


def attention(length, tokens, gain, weight, cosine, sine, routes, n, collective_id):
    rows = tokens.shape[0]
    rank = jax.ShapeDtypeStruct((EXPERTS, rows), BF)
    keys, width = n * rows, 2 * LANES
    pairs = KEY_VALUE_HEADS // 2
    return pl.pallas_call(
        functools.partial(attention_kernel, n),
        grid=(pairs,),
        out_shape=(
            jax.ShapeDtypeStruct((rows, pairs * width), BF),
            jax.ShapeDtypeStruct((pairs, 2, 2 * rows), F32),
            jax.ShapeDtypeStruct((keys, pairs * width), BF),
            jax.ShapeDtypeStruct((pairs, rows, width), BF),
            jax.ShapeDtypeStruct((n,) + rank.shape, rank.dtype),
        ),
        in_specs=[pl.BlockSpec(memory_space=pltpu.SMEM)] + [IN_VMEM] * 6,
        out_specs=(
            pl.BlockSpec((rows, width), lambda j: (0, j)),
            pl.BlockSpec((1, 2, 2 * rows), lambda j: (j, 0, 0)),
            pl.BlockSpec((keys, width), lambda j: (0, j)),
            pl.BlockSpec((1, rows, width), lambda j: (j, 0, 0)),
            IN_VMEM,
        ),
        scratch_shapes=[
            pltpu.VMEM((keys, rows), F32),
            pltpu.VMEM((pairs, rows, width), BF),
            pltpu.VMEM((pairs, rows, width), BF),
            pltpu.VMEM((pairs, n, rows, width), BF),
            pltpu.VMEM((n,) + rank.shape, rank.dtype),
            pltpu.SemaphoreType.DMA((pairs, 2, n - 1)),
            pltpu.SemaphoreType.DMA((pairs, 2, n - 1)),
            pltpu.SemaphoreType.DMA((2, n - 1)),
            pltpu.SemaphoreType.DMA((2, n - 1)),
        ],
        compiler_params=pltpu.CompilerParams(
            dimension_semantics=("arbitrary",),
            vmem_limit_bytes=56 * 1024 * 1024,
            collective_id=collective_id,
            has_side_effects=True,
        ),
        cost_estimate=pl.CostEstimate(
            flops=16 * rows * keys * D, bytes_accessed=100000000, transcendentals=0
        ),
        name="attention",
    )(length, tokens, gain, weight, cosine, sine, routes)


def attention_back_kernel(
    n,
    plane,
    length_ref,
    q_ref,
    kv_ref,
    log_total_ref,
    gs_ref,
    residual_ref,
    second_ref,
    ct_ref,
    routes_ref,
    gain_ref,
    router_ref,
    out_weight_ref,
    *refs,
):
    owns, refs = refs[: 3 * plane], refs[3 * plane :]
    grad_q_ref, grad_kv_ref, grad_residual_ref, grad_attn_ref, grad_router_ref, grad_gain_ref = refs[:6]
    wholes, refs = refs[6 : 6 + 3 * plane], refs[6 + 3 * plane :]
    bias_ref, grad_ref, terms_ref, landing, staging, send, recv = refs[:7]
    step, pairs = pl.program_id(0), pl.num_programs(0) - 1
    partners = []
    if plane:
        gather = PlaneGather(owns, wholes, 0, *refs[7:])
        partners = [(None, device) for device in gather.partners]

    def line(j):
        return LineSum(
            n, terms_ref.at[j], landing.at[j], staging.at[j], send.at[j], recv.at[j]
        )

    @pl.when(step == 0)
    def _():
        greet(line(0).neighbours() + partners)
        if plane:
            gather.begin()
        mask_bias(bias_ref, length_ref, q_ref.shape[1])
        routes = routes_ref[...]
        expert_id = lax.broadcasted_iota(jnp.int32, (routes.shape[0], EXPERTS), 1)
        hot = expert_id == routes[:, 0:1]
        for k in range(1, TOP):
            hot = hot | (expert_id == routes[:, k : k + 1])
        second, router = second_ref[...], router_ref[:, :EXPERTS]
        logits = dot(second, router)
        top = jnp.max(jnp.where(hot, logits, NEGATIVE_LARGE), axis=-1, keepdims=True)
        weight = jnp.where(hot, jnp.exp(jnp.minimum(logits - top, 0.0)), 0.0)
        gates = weight / jnp.sum(weight, axis=-1, keepdims=True)
        grad_gates = gs_ref[:, D : D + EXPERTS] + gs_ref[:, D + EXPERTS : D + 2 * EXPERTS]
        grad_gates = grad_gates + gs_ref[:, D + 2 * EXPERTS : D + 3 * EXPERTS]
        mean = jnp.sum(gates * grad_gates, axis=-1, keepdims=True)
        grad_logits = (gates * (grad_gates - mean)).astype(BF)
        grad_second = gs_ref[:, :D] + dot_nt(grad_logits, router)
        grad_router_ref[...] = jnp.zeros_like(grad_router_ref)
        grad_router_ref[:, :EXPERTS] = dot_tn(second, grad_logits)
        unit, inverse = normed(residual_ref)
        grad_gain_ref[...] = jnp.sum(grad_second * unit, axis=0, keepdims=True)
        scaled = grad_second * gain_ref[1:2, :]
        mean = jnp.mean(scaled * unit, axis=-1, keepdims=True)
        grad_residual = ct_ref[...].astype(F32) + inverse * (scaled - unit * mean)
        grad_residual_ref[...] = grad_residual
        grad_attn_ref[...] = grad_residual.astype(BF)
        grad_mixed = dot_nt(grad_residual.astype(BF), out_weight_ref[...]).astype(BF)
        width = grad_ref.shape[2]
        for j in range(grad_ref.shape[0]):
            grad_ref[j] = grad_mixed[:, j * width : (j + 1) * width]

    @pl.when(step == 2)
    def _():
        if plane:
            gather.second()

    @pl.when(step < pairs)
    def _():
        attention_back_pair(
            q_ref, kv_ref, grad_ref.at[step], log_total_ref, grad_q_ref, terms_ref.at[step], bias_ref
        )
        line(step).start()

    @pl.when(step > 0)
    def _():
        for hop in range(1, n - 1):
            line(step - 1).forward(hop)
        line(step - 1).finish(grad_kv_ref)

    @pl.when(step == pairs)
    def _():
        if plane:
            gather.third()
            gather.finish()


def attention_back_pair(q_ref, kv_ref, grad_ref, log_total_ref, grad_q_ref, grad_kv_ref, bias_ref):
    scale = HEAD_DIMENSION**-0.5
    blocks, rows, _ = grad_kv_ref.shape
    q_ref = q_ref.at[0]
    bias = jnp.concatenate([bias_ref[...]] * 2, axis=1)
    for head in (0, 1):
        columns = slice(head * HEAD_DIMENSION, (head + 1) * HEAD_DIMENSION)
        key, value = kv_ref[:, :LANES][:, columns], kv_ref[:, LANES:][:, columns]
        query = head_columns(q_ref, head) * jnp.asarray(scale, BF)
        grad = head_columns(grad_ref, head)
        scores = dot_nt(key, query) + bias
        probs = jnp.exp(scores - log_total_ref[0, head : head + 1, :])
        grad_probs = dot_nt(value, grad)
        delta = jnp.sum(probs * grad_probs, axis=0, keepdims=True)
        grad_scores = (probs * (grad_probs - delta)).astype(BF)
        grad_key = dot(grad_scores, query).astype(BF).reshape(blocks, rows, HEAD_DIMENSION)
        grad_kv_ref[:, :, columns] = grad_key
        grad_value = dot(probs.astype(BF), grad).astype(BF).reshape(blocks, rows, HEAD_DIMENSION)
        start = LANES + head * HEAD_DIMENSION
        grad_kv_ref[:, :, start : start + HEAD_DIMENSION] = grad_value
        put_heads(grad_q_ref, head, dot_tn(key, grad_scores) * scale)


def attention_back(length, query, kv_all, log_total, sources, sums, n, collective_id):
    plane = len(sums) > 0
    rows, keys = query.shape[1], kv_all.shape[0]
    pairs, width = KEY_VALUE_HEADS // 2, 2 * LANES
    now = lambda j: jnp.minimum(j, pairs - 1)
    row_spec = pl.BlockSpec((rows, width), lambda j: (0, now(j)))
    return pl.pallas_call(
        functools.partial(attention_back_kernel, n, plane),
        grid=(pairs + 1,),
        out_shape=(
            jax.ShapeDtypeStruct((rows, pairs * width), F32),
            jax.ShapeDtypeStruct((rows, pairs * width), BF),
            jax.ShapeDtypeStruct((rows, D), F32),
            jax.ShapeDtypeStruct((rows, D), BF),
            jax.ShapeDtypeStruct((D, LANES), F32),
            jax.ShapeDtypeStruct((1, D), F32),
        )
        + (tuple(plane_gather_shapes(sums)) if plane else ()),
        in_specs=[
            pl.BlockSpec(memory_space=pltpu.SMEM),
            pl.BlockSpec((1, rows, width), lambda j: (now(j), 0, 0)),
            pl.BlockSpec((keys, width), lambda j: (0, now(j))),
            pl.BlockSpec((1, 2, 2 * rows), lambda j: (now(j), 0, 0)),
        ]
        + [IN_VMEM] * (len(sources) + len(sums)),
        out_specs=(
            row_spec,
            pl.BlockSpec((rows, width), lambda j: (0, jnp.maximum(j - 1, 0))),
        )
        + (IN_VMEM,) * 4
        + (ANY,) * len(sums),
        scratch_shapes=[
            pltpu.VMEM((keys, rows), F32),
            pltpu.VMEM((pairs, rows, width), BF),
            pltpu.VMEM((pairs, n, rows, width), BF),
            pltpu.VMEM((pairs, 2, n - 1, rows, width), BF),
            pltpu.VMEM((pairs, 2, n - 2, rows, width), BF),
            pltpu.SemaphoreType.DMA((pairs, 2, n - 1)),
            pltpu.SemaphoreType.DMA((pairs, 2, n - 1)),
        ]
        + (plane_gather_sems() if plane else []),
        compiler_params=pltpu.CompilerParams(
            dimension_semantics=("arbitrary",),
            vmem_limit_bytes=60 * 1024 * 1024,
            collective_id=collective_id,
            has_side_effects=True,
        ),
        cost_estimate=pl.CostEstimate(
            flops=40 * rows * keys * D, bytes_accessed=100000000, transcendentals=0
        ),
        name="attention_back",
    )(length, query, kv_all, log_total, *sources, *sums)


def widen_kernel(count, *refs):
    step = pl.program_id(0)
    for i, ref in enumerate(refs[:-1]):

        @pl.when((step >= i * count) & (step < (i + 1) * count))
        def _():
            refs[-1][...] = ref[...].astype(F32)


def widen(values):
    count = values[0].shape[0]
    block = (1,) + values[0].shape[1:]

    def spec(i):
        return pl.BlockSpec(block, lambda e: (jnp.clip(e - i * count, 0, count - 1), 0, 0))

    total = count * len(values)
    size = total * block[1] * block[2]
    return pl.pallas_call(
        functools.partial(widen_kernel, count),
        grid=(total,),
        out_shape=jax.ShapeDtypeStruct((total,) + block[1:], F32),
        in_specs=[spec(i) for i in range(len(values))],
        out_specs=pl.BlockSpec(block, lambda e: (e, 0, 0)),
        compiler_params=pltpu.CompilerParams(dimension_semantics=("arbitrary",)),
        cost_estimate=pl.CostEstimate(flops=0, bytes_accessed=6 * size, transcendentals=0),
        name="widen",
    )(*values)


def unpair_columns(value):
    rows = value.shape[0]
    value = value.reshape(rows, -1, 2, LANES)
    return value[:, :, 0].reshape(rows, -1), value[:, :, 1].reshape(rows, -1)


def gather_rows(value):
    return lax.all_gather(value, "expert", axis=0, tiled=True)


def scatter_rows(value):
    return lax.psum_scatter(value, "expert", scatter_dimension=0, tiled=True)


def per_device(
    tokens,
    lengths,
    routes,
    norm_gain1,
    w_query,
    key_projection,
    value_projection,
    w_out,
    norm_gain2,
    w_router,
    w_gate,
    w_up,
    w_down,
    cotangent,
):
    rows = tokens.shape[0]
    n, groups = lax.axis_size("expert"), lax.axis_size("group")
    plane = groups == 8 and w_gate.shape[0] == 8
    my_index = lax.axis_index("expert")
    capacity = 3 * rows * TOP // (2 * EXPERTS)
    query_width, key_width = w_query.shape[1], key_projection.shape[1]
    length = lengths[0]
    positions = my_index * rows + jnp.arange(rows, dtype=jnp.int32)
    valid_rows = (positions < length)[:, None]
    grad_output = jnp.where(valid_rows, cotangent, jnp.zeros_like(cotangent))

    small = jnp.pad(w_router, ((0, 0), (0, LANES - EXPERTS)))
    gains = jnp.pad(jnp.concatenate([norm_gain1, norm_gain2]), (0, D - 2 * norm_gain1.shape[0]))
    below = jnp.broadcast_to(gains, (16, D))
    qkv_weight, out_weight, router, extra_all = gather_weights(
        w_query,
        key_projection,
        value_projection,
        w_out,
        small,
        jnp.concatenate([grad_output, below], axis=0),
        n,
        1,
    )
    extra_all = extra_all.reshape(n, rows + 16, D)
    gains = extra_all[:, rows, : 2 * norm_gain1.shape[0]].reshape(n, 2, -1)
    gains = jnp.transpose(gains, (1, 0, 2)).reshape(2, D).astype(F32)

    cosine_lookup, sine_lookup = [table[:, 0] for table in rotary_tables(positions, HEAD_DIMENSION)]
    cosine = jnp.tile(cosine_lookup, (1, 4))
    sine = jnp.tile(jnp.concatenate([-sine_lookup, sine_lookup], axis=1), (1, 2))
    token_f32 = tokens.astype(F32)
    mixed_low, log_total, kv_all, query_pairs, rank_all = attention(
        lengths, tokens, gains, qkv_weight, cosine, sine, routes, n, 2
    )
    expert_args = (extra_all, router, rank_all, w_gate, w_up, w_down, capacity)
    if plane:
        sources = (mixed_low, tokens, out_weight, gains)
        y_part, gs, grad_gate, grad_up, grad_down, second_norm, residual = run_experts(
            sources, *expert_args, plane, 7
        )
    else:
        residual = token_f32 + dot(mixed_low, out_weight)
        inverse_two = lax.rsqrt(jnp.mean(residual * residual, axis=-1, keepdims=True) + EPSILON)
        second_norm = (residual * inverse_two * gains[1]).astype(BF)
        sources = line_gather([second_norm], n, 3, "gather_rows")
        y_part, gs, grad_gate, grad_up, grad_down = run_experts(sources, *expert_args, plane, 7)
        gs = line_scatter(gs, n, F32, 4, "scatter_grads")

    sources = (
        gs,
        residual,
        second_norm,
        grad_output,
        routes,
        gains,
        router,
        out_weight,
    )
    sums = (grad_gate, grad_up, grad_down) if plane else ()
    grad_query_acc, kv_gradient, grad_residual, grad_attn, grad_router, gain_two_row, *low = (
        attention_back(lengths, query_pairs, kv_all, log_total, sources, sums, n, 5)
    )
    if plane:
        *shares, expert_sum, grad_rest, high = reduce_weights(
            grad_query_acc,
            kv_gradient,
            tokens,
            gains,
            qkv_weight,
            cosine,
            sine,
            mixed_low,
            grad_attn,
            grad_router,
            gain_two_row,
            y_part,
            sums,
            n,
            6,
        )
        grad_tokens = grad_residual + grad_rest
    else:
        inverse_one = lax.rsqrt(jnp.mean(token_f32 * token_f32, axis=-1, keepdims=True) + EPSILON)
        unit_one = token_f32 * inverse_one
        first_norm = (unit_one * gains[0]).astype(BF)
        own_key_gradient, own_value_gradient = unpair_columns(kv_gradient)
        back = lambda value: apply_rotation(
            value.astype(F32).reshape(rows, -1, HEAD_DIMENSION),
            cosine_lookup[:, None],
            -sine_lookup[:, None],
        )
        grad_query_pre = back(grad_query_acc).reshape(rows, query_width).astype(BF)
        grad_key_pre = back(own_key_gradient).reshape(rows, key_width).astype(BF)
        grad_qkv_pre = jnp.concatenate([grad_query_pre, grad_key_pre, own_value_gradient], axis=1)
        grad_first = dot_nt(grad_qkv_pre, qkv_weight)
        scaled_one = grad_first * gains[0]
        grad_gain1 = jnp.sum(grad_first * unit_one, axis=0)
        grad_tokens = grad_residual + inverse_one * (
            scaled_one - unit_one * jnp.mean(scaled_one * unit_one, axis=-1, keepdims=True)
        )
        gains = [grad_gain1[:, None], gain_two_row.T]
        rest = grad_router[:, EXPERTS + 2 :]
        grad_small = jnp.concatenate([grad_router[:, :EXPERTS]] + gains + [rest], axis=1)
        shares = (dot_tn(first_norm, grad_qkv_pre), dot_tn(mixed_low, grad_attn), grad_small)
        shares = [lax.psum(scatter_rows(share.astype(BF)), "group") for share in shares]
        share_qkv, share_out, share_small = shares
        split = (query_width, query_width + key_width)
        shares = jnp.split(share_qkv, split, axis=1) + [share_out, share_small]
        expert_sum = line_scatter(y_part, n, F32, 8, "scatter_outputs")
    mixed = (residual + expert_sum).astype(BF)
    shares = [share.astype(F32) for share in shares]
    share_query, share_key, share_value, share_out, share_small = shares

    if plane:
        widths = (FF, FF, D)
        halves = [[h.reshape(h.shape[0], -1, w) for h in p] for *p, w in zip(low, high, widths)]
        grad_experts = [widen(pair) for pair in halves]
    else:
        grad_experts = []
        for value in (grad_gate, grad_up, grad_down):
            value = lax.psum_scatter(value, "group", scatter_dimension=1, tiled=True)
            grad_experts.append(widen([lax.all_gather(value, "group", axis=1, tiled=True)]))

    return (
        mixed,
        grad_tokens,
        share_small[:, EXPERTS],
        share_query,
        share_key,
        share_value,
        share_out,
        share_small[:, EXPERTS + 1],
        share_small[:, :EXPERTS],
        *grad_experts,
    )


def solution(mesh):
    rows = P(("group", "expert"), None)
    vector, matrix, stack = P("expert"), P("expert", None), P("expert", None, None)
    return jax.shard_map(
        per_device,
        mesh=mesh,
        in_specs=(
            rows,
            P("group"),
            rows,
            vector,
            matrix,
            matrix,
            matrix,
            matrix,
            vector,
            matrix,
            stack,
            stack,
            stack,
            rows,
        ),
        out_specs=(
            rows,
            rows,
            vector,
            matrix,
            matrix,
            matrix,
            matrix,
            vector,
            matrix,
            stack,
            stack,
            stack,
        ),
        check_vma=False,
    )
```

```python
import functools
import itertools

import jax
import jax.numpy as jnp
from jax import lax
from jax.experimental import pallas as pl
from jax.experimental.pallas import tpu as pltpu
from jax.sharding import PartitionSpec as P

D = 1024
QUERY_HEADS = 16
KEY_VALUE_HEADS = 8
HEAD_DIMENSION = 64
EXPERTS = 32
TOP = 8
FF = 512
LANES = 128
STAGES = 4

EPSILON = 1e-05
NEGATIVE_LARGE = -1e30
BF = jnp.bfloat16
F32 = jnp.float32


def rotary_tables(positions, head_size):
    half_width = head_size // 2
    frequency = 10000.0 ** (-2.0 * jnp.arange(half_width).astype(F32) / head_size)
    angles = positions.astype(F32)[:, None] * frequency[None, :]
    return (jnp.cos(angles)[:, None, :], jnp.sin(angles)[:, None, :])


def apply_rotation(tensor_in, cosine_lookup, sine_lookup):
    half_width = tensor_in.shape[-1] // 2
    first_half = tensor_in[..., :half_width]
    second_half = tensor_in[..., half_width:]
    return jnp.concatenate(
        [
            first_half * cosine_lookup - second_half * sine_lookup,
            second_half * cosine_lookup + first_half * sine_lookup,
        ],
        axis=-1,
    )


def dot(a, b):
    return jnp.dot(a, b, preferred_element_type=F32)


def dot_nt(a, b):
    return lax.dot_general(a, b, (((1,), (1,)), ((), ())), preferred_element_type=F32)


def dot_tn(a, b):
    return lax.dot_general(a, b, (((0,), (0,)), ((), ())), preferred_element_type=F32)


MESH = pl.DeviceIdType.MESH
ANY = pl.BlockSpec(memory_space=pl.ANY)
IN_VMEM = pl.BlockSpec(memory_space=pltpu.VMEM)


def remote(source, target, send, receive, device):
    return pltpu.make_async_remote_copy(
        src_ref=source,
        dst_ref=target,
        send_sem=send,
        recv_sem=receive,
        device_id=device,
        device_id_type=MESH,
    )


def greet(devices):
    barrier = pltpu.get_barrier_semaphore()
    count = 0
    for condition, device in devices:
        if condition is None:
            pl.semaphore_signal(barrier, inc=1, device_id=device, device_id_type=MESH)
            count = count + 1
        else:

            @pl.when(condition)
            def _():
                pl.semaphore_signal(barrier, inc=1, device_id=device, device_id_type=MESH)

            count = count + jnp.where(condition, 1, 0)
    pl.semaphore_wait(barrier, count)


def line_gather_kernel(n, count, *refs):
    ins, outs = refs[:count], refs[count : 2 * count]
    local, send, receive = refs[2 * count :]
    group, me = lax.axis_index("group"), lax.axis_index("expert")
    left, right = (group, me - 1), (group, me + 1)
    own = [
        pltpu.make_async_copy(ins[i], outs[i].at[me], local.at[i]) for i in range(count)
    ]
    for copy in own:
        copy.start()
    greet([(me > 0, left), (me < n - 1, right)])

    def hop(i, step, side):
        block = me - step if side == 0 else me + step
        source = ins[i] if step == 0 else outs[i].at[block]
        index = (side, step, i)
        return remote(
            source, outs[i].at[block], send.at[index], receive.at[index], right if side == 0 else left
        )

    def arrival(i, step, side):
        block = me - 1 - step if side == 0 else me + 1 + step
        index = (side, step, i)
        return remote(
            outs[i].at[block], outs[i].at[block], send.at[index], receive.at[index], left if side == 0 else right
        )

    def sends(step, side):
        return (me - step >= 0) & (me < n - 1) if side == 0 else (me + step < n) & (me > 0)

    def arrives(step, side):
        return me - 1 - step >= 0 if side == 0 else me + 1 + step < n

    for step in range(n - 1):
        for side in (0, 1):

            @pl.when(sends(step, side))
            def _():
                for i in range(count):
                    hop(i, step, side).start()

        for side in (0, 1):

            @pl.when(arrives(step, side))
            def _():
                for i in range(count):
                    arrival(i, step, side).wait_recv()

    for step in range(n - 1):
        for side in (0, 1):

            @pl.when(sends(step, side))
            def _():
                for i in range(count):
                    hop(i, step, side).wait_send()

    for copy in own:
        copy.wait()


def line_gather(values, n, collective_id, name):
    count = len(values)
    outs = pl.pallas_call(
        functools.partial(line_gather_kernel, n, count),
        out_shape=[jax.ShapeDtypeStruct((n,) + v.shape, v.dtype) for v in values],
        in_specs=[IN_VMEM] * count,
        out_specs=[ANY] * count,
        scratch_shapes=[
            pltpu.SemaphoreType.DMA((count,)),
            pltpu.SemaphoreType.DMA((2, n - 1, count)),
            pltpu.SemaphoreType.DMA((2, n - 1, count)),
        ],
        compiler_params=pltpu.CompilerParams(collective_id=collective_id, has_side_effects=True),
        cost_estimate=pl.CostEstimate(flops=0, bytes_accessed=100000000, transcendentals=0),
        name=name,
    )(*values)
    return [o.reshape((n * v.shape[0],) + v.shape[1:]) for o, v in zip(outs, values)]


class LineSum:
    def __init__(self, n, part, landing, staging, send, receive):
        self.n, self.part, self.landing, self.staging = n, part, landing, staging
        self.send, self.receive = send, receive
        self.group, self.me = lax.axis_index("group"), lax.axis_index("expert")
        self.rows = part.shape[1]
        self.tile = min(32, self.rows)

    def neighbours(self):
        left, right = (self.group, self.me - 1), (self.group, self.me + 1)
        return [(self.me > 0, left), (self.me < self.n - 1, right)]

    def copy(self, source, step, side):
        index = (side, step)
        device = (self.group, self.me + 1 if side == 0 else self.me - 1)
        return remote(
            source, self.landing.at[index], self.send.at[index], self.receive.at[index], device
        )

    def places(self):
        me, n = self.me, self.n
        for step in range(n - 1):
            for side in (0, 1):
                owner = n - 1 - step if side == 0 else step
                beyond = me < owner if side == 0 else me > owner
                edge = me == 0 if side == 0 else me == n - 1
                yield step, side, owner, beyond, edge

    def start(self):
        for step, side, owner, beyond, edge in self.places():

            @pl.when(beyond & edge)
            def _():
                self.copy(self.part.at[owner], step, side).start()

    def spans(self, body):
        def tile_body(t, carry):
            body(pl.ds(pl.multiple_of(t * self.tile, self.tile), self.tile))
            return carry

        lax.fori_loop(0, self.rows // self.tile, tile_body, 0)

    def forward(self, hop):
        me, n = self.me, self.n
        for side in (0, 1):
            step = hop - me if side == 0 else hop - (n - 1 - me)
            owner = n - 1 - step if side == 0 else step
            inner = me > 0 if side == 0 else me < n - 1
            beyond = me < owner if side == 0 else me > owner

            @pl.when(inner & (step >= 0) & beyond)
            def _():
                self.copy(self.part.at[owner], step, side).wait_recv()

                def add(span):
                    total = self.part[owner, span, :].astype(F32)
                    total = total + self.landing[side, step, span, :].astype(F32)
                    self.staging[side, step, span, :] = total.astype(BF)

                self.spans(add)
                self.copy(self.staging.at[side, step], step, side).start()

    def finish(self, out_ref):
        me, n = self.me, self.n

        @pl.when(me > 0)
        def _():
            self.copy(self.part.at[me], n - 1 - me, 0).wait_recv()

        @pl.when(me < n - 1)
        def _():
            self.copy(self.part.at[me], me, 1).wait_recv()

        def total(span):
            value = self.part[me, span, :].astype(F32)
            from_left = self.landing[0, jnp.minimum(n - 1 - me, n - 2), span, :].astype(F32)
            from_right = self.landing[1, jnp.minimum(me, n - 2), span, :].astype(F32)
            value = value + jnp.where(me > 0, from_left, 0.0)
            value = value + jnp.where(me < n - 1, from_right, 0.0)
            out_ref[span, :] = value.astype(out_ref.dtype)

        self.spans(total)
        for step, side, owner, beyond, edge in self.places():

            @pl.when(beyond)
            def _():
                self.copy(self.part.at[owner], step, side).wait_send()


def line_sum_scratch(n, rows, width):
    return [
        pltpu.VMEM((2, n - 1, rows, width), BF),
        pltpu.VMEM((2, n - 2, rows, width), BF),
        pltpu.SemaphoreType.DMA((2, n - 1)),
        pltpu.SemaphoreType.DMA((2, n - 1)),
    ]


def line_scatter_kernel(n, part_ref, out_ref, *scratch):
    line = LineSum(n, part_ref, *scratch)
    greet(line.neighbours())
    line.start()
    for hop in range(1, n - 1):
        line.forward(hop)
    line.finish(out_ref)


def line_scatter(value, n, dtype, collective_id, name):
    total, width = value.shape
    rows = total // n
    return pl.pallas_call(
        functools.partial(line_scatter_kernel, n),
        out_shape=jax.ShapeDtypeStruct((rows, width), dtype),
        in_specs=[IN_VMEM],
        out_specs=IN_VMEM,
        scratch_shapes=line_sum_scratch(n, rows, width),
        compiler_params=pltpu.CompilerParams(collective_id=collective_id, has_side_effects=True),
        cost_estimate=pl.CostEstimate(flops=0, bytes_accessed=100000000, transcendentals=0),
        name=name,
    )(value.reshape(n, rows, width))


def plane_position():
    group, me = lax.axis_index("group"), lax.axis_index("expert")
    c, x, y = group % 2, (group // 2) % 2, (group // 4) % 2
    by_c, by_x, by_y = (group + 1 - 2 * c, me), (group + 2 - 4 * x, me), (group + 4 - 8 * y, me)
    return group, me, (y, x, c), (by_y, by_x, by_c)


def weights_kernel(n, pieces, widths, *refs):
    wq, wk, wv, wo, small, extra = refs[:6]
    outs, extra_out, owns = refs[6:9], refs[9], refs[10:13]
    load, store, zsend, zrecv, psend, precv, csend, crecv, xsend, xrecv = refs[13:]
    group, me, (y, x, c), (by_y, by_x, by_c) = plane_position()
    left, right = (group, me - 1), (group, me + 1)
    eighth = owns[0].shape[0]
    span = pl.ds(pl.multiple_of((y * 4 + x * 2 + c) * eighth, eighth), eighth)
    query_width, key_width = wq.shape[1], wk.shape[1]
    targets = (
        owns[0].at[:, :query_width],
        owns[0].at[:, query_width : query_width + key_width],
        owns[0].at[:, query_width + key_width :],
        owns[1],
        owns[2],
    )
    loads = [
        pltpu.make_async_copy(source.at[span, :], target, load.at[i])
        for i, (source, target) in enumerate(zip((wq, wk, wv, wo, small), targets))
    ]
    for copy in loads:
        copy.start()
    for copy in loads:
        copy.wait()
    stores = [
        pltpu.make_async_copy(owns[i], outs[i].at[me, y, x, c], store.at[i]) for i in range(3)
    ]
    stores.append(pltpu.make_async_copy(extra, extra_out.at[me], store.at[3]))
    for copy in stores:
        copy.start()
    greet(
        [(me > 0, left), (me < n - 1, right), (None, by_c), (None, by_x), (None, by_y)]
    )

    def hop(i, step, side):
        block = me - step if side == 0 else me + step
        source = owns[i] if step == 0 else outs[i].at[block, y, x, c]
        index = (side, step, i)
        return remote(
            source,
            outs[i].at[block, y, x, c],
            zsend.at[index],
            zrecv.at[index],
            right if side == 0 else left,
        )

    def sends(step, side):
        return (me - step >= 0) & (me < n - 1) if side == 0 else (me + step < n) & (me > 0)

    def extra_hop(part, step, side):
        block = me - step if side == 0 else me + step
        middle = extra.shape[1] // 2
        columns = slice(part * middle, (part + 1) * middle)
        source = extra.at[:, columns] if step == 0 else extra_out.at[block, :, columns]
        return remote(
            source,
            extra_out.at[block, :, columns],
            xsend.at[part, side, step],
            xrecv.at[part, side, step],
            right if side == 0 else left,
        )

    def first(slot, block, p):
        i, start, width, along_x = pieces[p]
        spot = outs[i].at[block, y, x, c, :, start : start + width]
        source = owns[i].at[:, start : start + width] if slot == 0 else spot
        index = (0, slot, p)
        return remote(source, spot, psend.at[index], precv.at[index], by_x if along_x else by_y)

    def second(slot, block, p):
        i, start, width, along_x = pieces[p]
        columns = slice(start, start + width)
        if along_x:
            spot = outs[i].at[block, y, :, c, :, columns]
        else:
            spot = outs[i].at[block, :, x, c, :, columns]
        index = (1, slot, p)
        return remote(spot, spot, psend.at[index], precv.at[index], by_y if along_x else by_x)

    def third(slot, block, i):
        spot = outs[i].at[block, :, :, c]
        index = (slot, i)
        return remote(spot, spot, csend.at[index], crecv.at[index], by_c)

    def held(step):
        if step == 0:
            return [(0, me, me >= 0)]
        return [(step, me - step, me - step >= 0), (n - 1 + step, me + step, me + step < n)]

    def extra_step(part, far):
        for side in (0, 1):
            if far > 0:

                @pl.when(me - far >= 0 if side == 0 else me + far < n)
                def _():
                    extra_hop(part, far - 1, side).wait_recv()

        for side in (0, 1):
            if far < n - 1:

                @pl.when(sends(far, side))
                def _():
                    extra_hop(part, far, side).start()

    count = len(pieces)
    for step in range(n + 2):
        if step < n:
            for slot, block, there in held(step):

                @pl.when(there)
                def _():
                    if step > 0:
                        side = 0 if slot < n else 1
                        for i in range(3):
                            hop(i, step - 1, side).wait_recv()
                    for p in range(count):
                        first(slot, block, p).start()

            if step < n - 1:
                for side in (0, 1):

                    @pl.when(sends(step, side))
                    def _():
                        for i in range(3):
                            hop(i, step, side).start()

        if 1 <= step < n + 1:
            if step == 1:
                for copy in stores:
                    copy.wait()
            for slot, block, there in held(step - 1):

                @pl.when(there)
                def _():
                    for p in range(count):
                        first(slot, block, p).wait_recv()
                    for p in range(count):
                        second(slot, block, p).start()

        if step >= 2:
            for slot, block, there in held(step - 2):

                @pl.when(there)
                def _():
                    for p in range(count):
                        second(slot, block, p).wait_recv()
                    for i in range(3):
                        third(slot, block, i).start()

        for part in (0, 1):
            if 0 <= step - 1 - part < n:
                extra_step(part, step - 1 - part)

    for step in range(n):
        for slot, block, there in held(step):

            @pl.when(there)
            def _():
                for p in range(count):
                    first(slot, block, p).wait_send()
                    second(slot, block, p).wait_send()
                for i in range(3):
                    third(slot, block, i).wait()

        if step < n - 1:
            for side in (0, 1):

                @pl.when(sends(step, side))
                def _():
                    for i in range(3):
                        hop(i, step, side).wait_send()
                    for part in (0, 1):
                        extra_hop(part, step, side).wait_send()


def path_pieces(query_width, key_width, out_width, small_width):
    half = query_width + key_width
    return (
        (0, 0, half, True),
        (0, half, query_width + 2 * key_width - half, False),
        (1, 0, out_width, False),
        (2, 0, small_width, True),
    )


def gather_weights(wq, wk, wv, wo, small, extra, n, collective_id):
    rows = wq.shape[0]
    eighth = rows // 8
    widths = (wq.shape[1] + wk.shape[1] + wv.shape[1], wo.shape[1], small.shape[1])
    pieces = path_pieces(wq.shape[1], wk.shape[1], wo.shape[1], small.shape[1])
    outs = pl.pallas_call(
        functools.partial(weights_kernel, n, pieces, widths),
        out_shape=[jax.ShapeDtypeStruct((n, 2, 2, 2, eighth, w), BF) for w in widths]
        + [jax.ShapeDtypeStruct((n,) + extra.shape, BF)],
        in_specs=[ANY] * 5 + [IN_VMEM],
        out_specs=[ANY] * 4,
        scratch_shapes=[pltpu.VMEM((eighth, w), BF) for w in widths]
        + [
            pltpu.SemaphoreType.DMA((5,)),
            pltpu.SemaphoreType.DMA((4,)),
            pltpu.SemaphoreType.DMA((2, n - 1, 3)),
            pltpu.SemaphoreType.DMA((2, n - 1, 3)),
            pltpu.SemaphoreType.DMA((2, 2 * n - 1, 4)),
            pltpu.SemaphoreType.DMA((2, 2 * n - 1, 4)),
            pltpu.SemaphoreType.DMA((2 * n - 1, 3)),
            pltpu.SemaphoreType.DMA((2 * n - 1, 3)),
            pltpu.SemaphoreType.DMA((2, 2, n - 1)),
            pltpu.SemaphoreType.DMA((2, 2, n - 1)),
        ],
        compiler_params=pltpu.CompilerParams(collective_id=collective_id, has_side_effects=True),
        cost_estimate=pl.CostEstimate(flops=0, bytes_accessed=100000000, transcendentals=0),
        name="gather_weights",
    )(wq, wk, wv, wo, small, extra)
    weights = [o.reshape(n * rows, w) for o, w in zip(outs, widths)]
    return weights + [outs[3].reshape(-1, extra.shape[1])]


def reduce_kernel(n, pieces, *refs):
    (
        grad_q_ref,
        grad_kv_ref,
        tokens_ref,
        gain_ref,
        weight_ref,
        cosine_ref,
        sine_ref,
        mixed_ref,
        grad_attn_ref,
        router_ref,
        gain_two_ref,
        y_part,
    ) = refs[:12]
    outs, y_out, grad_tokens_ref = refs[12:14], refs[14], refs[15]
    ins, grad_pre_ref = refs[16:19], refs[19]
    refs = refs[20:]
    pair, one, two, landing, staging = refs[:2], refs[2:4], refs[4:6], refs[6:8], refs[8:10]
    csend, crecv, psend, precv, zsend, zrecv, gsend, grecv = refs[10:18]
    line = LineSum(n, y_part, *refs[18:])
    group, me, (y, x, c), (by_y, by_x, by_c) = plane_position()
    left, right = (group, me - 1), (group, me + 1)
    eighth = pair[0].shape[3]
    greet(
        [(me > 0, left), (me < n - 1, right), (None, by_c), (None, by_x), (None, by_y)]
    )

    places, ends = [], [0, 0]
    for array, start, width, along_x in pieces:
        path = 0 if along_x else 1
        places.append((array, start, width, path, ends[path]))
        ends[path] += width

    def swap(p):
        array, start, width, path, at = places[p]
        return remote(
            ins[array].at[:, :, :, 1 - c, :, start : start + width],
            pair[path].at[:, :, :, :, at : at + width],
            csend.at[p],
            crecv.at[p],
            by_c,
        )

    line.start()
    D_rows = weight_ref.shape[0]
    query_width = grad_q_ref.shape[1]
    key_width = (weight_ref.shape[1] - query_width) // 2

    def put(array, columns, value):
        ins[array][:, :, :, :, :, columns] = value.astype(BF).reshape(
            ins[array].shape[:5] + (value.shape[1],)
        )

    tile = 4 * LANES
    for start in range(0, grad_attn_ref.shape[1], tile):
        columns = slice(start, start + tile)
        put(1, columns, dot_tn(mixed_ref[...], grad_attn_ref[:, columns]))
    swap(2).start()
    unit, inverse = normed(tokens_ref)
    gain = gain_ref[0:1, :]
    first_norm = (unit * gain).astype(BF)
    cosine, sine = cosine_ref[...], -sine_ref[...]
    for j in range(query_width // LANES):
        columns = slice(j * LANES, (j + 1) * LANES)
        grad_pre_ref[:, columns] = rotate(grad_q_ref[:, columns], cosine, sine).astype(BF)
    for j in range(key_width // LANES):
        start = 2 * j * LANES
        key = grad_kv_ref[:, start : start + LANES].astype(F32)
        at = query_width + j * LANES
        grad_pre_ref[:, at : at + LANES] = rotate(key, cosine, sine).astype(BF)
        at = at + key_width
        grad_pre_ref[:, at : at + LANES] = grad_kv_ref[:, start + LANES : start + 2 * LANES]
    for start in range(0, weight_ref.shape[1], tile):
        columns = slice(start, start + tile)
        put(0, columns, dot_tn(first_norm, grad_pre_ref[:, columns]))
    swap(0).start()
    swap(1).start()
    grad_first = dot_nt(grad_pre_ref[...], weight_ref[...])
    gain_one_row = jnp.sum(grad_first * unit, axis=0, keepdims=True)
    lane = lax.broadcasted_iota(jnp.int32, (LANES, D_rows), 0)
    gains = jnp.where(lane == EXPERTS, gain_one_row, 0.0)
    gains = jnp.where(lane == EXPERTS + 1, gain_two_ref[...], gains)
    put(2, slice(0, LANES), router_ref[...] + gains.T)
    swap(3).start()
    scaled = grad_first * gain
    mean = jnp.mean(scaled * unit, axis=-1, keepdims=True)
    grad_tokens_ref[...] = inverse * (scaled - unit * mean)
    for p in range(len(places)):
        swap(p).wait_recv()
        array, start, width, path, at = places[p]

        def pair_sum(t, carry):
            z, a, b = t // 4, (t // 2) % 2, t % 2
            mine = ins[array][z, a, b, c, :, start : start + width].astype(F32)
            theirs = pair[path][z, a, b, :, at : at + width].astype(F32)
            pair[path][z, a, b, :, at : at + width] = (mine + theirs).astype(BF)
            return carry

        lax.fori_loop(0, 4 * n, pair_sum, 0)

    def first(path):
        source = pair[0].at[:, :, 1 - x] if path == 0 else pair[1].at[:, 1 - y]
        return remote(
            source, one[path], psend.at[0, path], precv.at[0, path], by_x if path == 0 else by_y
        )

    def second(path):
        source = one[path].at[:, 1 - y] if path == 0 else one[path].at[:, 1 - x]
        return remote(
            source, two[path], psend.at[1, path], precv.at[1, path], by_y if path == 0 else by_x
        )

    for path in (0, 1):
        first(path).start()
    line.forward(1)
    for path in (0, 1):
        first(path).wait_recv()

        def first_sum(t, carry):
            z, a = t // 2, t % 2
            mine = pair[0][z, a, x] if path == 0 else pair[1][z, y, a]
            one[path][z, a] = (mine.astype(F32) + one[path][z, a].astype(F32)).astype(BF)
            return carry

        lax.fori_loop(0, 2 * n, first_sum, 0)
        second(path).start()
    for far in range(2, n - 1):
        line.forward(far)
    for path in (0, 1):
        second(path).wait_recv()

        def second_sum(z, carry):
            mine = one[0][z, y] if path == 0 else one[1][z, x]
            two[path][z] = (mine.astype(F32) + two[path][z].astype(F32)).astype(BF)
            return carry

        lax.fori_loop(0, n, second_sum, 0)

    def hop(source, path, step, side):
        index = (path, side, step)
        return remote(
            source,
            landing[path].at[side, step],
            zsend.at[index],
            zrecv.at[index],
            right if side == 0 else left,
        )

    for step in range(n - 1):
        for side in (0, 1):
            owner = n - 1 - step if side == 0 else step
            beyond = me < owner if side == 0 else me > owner
            edge = me == 0 if side == 0 else me == n - 1

            @pl.when(beyond & edge)
            def _():
                for path in (0, 1):
                    hop(two[path].at[owner], path, step, side).start()

    for far in range(1, n - 1):
        for side in (0, 1):
            step = far - me if side == 0 else far - (n - 1 - me)
            owner = n - 1 - step if side == 0 else step
            inner = me > 0 if side == 0 else me < n - 1
            beyond = me < owner if side == 0 else me > owner

            @pl.when(inner & (step >= 0) & beyond)
            def _():
                for path in (0, 1):
                    hop(two[path].at[owner], path, step, side).wait_recv()
                    staging[path][side, step] = (
                        two[path][owner].astype(F32) + landing[path][side, step].astype(F32)
                    ).astype(BF)
                    hop(staging[path].at[side, step], path, step, side).start()

    @pl.when(me > 0)
    def _():
        for path in (0, 1):
            hop(two[path].at[me], path, n - 1 - me, 0).wait_recv()

    @pl.when(me < n - 1)
    def _():
        for path in (0, 1):
            hop(two[path].at[me], path, me, 1).wait_recv()

    for path in (0, 1):
        total = two[path][me].astype(F32)
        from_left = landing[path][0, jnp.minimum(n - 1 - me, n - 2)].astype(F32)
        from_right = landing[path][1, jnp.minimum(me, n - 2)].astype(F32)
        total = total + jnp.where(me > 0, from_left, 0.0)
        total = total + jnp.where(me < n - 1, from_right, 0.0)
        outs[path][y, x, c] = total.astype(BF)

    def spread(path, stage):
        out = outs[path]
        if stage == 2:
            spot, device = out.at[:, :, c], by_c
        elif stage == 0:
            spot, device = out.at[y, x, c], by_x if path == 0 else by_y
        elif path == 0:
            spot, device = out.at[y, :, c], by_y
        else:
            spot, device = out.at[:, x, c], by_x
        return remote(spot, spot, gsend.at[path, stage], grecv.at[path, stage], device)

    for stage in range(3):
        for path in (0, 1):
            spread(path, stage).start()
        if stage == 0:
            line.finish(y_out)
        for path in (0, 1):
            spread(path, stage).wait_recv()

    for path in (0, 1):
        for stage in range(3):
            spread(path, stage).wait_send()
        first(path).wait_send()
        second(path).wait_send()
    for p in range(len(places)):
        swap(p).wait_send()
    for step in range(n - 1):
        for side in (0, 1):
            owner = n - 1 - step if side == 0 else step
            beyond = me < owner if side == 0 else me > owner

            @pl.when(beyond)
            def _():
                for path in (0, 1):
                    hop(two[path].at[owner], path, step, side).wait_send()


def reduce_weights(
    grad_q,
    grad_kv,
    tokens,
    gain,
    weight,
    cosine,
    sine,
    mixed_low,
    grad_attn,
    grad_router,
    gain_two_row,
    y_part,
    n,
    collective_id,
):
    rows_all, width_all = weight.shape
    query_width = grad_q.shape[1]
    key_width = (width_all - query_width) // 2
    array_widths = (width_all, grad_attn.shape[1], LANES)
    rows = rows_all // n
    eighth = rows // 8
    pieces = path_pieces(query_width, key_width, grad_attn.shape[1], LANES)
    widths = [sum(p[2] for p in pieces if p[3]), sum(p[2] for p in pieces if not p[3])]
    scratch = [pltpu.VMEM((n, 2, 2, 2, eighth, w), BF) for w in array_widths]
    scratch += [pltpu.VMEM((grad_q.shape[0], width_all), BF)]
    scratch += [pltpu.VMEM((n, 2, 2, eighth, w), BF) for w in widths]
    scratch += [pltpu.VMEM((n, 2, eighth, w), BF) for w in widths]
    scratch += [pltpu.VMEM((n, eighth, w), BF) for w in widths]
    scratch += [pltpu.VMEM((2, n - 1, eighth, w), BF) for w in widths] * 2
    sems = [(4,), (4,), (2, 2), (2, 2), (2, 2, n - 1), (2, 2, n - 1), (2, 3), (2, 3)]
    y_rows = y_part.shape[0] // n
    first, second, y_sum, grad_rest = pl.pallas_call(
        functools.partial(reduce_kernel, n, pieces),
        out_shape=[jax.ShapeDtypeStruct((2, 2, 2, eighth, w), BF) for w in widths]
        + [jax.ShapeDtypeStruct(tokens.shape, F32)] * 2,
        in_specs=[IN_VMEM] * 12,
        out_specs=[IN_VMEM] * 4,
        scratch_shapes=scratch
        + [pltpu.SemaphoreType.DMA(s) for s in sems]
        + line_sum_scratch(n, y_rows, y_part.shape[1]),
        compiler_params=pltpu.CompilerParams(
            collective_id=collective_id, has_side_effects=True, vmem_limit_bytes=60 * 1024 * 1024
        ),
        cost_estimate=pl.CostEstimate(flops=0, bytes_accessed=100000000, transcendentals=0),
        name="reduce_weights",
    )(
        grad_q,
        grad_kv,
        tokens,
        gain,
        weight,
        cosine,
        sine,
        mixed_low,
        grad_attn,
        grad_router,
        gain_two_row,
        y_part.reshape(n, y_rows, y_part.shape[1]),
    )
    first, second = [o.reshape(rows, w) for o, w in zip((first, second), widths)]
    first = jnp.split(first, (query_width, query_width + key_width), axis=1)
    second = jnp.split(second, (key_width,), axis=1)
    return first[0], first[1], second[0], second[1], first[2], y_sum, grad_rest


def plane_tick(step, local):
    tick = jnp.where(step <= 2, step, jnp.where(step < local, (step + 2) // 2, step - 3))
    runs = (step <= 2) | (step >= local) | (step % 2 == 0)
    return tick, runs


def expert_kernel(sizes, plane, *refs):
    blocks, rows, local, capacity = sizes
    if plane:
        mixed_in, tokens_in, out_weight_in, gain_ref = refs[:4]
        refs = refs[4:]
    else:
        x_ref = refs[0]
        refs = refs[1:]
    ct_ref, router_ref, rank_all_ref = refs[:3]
    w_gate_ref, w_up_ref, w_down_ref = refs[3:6]
    y_ref, gs_ref, out_gate_ref, out_up_ref, out_down_ref = refs[6:11]
    refs = refs[11:]
    if plane:
        second_ref, residual_ref = refs[:2]
        refs = refs[2:]
    xs_ref, g_ref, rank_ref, gate_ref, dots_ref, y_sem = refs[:6]
    refs = refs[6:]
    slots = local * capacity
    step = pl.program_id(0)
    tick, ticks = plane_tick(step, local)
    me = lax.axis_index("expert")
    base = me * local
    if plane:
        stage_refs, pair_refs, one_refs, two_refs = refs[:3], refs[3:6], refs[6:10], refs[10:14]
        csend, crecv, psend, precv, qsend, qrecv = refs[14:20]
        gs_part = refs[20]
        line = LineSum(blocks, gs_part, *refs[21:25])
        x_ref, xsend, xrecv, in_sem, out_sem = refs[25:]
        group, _, (y, x, c), (by_y, by_x, by_c) = plane_position()
        half = stage_refs[2].shape[4] // 2

    def expert_id():
        return lax.broadcasted_iota(jnp.int32, (EXPERTS, rows), 0)

    def note_ranks(b):
        ranks = rank_all_ref[b].astype(F32)
        for e in range(local):
            mine = jnp.where(expert_id() == base + e, ranks, 0.0)
            rank_ref[b, e : e + 1, :] = jnp.sum(mine, axis=0, keepdims=True)

    def pick(b):
        slot_id = lax.broadcasted_iota(jnp.int32, (capacity, rows), 0).astype(F32)
        pieces = [
            jnp.where(rank_ref[b, e : e + 1, :] == slot_id, 1.0, 0.0).astype(BF)
            for e in range(local)
        ]
        return jnp.concatenate(pieces, axis=0)

    def dispatch_grads(b):
        g_ref[b] = dot(pick(b), ct_ref[b, :rows, :]).astype(BF)

    def dispatch_rows(b):
        logits = lax.dot_general(
            router_ref[...], x_ref[b], (((0,), (1,)), ((), ())), preferred_element_type=F32
        )[:EXPERTS]
        hot = rank_all_ref[b].astype(F32) < 200.0
        top = jnp.max(jnp.where(hot, logits, NEGATIVE_LARGE), axis=0, keepdims=True)
        weight = jnp.where(hot, jnp.exp(jnp.minimum(logits - top, 0.0)), 0.0)
        gates = weight / jnp.sum(weight, axis=0, keepdims=True)
        for e in range(local):
            mine = jnp.where(expert_id() == base + e, gates, 0.0)
            gate_ref[b, e : e + 1, :] = jnp.sum(mine, axis=0, keepdims=True)
        xs_ref[b] = dot(pick(b), x_ref[b]).astype(BF)

    if plane:
        n = blocks
        leave_second = pltpu.make_async_copy(x_ref.at[me], second_ref, out_sem.at[0])
        leave_residual = pltpu.make_async_copy(gs_ref.at[:, :D], residual_ref, out_sem.at[1])

        def hop(far, side):
            block = me - far if side == 0 else me + far
            device = (group, me + 1 if side == 0 else me - 1)
            index = (side, far)
            return remote(
                x_ref.at[block], x_ref.at[block], xsend.at[index], xrecv.at[index], device
            )

        def sends(far, side):
            if side == 0:
                return (far < n - 1) & (me - far >= 0) & (me < n - 1)
            return (far < n - 1) & (me + far < n) & (me > 0)

        def arrives(far, side):
            return me - 1 - far >= 0 if side == 0 else me + 1 + far < n

        @pl.when(step == 0)
        def _():
            loads = [
                pltpu.make_async_copy(out_weight_in, stage_refs[2].at[2:4], in_sem.at[0]),
                pltpu.make_async_copy(tokens_in, xs_ref.at[0, :rows, :], in_sem.at[1]),
                pltpu.make_async_copy(mixed_in, xs_ref.at[1, :rows, :], in_sem.at[2]),
            ]
            for copy in loads:
                copy.start()
            for b in range(blocks):
                note_ranks(b)
            for copy in loads:
                copy.wait()
            out_weight = stage_refs[2][2:4].reshape(D, D)
            residual = xs_ref[0, :rows, :].astype(F32) + dot(xs_ref[1, :rows, :], out_weight)
            inverse = lax.rsqrt(jnp.mean(residual * residual, axis=-1, keepdims=True) + EPSILON)
            x_ref[me] = (residual * inverse * gain_ref[1:2, :]).astype(BF)
            gs_ref[:, :D] = residual
            greet([(None, by_c), (None, by_x), (None, by_y)] + line.neighbours())
            for side in (0, 1):

                @pl.when(sends(0, side))
                def _():
                    hop(0, side).start()

            leave_second.start()
            leave_residual.start()
            for b in range(blocks):
                dispatch_grads(b)
            dispatch_rows(me)

            def arrived(far, carry):
                for side in (0, 1):

                    @pl.when(arrives(far, side))
                    def _():
                        hop(far, side).wait_recv()

                    @pl.when(sends(far + 1, side))
                    def _():
                        hop(far + 1, side).start()

                for side in (0, 1):

                    @pl.when(arrives(far, side))
                    def _():
                        dispatch_rows(me - 1 - far if side == 0 else me + 1 + far)

                return carry

            lax.fori_loop(0, n - 1, arrived, 0)

        @pl.when(step == 1)
        def _():
            leave_second.wait()
            leave_residual.wait()
            for far in range(n - 1):
                for side in (0, 1):

                    @pl.when(sends(far, side))
                    def _():
                        hop(far, side).wait_send()

    else:

        @pl.when(step == 0)
        def _():
            for b in range(blocks):
                note_ranks(b)
                dispatch_grads(b)
                dispatch_rows(b)

    @pl.when(step < local)
    def _():
        here = pl.ds(pl.multiple_of(step * capacity, capacity), capacity)
        xs = jnp.concatenate([xs_ref[b, here, :] for b in range(blocks)], axis=0)
        g = jnp.concatenate([g_ref[b, here, :] for b in range(blocks)], axis=0).astype(F32)
        slot_id = lax.broadcasted_iota(jnp.int32, (capacity, rows), 0).astype(F32)
        gates = []
        for b in range(blocks):
            taken = rank_ref[b, pl.ds(step, 1), :] == slot_id
            gate = jnp.where(taken, gate_ref[b, pl.ds(step, 1), :], 0.0)
            gates.append(jnp.sum(gate, axis=1, keepdims=True))
        gate_slot = jnp.concatenate(gates, axis=0)
        w_gate, w_up, w_down = w_gate_ref[0], w_up_ref[0], w_down_ref[0]
        gate_pre = dot(xs, w_gate)
        up_pre = dot(xs, w_up)
        sigmoid = jax.nn.sigmoid(gate_pre)
        silu = gate_pre * sigmoid
        activation = (silu * up_pre).astype(BF)
        expert_out = dot(activation, w_down).astype(BF).astype(F32)
        slot_dot = jnp.sum(g * expert_out, axis=1, keepdims=True)
        grad_out = (gate_slot * g).astype(BF)
        scaled_out = (gate_slot * expert_out).astype(BF)
        grad_down = dot_tn(activation, grad_out).astype(BF)
        grad_activation = dot_nt(grad_out, w_down)
        grad_gate_pre = (
            grad_activation * up_pre * sigmoid * (1.0 + gate_pre * (1.0 - sigmoid))
        ).astype(BF)
        grad_up_pre = (grad_activation * silu).astype(BF)
        grad_gate = dot_tn(xs, grad_gate_pre).astype(BF)
        grad_up = dot_tn(xs, grad_up_pre).astype(BF)
        if plane:
            for ref, value in zip(stage_refs, (grad_gate, grad_up, grad_down)):
                ref[step % STAGES] = value.reshape(ref.shape[1:])
        else:
            out_gate_ref[0], out_up_ref[0], out_down_ref[0] = grad_gate, grad_up, grad_down
        grad_in = (dot_nt(grad_gate_pre, w_gate) + dot_nt(grad_up_pre, w_up)).astype(BF)
        lane = lax.broadcasted_iota(jnp.int32, (blocks * capacity, LANES), 1)
        high = slot_dot.astype(BF).astype(F32)
        middle = (slot_dot - high).astype(BF).astype(F32)
        low = slot_dot - high - middle
        mine = base + step
        dots = jnp.where(lane == mine, high, 0.0)
        dots = jnp.where(lane == mine + EXPERTS, middle, dots)
        dots = jnp.where(lane == mine + 2 * EXPERTS, low, dots).astype(BF)
        for b in range(blocks):
            part = slice(b * capacity, (b + 1) * capacity)
            xs_ref[b, here, :] = grad_in[part]
            g_ref[b, here, :] = scaled_out[part]
            dots_ref[b, here, :] = dots[part]

    def store_y(b):
        there = pl.ds(b * rows, rows)
        return pltpu.make_async_copy(g_ref.at[b, :rows, :], y_ref.at[there, :], y_sem.at[b])

    @pl.when(step == local - 1)
    def _():
        slot_expert = lax.broadcasted_iota(jnp.int32, (EXPERTS, slots), 1) // capacity
        spread_row = lax.broadcasted_iota(jnp.int32, (EXPERTS, slots), 0)
        spread = jnp.where(spread_row == slot_expert + base, 1.0, 0.0).astype(BF)
        slot_rank = (lax.broadcasted_iota(jnp.int32, (rows, slots), 1) % capacity).astype(F32)
        for b in range(blocks):
            there = slice(b * rows, (b + 1) * rows)
            ranks = dot_tn(rank_all_ref[b], spread)
            put = jnp.where(ranks == slot_rank, 1.0, 0.0).astype(BF)
            g_ref[b, :rows, :] = dot(put, g_ref[b]).astype(BF)
            store_y(b).start()
            back = dot(put, xs_ref[b]).astype(BF), dot(put, dots_ref[b]).astype(BF)
            if plane:
                gs_part[b, :, :D], gs_part[b, :, D:] = back
            else:
                gs_ref[there, :D], gs_ref[there, D:] = back
        if plane:
            line.start()

    @pl.when(step == pl.num_programs(0) - 1)
    def _():
        for b in range(blocks):
            store_y(b).wait()

    if not plane:
        return

    gate, up, low_down, high_down = range(4)
    low_rows, high_rows = slice(0, half), slice(half, 2 * half)

    def swap(e, i):
        return remote(
            stage_refs[i].at[e % STAGES, :, :, 1 - c],
            pair_refs[i].at[e % 3],
            csend.at[e % 2, i],
            crecv.at[e % 3, i],
            by_c,
        )

    def first(e, k):
        slot = e % 3
        source = {
            gate: lambda: pair_refs[0].at[slot, :, 1 - x],
            up: lambda: pair_refs[1].at[slot, 1 - y],
            low_down: lambda: pair_refs[2].at[slot, :, 1 - x, low_rows],
            high_down: lambda: pair_refs[2].at[slot, 1 - y, :, high_rows],
        }[k]()
        device = by_x if k in (gate, low_down) else by_y
        return remote(source, one_refs[k].at[slot], psend.at[slot, k], precv.at[slot, k], device)

    def second(e, k):
        along_x = k in (gate, low_down)
        source = one_refs[k].at[e % 3, 1 - y] if along_x else one_refs[k].at[e % 3, 1 - x]
        slot = e % 2
        return remote(
            source,
            two_refs[k].at[slot],
            qsend.at[slot, k],
            qrecv.at[slot, k],
            by_y if along_x else by_x,
        )

    def add(first_value, second_value):
        return (first_value.astype(F32) + second_value.astype(F32)).astype(BF)

    @pl.when(ticks & (tick >= 3))
    def _():
        e = tick - 3
        for k in range(4):
            second(e, k).wait()
        own = [one_refs[k][e % 3, y if k in (gate, low_down) else x] for k in range(4)]
        out_gate_ref[0] = add(own[gate], two_refs[gate][e % 2])
        out_up_ref[0] = add(own[up], two_refs[up][e % 2])
        out_down_ref[0, low_rows] = add(own[low_down], two_refs[low_down][e % 2])
        out_down_ref[0, high_rows] = add(own[high_down], two_refs[high_down][e % 2])

    @pl.when(ticks & (tick >= 2) & (tick < local + 2))
    def _():
        e = tick - 2
        slot = e % 3
        for k in range(4):
            first(e, k).wait()
            for t in (0, 1):
                mine = {
                    gate: lambda: pair_refs[0][slot, t, x],
                    up: lambda: pair_refs[1][slot, y, t],
                    low_down: lambda: pair_refs[2][slot, t, x, low_rows],
                    high_down: lambda: pair_refs[2][slot, y, t, high_rows],
                }[k]()
                one_refs[k][slot, t] = add(mine, one_refs[k][slot, t])
            second(e, k).start()

    @pl.when(ticks & (tick >= 1) & (tick < local + 1))
    def _():
        e = tick - 1
        slot = e % 3
        for i in range(3):
            swap(e, i).wait()

            def pair_sum(t, carry):
                a, b = t // 2, t % 2
                pair_refs[i][slot, a, b] = add(
                    stage_refs[i][e % STAGES, a, b, c], pair_refs[i][slot, a, b]
                )
                return carry

            lax.fori_loop(0, 4, pair_sum, 0)
        for k in range(4):
            first(e, k).start()

    @pl.when(ticks & (tick < local))
    def _():
        for i in range(3):
            swap(tick, i).start()

    for hop in range(1, blocks - 1):

        @pl.when(step == local + hop)
        def _():
            line.forward(hop)

    @pl.when(step == local + blocks - 1)
    def _():
        line.finish(gs_ref)


def run_experts(
    sources, ct_all, router, rank_all, w_gate, w_up, w_down, capacity, plane, collective_id
):
    blocks, _, rows = rank_all.shape
    total, local = blocks * rows, w_gate.shape[0]
    slots = local * capacity
    sizes = (blocks, rows, local, capacity)
    whole = lambda shape: pl.BlockSpec(
        shape, lambda e: (0,) * len(shape), pipeline_mode=pl.Buffered(1)
    )
    per = lambda shape: pl.BlockSpec((1,) + shape, lambda e: (jnp.minimum(e, local - 1), 0, 0))
    shapes = ((D, FF), (D, FF), (FF, D))
    scratch = [
        pltpu.VMEM((blocks, slots, D), BF),
        pltpu.VMEM((blocks, slots, D), BF),
        pltpu.VMEM((blocks, local, rows), F32),
        pltpu.VMEM((blocks, local, rows), F32),
        pltpu.VMEM((blocks, slots, LANES), BF),
        pltpu.SemaphoreType.DMA((blocks,)),
    ]
    params = dict(dimension_semantics=("arbitrary",), vmem_limit_bytes=63 * 1024 * 1024)
    if plane:
        eighths = [(a // 8, b) for a, b in shapes]
        out = lambda shape: pl.BlockSpec(
            (1,) + shape, lambda e: (jnp.maximum(plane_tick(e, local)[0] - 3, 0), 0, 0)
        )
        grad_shapes, grad_specs = eighths, [out(shape) for shape in eighths]
        low = (eighths[2][0] // 2, eighths[2][1])
        passed = (eighths[0], eighths[1], low, low)
        scratch += [pltpu.VMEM((STAGES, 2, 2, 2) + shape, BF) for shape in eighths]
        scratch += [pltpu.VMEM((3, 2, 2) + shape, BF) for shape in eighths]
        scratch += [pltpu.VMEM((3, 2) + shape, BF) for shape in passed]
        scratch += [pltpu.VMEM((2,) + shape, BF) for shape in passed]
        sems = [(2, 3), (3, 3), (3, 4), (3, 4), (2, 4), (2, 4)]
        scratch += [pltpu.SemaphoreType.DMA(shape) for shape in sems]
        scratch += [pltpu.VMEM((blocks, rows, D + LANES), BF)]
        scratch += line_sum_scratch(blocks, rows, D + LANES)
        scratch += [pltpu.VMEM((blocks, rows, D), BF)]
        sems = [(2, blocks - 1), (2, blocks - 1), (3,), (2,)]
        scratch += [pltpu.SemaphoreType.DMA(shape) for shape in sems]
        mixed_low, tokens, out_weight, gain = sources
        sources = [mixed_low, tokens, out_weight.reshape((2, 2, 2, 2) + eighths[2]), gain]
        source_specs = [ANY] * 3 + [whole(gain.shape)]
        more_shapes = [
            jax.ShapeDtypeStruct((rows, D), BF),
            jax.ShapeDtypeStruct((rows, D), F32),
        ]
        gs_shape, gs_type = (rows, D + LANES), F32
        params |= dict(collective_id=collective_id, has_side_effects=True)
    else:
        grad_shapes, grad_specs = shapes, [per(shape) for shape in shapes]
        gs_shape, gs_type = (total, D + LANES), BF
        sources = [sources[0].reshape(blocks, rows, D)]
        source_specs = [whole(sources[0].shape)]
        more_shapes = []
    flops = 2 * total * D * slots * 4 // blocks + 18 * blocks * slots * D * FF
    return pl.pallas_call(
        functools.partial(expert_kernel, sizes, plane),
        grid=(local + 6 if plane else local,),
        out_shape=[
            jax.ShapeDtypeStruct((total, D), BF),
            jax.ShapeDtypeStruct(gs_shape, gs_type),
        ]
        + [jax.ShapeDtypeStruct((local,) + shape, BF) for shape in grad_shapes]
        + more_shapes,
        in_specs=source_specs
        + [
            whole(ct_all.shape),
            whole(router.shape),
            whole(rank_all.shape),
        ]
        + [per(shape) for shape in shapes],
        out_specs=[ANY, whole(gs_shape)] + grad_specs + [ANY] * len(more_shapes),
        scratch_shapes=scratch,
        compiler_params=pltpu.CompilerParams(**params),
        cost_estimate=pl.CostEstimate(
            flops=flops, bytes_accessed=2 * (6 * local * D * FF + 4 * total * D), transcendentals=0
        ),
        name="experts",
    )(*sources, ct_all, router, rank_all, w_gate, w_up, w_down)


def rotate(tile, cosine, sine):
    half = HEAD_DIMENSION // 2
    lane = lax.broadcasted_iota(jnp.int32, tile.shape, 1) % HEAD_DIMENSION
    other = jnp.where(lane < half, pltpu.roll(tile, LANES - half, 1), pltpu.roll(tile, half, 1))
    return tile * cosine + other * sine


def normed(tokens_ref):
    value = tokens_ref[...].astype(F32)
    inverse = lax.rsqrt(jnp.mean(value * value, axis=-1, keepdims=True) + EPSILON)
    return value * inverse, inverse


def mask_bias(bias_ref, length_ref, rows):
    base = lax.axis_index("expert") * rows
    key = lax.broadcasted_iota(jnp.int32, bias_ref.shape, 0)
    query = lax.broadcasted_iota(jnp.int32, bias_ref.shape, 1) + base
    allowed = (key <= query) & (key < length_ref[0])
    bias_ref[...] = jnp.where(allowed, 0.0, NEGATIVE_LARGE)


def head_columns(ref, head):
    start = 2 * HEAD_DIMENSION * head
    middle = start + HEAD_DIMENSION
    return jnp.concatenate([ref[:, start:middle], ref[:, middle : middle + HEAD_DIMENSION]], 0)


def put_heads(ref, head, transposed):
    rows = ref.shape[0]
    value = transposed.T
    start = 2 * HEAD_DIMENSION * head
    middle = start + HEAD_DIMENSION
    ref[:, start:middle] = value[:rows].astype(ref.dtype)
    ref[:, middle : middle + HEAD_DIMENSION] = value[rows:].astype(ref.dtype)


def attention_kernel(
    n,
    length_ref,
    tokens_ref,
    gain_ref,
    weight_ref,
    cosine_ref,
    sine_ref,
    routes_ref,
    mixed_ref,
    log_total_ref,
    kv_all_ref,
    query_out_ref,
    rank_all_ref,
    *scratch,
):
    bias_ref, query_ref, kv_ref, chunk_ref, rank_buffer, send, recv, rank_send, rank_recv = scratch
    pair, pairs = pl.program_id(0), pl.num_programs(0)
    group, me = lax.axis_index("group"), lax.axis_index("expert")
    left, right = (group, me - 1), (group, me + 1)
    rows, width = kv_ref.shape[1:]

    def hop(j, step, side):
        block = me - step if side == 0 else me + step
        source = kv_ref.at[j] if step == 0 else chunk_ref.at[j, block]
        index = (j, side, step)
        return remote(
            source,
            chunk_ref.at[j, block],
            send.at[index],
            recv.at[index],
            right if side == 0 else left,
        )

    def rank_hop(step, side):
        block = me - step if side == 0 else me + step
        source = rank_buffer.at[block]
        index = (side, step)
        return remote(
            source,
            rank_buffer.at[block],
            rank_send.at[index],
            rank_recv.at[index],
            right if side == 0 else left,
        )

    def sends(step, side):
        return (me - step >= 0) & (me < n - 1) if side == 0 else (me + step < n) & (me > 0)

    def arrives(step, side):
        return me - 1 - step >= 0 if side == 0 else me + 1 + step < n

    def launch(make, step):
        for side in (0, 1):

            @pl.when(sends(step, side))
            def _():
                make(step, side).start()

    def await_hop(make, step):
        for side in (0, 1):

            @pl.when(arrives(step, side))
            def _():
                make(step, side).wait_recv()

    def drain(make):
        for step in range(n - 1):
            for side in (0, 1):

                @pl.when(sends(step, side))
                def _():
                    make(step, side).wait_send()

    def chunk(j):
        return lambda step, side: hop(j, step, side)

    @pl.when(pair == 0)
    def _():
        unit, _ = normed(tokens_ref)
        first_norm = (unit * gain_ref[0:1, :]).astype(BF)
        cosine, sine = cosine_ref[...], sine_ref[...]
        count = kv_ref.shape[0]
        query_width = count * width
        key_width = query_width // 2
        keys = dot(first_norm, weight_ref[:, query_width : query_width + key_width])
        values = dot(first_norm, weight_ref[:, query_width + key_width :])
        for j in range(count):
            columns = slice(j * LANES, (j + 1) * LANES)
            kv_ref[j, :, :LANES] = rotate(keys[:, columns], cosine, sine).astype(BF)
            kv_ref[j, :, LANES:] = values[:, columns].astype(BF)
        greet([(me > 0, left), (me < n - 1, right)])
        launch(chunk(0), 0)
        launch(chunk(1), 0)
        routes = routes_ref[...].astype(F32).T
        expert_id = lax.broadcasted_iota(jnp.int32, (EXPERTS, rows), 0).astype(F32)
        hot = jnp.zeros((EXPERTS, rows), F32)
        for k in range(TOP):
            hot = jnp.where(routes[k : k + 1, :] == expert_id, 1.0, hot)
        row_id = lax.broadcasted_iota(jnp.int32, (rows, rows), 0)
        earlier = jnp.where(row_id < lax.broadcasted_iota(jnp.int32, (rows, rows), 1), 1.0, 0.0)
        rank = dot(hot.astype(BF), earlier.astype(BF))
        rank_buffer[me] = jnp.where(hot > 0.5, rank, 255.0).astype(BF)
        queries = dot(first_norm, weight_ref[:, :query_width])
        for j in range(2 * count):
            start = (j % 2) * LANES
            tile = queries[:, j * LANES : (j + 1) * LANES]
            query_ref[j // 2, :, start : start + LANES] = rotate(tile, cosine, sine).astype(BF)
        mask_bias(bias_ref, length_ref, rows)
        await_hop(chunk(0), 0)
        launch(chunk(0), 1)

    for step in range(1, n - 1):
        await_hop(chunk(pair), step)
        if step < n - 2:
            launch(chunk(pair), step + 1)

    @pl.when(pair + 1 < pairs)
    def _():
        await_hop(chunk(pair + 1), 0)
        launch(chunk(pair + 1), 1)

    @pl.when(pair + 2 < pairs)
    def _():
        launch(chunk(pair + 2), 0)

    @pl.when(pair == 1)
    def _():
        launch(rank_hop, 0)

    for step in range(n - 1):

        @pl.when(pair == jnp.minimum(2 + step, pairs - 1))
        def _():
            await_hop(rank_hop, step)
            if step < n - 2:
                launch(rank_hop, step + 1)

    chunk_ref[pair, me] = kv_ref[pair]
    kv = chunk_ref[pair].reshape(n * rows, width)
    kv_all_ref[...] = kv
    query_out_ref[0] = query_ref[pair]
    bias = jnp.concatenate([bias_ref[...]] * 2, axis=1)
    for head in (0, 1):
        start = head * HEAD_DIMENSION
        key = kv[:, start : start + HEAD_DIMENSION]
        value = kv[:, LANES + start : LANES + start + HEAD_DIMENSION]
        query = head_columns(query_ref.at[pair], head) * jnp.asarray(HEAD_DIMENSION**-0.5, BF)
        scores = dot_nt(key, query) + bias
        top = jnp.max(scores, axis=0, keepdims=True)
        weights = jnp.exp(scores - top)
        total = jnp.sum(weights, axis=0, keepdims=True)
        put_heads(mixed_ref, head, dot_tn(value, weights.astype(BF)) / total)
        log_total_ref[0, head : head + 1, :] = top + jnp.log(total)

    @pl.when(pair == pairs - 1)
    def _():
        drain(rank_hop)
        rank_all_ref[...] = rank_buffer[...]
        for j in range(KEY_VALUE_HEADS // 2):
            drain(chunk(j))


def attention(length, tokens, gain, weight, cosine, sine, routes, n, collective_id):
    rows = tokens.shape[0]
    rank = jax.ShapeDtypeStruct((EXPERTS, rows), BF)
    keys, width = n * rows, 2 * LANES
    pairs = KEY_VALUE_HEADS // 2
    return pl.pallas_call(
        functools.partial(attention_kernel, n),
        grid=(pairs,),
        out_shape=(
            jax.ShapeDtypeStruct((rows, pairs * width), BF),
            jax.ShapeDtypeStruct((pairs, 2, 2 * rows), F32),
            jax.ShapeDtypeStruct((keys, pairs * width), BF),
            jax.ShapeDtypeStruct((pairs, rows, width), BF),
            jax.ShapeDtypeStruct((n,) + rank.shape, rank.dtype),
        ),
        in_specs=[pl.BlockSpec(memory_space=pltpu.SMEM)] + [IN_VMEM] * 6,
        out_specs=(
            pl.BlockSpec((rows, width), lambda j: (0, j)),
            pl.BlockSpec((1, 2, 2 * rows), lambda j: (j, 0, 0)),
            pl.BlockSpec((keys, width), lambda j: (0, j)),
            pl.BlockSpec((1, rows, width), lambda j: (j, 0, 0)),
            IN_VMEM,
        ),
        scratch_shapes=[
            pltpu.VMEM((keys, rows), F32),
            pltpu.VMEM((pairs, rows, width), BF),
            pltpu.VMEM((pairs, rows, width), BF),
            pltpu.VMEM((pairs, n, rows, width), BF),
            pltpu.VMEM((n,) + rank.shape, rank.dtype),
            pltpu.SemaphoreType.DMA((pairs, 2, n - 1)),
            pltpu.SemaphoreType.DMA((pairs, 2, n - 1)),
            pltpu.SemaphoreType.DMA((2, n - 1)),
            pltpu.SemaphoreType.DMA((2, n - 1)),
        ],
        compiler_params=pltpu.CompilerParams(
            dimension_semantics=("arbitrary",),
            vmem_limit_bytes=56 * 1024 * 1024,
            collective_id=collective_id,
            has_side_effects=True,
        ),
        cost_estimate=pl.CostEstimate(
            flops=16 * rows * keys * D, bytes_accessed=100000000, transcendentals=0
        ),
        name="attention",
    )(length, tokens, gain, weight, cosine, sine, routes)


def attention_back_kernel(
    n,
    length_ref,
    q_ref,
    kv_ref,
    log_total_ref,
    gs_ref,
    residual_ref,
    second_ref,
    ct_ref,
    routes_ref,
    gain_ref,
    router_ref,
    out_weight_ref,
    grad_q_ref,
    grad_kv_ref,
    grad_residual_ref,
    grad_attn_ref,
    grad_router_ref,
    grad_gain_ref,
    bias_ref,
    grad_ref,
    terms_ref,
    landing,
    staging,
    send,
    recv,
):
    step, pairs = pl.program_id(0), pl.num_programs(0) - 1

    def line(j):
        return LineSum(
            n, terms_ref.at[j], landing.at[j], staging.at[j], send.at[j], recv.at[j]
        )

    @pl.when(step == 0)
    def _():
        greet(line(0).neighbours())
        mask_bias(bias_ref, length_ref, q_ref.shape[1])
        routes = routes_ref[...]
        expert_id = lax.broadcasted_iota(jnp.int32, (routes.shape[0], EXPERTS), 1)
        hot = expert_id == routes[:, 0:1]
        for k in range(1, TOP):
            hot = hot | (expert_id == routes[:, k : k + 1])
        second, router = second_ref[...], router_ref[:, :EXPERTS]
        logits = dot(second, router)
        top = jnp.max(jnp.where(hot, logits, NEGATIVE_LARGE), axis=-1, keepdims=True)
        weight = jnp.where(hot, jnp.exp(jnp.minimum(logits - top, 0.0)), 0.0)
        gates = weight / jnp.sum(weight, axis=-1, keepdims=True)
        grad_gates = gs_ref[:, D : D + EXPERTS] + gs_ref[:, D + EXPERTS : D + 2 * EXPERTS]
        grad_gates = grad_gates + gs_ref[:, D + 2 * EXPERTS : D + 3 * EXPERTS]
        mean = jnp.sum(gates * grad_gates, axis=-1, keepdims=True)
        grad_logits = (gates * (grad_gates - mean)).astype(BF)
        grad_second = gs_ref[:, :D] + dot_nt(grad_logits, router)
        grad_router_ref[...] = jnp.zeros_like(grad_router_ref)
        grad_router_ref[:, :EXPERTS] = dot_tn(second, grad_logits)
        unit, inverse = normed(residual_ref)
        grad_gain_ref[...] = jnp.sum(grad_second * unit, axis=0, keepdims=True)
        scaled = grad_second * gain_ref[1:2, :]
        mean = jnp.mean(scaled * unit, axis=-1, keepdims=True)
        grad_residual = ct_ref[...].astype(F32) + inverse * (scaled - unit * mean)
        grad_residual_ref[...] = grad_residual
        grad_attn_ref[...] = grad_residual.astype(BF)
        grad_mixed = dot_nt(grad_residual.astype(BF), out_weight_ref[...]).astype(BF)
        width = grad_ref.shape[2]
        for j in range(grad_ref.shape[0]):
            grad_ref[j] = grad_mixed[:, j * width : (j + 1) * width]

    @pl.when(step < pairs)
    def _():
        attention_back_pair(
            q_ref, kv_ref, grad_ref.at[step], log_total_ref, grad_q_ref, terms_ref.at[step], bias_ref
        )
        line(step).start()

    @pl.when(step > 0)
    def _():
        for hop in range(1, n - 1):
            line(step - 1).forward(hop)
        line(step - 1).finish(grad_kv_ref)


def attention_back_pair(q_ref, kv_ref, grad_ref, log_total_ref, grad_q_ref, grad_kv_ref, bias_ref):
    scale = HEAD_DIMENSION**-0.5
    blocks, rows, _ = grad_kv_ref.shape
    q_ref = q_ref.at[0]
    bias = jnp.concatenate([bias_ref[...]] * 2, axis=1)
    for head in (0, 1):
        columns = slice(head * HEAD_DIMENSION, (head + 1) * HEAD_DIMENSION)
        key, value = kv_ref[:, :LANES][:, columns], kv_ref[:, LANES:][:, columns]
        query = head_columns(q_ref, head) * jnp.asarray(scale, BF)
        grad = head_columns(grad_ref, head)
        scores = dot_nt(key, query) + bias
        probs = jnp.exp(scores - log_total_ref[0, head : head + 1, :])
        grad_probs = dot_nt(value, grad)
        delta = jnp.sum(probs * grad_probs, axis=0, keepdims=True)
        grad_scores = (probs * (grad_probs - delta)).astype(BF)
        grad_key = dot(grad_scores, query).astype(BF).reshape(blocks, rows, HEAD_DIMENSION)
        grad_kv_ref[:, :, columns] = grad_key
        grad_value = dot(probs.astype(BF), grad).astype(BF).reshape(blocks, rows, HEAD_DIMENSION)
        start = LANES + head * HEAD_DIMENSION
        grad_kv_ref[:, :, start : start + HEAD_DIMENSION] = grad_value
        put_heads(grad_q_ref, head, dot_tn(key, grad_scores) * scale)


def attention_back(length, query, kv_all, log_total, sources, n, collective_id):
    rows, keys = query.shape[1], kv_all.shape[0]
    pairs, width = KEY_VALUE_HEADS // 2, 2 * LANES
    now = lambda j: jnp.minimum(j, pairs - 1)
    row_spec = pl.BlockSpec((rows, width), lambda j: (0, now(j)))
    return pl.pallas_call(
        functools.partial(attention_back_kernel, n),
        grid=(pairs + 1,),
        out_shape=(
            jax.ShapeDtypeStruct((rows, pairs * width), F32),
            jax.ShapeDtypeStruct((rows, pairs * width), BF),
            jax.ShapeDtypeStruct((rows, D), F32),
            jax.ShapeDtypeStruct((rows, D), BF),
            jax.ShapeDtypeStruct((D, LANES), F32),
            jax.ShapeDtypeStruct((1, D), F32),
        ),
        in_specs=[
            pl.BlockSpec(memory_space=pltpu.SMEM),
            pl.BlockSpec((1, rows, width), lambda j: (now(j), 0, 0)),
            pl.BlockSpec((keys, width), lambda j: (0, now(j))),
            pl.BlockSpec((1, 2, 2 * rows), lambda j: (now(j), 0, 0)),
        ]
        + [IN_VMEM] * len(sources),
        out_specs=(
            row_spec,
            pl.BlockSpec((rows, width), lambda j: (0, jnp.maximum(j - 1, 0))),
        )
        + (IN_VMEM,) * 4,
        scratch_shapes=[
            pltpu.VMEM((keys, rows), F32),
            pltpu.VMEM((pairs, rows, width), BF),
            pltpu.VMEM((pairs, n, rows, width), BF),
            pltpu.VMEM((pairs, 2, n - 1, rows, width), BF),
            pltpu.VMEM((pairs, 2, n - 2, rows, width), BF),
            pltpu.SemaphoreType.DMA((pairs, 2, n - 1)),
            pltpu.SemaphoreType.DMA((pairs, 2, n - 1)),
        ],
        compiler_params=pltpu.CompilerParams(
            dimension_semantics=("arbitrary",),
            vmem_limit_bytes=60 * 1024 * 1024,
            collective_id=collective_id,
            has_side_effects=True,
        ),
        cost_estimate=pl.CostEstimate(
            flops=40 * rows * keys * D, bytes_accessed=100000000, transcendentals=0
        ),
        name="attention_back",
    )(length, query, kv_all, log_total, *sources)


def widen_kernel(value_ref, out_ref):
    out_ref[...] = value_ref[...].astype(F32)


def widen(value):
    block = (1,) + value.shape[1:]
    spec = pl.BlockSpec(block, lambda e: (e, 0, 0))
    return pl.pallas_call(
        widen_kernel,
        grid=(value.shape[0],),
        out_shape=jax.ShapeDtypeStruct(value.shape, F32),
        in_specs=[spec],
        out_specs=spec,
        compiler_params=pltpu.CompilerParams(dimension_semantics=("arbitrary",)),
        cost_estimate=pl.CostEstimate(flops=0, bytes_accessed=6 * value.size, transcendentals=0),
        name="widen",
    )(value)


def unpair_columns(value):
    rows = value.shape[0]
    value = value.reshape(rows, -1, 2, LANES)
    return value[:, :, 0].reshape(rows, -1), value[:, :, 1].reshape(rows, -1)


def gather_rows(value):
    return lax.all_gather(value, "expert", axis=0, tiled=True)


def scatter_rows(value):
    return lax.psum_scatter(value, "expert", scatter_dimension=0, tiled=True)


def per_device(
    tokens,
    lengths,
    routes,
    norm_gain1,
    w_query,
    key_projection,
    value_projection,
    w_out,
    norm_gain2,
    w_router,
    w_gate,
    w_up,
    w_down,
    cotangent,
):
    rows = tokens.shape[0]
    n, groups = lax.axis_size("expert"), lax.axis_size("group")
    plane = groups == 8 and w_gate.shape[0] == 8
    my_index = lax.axis_index("expert")
    capacity = 3 * rows * TOP // (2 * EXPERTS)
    query_width, key_width = w_query.shape[1], key_projection.shape[1]
    length = lengths[0]
    positions = my_index * rows + jnp.arange(rows, dtype=jnp.int32)
    valid_rows = (positions < length)[:, None]
    grad_output = jnp.where(valid_rows, cotangent, jnp.zeros_like(cotangent))

    small = jnp.pad(w_router, ((0, 0), (0, LANES - EXPERTS)))
    gains = jnp.pad(jnp.concatenate([norm_gain1, norm_gain2]), (0, D - 2 * norm_gain1.shape[0]))
    below = jnp.broadcast_to(gains, (16, D))
    qkv_weight, out_weight, router, extra_all = gather_weights(
        w_query,
        key_projection,
        value_projection,
        w_out,
        small,
        jnp.concatenate([grad_output, below], axis=0),
        n,
        1,
    )
    extra_all = extra_all.reshape(n, rows + 16, D)
    gains = extra_all[:, rows, : 2 * norm_gain1.shape[0]].reshape(n, 2, -1)
    gains = jnp.transpose(gains, (1, 0, 2)).reshape(2, D).astype(F32)

    cosine_lookup, sine_lookup = [table[:, 0] for table in rotary_tables(positions, HEAD_DIMENSION)]
    cosine = jnp.tile(cosine_lookup, (1, 4))
    sine = jnp.tile(jnp.concatenate([-sine_lookup, sine_lookup], axis=1), (1, 2))
    token_f32 = tokens.astype(F32)
    mixed_low, log_total, kv_all, query_pairs, rank_all = attention(
        lengths, tokens, gains, qkv_weight, cosine, sine, routes, n, 2
    )
    expert_args = (extra_all, router, rank_all, w_gate, w_up, w_down, capacity)
    if plane:
        sources = (mixed_low, tokens, out_weight, gains)
        y_part, gs, grad_gate, grad_up, grad_down, second_norm, residual = run_experts(
            sources, *expert_args, plane, 7
        )
    else:
        residual = token_f32 + dot(mixed_low, out_weight)
        inverse_two = lax.rsqrt(jnp.mean(residual * residual, axis=-1, keepdims=True) + EPSILON)
        second_norm = (residual * inverse_two * gains[1]).astype(BF)
        sources = line_gather([second_norm], n, 3, "gather_rows")
        y_part, gs, grad_gate, grad_up, grad_down = run_experts(sources, *expert_args, plane, 7)
        gs = line_scatter(gs, n, F32, 4, "scatter_grads")

    sources = (
        gs,
        residual,
        second_norm,
        grad_output,
        routes,
        gains,
        router,
        out_weight,
    )
    grad_query_acc, kv_gradient, grad_residual, grad_attn, grad_router, gain_two_row = (
        attention_back(lengths, query_pairs, kv_all, log_total, sources, n, 5)
    )
    if plane:
        *shares, expert_sum, grad_rest = reduce_weights(
            grad_query_acc,
            kv_gradient,
            tokens,
            gains,
            qkv_weight,
            cosine,
            sine,
            mixed_low,
            grad_attn,
            grad_router,
            gain_two_row,
            y_part,
            n,
            6,
        )
        grad_tokens = grad_residual + grad_rest
    else:
        inverse_one = lax.rsqrt(jnp.mean(token_f32 * token_f32, axis=-1, keepdims=True) + EPSILON)
        unit_one = token_f32 * inverse_one
        first_norm = (unit_one * gains[0]).astype(BF)
        own_key_gradient, own_value_gradient = unpair_columns(kv_gradient)
        back = lambda value: apply_rotation(
            value.astype(F32).reshape(rows, -1, HEAD_DIMENSION),
            cosine_lookup[:, None],
            -sine_lookup[:, None],
        )
        grad_query_pre = back(grad_query_acc).reshape(rows, query_width).astype(BF)
        grad_key_pre = back(own_key_gradient).reshape(rows, key_width).astype(BF)
        grad_qkv_pre = jnp.concatenate([grad_query_pre, grad_key_pre, own_value_gradient], axis=1)
        grad_first = dot_nt(grad_qkv_pre, qkv_weight)
        scaled_one = grad_first * gains[0]
        grad_gain1 = jnp.sum(grad_first * unit_one, axis=0)
        grad_tokens = grad_residual + inverse_one * (
            scaled_one - unit_one * jnp.mean(scaled_one * unit_one, axis=-1, keepdims=True)
        )
        gains = [grad_gain1[:, None], gain_two_row.T]
        rest = grad_router[:, EXPERTS + 2 :]
        grad_small = jnp.concatenate([grad_router[:, :EXPERTS]] + gains + [rest], axis=1)
        shares = (dot_tn(first_norm, grad_qkv_pre), dot_tn(mixed_low, grad_attn), grad_small)
        shares = [lax.psum(scatter_rows(share.astype(BF)), "group") for share in shares]
        share_qkv, share_out, share_small = shares
        split = (query_width, query_width + key_width)
        shares = jnp.split(share_qkv, split, axis=1) + [share_out, share_small]
        expert_sum = line_scatter(y_part, n, F32, 8, "scatter_outputs")
    mixed = (residual + expert_sum).astype(BF)
    shares = [share.astype(F32) for share in shares]
    share_query, share_key, share_value, share_out, share_small = shares

    def sum_over_groups(value):
        if not plane:
            value = lax.psum_scatter(value, "group", scatter_dimension=1, tiled=True)
        return widen(lax.all_gather(value, "group", axis=1, tiled=True))

    return (
        mixed,
        grad_tokens,
        share_small[:, EXPERTS],
        share_query,
        share_key,
        share_value,
        share_out,
        share_small[:, EXPERTS + 1],
        share_small[:, :EXPERTS],
        sum_over_groups(grad_gate),
        sum_over_groups(grad_up),
        sum_over_groups(grad_down),
    )


def solution(mesh):
    rows = P(("group", "expert"), None)
    vector, matrix, stack = P("expert"), P("expert", None), P("expert", None, None)
    return jax.shard_map(
        per_device,
        mesh=mesh,
        in_specs=(
            rows,
            P("group"),
            rows,
            vector,
            matrix,
            matrix,
            matrix,
            matrix,
            vector,
            matrix,
            stack,
            stack,
            stack,
            rows,
        ),
        out_specs=(
            rows,
            rows,
            vector,
            matrix,
            matrix,
            matrix,
            matrix,
            vector,
            matrix,
            stack,
            stack,
            stack,
        ),
        check_vma=False,
    )
```
